32 devices in a mesh: ctx: 16 (over z, y, x), fsdp: 2 (over core).
Axes of the slice: x: 2, y: 2, z: 4, core: 2. Of those that a mesh axis runs over, the one named last changes fastest.
Arguments:
- stream: bfloat16 [2, 4096, 768], P('fsdp', 'ctx'), may hold values from -6 to 6
- doc_starts: int32 [2, 8], P('fsdp'), may hold values from 0 to 4095, as said below
- ln1_gain: bfloat16 [768], P('fsdp'), may hold values from 0.5 to 1.5
- ln1_bias: bfloat16 [768], P('fsdp'), may hold values from -3 to 3
- qkv_weight: bfloat16 [768, 2304], P('fsdp'), may hold values from -0.21875 to 0.21875
- q_bias: bfloat16 [768], P('fsdp'), may hold values from -4 to 4
- v_bias: bfloat16 [768], P('fsdp'), may hold values from -2 to 2
- out_weight: bfloat16 [768, 768], P('fsdp'), may hold values from -0.625 to 0.625
- out_bias: bfloat16 [768], P('fsdp'), may hold values from -3 to 3
- ln2_gain: bfloat16 [768], P('fsdp'), may hold values from 0.5 to 1.5
- ln2_bias: bfloat16 [768], P('fsdp'), may hold values from -3 to 3
- fc1_weight: bfloat16 [768, 3072], P('fsdp'), may hold values from -0.21875 to 0.21875
- fc1_bias: bfloat16 [3072], P('fsdp'), may hold values from -4 to 4
- fc2_weight: bfloat16 [3072, 768], P('fsdp'), may hold values from -0.109375 to 0.109375
- fc2_bias: bfloat16 [768], P('fsdp'), may hold values from -3 to 3
- cotangent: bfloat16 [2, 4096, 768], P('fsdp', 'ctx'), may hold values from -6 to 6
Outputs:
- layer_out: bfloat16 [2, 4096, 768], P('fsdp', 'ctx')
- input_grad: float32 [2, 4096, 768], P('fsdp', 'ctx')
- ln1_gain_grad: float32 [768], P('fsdp')
- ln1_bias_grad: float32 [768], P('fsdp')
- qkv_weight_grad: float32 [768, 2304], P('fsdp')
- q_bias_grad: float32 [768], P('fsdp')
- v_bias_grad: float32 [768], P('fsdp')
- out_weight_grad: float32 [768, 768], P('fsdp')
- out_bias_grad: float32 [768], P('fsdp')
- ln2_gain_grad: float32 [768], P('fsdp')
- ln2_bias_grad: float32 [768], P('fsdp')
- fc1_weight_grad: float32 [768, 3072], P('fsdp')
- fc1_bias_grad: float32 [3072], P('fsdp')
- fc2_weight_grad: float32 [3072, 768], P('fsdp')
- fc2_bias_grad: float32 [768], P('fsdp')
The draws below stay inside these ranges and needn't reach their ends.
Inputs may be any that keep to these rules, and one draw needn't show every extreme that they name: `doc_starts`: each row starts with 0 and rises strictly. A document runs from its start to the next one (the last to 4096) in position order. Every document has at most 2048 positions, and either the first or the last document has exactly 2048. Some stream's last document starts at 4095.
All inputs are finite; a program needn't handle non-finite values.
Results may differ from the reference program's by a relative error of at most 0.02.
Values may be sent and summed in bfloat16 or wider, within the bound.
A program may use at most 320 MiB of HBM per device.

```python
import jax
import jax.numpy as jnp
from jax import lax

D = 768
H = 12
HD = 64
FF = 3072
DOCS = 8
LEN = 4096
STREAMS = 2
N_CTX = 16


def stream_starts(key, first_side, stream_index):
    half_len = LEN // 2
    picks = jax.random.permutation(jax.random.fold_in(key, 11), half_len - 2)[:DOCS - 3] + 1
    ending_cut = jnp.full((1,), half_len - 1, jnp.int32)
    cut_points = jnp.sort(jnp.concatenate([picks.astype(jnp.int32), ending_cut])).astype(jnp.int32)
    long_side = (first_side + stream_index) % 2
    zero_start = jnp.zeros((1,), jnp.int32)
    mid_start = jnp.full((1,), half_len, jnp.int32)
    long_second = jnp.concatenate([zero_start, cut_points, mid_start])
    long_first = jnp.concatenate([zero_start, mid_start, cut_points + half_len])
    return jnp.where(long_side == 0, long_second, long_first).astype(jnp.int32)


def draw_doc_starts(key, part):
    stream_keys = jax.random.split(key, STREAMS)
    first_side = jax.random.randint(jax.random.fold_in(key, 13), (), 0, 2).astype(jnp.int32)
    indices = jnp.arange(STREAMS, dtype=jnp.int32)
    return jax.vmap(lambda one_key, index: stream_starts(one_key, first_side, index))(stream_keys, indices).astype(jnp.int32)


def shard_levels(own_key, shape, cuts, low, largest):
    def one(axis_at, shards_of):
        heights = jax.random.uniform(jax.random.fold_in(jax.random.fold_in(own_key, 6), axis_at), (shards_of,), jnp.float32, low / len(cuts), largest / len(cuts))
        return jnp.repeat(jnp.exp(heights), shape[axis_at] // shards_of).reshape((-1,) + (1,) * (len(shape) - axis_at - 1))

    factor_of = one(*cuts[0])
    for cut in cuts[1:]:
        factor_of = factor_of * one(*cut)
    return factor_of


def gaussian(stream_key, extent, deviation, most, pieces=(), kind=jnp.bfloat16):
    entries = deviation * jax.random.normal(stream_key, extent, jnp.float32)
    if pieces:
        entries = entries * shard_levels(stream_key, extent, pieces, -0.22, 0.18)
    return jnp.clip(entries, -most, most).astype(kind)


def setup_inputs(seed: int = 0) -> dict:
    key_list = jax.random.split(jax.random.key(seed), 17)
    stream = gaussian(key_list[0], (STREAMS, LEN, D), 1.0, 6.0, ((0, 2), (1, 16)))
    doc_starts = draw_doc_starts(jax.random.fold_in(key_list[16], 71), 0)
    ln1_gain = jnp.clip(1.0 + 0.1 * jax.random.normal(key_list[2], (D,), jnp.float32), 0.5, 1.5).astype(jnp.bfloat16)
    ln1_bias = gaussian(key_list[3], (D,), 0.3, 3.0, ((0, 2),))
    qkv_weight = gaussian(key_list[4], (D, 3 * D), D ** -0.5, 0.21875, ((0, 2),))
    q_bias = gaussian(key_list[5], (D,), 0.5, 4.0, ((0, 2),))
    v_bias = gaussian(key_list[6], (D,), 0.2, 2.0, ((0, 2),))
    out_weight = gaussian(key_list[7], (D, D), (D // 8) ** -0.5, 0.625, ((0, 2),))
    out_bias = gaussian(key_list[8], (D,), 0.3, 3.0, ((0, 2),))
    ln2_gain = jnp.clip(1.0 + 0.1 * jax.random.normal(key_list[9], (D,), jnp.float32), 0.5, 1.5).astype(jnp.bfloat16)
    ln2_bias = gaussian(key_list[10], (D,), 0.3, 3.0, ((0, 2),))
    fc1_weight = gaussian(key_list[11], (D, FF), D ** -0.5, 0.21875, ((0, 2),))
    fc1_bias = gaussian(key_list[12], (FF,), 0.5, 4.0, ((0, 2),))
    fc2_weight = gaussian(key_list[13], (FF, D), FF ** -0.5, 0.109375, ((0, 2),))
    fc2_bias = gaussian(key_list[14], (D,), 0.3, 3.0, ((0, 2),))
    cotangent = gaussian(key_list[15], (STREAMS, LEN, D), 1.0, 6.0, ((0, 2), (1, 16)))
    return {"stream": stream, "doc_starts": doc_starts, "ln1_gain": ln1_gain, "ln1_bias": ln1_bias, "qkv_weight": qkv_weight, "q_bias": q_bias, "v_bias": v_bias, "out_weight": out_weight, "out_bias": out_bias, "ln2_gain": ln2_gain, "ln2_bias": ln2_bias, "fc1_weight": fc1_weight, "fc1_bias": fc1_bias, "fc2_weight": fc2_weight, "fc2_bias": fc2_bias, "cotangent": cotangent}


@jax.custom_vjp
def low(v):
    return lax.optimization_barrier(v.astype(jnp.bfloat16)).astype(jnp.float32)

@jax.custom_vjp
def low_back(v):
    return v

def low_keep(v):
    return (low(v), None)

def low_pass(kept, grad):
    return (grad,)

def back_keep(v):
    return (v, None)

def back_low(kept, grad):
    return (low(grad),)
low.defvjp(low_keep, low_pass)
low_back.defvjp(back_keep, back_low)
EPS = 1e-05
NEG = -1e+30
HIGH = lax.Precision.HIGHEST

def layer_norm(values, gain, shift):
    center = values - lax.optimization_barrier(jnp.mean(values, axis=-1, keepdims=True))
    spread = lax.optimization_barrier(jnp.mean(center * center, axis=-1, keepdims=True))
    return center * lax.rsqrt(spread + EPS) * gain + shift

def stream_places(starts):
    blk_rows = LEN // (2 * N_CTX)
    row_ids = jnp.arange(LEN, dtype=jnp.int32)
    owner_dev = row_ids // (2 * blk_rows)
    within = row_ids % (2 * blk_rows)
    positions = jnp.where(within < blk_rows, owner_dev * blk_rows + within, (2 * N_CTX - 1 - owner_dev) * blk_rows + within - blk_rows).astype(jnp.int32)
    doc_ids = (lax.optimization_barrier(jnp.sum((starts[None, :] <= positions[:, None]).astype(jnp.int32), axis=1)) - 1).astype(jnp.int32)
    return (positions, doc_ids)

def attend(query, keys, values, positions, doc_ids):
    block_rows = 2 * (LEN // (2 * N_CTX))
    blocks = LEN // block_rows
    scale = HD ** (-0.5)

    def one_block(block_args):
        q_block, q_pos, q_doc = block_args
        scores = low_back(jnp.einsum('qhd,khd->hqk', q_block, keys, precision=HIGH) * scale)
        allowed = (doc_ids[None, :] == q_doc[:, None]) & (positions[None, :] <= q_pos[:, None])
        scores = jnp.where(allowed[None], scores, NEG)
        shifted = jnp.exp(scores - lax.optimization_barrier(jnp.max(scores, axis=-1, keepdims=True)))
        probs = shifted / lax.optimization_barrier(jnp.sum(shifted, axis=-1, keepdims=True))
        return jnp.einsum('hqk,khd->qhd', low(probs), values, precision=HIGH)
    mixed = lax.map(jax.checkpoint(one_block), (query.reshape(blocks, block_rows, H, HD), positions.reshape(blocks, block_rows), doc_ids.reshape(blocks, block_rows)))
    return mixed.reshape(LEN, H * HD)

def one_stream(inputs, starts, params):
    g_one, b_one, w_qkv, q_shift, v_shift, w_out, o_shift, g_two, b_two, w_fc1, c_fc1, w_fc2, c_fc2 = params
    positions, doc_ids = stream_places(starts)
    normed_in = low(layer_norm(inputs, g_one, b_one))
    shift_qkv = jnp.concatenate([q_shift, jnp.zeros_like(q_shift), v_shift])
    projected = jnp.dot(normed_in, w_qkv, precision=HIGH) + shift_qkv
    query = low(low_back(projected[:, :D])).reshape(LEN, H, HD)
    keys = low(low_back(projected[:, D:2 * D])).reshape(LEN, H, HD)
    values = low(low_back(projected[:, 2 * D:])).reshape(LEN, H, HD)
    attn_f = attend(query, keys, values, positions, doc_ids)
    attn = low(low_back(attn_f))
    branch = low_back(jnp.dot(attn, w_out, precision=HIGH) + o_shift)
    hidden = inputs + branch
    normed_mid = low(layer_norm(hidden, g_two, b_two))
    pre_act = low_back(jnp.dot(normed_mid, w_fc1, precision=HIGH) + c_fc1)
    activ = low(jax.nn.gelu(pre_act, approximate=True))
    return hidden + jnp.dot(activ, w_fc2, precision=HIGH) + c_fc2

def reference(stream, doc_starts, ln1_gain, ln1_bias, qkv_weight, q_bias, v_bias, out_weight, out_bias, ln2_gain, ln2_bias, fc1_weight, fc1_bias, fc2_weight, fc2_bias, cotangent):
    params = tuple((p_arg.astype(jnp.float32) for p_arg in (ln1_gain, ln1_bias, qkv_weight, q_bias, v_bias, out_weight, out_bias, ln2_gain, ln2_bias, fc1_weight, fc1_bias, fc2_weight, fc2_bias)))
    inputs = stream.astype(jnp.float32)

    def forward(all_inputs, *weights):
        return lax.map(lambda pair: one_stream(pair[0], pair[1], weights), (all_inputs, doc_starts))
    result, pull = jax.vjp(forward, inputs, *params)
    grads = pull(cotangent.astype(jnp.float32))
    return (result.astype(jnp.bfloat16), grads[0], grads[1], grads[2], grads[3], grads[4], grads[5], grads[6], grads[7], grads[8], grads[9], grads[10], grads[11], grads[12], grads[13])
```

```python
import functools

import jax
import jax.numpy as jnp
from jax import lax
from jax.experimental import pallas as pl
from jax.experimental.pallas import tpu as pltpu
from jax.sharding import PartitionSpec as P

H = 12
HD = 64
MESH = pl.DeviceIdType.MESH
BF = jnp.bfloat16
F32 = jnp.float32


def ring_of(ctx, n):
    g = ctx // 2
    return jnp.where(g % 2 == 0, g // 2, n - 1 - g // 2)

def ring_ctx(r, n, bit):
    r = lax.rem(r + n, n)
    g = jnp.where(r < n // 2, 2 * r, 2 * (n - 1 - r) + 1)
    return g * 2 + bit

def grads_kernel(n, fs, s_one, s_two, subs, g_ref, v_ref, out_ref, vout_ref,
                 acc, fbuf, xbuf1, rbuf1, xbuf2, rbuf2, outb,
                 vacc, vf, vx, vr,
                 lsem, fsem, frec, xs, xr, rs, rr, vfs, vfr, vxs, vxr, vrs, vrr, osem):
    c = lax.axis_index("ctx")
    f = lax.axis_index("fsdp")
    bit = c % 2
    pos = ring_of(c, n)
    xpeer = (c + 1 - 2 * bit, f)
    right = (ring_ctx(pos + 1, n, bit), f)
    left = (ring_ctx(pos - 1, n, bit), f)
    rows = s_one + s_two
    half = g_ref.shape[2] // 2
    lanes = (pl.ds(0, half), pl.ds(half, half))
    fpeers = [(c, lax.rem(f + k, fs)) for k in range(1, fs)]
    barrier = pltpu.get_barrier_semaphore()
    for peer in [xpeer, right, left] + fpeers:
        pl.semaphore_signal(barrier, inc=1, device_id=peer, device_id_type=MESH)
    pl.semaphore_wait(barrier, 2 + fs)

    def remote(src, dst, ssem, rsem, peer):
        cp = pltpu.make_async_remote_copy(src_ref=src, dst_ref=dst, send_sem=ssem, recv_sem=rsem,
                                          device_id=peer, device_id_type=MESH)
        return cp

    pend = []

    def go(cp):
        cp.start()
        pend.append(cp)
        return cp
    own = pltpu.make_async_copy(g_ref.at[f], acc, lsem.at[0])
    own.start()
    vown = pltpu.make_async_copy(v_ref.at[f], vacc, lsem.at[1])
    vown.start()
    fcs = []
    parts = ((s_one, s_two), (0, s_one))
    for k in range(1, fs):
        peer = fpeers[k - 1]
        for j, (a, m) in enumerate(parts):
            fcs.append(go(remote(g_ref.at[peer[1], pl.ds(a, m)], fbuf.at[k - 1, pl.ds(a, m)],
                                 fsem.at[k - 1, j], frec.at[k - 1, j], peer)))
        fcs.append(go(remote(v_ref.at[peer[1]], vf.at[k - 1], vfs.at[k - 1], vfr.at[k - 1], peer)))
    own.wait()
    vown.wait()

    def fadd(a, m):
        blk = 32

        @pl.loop(0, m // blk)
        def _(i):
            rws = pl.ds(pl.multiple_of(a + i * blk, blk), blk)
            tot = acc[rws, :].astype(F32)
            for k in range(fs - 1):
                tot = tot + fbuf[k, rws, :].astype(F32)
            acc[rws, :] = tot.astype(BF)

    for k in range(1, fs):
        fcs[3 * (k - 1)].wait_recv()
    fadd(s_one, s_two)

    chunk2 = s_two // n
    sub2 = chunk2 // subs
    h1 = s_one // 2
    chunk1 = h1 // n
    sub1 = chunk1 // subs

    def rows_of(base, chunk, k, sub, j):
        k = lax.rem(k + 2 * n, n)
        return pl.ds(pl.multiple_of(base + k * chunk + j * sub, 16), sub)

    def rs_send(st, base, chunk, sub, rbuf, s, j):
        for d in range(2):
            k = pos - 1 - s if d == 0 else pos + 1 + s
            go(remote(acc.at[rows_of(base, chunk, k, sub, j), lanes[d]],
                      rbuf.at[s, pl.ds(j * sub, sub), lanes[d]],
                      rs.at[st, 0, d, s, j], rr.at[st, 0, d, s, j], right if d == 0 else left))

    def rs_recv(st, base, chunk, sub, rbuf, s, j):
        for d in range(2):
            k = pos - 2 - s if d == 0 else pos + 2 + s
            rws = rows_of(base, chunk, k, sub, j)
            cp = remote(acc.at[rws, lanes[d]], rbuf.at[s, pl.ds(j * sub, sub), lanes[d]],
                        rs.at[st, 0, d, s, j], rr.at[st, 0, d, s, j], right)
            cp.wait_recv()
            acc[rws, lanes[d]] = (acc[rws, lanes[d]].astype(F32)
                                  + rbuf[s, pl.ds(j * sub, sub), lanes[d]].astype(F32)).astype(BF)

    def ag_send(st, base, chunk, sub, s, j):
        for d in range(2):
            k = pos - s if d == 0 else pos + s
            rws = rows_of(base, chunk, k, sub, j)
            go(remote(outb.at[rws, lanes[d]], outb.at[rws, lanes[d]],
                      rs.at[st, 1, d, s, j], rr.at[st, 1, d, s, j], right if d == 0 else left))

    def ag_recv(st, base, chunk, sub, s, j):
        for d in range(2):
            k = pos - 1 - s if d == 0 else pos + 1 + s
            rws = rows_of(base, chunk, k, sub, j)
            remote(outb.at[rws, lanes[d]], outb.at[rws, lanes[d]],
                   rs.at[st, 1, d, s, j], rr.at[st, 1, d, s, j], right).wait_recv()

    two = (1, s_one, chunk2, sub2)
    base1 = pl.multiple_of(bit * h1, 16)
    other1 = pl.multiple_of((1 - bit) * h1, 16)
    one = (0, base1, chunk1, sub1)

    for k in range(1, fs):
        fcs[3 * (k - 1) + 2].wait_recv()
    vtot = vacc[...]
    for k in range(fs - 1):
        vtot = vtot + vf[k]
    vacc[...] = vtot
    vxc = go(remote(vacc, vx, vxs, vxr, xpeer))

    for j in range(subs):
        rs_send(*two, rbuf2, 0, j)
    for k in range(1, fs):
        fcs[3 * (k - 1) + 1].wait_recv()
    fadd(0, s_one)
    xc1 = go(remote(acc.at[pl.ds(other1, h1)], xbuf1, xs.at[0], xr.at[0], xpeer))

    vxc.wait_recv()
    vr[pos] = vacc[...] + vx[...]

    for s in range(n - 1):
        vcp = go(remote(vr.at[lax.rem(pos - s + n, n)], vr.at[lax.rem(pos - s + n, n)],
                        vrs.at[s], vrr.at[s], right))
        for j in range(subs):
            rs_recv(*two, rbuf2, s, j)
            if s < n - 2:
                rs_send(*two, rbuf2, s + 1, j)
        w = lax.rem(pos - 1 - s + n, n)
        remote(vr.at[w], vr.at[w], vrs.at[s], vrr.at[s], right).wait_recv()
    hx = chunk2 // 2
    mine2 = pl.multiple_of(s_one + pos * chunk2 + bit * hx, 16)
    theirs2 = pl.multiple_of(s_one + pos * chunk2 + (1 - bit) * hx, 16)
    xc2 = go(remote(acc.at[pl.ds(theirs2, hx)], xbuf2, xs.at[1], xr.at[1], xpeer))
    xc1.wait_recv()
    blk = 16 * 5 if h1 % 80 == 0 else 16

    @pl.loop(0, h1 // blk)
    def _(i):
        rws = pl.ds(pl.multiple_of(base1 + i * blk, 16), blk)
        acc[rws, :] = (acc[rws, :].astype(F32)
                       + xbuf1[pl.ds(pl.multiple_of(i * blk, 16), blk), :].astype(F32)).astype(BF)
    for j in range(subs):
        rs_send(*one, rbuf1, 0, j)
    vsum = vr[0]
    for k in range(1, n):
        vsum = vsum + vr[k]
    vout_ref[...] = vsum
    xc2.wait_recv()
    outb[pl.ds(mine2, hx), :] = (acc[pl.ds(mine2, hx), :].astype(F32) + xbuf2[...].astype(F32)).astype(BF)
    xg2 = go(remote(outb.at[pl.ds(mine2, hx)], outb.at[pl.ds(mine2, hx)], xs.at[2], xr.at[2], xpeer))
    for s in range(n - 1):
        for j in range(subs):
            rs_recv(*one, rbuf1, s, j)
            if s < n - 2:
                rs_send(*one, rbuf1, s + 1, j)
            else:
                rws = rows_of(base1, chunk1, pos, sub1, j)
                outb[rws, :] = acc[rws, :]
                ag_send(*one, 0, j)
    remote(outb.at[pl.ds(theirs2, hx)], outb.at[pl.ds(theirs2, hx)], xs.at[2], xr.at[2], xpeer).wait_recv()
    for s in range(n - 1):
        for j in range(subs):
            ag_recv(*one, s, j)
            if s < n - 2:
                ag_send(*one, s + 1, j)
    xg1 = go(remote(outb.at[pl.ds(base1, h1)], outb.at[pl.ds(base1, h1)], xs.at[3], xr.at[3], xpeer))
    for j in range(subs):
        ag_send(*two, 0, j)
    for s in range(n - 1):
        for j in range(subs):
            ag_recv(*two, s, j)
            if s < n - 2:
                ag_send(*two, s + 1, j)
    o2 = pltpu.make_async_copy(outb.at[pl.ds(s_one, s_two)], out_ref.at[pl.ds(s_one, s_two)], osem.at[0])
    o2.start()
    remote(outb.at[pl.ds(other1, h1)], outb.at[pl.ds(other1, h1)], xs.at[3], xr.at[3], xpeer).wait_recv()
    o1 = pltpu.make_async_copy(outb.at[pl.ds(0, s_one)], out_ref.at[pl.ds(0, s_one)], osem.at[1])
    o1.start()
    for cp in pend:
        cp.wait_send()
    o1.wait()
    o2.wait()

def split_rows(rows, n, subs):
    unit = 2 * n * subs * 16
    units = -(-rows // unit)
    one = max(1, (units * 5 + 4) // 9)
    return one * unit, max(1, units - one) * unit

def reduce_grads(g, v, cid, subs=2):
    fs = lax.axis_size("fsdp")
    n = lax.axis_size("ctx") // 2
    rows, width = g.shape[1:]
    s_one, s_two = split_rows(rows, n, subs)
    pad = s_one + s_two - rows
    if pad:
        g = jnp.pad(g, ((0, 0), (0, pad), (0, 0)))
    tot = s_one + s_two
    vs = v.shape[1:]
    dma = pltpu.SemaphoreType.DMA
    chunk1, chunk2 = s_one // 2 // n, s_two // n
    out, vout = pl.pallas_call(
        functools.partial(grads_kernel, n, fs, s_one, s_two, subs),
        out_shape=(jax.ShapeDtypeStruct((tot, width), BF), jax.ShapeDtypeStruct(vs, F32)),
        in_specs=[pl.BlockSpec(memory_space=pl.ANY)] * 2,
        out_specs=(pl.BlockSpec(memory_space=pl.ANY), pl.BlockSpec(memory_space=pltpu.VMEM)),
        scratch_shapes=[
            pltpu.VMEM((tot, width), BF),
            pltpu.VMEM((fs - 1, tot, width), BF),
            pltpu.VMEM((s_one // 2, width), BF),
            pltpu.VMEM((n - 1, chunk1, width), BF),
            pltpu.VMEM((chunk2 // 2, width), BF),
            pltpu.VMEM((n - 1, chunk2, width), BF),
            pltpu.VMEM((tot, width), BF),
            pltpu.VMEM(vs, F32),
            pltpu.VMEM((fs - 1,) + vs, F32),
            pltpu.VMEM(vs, F32),
            pltpu.VMEM((n,) + vs, F32),
            dma((2,)), dma((fs - 1, 2)), dma((fs - 1, 2)), dma((4,)), dma((4,)),
            dma((2, 2, 2, n - 1, subs)), dma((2, 2, 2, n - 1, subs)),
            dma((fs - 1,)), dma((fs - 1,)), dma(()), dma(()), dma((n - 1,)), dma((n - 1,)), dma((2,)),
        ],
        compiler_params=pltpu.CompilerParams(collective_id=cid, has_side_effects=True, vmem_limit_bytes=56 << 20),
        name="reduce_grads",
    )(g, v)
    return out[:rows], vout

EPS = 1e-05
NEG = -1e30


def layer_norm(values, gain, shift):
    center = values - jnp.mean(values, axis=-1, keepdims=True)
    spread = jnp.mean(center * center, axis=-1, keepdims=True)
    return center * lax.rsqrt(spread + EPS) * gain + shift


def gelu_tanh(values):
    return jax.nn.gelu(values, approximate=True)


def row_places(row_ids, blk_rows, ctx_count):
    owner_dev = row_ids // (2 * blk_rows)
    within = row_ids % (2 * blk_rows)
    return jnp.where(
        within < blk_rows,
        owner_dev * blk_rows + within,
        (2 * ctx_count - 1 - owner_dev) * blk_rows + within - blk_rows,
    )


def row_docs(positions, starts):
    return jnp.sum((starts[None, :] <= positions[:, None]).astype(jnp.int32), axis=1) - 1


def per_device(
    stream,
    doc_starts,
    ln1_gain,
    ln1_bias,
    qkv_weight,
    q_bias,
    v_bias,
    out_weight,
    out_bias,
    ln2_gain,
    ln2_bias,
    fc1_weight,
    fc1_bias,
    fc2_weight,
    fc2_bias,
    cotangent,
):
    f32 = jnp.float32
    bf16 = jnp.bfloat16
    ctx_count = lax.axis_size("ctx")
    tok_rows = stream.shape[1]
    blk_rows = tok_rows // 2
    width = stream.shape[2]
    heads = H
    head_dim = HD
    scale = head_dim ** (-0.5)
    starts = doc_starts[0]
    own_rows = lax.axis_index("ctx") * tok_rows + jnp.arange(tok_rows, dtype=jnp.int32)
    q_pos = row_places(own_rows, blk_rows, ctx_count)
    q_doc = row_docs(q_pos, starts)

    def piece_allowed(start, rows):
        k_pos = row_places(start + jnp.arange(rows, dtype=jnp.int32), blk_rows, ctx_count)
        k_doc = row_docs(k_pos, starts)
        return (k_doc[None, :] == q_doc[:, None]) & (k_pos[None, :] <= q_pos[:, None])

    params = (
        lax.all_gather(ln1_gain, "fsdp", axis=0, tiled=True),
        lax.all_gather(ln1_bias, "fsdp", axis=0, tiled=True),
        lax.all_gather(qkv_weight, "fsdp", axis=0, tiled=True),
        lax.all_gather(q_bias, "fsdp", axis=0, tiled=True),
        lax.all_gather(v_bias, "fsdp", axis=0, tiled=True),
        lax.all_gather(out_weight, "fsdp", axis=0, tiled=True),
        lax.all_gather(out_bias, "fsdp", axis=0, tiled=True),
        lax.all_gather(ln2_gain, "fsdp", axis=0, tiled=True),
        lax.all_gather(ln2_bias, "fsdp", axis=0, tiled=True),
        lax.all_gather(fc1_weight, "fsdp", axis=0, tiled=True),
        lax.all_gather(fc1_bias, "fsdp", axis=0, tiled=True),
        lax.all_gather(fc2_weight, "fsdp", axis=0, tiled=True),
        lax.all_gather(fc2_bias, "fsdp", axis=0, tiled=True),
    )
    (
        g_one,
        b_one,
        w_qkv,
        q_shift,
        v_shift,
        w_out,
        o_shift,
        g_two,
        b_two,
        w_fc1,
        c_fc1,
        w_fc2,
        c_fc2,
    ) = params
    inputs = stream[0].astype(f32)
    normed_f, ln1_pull = jax.vjp(layer_norm, inputs, g_one.astype(f32), b_one.astype(f32))
    normed_in = normed_f.astype(bf16)
    shift_qkv = jnp.concatenate([q_shift, jnp.zeros_like(q_shift), v_shift]).astype(f32)
    projected = jnp.dot(normed_in, w_qkv, preferred_element_type=f32) + shift_qkv
    query = projected[:, :width].astype(bf16).reshape(tok_rows, heads, head_dim)
    k_own = projected[:, width : 2 * width].astype(bf16)
    v_own = projected[:, 2 * width :].astype(bf16)
    piece_starts = jnp.arange(ctx_count, dtype=jnp.int32) * tok_rows
    run_max = jnp.full((heads, tok_rows), NEG, f32)
    run_acc = jnp.zeros((tok_rows, heads, head_dim), f32)
    k_piece = lax.all_gather(k_own, "ctx", axis=0, tiled=True).reshape(-1, heads, head_dim)
    v_piece = lax.all_gather(v_own, "ctx", axis=0, tiled=True).reshape(-1, heads, head_dim)
    allowed = piece_allowed(jnp.int32(0), k_piece.shape[0])
    scores = jnp.einsum("qhd,khd->hqk", query, k_piece, preferred_element_type=f32) * scale
    scores = jnp.where(allowed[None], scores, NEG)
    new_max = jnp.maximum(run_max, jnp.max(scores, axis=-1))
    weights = jnp.where(allowed[None], jnp.exp(scores - new_max[..., None]), 0.0)
    fade = jnp.exp(run_max - new_max)
    new_sum = jnp.sum(weights, axis=-1)
    new_acc = run_acc * fade.T[:, :, None] + jnp.einsum(
        "hqk,khd->qhd", weights.astype(bf16), v_piece, preferred_element_type=f32
    )
    folded = (new_max, new_sum, new_acc)
    run_max, run_sum, run_acc = folded
    log_total = run_max + jnp.log(run_sum)
    attn_f = run_acc / run_sum.T[:, :, None]
    attn = attn_f.reshape(tok_rows, width).astype(bf16)
    hidden = inputs + jnp.dot(attn, w_out, preferred_element_type=f32) + o_shift.astype(f32)
    normed_mf, ln2_pull = jax.vjp(layer_norm, hidden, g_two.astype(f32), b_two.astype(f32))
    normed_mid = normed_mf.astype(bf16)
    pre_act = jnp.dot(normed_mid, w_fc1, preferred_element_type=f32) + c_fc1.astype(f32)
    activ_f, gelu_pull = jax.vjp(gelu_tanh, pre_act)
    activ = activ_f.astype(bf16)
    result = hidden + jnp.dot(activ, w_fc2, preferred_element_type=f32) + c_fc2.astype(f32)
    layer_out = result.astype(bf16)[None]
    params_back = (
        lax.all_gather(ln1_gain, "fsdp", axis=0, tiled=True),
        lax.all_gather(ln1_bias, "fsdp", axis=0, tiled=True),
        lax.all_gather(qkv_weight, "fsdp", axis=0, tiled=True),
        lax.all_gather(q_bias, "fsdp", axis=0, tiled=True),
        lax.all_gather(v_bias, "fsdp", axis=0, tiled=True),
        lax.all_gather(out_weight, "fsdp", axis=0, tiled=True),
        lax.all_gather(out_bias, "fsdp", axis=0, tiled=True),
        lax.all_gather(ln2_gain, "fsdp", axis=0, tiled=True),
        lax.all_gather(ln2_bias, "fsdp", axis=0, tiled=True),
        lax.all_gather(fc1_weight, "fsdp", axis=0, tiled=True),
        lax.all_gather(fc1_bias, "fsdp", axis=0, tiled=True),
        lax.all_gather(fc2_weight, "fsdp", axis=0, tiled=True),
        lax.all_gather(fc2_bias, "fsdp", axis=0, tiled=True),
    )
    wb_qkv = params_back[2]
    wb_out = params_back[5]
    wb_fc1 = params_back[9]
    wb_fc2 = params_back[11]
    grad_out = cotangent[0]
    grad_w_fc2 = jnp.einsum("tf,td->fd", activ, grad_out, preferred_element_type=f32)
    grad_c_fc2 = jnp.sum(grad_out.astype(f32), axis=0)
    grad_activ = jnp.einsum("td,fd->tf", grad_out, wb_fc2, preferred_element_type=f32)
    grad_pre = gelu_pull(grad_activ)[0].astype(bf16)
    grad_w_fc1 = jnp.einsum("td,tf->df", normed_mid, grad_pre, preferred_element_type=f32)
    grad_c_fc1 = jnp.sum(grad_pre.astype(f32), axis=0)
    grad_norm_mid = jnp.einsum("tf,df->td", grad_pre, wb_fc1, preferred_element_type=f32)
    grad_hid_part, grad_g_two, grad_b_two = ln2_pull(grad_norm_mid)
    grad_hidden = grad_out.astype(f32) + grad_hid_part
    grad_branch = grad_hidden.astype(bf16)
    grad_w_out = jnp.einsum("td,te->de", attn, grad_branch, preferred_element_type=f32)
    grad_o_shift = jnp.sum(grad_branch.astype(f32), axis=0)
    grad_attn = jnp.einsum("te,de->td", grad_branch, wb_out, preferred_element_type=f32).astype(
        bf16
    )
    grad_attn3 = grad_attn.reshape(tok_rows, heads, head_dim)
    row_dot = jnp.einsum("qhd,qhd->hq", grad_attn3.astype(f32), attn_f)
    all_keys, all_values = (
        lax.all_gather(k_own, "ctx", axis=0, tiled=True),
        lax.all_gather(v_own, "ctx", axis=0, tiled=True),
    )

    def score_grads(k_piece, v_piece, allowed):
        scores = jnp.einsum("qhd,khd->hqk", query, k_piece, preferred_element_type=f32) * scale
        probs = jnp.where(allowed[None], jnp.exp(scores - log_total[..., None]), 0.0)
        grad_probs = jnp.einsum("qhd,khd->hqk", grad_attn3, v_piece, preferred_element_type=f32)
        grad_scores = (probs * (grad_probs - row_dot[..., None])).astype(bf16)
        return (probs, grad_scores)

    def back_step(grad_q_acc, piece_args):
        k_piece = piece_args[0].reshape(tok_rows, heads, head_dim)
        v_piece = piece_args[1].reshape(tok_rows, heads, head_dim)
        allowed = piece_allowed(piece_args[2], tok_rows)
        probs, grad_scores = score_grads(k_piece, v_piece, allowed)
        grad_v_piece = jnp.einsum(
            "hqk,qhd->khd", probs.astype(bf16), grad_attn3, preferred_element_type=f32
        )
        grad_q_piece = (
            jnp.einsum("hqk,khd->qhd", grad_scores, k_piece, preferred_element_type=f32) * scale
        )
        grad_k_piece = (
            jnp.einsum("hqk,qhd->khd", grad_scores, query, preferred_element_type=f32) * scale
        )
        return (
            grad_q_acc + grad_q_piece,
            (grad_k_piece.reshape(tok_rows, width), grad_v_piece.reshape(tok_rows, width)),
        )

    scan_inputs = (
        all_keys.reshape(ctx_count, tok_rows, width),
        all_values.reshape(ctx_count, tok_rows, width),
        piece_starts,
    )
    zero_q = jnp.zeros((tok_rows, heads, head_dim), f32)
    grad_q_total, kv_terms = lax.scan(back_step, zero_q, scan_inputs)
    grad_k_sum, grad_v_sum = (
        lax.psum_scatter(
            kv_terms[0].reshape(ctx_count * tok_rows, width).astype(jnp.bfloat16),
            "ctx",
            scatter_dimension=0,
            tiled=True,
        ).astype(jnp.float32),
        lax.psum_scatter(
            kv_terms[1].reshape(ctx_count * tok_rows, width).astype(jnp.bfloat16),
            "ctx",
            scatter_dimension=0,
            tiled=True,
        ).astype(jnp.float32),
    )
    grad_keys = grad_k_sum.astype(bf16)
    grad_values = grad_v_sum.astype(bf16)
    grad_query = grad_q_total.reshape(tok_rows, width).astype(bf16)
    grad_qkv = jnp.concatenate([grad_query, grad_keys, grad_values], axis=1)
    grad_w_qkv = jnp.einsum("td,te->de", normed_in, grad_qkv, preferred_element_type=f32)
    grad_q_shift = jnp.sum(grad_query.astype(f32), axis=0)
    grad_v_shift = jnp.sum(grad_values.astype(f32), axis=0)
    grad_norm_in = jnp.einsum("te,de->td", grad_qkv, wb_qkv, preferred_element_type=f32)
    grad_in_part, grad_g_one, grad_b_one = ln1_pull(grad_norm_in)
    input_grad = (grad_hidden + grad_in_part)[None]
    shards = lax.axis_size("fsdp")
    part = width // shards
    blocks = []
    for grad in (grad_w_qkv, grad_w_out, grad_w_fc1):
        cols = grad.shape[1] // width
        blocks.append(grad.reshape(shards, part, cols, width).transpose(0, 2, 1, 3).reshape(shards, cols * part, width).astype(bf16))
    blocks.append(grad_w_fc2.reshape(shards, -1, width).astype(bf16))
    packed = jnp.concatenate(blocks, axis=1)
    vectors = [grad_g_one, grad_b_one, grad_q_shift, grad_v_shift, grad_o_shift, grad_g_two, grad_b_two, grad_c_fc2]
    lines = [one.reshape(shards, 1, part) for one in vectors]
    lines.append(grad_c_fc1.reshape(shards, -1, part))
    lines.append(jnp.zeros((shards, 4, part), f32))
    total, vec = reduce_grads(packed, jnp.concatenate(lines, axis=1), 0)
    total = total.astype(f32)
    edges = [0, 3 * part, 4 * part, 8 * part, 12 * part]
    t_qkv, t_out, t_fc1, t_fc2 = [total[a:b] for a, b in zip(edges[:-1], edges[1:])]

    def unpack(block):
        cols = block.shape[0] // part
        return block.reshape(cols, part, width).transpose(1, 0, 2).reshape(part, cols * width)

    return (
        layer_out, input_grad, vec[0], vec[1], unpack(t_qkv), vec[2], vec[3], t_out, vec[4], vec[5], vec[6],
        unpack(t_fc1), vec[8:12].reshape(-1), t_fc2, vec[7],
    )


def solution(mesh):
    in_specs = (
        P("fsdp", "ctx", None),
        P("fsdp", None),
        P("fsdp"),
        P("fsdp"),
        P("fsdp", None),
        P("fsdp"),
        P("fsdp"),
        P("fsdp", None),
        P("fsdp"),
        P("fsdp"),
        P("fsdp"),
        P("fsdp", None),
        P("fsdp"),
        P("fsdp", None),
        P("fsdp"),
        P("fsdp", "ctx", None),
    )
    out_specs = (
        P("fsdp", "ctx", None),
        P("fsdp", "ctx", None),
        P("fsdp"),
        P("fsdp"),
        P("fsdp", None),
        P("fsdp"),
        P("fsdp"),
        P("fsdp", None),
        P("fsdp"),
        P("fsdp"),
        P("fsdp"),
        P("fsdp", None),
        P("fsdp"),
        P("fsdp", None),
        P("fsdp"),
    )
    return jax.shard_map(
        per_device, mesh=mesh, in_specs=in_specs, out_specs=out_specs, check_vma=False
    )
```

```python
import functools

import jax
import jax.numpy as jnp
from jax import lax
from jax.experimental import pallas as pl
from jax.experimental.pallas import tpu as pltpu
from jax.sharding import PartitionSpec as P

H = 12
HD = 64
MESH = pl.DeviceIdType.MESH
BF = jnp.bfloat16
F32 = jnp.float32


def ring_of(ctx, n):
    g = ctx // 2
    return jnp.where(g % 2 == 0, g // 2, n - 1 - g // 2)

def ring_ctx(r, n, bit):
    r = lax.rem(r + n, n)
    g = jnp.where(r < n // 2, 2 * r, 2 * (n - 1 - r) + 1)
    return g * 2 + bit

def grads_kernel(n, fs, s_one, s_two, subs, g_ref, v_ref, out_ref, vout_ref,
                 acc, fbuf, xbuf1, rbuf1, xbuf2, rbuf2, outb,
                 vacc, vf, vx, vr,
                 lsem, fsem, frec, xs, xr, rs, rr, vfs, vfr, vxs, vxr, vrs, vrr, osem):
    c = lax.axis_index("ctx")
    f = lax.axis_index("fsdp")
    bit = c % 2
    pos = ring_of(c, n)
    xpeer = (c + 1 - 2 * bit, f)
    right = (ring_ctx(pos + 1, n, bit), f)
    left = (ring_ctx(pos - 1, n, bit), f)
    rows = s_one + s_two
    half = g_ref.shape[2] // 2
    lanes = (pl.ds(0, half), pl.ds(half, half))
    fpeers = [(c, lax.rem(f + k, fs)) for k in range(1, fs)]
    barrier = pltpu.get_barrier_semaphore()
    for peer in [xpeer, right, left] + fpeers:
        pl.semaphore_signal(barrier, inc=1, device_id=peer, device_id_type=MESH)
    pl.semaphore_wait(barrier, 2 + fs)

    def remote(src, dst, ssem, rsem, peer):
        cp = pltpu.make_async_remote_copy(src_ref=src, dst_ref=dst, send_sem=ssem, recv_sem=rsem,
                                          device_id=peer, device_id_type=MESH)
        return cp

    pend = []

    def go(cp):
        cp.start()
        pend.append(cp)
        return cp
    own = pltpu.make_async_copy(g_ref.at[f], acc, lsem.at[0])
    own.start()
    vown = pltpu.make_async_copy(v_ref.at[f], vacc, lsem.at[1])
    vown.start()
    fcs = []
    parts = ((s_one, s_two), (0, s_one))
    for k in range(1, fs):
        peer = fpeers[k - 1]
        for j, (a, m) in enumerate(parts):
            fcs.append(go(remote(g_ref.at[peer[1], pl.ds(a, m)], fbuf.at[k - 1, pl.ds(a, m)],
                                 fsem.at[k - 1, j], frec.at[k - 1, j], peer)))
        fcs.append(go(remote(v_ref.at[peer[1]], vf.at[k - 1], vfs.at[k - 1], vfr.at[k - 1], peer)))
    own.wait()
    vown.wait()

    def fadd(a, m):
        blk = 32

        @pl.loop(0, m // blk)
        def _(i):
            rws = pl.ds(pl.multiple_of(a + i * blk, blk), blk)
            tot = acc[rws, :].astype(F32)
            for k in range(fs - 1):
                tot = tot + fbuf[k, rws, :].astype(F32)
            acc[rws, :] = tot.astype(BF)

    for k in range(1, fs):
        fcs[3 * (k - 1)].wait_recv()
    fadd(s_one, s_two)

    chunk2 = s_two // n
    sub2 = chunk2 // subs
    h1 = s_one // 2
    chunk1 = h1 // n
    sub1 = chunk1 // subs

    def rows_of(base, chunk, k, sub, j):
        k = lax.rem(k + 2 * n, n)
        return pl.ds(pl.multiple_of(base + k * chunk + j * sub, 16), sub)

    def rs_send(st, base, chunk, sub, rbuf, s, j):
        for d in range(2):
            k = pos - 1 - s if d == 0 else pos + 1 + s
            go(remote(acc.at[rows_of(base, chunk, k, sub, j), lanes[d]],
                      rbuf.at[s, pl.ds(j * sub, sub), lanes[d]],
                      rs.at[st, 0, d, s, j], rr.at[st, 0, d, s, j], right if d == 0 else left))

    def rs_recv(st, base, chunk, sub, rbuf, s, j):
        for d in range(2):
            k = pos - 2 - s if d == 0 else pos + 2 + s
            rws = rows_of(base, chunk, k, sub, j)
            cp = remote(acc.at[rws, lanes[d]], rbuf.at[s, pl.ds(j * sub, sub), lanes[d]],
                        rs.at[st, 0, d, s, j], rr.at[st, 0, d, s, j], right)
            cp.wait_recv()
            acc[rws, lanes[d]] = (acc[rws, lanes[d]].astype(F32)
                                  + rbuf[s, pl.ds(j * sub, sub), lanes[d]].astype(F32)).astype(BF)

    def ag_send(st, base, chunk, sub, s, j):
        for d in range(2):
            k = pos - s if d == 0 else pos + s
            rws = rows_of(base, chunk, k, sub, j)
            go(remote(outb.at[rws, lanes[d]], outb.at[rws, lanes[d]],
                      rs.at[st, 1, d, s, j], rr.at[st, 1, d, s, j], right if d == 0 else left))

    def ag_recv(st, base, chunk, sub, s, j):
        for d in range(2):
            k = pos - 1 - s if d == 0 else pos + 1 + s
            rws = rows_of(base, chunk, k, sub, j)
            remote(outb.at[rws, lanes[d]], outb.at[rws, lanes[d]],
                   rs.at[st, 1, d, s, j], rr.at[st, 1, d, s, j], right).wait_recv()

    two = (1, s_one, chunk2, sub2)
    base1 = pl.multiple_of(bit * h1, 16)
    other1 = pl.multiple_of((1 - bit) * h1, 16)
    one = (0, base1, chunk1, sub1)

    for k in range(1, fs):
        fcs[3 * (k - 1) + 2].wait_recv()
    vtot = vacc[...]
    for k in range(fs - 1):
        vtot = vtot + vf[k]
    vacc[...] = vtot
    vxc = go(remote(vacc, vx, vxs, vxr, xpeer))

    for j in range(subs):
        rs_send(*two, rbuf2, 0, j)
    for k in range(1, fs):
        fcs[3 * (k - 1) + 1].wait_recv()
    fadd(0, s_one)
    xc1 = go(remote(acc.at[pl.ds(other1, h1)], xbuf1, xs.at[0], xr.at[0], xpeer))

    vxc.wait_recv()
    vr[pos] = vacc[...] + vx[...]

    for s in range(n - 1):
        vcp = go(remote(vr.at[lax.rem(pos - s + n, n)], vr.at[lax.rem(pos - s + n, n)],
                        vrs.at[s], vrr.at[s], right))
        for j in range(subs):
            rs_recv(*two, rbuf2, s, j)
            if s < n - 2:
                rs_send(*two, rbuf2, s + 1, j)
        w = lax.rem(pos - 1 - s + n, n)
        remote(vr.at[w], vr.at[w], vrs.at[s], vrr.at[s], right).wait_recv()
    hx = chunk2 // 2
    mine2 = pl.multiple_of(s_one + pos * chunk2 + bit * hx, 16)
    theirs2 = pl.multiple_of(s_one + pos * chunk2 + (1 - bit) * hx, 16)
    xc2 = go(remote(acc.at[pl.ds(theirs2, hx)], xbuf2, xs.at[1], xr.at[1], xpeer))
    xc1.wait_recv()
    blk = 16 * 5 if h1 % 80 == 0 else 16

    @pl.loop(0, h1 // blk)
    def _(i):
        rws = pl.ds(pl.multiple_of(base1 + i * blk, 16), blk)
        acc[rws, :] = (acc[rws, :].astype(F32)
                       + xbuf1[pl.ds(pl.multiple_of(i * blk, 16), blk), :].astype(F32)).astype(BF)
    for j in range(subs):
        rs_send(*one, rbuf1, 0, j)
    vsum = vr[0]
    for k in range(1, n):
        vsum = vsum + vr[k]
    vout_ref[...] = vsum
    xc2.wait_recv()
    outb[pl.ds(mine2, hx), :] = (acc[pl.ds(mine2, hx), :].astype(F32) + xbuf2[...].astype(F32)).astype(BF)
    xg2 = go(remote(outb.at[pl.ds(mine2, hx)], outb.at[pl.ds(mine2, hx)], xs.at[2], xr.at[2], xpeer))
    for s in range(n - 1):
        for j in range(subs):
            rs_recv(*one, rbuf1, s, j)
            if s < n - 2:
                rs_send(*one, rbuf1, s + 1, j)
            else:
                rws = rows_of(base1, chunk1, pos, sub1, j)
                outb[rws, :] = acc[rws, :]
                ag_send(*one, 0, j)
    remote(outb.at[pl.ds(theirs2, hx)], outb.at[pl.ds(theirs2, hx)], xs.at[2], xr.at[2], xpeer).wait_recv()
    for s in range(n - 1):
        for j in range(subs):
            ag_recv(*one, s, j)
            if s < n - 2:
                ag_send(*one, s + 1, j)
    xg1 = go(remote(outb.at[pl.ds(base1, h1)], outb.at[pl.ds(base1, h1)], xs.at[3], xr.at[3], xpeer))
    for j in range(subs):
        ag_send(*two, 0, j)
    for s in range(n - 1):
        for j in range(subs):
            ag_recv(*two, s, j)
            if s < n - 2:
                ag_send(*two, s + 1, j)
    o2 = pltpu.make_async_copy(outb.at[pl.ds(s_one, s_two)], out_ref.at[pl.ds(s_one, s_two)], osem.at[0])
    o2.start()
    remote(outb.at[pl.ds(other1, h1)], outb.at[pl.ds(other1, h1)], xs.at[3], xr.at[3], xpeer).wait_recv()
    o1 = pltpu.make_async_copy(outb.at[pl.ds(0, s_one)], out_ref.at[pl.ds(0, s_one)], osem.at[1])
    o1.start()
    for cp in pend:
        cp.wait_send()
    o1.wait()
    o2.wait()

def split_rows(rows, n, subs):
    unit = 2 * n * subs * 16
    units = -(-rows // unit)
    one = max(1, (units * 5 + 4) // 9)
    return one * unit, max(1, units - one) * unit

def reduce_grads(g, v, cid, subs=2):
    fs = lax.axis_size("fsdp")
    n = lax.axis_size("ctx") // 2
    rows, width = g.shape[1:]
    s_one, s_two = split_rows(rows, n, subs)
    pad = s_one + s_two - rows
    if pad:
        g = jnp.pad(g, ((0, 0), (0, pad), (0, 0)))
    tot = s_one + s_two
    vs = v.shape[1:]
    dma = pltpu.SemaphoreType.DMA
    chunk1, chunk2 = s_one // 2 // n, s_two // n
    out, vout = pl.pallas_call(
        functools.partial(grads_kernel, n, fs, s_one, s_two, subs),
        out_shape=(jax.ShapeDtypeStruct((tot, width), BF), jax.ShapeDtypeStruct(vs, F32)),
        in_specs=[pl.BlockSpec(memory_space=pl.ANY)] * 2,
        out_specs=(pl.BlockSpec(memory_space=pl.ANY), pl.BlockSpec(memory_space=pltpu.VMEM)),
        scratch_shapes=[
            pltpu.VMEM((tot, width), BF),
            pltpu.VMEM((fs - 1, tot, width), BF),
            pltpu.VMEM((s_one // 2, width), BF),
            pltpu.VMEM((n - 1, chunk1, width), BF),
            pltpu.VMEM((chunk2 // 2, width), BF),
            pltpu.VMEM((n - 1, chunk2, width), BF),
            pltpu.VMEM((tot, width), BF),
            pltpu.VMEM(vs, F32),
            pltpu.VMEM((fs - 1,) + vs, F32),
            pltpu.VMEM(vs, F32),
            pltpu.VMEM((n,) + vs, F32),
            dma((2,)), dma((fs - 1, 2)), dma((fs - 1, 2)), dma((4,)), dma((4,)),
            dma((2, 2, 2, n - 1, subs)), dma((2, 2, 2, n - 1, subs)),
            dma((fs - 1,)), dma((fs - 1,)), dma(()), dma(()), dma((n - 1,)), dma((n - 1,)), dma((2,)),
        ],
        compiler_params=pltpu.CompilerParams(collective_id=cid, has_side_effects=True, vmem_limit_bytes=56 << 20),
        name="reduce_grads",
    )(g, v)
    return out[:rows], vout

INNER = 4
QW, KW = 256, 384
GW = QW + KW
NEG = -1e30


def nt(a, b):
    return lax.dot_general(a, b, (((1,), (1,)), ((), ())), preferred_element_type=F32)


def nn(a, b):
    return lax.dot_general(a, b, (((1,), (0,)), ((), ())), preferred_element_type=F32)


def head_lanes(x, head):
    if head == 2:
        return x
    lane = lax.broadcasted_iota(jnp.int32, x.shape, 1)
    keep = lane < HD if head == 0 else lane >= HD
    return jnp.where(keep, x, jnp.zeros_like(x))


def first_keys(starts_ref, pos):
    first = jnp.zeros_like(pos)
    for d in range(starts_ref.shape[1]):
        one = starts_ref[0, d]
        first = jnp.maximum(first, jnp.where(one <= pos, one, 0))
    return first


def places():
    c = lax.axis_index("ctx")
    f = lax.axis_index("fsdp")
    return c // INNER, c % INNER, f


def greet(z, h, f, depth):
    barrier = pltpu.get_barrier_semaphore()
    for j in range(1, INNER):
        pl.semaphore_signal(barrier, inc=1, device_id=(z * INNER + (h + j) % INNER, f), device_id_type=MESH)

    @pl.when(z > 0)
    def _():
        pl.semaphore_signal(barrier, inc=1, device_id=((z - 1) * INNER + h, f), device_id_type=MESH)

    @pl.when(z < depth - 1)
    def _():
        pl.semaphore_signal(barrier, inc=1, device_id=((z + 1) * INNER + h, f), device_id_type=MESH)

    count = INNER - 1 + jnp.where(z > 0, 1, 0) + jnp.where(z < depth - 1, 1, 0)
    pl.semaphore_wait(barrier, count)


def send(src, dst, ssem, rsem, peer):
    return pltpu.make_async_remote_copy(
        src_ref=src, dst_ref=dst, send_sem=ssem, recv_sem=rsem, device_id=peer, device_id_type=MESH
    )


K_LANES = (0, 0, 256)
V_LANES = (128, 128, 256)
Q_LANES = (0, 0, 128)


def attend_kernel(depth, length, starts_ref, x_ref, out_ref, qb_ref, kv_ref, ot_ref, lse_ref,
                  qb, kv, acc, top, tot, ob, land,
                  lsem, as_kv, ar_kv, as_q, ar_q, zs, zr, bs, br, osem):
    z, h, f = places()
    blk = x_ref.shape[0] // 2
    rows = INNER * blk
    half_rows = (pl.ds(0, blk), pl.ds(blk, blk))
    my_piece = (h, INNER - 1 - h)

    def piece(half, i):
        p = i if half == 0 else INNER - 1 - i
        return pl.ds(pl.multiple_of(p * blk, blk), blk)

    own = (depth - 1, depth)
    greet(z, h, f, depth)

    def a2a(j, half, kind):
        i = (h + j) % INNER
        lanes = pl.ds(pl.multiple_of(i * GW + (QW if kind else 0), 128), KW if kind else QW)
        dst = kv.at[own[half], piece(half, h)] if kind else qb.at[half, piece(half, h)]
        sems = (as_kv.at[half, j - 1], ar_kv.at[half, j - 1]) if kind else (as_q.at[half, j - 1], ar_q.at[half, j - 1])
        return send(x_ref.at[half_rows[half], lanes], dst, *sems, (z * INNER + i, f))

    def local(half, kind):
        lanes = pl.ds(pl.multiple_of(h * GW + (QW if kind else 0), 128), KW if kind else QW)
        dst = kv.at[own[half], piece(half, h)] if kind else qb.at[half, piece(half, h)]
        return pltpu.make_async_copy(x_ref.at[half_rows[half], lanes], dst, lsem.at[half, kind])

    for kind in (1, 0):
        for half in range(2):
            for j in range(1, INNER):
                a2a(j, half, kind).start()
            local(half, kind).start()

    def relay(half, src_slot, step, p):
        rws = pl.ds(pl.multiple_of(p * blk, blk), blk)
        if half == 0:
            peer, slot = (z + 1) * INNER + h, step - 1
        else:
            peer, slot = (z - 1) * INNER + h, z - 1 + step - 1
        return send(kv.at[src_slot, rws], kv.at[slot, rws], zs.at[half, step - 1, p], zr.at[half, step - 1, p], (peer, f))

    can = (z < depth - 1, z > 0)
    for j in range(INNER):
        i = (h + INNER - j) % INNER
        for half in range(2):
            if j == 0:
                local(half, 1).wait()
            else:
                a2a(j, half, 1).wait_recv()

            @pl.when(can[half])
            def _():
                relay(half, own[half], 1, i if half == 0 else INNER - 1 - i).start()

    for half in range(2):
        local(half, 0).wait()
        for j in range(1, INNER):
            a2a(j, half, 0).wait_recv()

    def base_of(half, zz):
        return zz * rows if half == 0 else length - (zz + 1) * rows

    cols = rows // 2

    def tile(half, slot, q_base, k_base, diag):
        for head in range(3):
            k_all = kv[slot, :, K_LANES[head]:K_LANES[head] + 128]
            v_all = kv[slot, :, V_LANES[head]:V_LANES[head] + 128]
            v_t = v_all.T[(0 if head == 0 else HD):(HD if head == 0 else 2 * HD)]
            for part in range(2):
                keys = (part + 1) * cols if diag else rows
                lanes = slice(part * cols, (part + 1) * cols)
                q = head_lanes(qb[half, lanes, Q_LANES[head]:Q_LANES[head] + 128], head)
                pos = q_base + part * cols + lax.broadcasted_iota(jnp.int32, (1, cols), 1)
                first = first_keys(starts_ref, pos) - k_base
                s = nt(k_all[:keys], q)
                row = lax.broadcasted_iota(jnp.int32, (keys, cols), 0)
                ok = row >= first
                if diag:
                    ok = ok & (row <= pos - k_base)
                s = jnp.where(ok, s, NEG)
                line = slice(head, head + 1)
                feats = slice(head * HD, (head + 1) * HD)
                high = jnp.max(s, axis=0, keepdims=True)
                if not diag:
                    before = top[half, line, lanes]
                    high = jnp.maximum(before, high)
                    fade = jnp.exp(before - high)
                w = jnp.exp(s - high)
                add = jnp.sum(w, axis=0, keepdims=True)
                o = nn(v_t[:, :keys], w.astype(BF))
                if diag:
                    tot[half, line, lanes] = add
                    acc[half, feats, lanes] = o
                else:
                    tot[half, line, lanes] = tot[half, line, lanes] * fade + add
                    acc[half, feats, lanes] = acc[half, feats, lanes] * fade + o
                top[half, line, lanes] = high

    @pl.loop(0, 2)
    def _(half):
        q_base = jnp.where(half == 0, base_of(0, z), base_of(1, z))
        tile(half, depth - 1 + half, q_base, q_base, True)

    @pl.loop(1, depth)
    def _(step):
        valid = (z - step >= 0, z + step <= depth - 1)
        slots = (step - 1, z + step - 1)
        for half in range(2):
            for p in range(INNER):
                @pl.when(valid[half])
                def _():
                    rws = pl.ds(p * blk, blk)
                    send(kv.at[slots[half], rws], kv.at[slots[half], rws], zs.at[half, step - 1, p],
                         zr.at[half, step - 1, p], (z * INNER + (h + 1) % INNER, f)).wait_recv()

                @pl.when(valid[half] & can[half])
                def _():
                    relay(half, slots[half], step + 1, p).start()

        @pl.loop(0, 2)
        def _(half):
            @pl.when(jnp.where(half == 0, z - step, depth - 1 - z - step) >= 0)
            def _():
                zz = jnp.where(half == 0, z - step, z + step)
                q_base = jnp.where(half == 0, base_of(0, z), base_of(1, z))
                k_base = jnp.where(half == 0, base_of(0, zz), base_of(1, zz))
                tile(half, jnp.where(half == 0, step - 1, z + step - 1), q_base, k_base, False)

    ob[:, :, 2 * HD:3 * HD] = jnp.zeros((2, rows, HD), BF)
    for half in range(2):
        lse_ref[half] = top[half] + jnp.log(tot[half])
        for head in range(3):
            feats = slice(head * HD, (head + 1) * HD)
            acc[half, feats, :] = acc[half, feats, :] / tot[half, head:head + 1, :]
        ob[half, :, :2 * HD] = acc[half, :2 * HD, :].T.astype(BF)
        ob[half, :, 3 * HD:] = acc[half, 2 * HD:, :].T.astype(BF)
    outs = [pltpu.make_async_copy(qb, qb_ref, osem.at[0]), pltpu.make_async_copy(kv, kv_ref, osem.at[1]),
            pltpu.make_async_copy(acc, ot_ref, osem.at[2])]
    for cp in outs:
        cp.start()

    def back(j, half):
        i = (h + j) % INNER
        return send(ob.at[half, piece(half, i)], land.at[half_rows[half], pl.ds(pl.multiple_of(h * QW, 128), QW)],
                    bs.at[half, j - 1], br.at[half, j - 1], (z * INNER + i, f))

    for half in range(2):
        for j in range(1, INNER):
            back(j, half).start()
        mine = pltpu.make_async_copy(ob.at[half, piece(half, h)],
                                     land.at[half_rows[half], pl.ds(pl.multiple_of(h * QW, 128), QW)], lsem.at[half, 0])
        mine.start()
        mine.wait()
    for half in range(2):
        for j in range(1, INNER):
            back(j, half).wait_recv()
    out_ref[...] = land[...]
    for half in range(2):
        for j in range(1, INNER):
            a2a(j, half, 1).wait_send()
            a2a(j, half, 0).wait_send()
            back(j, half).wait_send()

        @pl.when(can[half])
        def _():
            for p in range(INNER):
                relay(half, own[half], 1, p).wait_send()

    @pl.loop(1, depth)
    def _(step):
        valid = (z - step >= 0, z + step <= depth - 1)
        for half in range(2):
            @pl.when(valid[half] & can[half])
            def _():
                for p in range(INNER):
                    relay(half, own[half], step + 1, p).wait_send()
    for cp in outs:
        cp.wait()


def attend(starts, x, length, cid):
    depth = lax.axis_size("ctx") // INNER
    blk = x.shape[0] // 2
    rows = INNER * blk
    dma = pltpu.SemaphoreType.DMA
    shapes = (
        jax.ShapeDtypeStruct((x.shape[0], INNER * QW), BF),
        jax.ShapeDtypeStruct((2, rows, QW), BF),
        jax.ShapeDtypeStruct((depth + 1, rows, KW), BF),
        jax.ShapeDtypeStruct((2, 3 * HD, rows), F32),
        jax.ShapeDtypeStruct((2, 8, rows), F32),
    )
    vm = pl.BlockSpec(memory_space=pltpu.VMEM)
    anyspec = pl.BlockSpec(memory_space=pl.ANY)
    return pl.pallas_call(
        functools.partial(attend_kernel, depth, length),
        out_shape=shapes,
        in_specs=[pl.BlockSpec(memory_space=pltpu.SMEM), vm],
        out_specs=(vm, anyspec, anyspec, anyspec, vm),
        scratch_shapes=[
            pltpu.VMEM((2, rows, QW), BF),
            pltpu.VMEM((depth + 1, rows, KW), BF),
            pltpu.VMEM((2, 3 * HD, rows), F32),
            pltpu.VMEM((2, 8, rows), F32),
            pltpu.VMEM((2, 8, rows), F32),
            pltpu.VMEM((2, rows, QW), BF),
            pltpu.VMEM((2 * blk, INNER * QW), BF),
            dma((2, 2)), dma((2, 3)), dma((2, 3)), dma((2, 3)), dma((2, 3)),
            dma((2, depth, INNER)), dma((2, depth, INNER)), dma((2, 3)), dma((2, 3)), dma((3,)),
        ],
        compiler_params=pltpu.CompilerParams(collective_id=cid, has_side_effects=True, vmem_limit_bytes=48 << 20),
        name="attend",
    )(starts, x)


def attend_back_kernel(depth, length, starts_ref, do_ref, qb, kv, ot, lse, out_ref,
                       dob, dots, dq, dkv, sbuf, rbuf, dqb, fin, land,
                       lsem, as_o, ar_o, zs, zr, bq, brq, bk, brk):
    z, h, f = places()
    blk = do_ref.shape[0] // 2
    rows = INNER * blk
    half_rows = (pl.ds(0, blk), pl.ds(blk, blk))

    def piece(half, i):
        p = i if half == 0 else INNER - 1 - i
        return pl.ds(pl.multiple_of(p * blk, blk), blk)

    greet(z, h, f, depth)

    def a2a(j, half):
        i = (h + j) % INNER
        return send(do_ref.at[half_rows[half], pl.ds(pl.multiple_of(i * QW, 128), QW)], dob.at[half, piece(half, h)],
                    as_o.at[half, j - 1], ar_o.at[half, j - 1], (z * INNER + i, f))

    mine = []
    for half in range(2):
        for j in range(1, INNER):
            a2a(j, half).start()
        cp = pltpu.make_async_copy(do_ref.at[half_rows[half], pl.ds(pl.multiple_of(h * QW, 128), QW)],
                                   dob.at[half, piece(half, h)], lsem.at[half])
        cp.start()
        mine.append(cp)
    dq[...] = jnp.zeros_like(dq)
    for half in range(2):
        mine[half].wait()
        for j in range(1, INNER):
            a2a(j, half).wait_recv()
        for head in range(3):
            lanes = slice(0, 128) if head < 2 else slice(128, 256)
            g = dob[half, :, lanes].astype(F32).T[(0 if head == 0 else HD):(HD if head == 0 else 2 * HD)]
            dots[half, head:head + 1, :] = jnp.sum(g * ot[half, head * HD:(head + 1) * HD, :], axis=0, keepdims=True)

    def base_of(half, zz):
        return zz * rows if half == 0 else length - (zz + 1) * rows

    cols = rows // 2

    def tile(half, slot, q_base, k_base, diag):
        for head in range(3):
            k_all = kv[slot, :, K_LANES[head]:K_LANES[head] + 128]
            v_all = kv[slot, :, V_LANES[head]:V_LANES[head] + 128]
            k_t = k_all.T[(HD if head == 1 else 0):(2 * HD if head == 1 else HD)]
            for part in range(2):
                keys = (part + 1) * cols if diag else rows
                lanes = slice(part * cols, (part + 1) * cols)
                q = head_lanes(qb[half, lanes, Q_LANES[head]:Q_LANES[head] + 128], head)
                g = head_lanes(dob[half, lanes, Q_LANES[head]:Q_LANES[head] + 128], head)
                pos = q_base + part * cols + lax.broadcasted_iota(jnp.int32, (1, cols), 1)
                first = first_keys(starts_ref, pos) - k_base
                s = nt(k_all[:keys], q)
                row = lax.broadcasted_iota(jnp.int32, (keys, cols), 0)
                ok = row >= first
                if diag:
                    ok = ok & (row <= pos - k_base)
                line = slice(head, head + 1)
                w = jnp.where(ok, jnp.exp(s - lse[half, line, lanes]), 0.0)
                gp = nt(v_all[:keys], g)
                ds = (w * (gp - dots[half, line, lanes])).astype(BF)
                wb = w.astype(BF)
                dv = nn(wb, g)
                dk = nn(ds, q)
                kl = slice(K_LANES[head], K_LANES[head] + 128)
                vl = slice(V_LANES[head], V_LANES[head] + 128)
                if head == 2:
                    both = dk + dv
                    if part == 0:
                        dkv[:keys, kl] = both
                    elif keys == rows and diag:
                        dkv[:cols, kl] = dkv[:cols, kl] + both[:cols]
                        dkv[cols:, kl] = both[cols:]
                    else:
                        dkv[:, kl] = dkv[:, kl] + both
                else:
                    for sl, val in ((kl, dk), (vl, dv)):
                        if head == 0 and part == 0:
                            dkv[:keys, sl] = val
                        elif head == 0 and diag:
                            dkv[:cols, sl] = dkv[:cols, sl] + val[:cols]
                            dkv[cols:, sl] = val[cols:]
                        else:
                            dkv[:keys, sl] = dkv[:keys, sl] + val
                feats = slice(head * HD, (head + 1) * HD)
                dq[half, feats, lanes] = dq[half, feats, lanes] + nn(k_t[:, :keys], ds)

    has = (z < depth - 1, z > 0)

    def pass_on(half, step):
        peer = (z - 1) * INNER + h if half == 0 else (z + 1) * INNER + h
        return send(sbuf.at[half, step - 1], rbuf.at[half, step - 1], zs.at[half, step - 1], zr.at[half, step - 1], (peer, f))

    def take(half, step):
        return send(sbuf.at[half, 0], rbuf.at[half, step], zs.at[half, step], zr.at[half, step],
                    (z * INNER + (h + 1) % INNER, f))

    @pl.loop(1, depth)
    def _(turn):
        step = depth - turn

        @pl.loop(0, 2)
        def _(half):
            @pl.when(jnp.where(half == 0, z - step, depth - 1 - z - step) >= 0)
            def _():
                zz = jnp.where(half == 0, z - step, z + step)
                q_base = jnp.where(half == 0, base_of(0, z), base_of(1, z))
                k_base = jnp.where(half == 0, base_of(0, zz), base_of(1, zz))
                tile(half, jnp.where(half == 0, step - 1, z + step - 1), q_base, k_base, False)

                @pl.when(jnp.where(half == 0, depth - 1 - z, z) > 0)
                def _():
                    take(half, step).wait_recv()

                    @pl.loop(0, rows // 64)
                    def _(b):
                        rws = pl.ds(pl.multiple_of(b * 64, 64), 64)
                        sbuf[half, step - 1, rws, :] = (dkv[rws, :] + rbuf[half, step, rws, :].astype(F32)).astype(BF)

                @pl.when(jnp.where(half == 0, depth - 1 - z, z) == 0)
                def _():
                    sbuf[half, step - 1] = dkv[...].astype(BF)

                @pl.when(half == 0)
                def _():
                    pass_on(0, step).start()

                @pl.when(half == 1)
                def _():
                    pass_on(1, step).start()

    def back(j, half, kind):
        i = (h + j) % INNER
        lanes = pl.ds(pl.multiple_of(h * GW + (QW if kind else 0), 128), KW if kind else QW)
        src = fin if kind else dqb
        sems = (bk.at[half, j - 1], brk.at[half, j - 1]) if kind else (bq.at[half, j - 1], brq.at[half, j - 1])
        return send(src.at[half, piece(half, i)], land.at[half_rows[half], lanes], *sems, (z * INNER + i, f))

    def keep(half, kind):
        lanes = pl.ds(pl.multiple_of(h * GW + (QW if kind else 0), 128), KW if kind else QW)
        src = fin if kind else dqb
        return pltpu.make_async_copy(src.at[half, piece(half, h)], land.at[half_rows[half], lanes], lsem.at[2 + 2 * half + kind])

    dqb[:, :, 3 * HD:] = jnp.zeros((2, rows, HD), BF)
    for half in range(2):
        q_base = base_of(half, z)
        tile(half, depth - 1 + half, q_base, q_base, True)
        dqb[half, :, :2 * HD] = (dq[half, :2 * HD, :] * (HD ** -0.5)).T.astype(BF)
        dqb[half, :, 2 * HD:3 * HD] = (dq[half, 2 * HD:, :] * (HD ** -0.5)).T.astype(BF)
        for j in range(1, INNER):
            back(j, half, 0).start()
        keep(half, 0).start()

        @pl.when(has[half])
        def _():
            take(half, 0).wait_recv()

            @pl.loop(0, rows // 64)
            def _(b):
                rws = pl.ds(pl.multiple_of(b * 64, 64), 64)
                fin[half, rws, :] = (dkv[rws, :] + rbuf[half, 0, rws, :].astype(F32)).astype(BF)

        @pl.when(jnp.logical_not(has[half]))
        def _():
            fin[half] = dkv[...].astype(BF)
        for j in range(1, INNER):
            back(j, half, 1).start()
        keep(half, 1).start()
    for half in range(2):
        for kind in range(2):
            keep(half, kind).wait()
            for j in range(1, INNER):
                back(j, half, kind).wait_recv()
    out_ref[...] = land[...]
    for half in range(2):
        for j in range(1, INNER):
            a2a(j, half).wait_send()
            for kind in range(2):
                back(j, half, kind).wait_send()

    @pl.loop(1, depth)
    def _(step):
        valid = (z - step >= 0, z + step <= depth - 1)
        for half in range(2):
            @pl.when(valid[half])
            def _():
                pass_on(half, step).wait_send()


def attend_back(starts, g, qb, kv, ot, lse, length, cid):
    depth = lax.axis_size("ctx") // INNER
    blk = g.shape[0] // 2
    rows = INNER * blk
    dma = pltpu.SemaphoreType.DMA
    vm = pl.BlockSpec(memory_space=pltpu.VMEM)
    return pl.pallas_call(
        functools.partial(attend_back_kernel, depth, length),
        out_shape=jax.ShapeDtypeStruct((2 * blk, INNER * GW), BF),
        in_specs=[pl.BlockSpec(memory_space=pltpu.SMEM)] + [vm] * 5,
        out_specs=vm,
        scratch_shapes=[
            pltpu.VMEM((2, rows, QW), BF),
            pltpu.VMEM((2, 8, rows), F32),
            pltpu.VMEM((2, 3 * HD, rows), F32),
            pltpu.VMEM((rows, KW), F32),
            pltpu.VMEM((2, depth - 1, rows, KW), BF),
            pltpu.VMEM((2, depth, rows, KW), BF),
            pltpu.VMEM((2, rows, QW), BF),
            pltpu.VMEM((2, rows, KW), BF),
            pltpu.VMEM((2 * blk, INNER * GW), BF),
            dma((6,)), dma((2, 3)), dma((2, 3)), dma((2, depth)), dma((2, depth)),
            dma((2, 3)), dma((2, 3)), dma((2, 3)), dma((2, 3)),
        ],
        compiler_params=pltpu.CompilerParams(collective_id=cid, has_side_effects=True, vmem_limit_bytes=56 << 20),
        name="attend_back",
    )(starts, g, qb, kv, ot, lse)


def group_qkv(q, k, v):
    zero = jnp.zeros(q.shape[:-1] + (HD,), q.dtype)

    def head(a, n):
        return lax.slice_in_dim(a, n * HD, (n + 1) * HD, axis=a.ndim - 1)

    cols = []
    for i in range(INNER):
        a = 3 * i
        cols += [lax.slice_in_dim(q, a * HD, (a + 3) * HD, axis=q.ndim - 1), zero,
                 lax.slice_in_dim(k, a * HD, (a + 2) * HD, axis=q.ndim - 1),
                 lax.slice_in_dim(v, a * HD, (a + 2) * HD, axis=q.ndim - 1), head(k, a + 2), head(v, a + 2)]
    return jnp.concatenate(cols, axis=-1)


def ungroup_qkv(x):
    def cut(lo, n):
        return lax.slice_in_dim(x, lo, lo + n, axis=x.ndim - 1)

    q, k, v = [], [], []
    for i in range(INNER):
        a = i * GW
        q.append(cut(a, 3 * HD))
        k += [cut(a + QW, 2 * HD), cut(a + QW + 4 * HD, HD)]
        v += [cut(a + QW + 2 * HD, 2 * HD), cut(a + QW + 5 * HD, HD)]
    return jnp.concatenate(q + k + v, axis=-1)


def group_rows(w):
    zero = jnp.zeros((HD,) + w.shape[1:], w.dtype)
    rows = []
    for i in range(INNER):
        a = 3 * i * HD
        rows += [w[a:a + 2 * HD], zero, w[a + 2 * HD:a + 3 * HD]]
    return jnp.concatenate(rows, axis=0)


def ungroup_rows(w):
    rows = []
    for i in range(INNER):
        a = i * QW
        rows += [w[a:a + 2 * HD], w[a + 3 * HD:a + 4 * HD]]
    return jnp.concatenate(rows, axis=0)


EPS = 1e-05


def layer_norm(values, gain, shift):
    center = values - jnp.mean(values, axis=-1, keepdims=True)
    spread = jnp.mean(center * center, axis=-1, keepdims=True)
    return center * lax.rsqrt(spread + EPS) * gain + shift


def gelu_tanh(values):
    return jax.nn.gelu(values, approximate=True)


def per_device(
    stream,
    doc_starts,
    ln1_gain,
    ln1_bias,
    qkv_weight,
    q_bias,
    v_bias,
    out_weight,
    out_bias,
    ln2_gain,
    ln2_bias,
    fc1_weight,
    fc1_bias,
    fc2_weight,
    fc2_bias,
    cotangent,
):
    f32 = jnp.float32
    bf16 = jnp.bfloat16
    ctx_count = lax.axis_size("ctx")
    tok_rows = stream.shape[1]
    width = stream.shape[2]
    length = ctx_count * tok_rows
    scale = HD ** (-0.5)
    params = (
        lax.all_gather(ln1_gain, "fsdp", axis=0, tiled=True),
        lax.all_gather(ln1_bias, "fsdp", axis=0, tiled=True),
        lax.all_gather(qkv_weight, "fsdp", axis=0, tiled=True),
        lax.all_gather(q_bias, "fsdp", axis=0, tiled=True),
        lax.all_gather(v_bias, "fsdp", axis=0, tiled=True),
        lax.all_gather(out_weight, "fsdp", axis=0, tiled=True),
        lax.all_gather(out_bias, "fsdp", axis=0, tiled=True),
        lax.all_gather(ln2_gain, "fsdp", axis=0, tiled=True),
        lax.all_gather(ln2_bias, "fsdp", axis=0, tiled=True),
        lax.all_gather(fc1_weight, "fsdp", axis=0, tiled=True),
        lax.all_gather(fc1_bias, "fsdp", axis=0, tiled=True),
        lax.all_gather(fc2_weight, "fsdp", axis=0, tiled=True),
        lax.all_gather(fc2_bias, "fsdp", axis=0, tiled=True),
    )
    (
        g_one,
        b_one,
        w_qkv,
        q_shift,
        v_shift,
        w_out,
        o_shift,
        g_two,
        b_two,
        w_fc1,
        c_fc1,
        w_fc2,
        c_fc2,
    ) = params
    inputs = stream[0].astype(f32)
    normed_f, ln1_pull = jax.vjp(layer_norm, inputs, g_one.astype(f32), b_one.astype(f32))
    normed_in = normed_f.astype(bf16)
    w_grp = group_qkv(w_qkv[:, :width] * bf16(scale), w_qkv[:, width : 2 * width], w_qkv[:, 2 * width :])
    shift = group_qkv(q_shift.astype(f32) * scale, jnp.zeros((width,), f32), v_shift.astype(f32))
    projected = (jnp.dot(normed_in, w_grp, preferred_element_type=f32) + shift).astype(bf16)
    attn, q_kept, kv_kept, out_kept, lse = attend(doc_starts, projected, length, 1)
    w_out = group_rows(w_out)
    hidden = inputs + jnp.dot(attn, w_out, preferred_element_type=f32) + o_shift.astype(f32)
    normed_mf, ln2_pull = jax.vjp(layer_norm, hidden, g_two.astype(f32), b_two.astype(f32))
    normed_mid = normed_mf.astype(bf16)
    pre_act = jnp.dot(normed_mid, w_fc1, preferred_element_type=f32) + c_fc1.astype(f32)
    activ_f, gelu_pull = jax.vjp(gelu_tanh, pre_act)
    activ = activ_f.astype(bf16)
    result = hidden + jnp.dot(activ, w_fc2, preferred_element_type=f32) + c_fc2.astype(f32)
    layer_out = result.astype(bf16)[None]
    params_back = (
        lax.all_gather(ln1_gain, "fsdp", axis=0, tiled=True),
        lax.all_gather(ln1_bias, "fsdp", axis=0, tiled=True),
        lax.all_gather(qkv_weight, "fsdp", axis=0, tiled=True),
        lax.all_gather(q_bias, "fsdp", axis=0, tiled=True),
        lax.all_gather(v_bias, "fsdp", axis=0, tiled=True),
        lax.all_gather(out_weight, "fsdp", axis=0, tiled=True),
        lax.all_gather(out_bias, "fsdp", axis=0, tiled=True),
        lax.all_gather(ln2_gain, "fsdp", axis=0, tiled=True),
        lax.all_gather(ln2_bias, "fsdp", axis=0, tiled=True),
        lax.all_gather(fc1_weight, "fsdp", axis=0, tiled=True),
        lax.all_gather(fc1_bias, "fsdp", axis=0, tiled=True),
        lax.all_gather(fc2_weight, "fsdp", axis=0, tiled=True),
        lax.all_gather(fc2_bias, "fsdp", axis=0, tiled=True),
    )
    wb_qkv = params_back[2]
    wb_out = w_out
    wb_fc1 = params_back[9]
    wb_fc2 = params_back[11]
    grad_out = cotangent[0]
    grad_w_fc2 = jnp.einsum("tf,td->fd", activ, grad_out, preferred_element_type=f32)
    grad_c_fc2 = jnp.sum(grad_out.astype(f32), axis=0)
    grad_activ = jnp.einsum("td,fd->tf", grad_out, wb_fc2, preferred_element_type=f32)
    grad_pre = gelu_pull(grad_activ)[0].astype(bf16)
    grad_w_fc1 = jnp.einsum("td,tf->df", normed_mid, grad_pre, preferred_element_type=f32)
    grad_c_fc1 = jnp.sum(grad_pre.astype(f32), axis=0)
    grad_norm_mid = jnp.einsum("tf,df->td", grad_pre, wb_fc1, preferred_element_type=f32)
    grad_hid_part, grad_g_two, grad_b_two = ln2_pull(grad_norm_mid)
    grad_hidden = grad_out.astype(f32) + grad_hid_part
    grad_branch = grad_hidden.astype(bf16)
    grad_w_out = ungroup_rows(jnp.einsum("td,te->de", attn, grad_branch, preferred_element_type=f32))
    grad_o_shift = jnp.sum(grad_branch.astype(f32), axis=0)
    grad_attn = jnp.einsum("te,de->td", grad_branch, wb_out, preferred_element_type=f32).astype(
        bf16
    )
    grad_qkv = ungroup_qkv(attend_back(doc_starts, grad_attn, q_kept, kv_kept, out_kept, lse, length, 2))
    grad_query = grad_qkv[:, :width]
    grad_values = grad_qkv[:, 2 * width :]
    grad_w_qkv = jnp.einsum("td,te->de", normed_in, grad_qkv, preferred_element_type=f32)
    grad_q_shift = jnp.sum(grad_query.astype(f32), axis=0)
    grad_v_shift = jnp.sum(grad_values.astype(f32), axis=0)
    grad_norm_in = jnp.einsum("te,de->td", grad_qkv, wb_qkv, preferred_element_type=f32)
    grad_in_part, grad_g_one, grad_b_one = ln1_pull(grad_norm_in)
    input_grad = (grad_hidden + grad_in_part)[None]
    shards = lax.axis_size("fsdp")
    part = width // shards
    blocks = []
    for grad in (grad_w_qkv, grad_w_out, grad_w_fc1):
        cols = grad.shape[1] // width
        blocks.append(grad.reshape(shards, part, cols, width).transpose(0, 2, 1, 3).reshape(shards, cols * part, width).astype(bf16))
    blocks.append(grad_w_fc2.reshape(shards, -1, width).astype(bf16))
    packed = jnp.concatenate(blocks, axis=1)
    vectors = [grad_g_one, grad_b_one, grad_q_shift, grad_v_shift, grad_o_shift, grad_g_two, grad_b_two, grad_c_fc2]
    lines = [one.reshape(shards, 1, part) for one in vectors]
    lines.append(grad_c_fc1.reshape(shards, -1, part))
    lines.append(jnp.zeros((shards, 4, part), f32))
    total, vec = reduce_grads(packed, jnp.concatenate(lines, axis=1), 0)
    total = total.astype(f32)
    edges = [0, 3 * part, 4 * part, 8 * part, 12 * part]
    t_qkv, t_out, t_fc1, t_fc2 = [total[a:b] for a, b in zip(edges[:-1], edges[1:])]

    def unpack(block):
        cols = block.shape[0] // part
        return block.reshape(cols, part, width).transpose(1, 0, 2).reshape(part, cols * width)

    return (
        layer_out, input_grad, vec[0], vec[1], unpack(t_qkv), vec[2], vec[3], t_out, vec[4], vec[5], vec[6],
        unpack(t_fc1), vec[8:12].reshape(-1), t_fc2, vec[7],
    )


def solution(mesh):
    in_specs = (
        P("fsdp", "ctx", None),
        P("fsdp", None),
        P("fsdp"),
        P("fsdp"),
        P("fsdp", None),
        P("fsdp"),
        P("fsdp"),
        P("fsdp", None),
        P("fsdp"),
        P("fsdp"),
        P("fsdp"),
        P("fsdp", None),
        P("fsdp"),
        P("fsdp", None),
        P("fsdp"),
        P("fsdp", "ctx", None),
    )
    out_specs = (
        P("fsdp", "ctx", None),
        P("fsdp", "ctx", None),
        P("fsdp"),
        P("fsdp"),
        P("fsdp", None),
        P("fsdp"),
        P("fsdp"),
        P("fsdp", None),
        P("fsdp"),
        P("fsdp"),
        P("fsdp"),
        P("fsdp", None),
        P("fsdp"),
        P("fsdp", None),
        P("fsdp"),
    )
    return jax.shard_map(
        per_device, mesh=mesh, in_specs=in_specs, out_specs=out_specs, check_vma=False
    )
```

```python
import functools

import jax
import jax.numpy as jnp
from jax import lax
from jax.experimental import pallas as pl
from jax.experimental.pallas import tpu as pltpu
from jax.sharding import PartitionSpec as P

H = 12
HD = 64
MESH = pl.DeviceIdType.MESH
BF = jnp.bfloat16
F32 = jnp.float32


def ring_of(ctx, n):
    g = ctx // 2
    return jnp.where(g % 2 == 0, g // 2, n - 1 - g // 2)

def ring_ctx(r, n, bit):
    r = lax.rem(r + n, n)
    g = jnp.where(r < n // 2, 2 * r, 2 * (n - 1 - r) + 1)
    return g * 2 + bit

def grads_kernel(n, fs, s_one, s_two, subs, x_one, g_qkv, x_out, g_out, x_mid, g_pre, x_act, g_top, v_ref,
                 o_qkv, o_out, o_fc1, o_fc2, vout_ref,
                 xt, gbuf, acc, fbuf, xbuf1, rbuf1, xbuf2, rbuf2, outb,
                 vacc, vf, vx, vr,
                 lsem, fsem, frec, xs, xr, rs, rr, vfs, vfr, vxs, vxr, vrs, vrr, osem):
    c = lax.axis_index("ctx")
    f = lax.axis_index("fsdp")
    bit = c % 2
    pos = ring_of(c, n)
    xpeer = (c + 1 - 2 * bit, f)
    right = (ring_ctx(pos + 1, n, bit), f)
    left = (ring_ctx(pos - 1, n, bit), f)
    rows = s_one + s_two
    width = acc.shape[1]
    half = width // 2
    part = width // fs
    used = 12 * part
    lanes = (pl.ds(0, half), pl.ds(half, half))
    fpeers = [(c, lax.rem(f + k, fs)) for k in range(1, fs)]
    barrier = pltpu.get_barrier_semaphore()
    for peer in [xpeer, right, left] + fpeers:
        pl.semaphore_signal(barrier, inc=1, device_id=peer, device_id_type=MESH)
    pl.semaphore_wait(barrier, 2 + fs)

    def remote(src, dst, ssem, rsem, peer):
        cp = pltpu.make_async_remote_copy(src_ref=src, dst_ref=dst, send_sem=ssem, recv_sem=rsem,
                                          device_id=peer, device_id_type=MESH)
        return cp

    pend = []

    def go(cp):
        cp.start()
        pend.append(cp)
        return cp
    vown = pltpu.make_async_copy(v_ref.at[f], vacc, lsem.at[1])
    vown.start()
    fcs = []
    for k in range(1, fs):
        fcs.append(go(remote(v_ref.at[fpeers[k - 1][1]], vf.at[k - 1], vfs.at[k - 1], vfr.at[k - 1], fpeers[k - 1])))
    eye_n = 256
    rr_i = lax.broadcasted_iota(jnp.int32, (eye_n, eye_n), 0)
    eye = (rr_i == lax.broadcasted_iota(jnp.int32, (eye_n, eye_n), 1)).astype(BF)
    first_row = {}
    at = 0
    for name, ref in (("act", x_act), ("mid", x_mid), ("out", x_out), ("one", x_one)):
        first_row[name] = at

        @pl.loop(0, ref.shape[1] // eye_n)
        def _(b):
            o = pl.multiple_of(b * eye_n, eye_n)
            xt[pl.ds(pl.multiple_of(at + o, eye_n), eye_n), :] = nt(eye, ref[:, pl.ds(o, eye_n)]).astype(BF)
        at += ref.shape[1]

    def unit(name, start, g, dst, row):
        lhs = xt[pl.ds(pl.multiple_of(first_row[name] + start, 16), part), :]
        dst[pl.ds(pl.multiple_of(row, 16), part), :] = nn(lhs, g).astype(BF)

    cuts = ((max(8 * part, s_one), used), (s_one, max(8 * part, s_one)), (0, s_one))

    def grads_for(owner, dst, after):
        @pl.loop(0, 4)
        def _(j):
            unit("act", owner * 4 * part + j * part, g_top[...], dst, (8 + j) * part)
        after(0)

        @pl.loop(0, 4)
        def _(j):
            unit("mid", owner * part, g_pre[:, pl.ds(pl.multiple_of(j * width, 128), width)], dst, (4 + j) * part)
        after(1)
        unit("out", owner * part, g_out[...], dst, 3 * part)

        @pl.loop(0, 3)
        def _(j):
            unit("one", owner * part, g_qkv[:, pl.ds(pl.multiple_of(j * width, 128), width)], dst, j * part)
        after(2)

    for k in range(1, fs):
        def post(j):
            a, b = cuts[j]
            if b > a:
                go(remote(gbuf.at[k - 1, pl.ds(a, b - a)], fbuf.at[k - 1, pl.ds(a, b - a)],
                          fsem.at[k - 1, j], frec.at[k - 1, j], fpeers[k - 1]))
        grads_for(fpeers[k - 1][1], gbuf.at[k - 1], post)
    if used < rows:
        acc[used:, :] = jnp.zeros((rows - used, width), BF)

    def fadd(a, m):
        blk = 32

        @pl.loop(0, m // blk)
        def _(i):
            rws = pl.ds(pl.multiple_of(a + i * blk, blk), blk)
            tot = acc[rws, :].astype(F32)
            for k in range(fs - 1):
                tot = tot + fbuf[k, rws, :].astype(F32)
            acc[rws, :] = tot.astype(BF)

    def own_part(j):
        a, b = cuts[j]
        if b > a:
            for k in range(1, fs):
                remote(gbuf.at[k - 1, pl.ds(a, b - a)], fbuf.at[k - 1, pl.ds(a, b - a)],
                       fsem.at[k - 1, j], frec.at[k - 1, j], fpeers[k - 1]).wait_recv()
            fadd(a, b - a)

    grads_for(f, acc, lambda j: None)
    vown.wait()
    own_part(0)
    own_part(1)

    chunk2 = s_two // n
    sub2 = chunk2 // subs
    h1 = s_one // 2
    chunk1 = h1 // n
    sub1 = chunk1 // subs

    def rows_of(base, chunk, k, sub, j):
        k = lax.rem(k + 2 * n, n)
        return pl.ds(pl.multiple_of(base + k * chunk + j * sub, 16), sub)

    def rs_send(st, base, chunk, sub, rbuf, s, j):
        for d in range(2):
            k = pos - 1 - s if d == 0 else pos + 1 + s
            go(remote(acc.at[rows_of(base, chunk, k, sub, j), lanes[d]],
                      rbuf.at[s, pl.ds(j * sub, sub), lanes[d]],
                      rs.at[st, 0, d, s, j], rr.at[st, 0, d, s, j], right if d == 0 else left))

    def rs_recv(st, base, chunk, sub, rbuf, s, j):
        for d in range(2):
            k = pos - 2 - s if d == 0 else pos + 2 + s
            rws = rows_of(base, chunk, k, sub, j)
            cp = remote(acc.at[rws, lanes[d]], rbuf.at[s, pl.ds(j * sub, sub), lanes[d]],
                        rs.at[st, 0, d, s, j], rr.at[st, 0, d, s, j], right)
            cp.wait_recv()
            acc[rws, lanes[d]] = (acc[rws, lanes[d]].astype(F32)
                                  + rbuf[s, pl.ds(j * sub, sub), lanes[d]].astype(F32)).astype(BF)

    def ag_send(st, base, chunk, sub, s, j):
        for d in range(2):
            k = pos - s if d == 0 else pos + s
            rws = rows_of(base, chunk, k, sub, j)
            go(remote(outb.at[rws, lanes[d]], outb.at[rws, lanes[d]],
                      rs.at[st, 1, d, s, j], rr.at[st, 1, d, s, j], right if d == 0 else left))

    def ag_recv(st, base, chunk, sub, s, j):
        for d in range(2):
            k = pos - 1 - s if d == 0 else pos + 1 + s
            rws = rows_of(base, chunk, k, sub, j)
            remote(outb.at[rws, lanes[d]], outb.at[rws, lanes[d]],
                   rs.at[st, 1, d, s, j], rr.at[st, 1, d, s, j], right).wait_recv()

    two = (1, s_one, chunk2, sub2)
    base1 = pl.multiple_of(bit * h1, 16)
    other1 = pl.multiple_of((1 - bit) * h1, 16)
    one = (0, base1, chunk1, sub1)

    for k in range(1, fs):
        fcs[k - 1].wait_recv()
    vtot = vacc[...]
    for k in range(fs - 1):
        vtot = vtot + vf[k]
    vacc[...] = vtot
    vxc = go(remote(vacc, vx, vxs, vxr, xpeer))

    for j in range(subs):
        rs_send(*two, rbuf2, 0, j)
    own_part(2)
    xc1 = go(remote(acc.at[pl.ds(other1, h1)], xbuf1, xs.at[0], xr.at[0], xpeer))

    vxc.wait_recv()
    vr[pos] = vacc[...] + vx[...]

    for s in range(n - 1):
        vcp = go(remote(vr.at[lax.rem(pos - s + n, n)], vr.at[lax.rem(pos - s + n, n)],
                        vrs.at[s], vrr.at[s], right))
        for j in range(subs):
            rs_recv(*two, rbuf2, s, j)
            if s < n - 2:
                rs_send(*two, rbuf2, s + 1, j)
        w = lax.rem(pos - 1 - s + n, n)
        remote(vr.at[w], vr.at[w], vrs.at[s], vrr.at[s], right).wait_recv()
    hx = chunk2 // 2
    mine2 = pl.multiple_of(s_one + pos * chunk2 + bit * hx, 16)
    theirs2 = pl.multiple_of(s_one + pos * chunk2 + (1 - bit) * hx, 16)
    xc2 = go(remote(acc.at[pl.ds(theirs2, hx)], xbuf2, xs.at[1], xr.at[1], xpeer))
    xc1.wait_recv()
    blk = 16 * 5 if h1 % 80 == 0 else 16

    @pl.loop(0, h1 // blk)
    def _(i):
        rws = pl.ds(pl.multiple_of(base1 + i * blk, 16), blk)
        acc[rws, :] = (acc[rws, :].astype(F32)
                       + xbuf1[pl.ds(pl.multiple_of(i * blk, 16), blk), :].astype(F32)).astype(BF)
    for j in range(subs):
        rs_send(*one, rbuf1, 0, j)
    vsum = vr[0]
    for k in range(1, n):
        vsum = vsum + vr[k]
    vout_ref[...] = vsum
    xc2.wait_recv()
    outb[pl.ds(mine2, hx), :] = (acc[pl.ds(mine2, hx), :].astype(F32) + xbuf2[...].astype(F32)).astype(BF)
    xg2 = go(remote(outb.at[pl.ds(mine2, hx)], outb.at[pl.ds(mine2, hx)], xs.at[2], xr.at[2], xpeer))
    for s in range(n - 1):
        for j in range(subs):
            rs_recv(*one, rbuf1, s, j)
            if s < n - 2:
                rs_send(*one, rbuf1, s + 1, j)
            else:
                rws = rows_of(base1, chunk1, pos, sub1, j)
                outb[rws, :] = acc[rws, :]
                ag_send(*one, 0, j)
    remote(outb.at[pl.ds(theirs2, hx)], outb.at[pl.ds(theirs2, hx)], xs.at[2], xr.at[2], xpeer).wait_recv()
    for s in range(n - 1):
        for j in range(subs):
            ag_recv(*one, s, j)
            if s < n - 2:
                ag_send(*one, s + 1, j)
    xg1 = go(remote(outb.at[pl.ds(base1, h1)], outb.at[pl.ds(base1, h1)], xs.at[3], xr.at[3], xpeer))
    for j in range(subs):
        ag_send(*two, 0, j)
    for s in range(n - 1):
        for j in range(subs):
            ag_recv(*two, s, j)
            if s < n - 2:
                ag_send(*two, s + 1, j)
    remote(outb.at[pl.ds(other1, h1)], outb.at[pl.ds(other1, h1)], xs.at[3], xr.at[3], xpeer).wait_recv()
    outs = []
    for u in range(12):
        src = outb.at[pl.ds(u * part, part)]
        if u < 3:
            dst = o_qkv.at[:, pl.ds(u * width, width)]
        elif u == 3:
            dst = o_out
        elif u < 8:
            dst = o_fc1.at[:, pl.ds((u - 4) * width, width)]
        else:
            dst = o_fc2.at[pl.ds((u - 8) * part, part)]
        cp = pltpu.make_async_copy(src, dst, osem.at[u])
        cp.start()
        outs.append(cp)
    for cp in pend:
        cp.wait_send()
    for cp in outs:
        cp.wait()


def split_rows(rows, n, subs):
    unit = 2 * n * subs * 16
    units = max(2, -(-rows // unit))
    one = max(1, (units * 4) // 9)
    return one * unit, (units - one) * unit


def reduce_grads(x_one, g_qkv, x_out, g_out, x_mid, g_pre, x_act, g_top, v, cid, subs=2):
    fs = lax.axis_size("fsdp")
    n = lax.axis_size("ctx") // 2
    toks, width = x_one.shape
    part = width // fs
    rows = 12 * part
    s_one, s_two = split_rows(rows, n, subs)
    tot = s_one + s_two
    vs = v.shape[1:]
    dma = pltpu.SemaphoreType.DMA
    chunk1, chunk2 = s_one // 2 // n, s_two // n
    feats = x_one.shape[1] + x_out.shape[1] + x_mid.shape[1] + x_act.shape[1]
    anyspec = pl.BlockSpec(memory_space=pl.ANY)
    vm = pl.BlockSpec(memory_space=pltpu.VMEM)
    return pl.pallas_call(
        functools.partial(grads_kernel, n, fs, s_one, s_two, subs),
        out_shape=(jax.ShapeDtypeStruct((part, 3 * width), BF), jax.ShapeDtypeStruct((part, width), BF),
                   jax.ShapeDtypeStruct((part, 4 * width), BF), jax.ShapeDtypeStruct((4 * part, width), BF),
                   jax.ShapeDtypeStruct(vs, F32)),
        in_specs=[vm] * 8 + [anyspec],
        out_specs=(anyspec, anyspec, anyspec, anyspec, vm),
        scratch_shapes=[
            pltpu.VMEM((feats, toks), BF),
            pltpu.VMEM((fs - 1, rows, width), BF),
            pltpu.VMEM((tot, width), BF),
            pltpu.VMEM((fs - 1, rows, width), BF),
            pltpu.VMEM((s_one // 2, width), BF),
            pltpu.VMEM((n - 1, chunk1, width), BF),
            pltpu.VMEM((chunk2 // 2, width), BF),
            pltpu.VMEM((n - 1, chunk2, width), BF),
            pltpu.VMEM((tot, width), BF),
            pltpu.VMEM(vs, F32),
            pltpu.VMEM((fs - 1,) + vs, F32),
            pltpu.VMEM(vs, F32),
            pltpu.VMEM((n,) + vs, F32),
            dma((2,)), dma((fs - 1, 3)), dma((fs - 1, 3)), dma((4,)), dma((4,)),
            dma((2, 2, 2, n - 1, subs)), dma((2, 2, 2, n - 1, subs)),
            dma((fs - 1,)), dma((fs - 1,)), dma(()), dma(()), dma((n - 1,)), dma((n - 1,)), dma((12,)),
        ],
        compiler_params=pltpu.CompilerParams(collective_id=cid, has_side_effects=True, vmem_limit_bytes=60 << 20),
        name="reduce_grads",
    )(x_one, g_qkv, x_out, g_out, x_mid, g_pre, x_act, g_top, v)


INNER = 4
QW, KW = 256, 384
GW = QW + KW
NEG = -1e30


def nt(a, b):
    return lax.dot_general(a, b, (((1,), (1,)), ((), ())), preferred_element_type=F32)


def nn(a, b):
    return lax.dot_general(a, b, (((1,), (0,)), ((), ())), preferred_element_type=F32)


def head_lanes(x, head):
    if head == 2:
        return x
    lane = lax.broadcasted_iota(jnp.int32, x.shape, 1)
    keep = lane < HD if head == 0 else lane >= HD
    return jnp.where(keep, x, jnp.zeros_like(x))


def first_keys(starts_ref, pos):
    first = jnp.zeros_like(pos)
    for d in range(starts_ref.shape[1]):
        one = starts_ref[0, d]
        first = jnp.maximum(first, jnp.where(one <= pos, one, 0))
    return first


def places():
    c = lax.axis_index("ctx")
    f = lax.axis_index("fsdp")
    return c // INNER, c % INNER, f


def greet(z, h, f, depth):
    barrier = pltpu.get_barrier_semaphore()
    for j in range(1, INNER):
        pl.semaphore_signal(barrier, inc=1, device_id=(z * INNER + (h + j) % INNER, f), device_id_type=MESH)

    @pl.when(z > 0)
    def _():
        pl.semaphore_signal(barrier, inc=1, device_id=((z - 1) * INNER + h, f), device_id_type=MESH)

    @pl.when(z < depth - 1)
    def _():
        pl.semaphore_signal(barrier, inc=1, device_id=((z + 1) * INNER + h, f), device_id_type=MESH)

    count = INNER - 1 + jnp.where(z > 0, 1, 0) + jnp.where(z < depth - 1, 1, 0)
    pl.semaphore_wait(barrier, count)


def send(src, dst, ssem, rsem, peer):
    return pltpu.make_async_remote_copy(
        src_ref=src, dst_ref=dst, send_sem=ssem, recv_sem=rsem, device_id=peer, device_id_type=MESH
    )


def group_qkv(src, dst):
    width = H * HD
    dst_zero = jnp.zeros((dst.shape[0], HD), dst.dtype)
    for i in range(INNER):
        a, o = 3 * i * HD, i * GW
        dst[:, o:o + 3 * HD] = (src[:, a:a + 3 * HD].astype(F32) * (HD ** -0.5)).astype(dst.dtype)
        dst[:, o + 3 * HD:o + QW] = dst_zero
        dst[:, o + QW:o + QW + 2 * HD] = src[:, width + a:width + a + 2 * HD]
        dst[:, o + QW + 2 * HD:o + QW + 4 * HD] = src[:, 2 * width + a:2 * width + a + 2 * HD]
        dst[:, o + QW + 4 * HD:o + QW + 5 * HD] = src[:, width + a + 2 * HD:width + a + 3 * HD]
        dst[:, o + QW + 5 * HD:o + QW + 6 * HD] = src[:, 2 * width + a + 2 * HD:2 * width + a + 3 * HD]


def ungroup_qkv(src, dst):
    width = H * HD
    for i in range(INNER):
        a, o = 3 * i * HD, i * GW
        dst[:, a:a + 3 * HD] = src[:, o:o + 3 * HD]
        dst[:, width + a:width + a + 2 * HD] = src[:, o + QW:o + QW + 2 * HD]
        dst[:, 2 * width + a:2 * width + a + 2 * HD] = src[:, o + QW + 2 * HD:o + QW + 4 * HD]
        dst[:, width + a + 2 * HD:width + a + 3 * HD] = src[:, o + QW + 4 * HD:o + QW + 5 * HD]
        dst[:, 2 * width + a + 2 * HD:2 * width + a + 3 * HD] = src[:, o + QW + 5 * HD:o + QW + 6 * HD]


def group_rows(src, dst):
    dst_zero = jnp.zeros((dst.shape[0], HD), dst.dtype)
    for i in range(INNER):
        a, o = 3 * i * HD, i * QW
        dst[:, o:o + 2 * HD] = src[:, a:a + 2 * HD]
        dst[:, o + 2 * HD:o + 3 * HD] = dst_zero
        dst[:, o + 3 * HD:o + 4 * HD] = src[:, a + 2 * HD:a + 3 * HD]


def ungroup_rows(src, dst):
    for i in range(INNER):
        a, o = 3 * i * HD, i * QW
        dst[:, a:a + 2 * HD] = src[:, o:o + 2 * HD]
        dst[:, a + 2 * HD:a + 3 * HD] = src[:, o + 3 * HD:o + 4 * HD]


K_LANES = (0, 0, 256)
V_LANES = (128, 128, 256)
Q_LANES = (0, 0, 128)


def attend_kernel(depth, length, starts_ref, raw_ref, out_ref, qb_ref, kv_ref, ot_ref, lse_ref,
                  x_ref, qb, kv, acc, top, tot, ob, land,
                  lsem, as_kv, ar_kv, as_q, ar_q, zs, zr, bs, br, osem):
    z, h, f = places()
    blk = raw_ref.shape[0] // 2
    rows = INNER * blk
    half_rows = (pl.ds(0, blk), pl.ds(blk, blk))
    my_piece = (h, INNER - 1 - h)

    def piece(half, i):
        p = i if half == 0 else INNER - 1 - i
        return pl.ds(pl.multiple_of(p * blk, blk), blk)

    own = (depth - 1, depth)
    group_qkv(raw_ref, x_ref)
    greet(z, h, f, depth)

    def a2a(j, half, kind):
        i = (h + j) % INNER
        lanes = pl.ds(pl.multiple_of(i * GW + (QW if kind else 0), 128), KW if kind else QW)
        dst = kv.at[own[half], piece(half, h)] if kind else qb.at[half, piece(half, h)]
        sems = (as_kv.at[half, j - 1], ar_kv.at[half, j - 1]) if kind else (as_q.at[half, j - 1], ar_q.at[half, j - 1])
        return send(x_ref.at[half_rows[half], lanes], dst, *sems, (z * INNER + i, f))

    def local(half, kind):
        lanes = pl.ds(pl.multiple_of(h * GW + (QW if kind else 0), 128), KW if kind else QW)
        dst = kv.at[own[half], piece(half, h)] if kind else qb.at[half, piece(half, h)]
        return pltpu.make_async_copy(x_ref.at[half_rows[half], lanes], dst, lsem.at[half, kind])

    for kind in (1, 0):
        for half in range(2):
            for j in range(1, INNER):
                a2a(j, half, kind).start()
            local(half, kind).start()

    def relay(half, src_slot, step, p):
        rws = pl.ds(pl.multiple_of(p * blk, blk), blk)
        if half == 0:
            peer, slot = (z + 1) * INNER + h, step - 1
        else:
            peer, slot = (z - 1) * INNER + h, z - 1 + step - 1
        return send(kv.at[src_slot, rws], kv.at[slot, rws], zs.at[half, step - 1, p], zr.at[half, step - 1, p], (peer, f))

    can = (z < depth - 1, z > 0)
    for j in range(INNER):
        i = (h + INNER - j) % INNER
        for half in range(2):
            if j == 0:
                local(half, 1).wait()
            else:
                a2a(j, half, 1).wait_recv()

            @pl.when(can[half])
            def _():
                relay(half, own[half], 1, i if half == 0 else INNER - 1 - i).start()

    for half in range(2):
        local(half, 0).wait()
        for j in range(1, INNER):
            a2a(j, half, 0).wait_recv()

    def base_of(half, zz):
        return zz * rows if half == 0 else length - (zz + 1) * rows

    cols = rows // 2

    def tile(half, slot, q_base, k_base, diag):
        for head in range(3):
            k_all = kv[slot, :, K_LANES[head]:K_LANES[head] + 128]
            v_all = kv[slot, :, V_LANES[head]:V_LANES[head] + 128]
            v_t = v_all.T[(0 if head == 0 else HD):(HD if head == 0 else 2 * HD)]
            for part in range(2):
                keys = (part + 1) * cols if diag else rows
                lanes = slice(part * cols, (part + 1) * cols)
                q = head_lanes(qb[half, lanes, Q_LANES[head]:Q_LANES[head] + 128], head)
                pos = q_base + part * cols + lax.broadcasted_iota(jnp.int32, (1, cols), 1)
                first = first_keys(starts_ref, pos) - k_base
                s = nt(k_all[:keys], q)
                row = lax.broadcasted_iota(jnp.int32, (keys, cols), 0)
                ok = row >= first
                if diag:
                    ok = ok & (row <= pos - k_base)
                s = jnp.where(ok, s, NEG)
                line = slice(head, head + 1)
                feats = slice(head * HD, (head + 1) * HD)
                high = jnp.max(s, axis=0, keepdims=True)
                if not diag:
                    before = top[half, line, lanes]
                    high = jnp.maximum(before, high)
                    fade = jnp.exp(before - high)
                w = jnp.exp(s - high)
                add = jnp.sum(w, axis=0, keepdims=True)
                o = nn(v_t[:, :keys], w.astype(BF))
                if diag:
                    tot[half, line, lanes] = add
                    acc[half, feats, lanes] = o
                else:
                    tot[half, line, lanes] = tot[half, line, lanes] * fade + add
                    acc[half, feats, lanes] = acc[half, feats, lanes] * fade + o
                top[half, line, lanes] = high

    @pl.loop(0, 2)
    def _(half):
        q_base = jnp.where(half == 0, base_of(0, z), base_of(1, z))
        tile(half, depth - 1 + half, q_base, q_base, True)

    @pl.loop(1, depth)
    def _(step):
        valid = (z - step >= 0, z + step <= depth - 1)
        slots = (step - 1, z + step - 1)
        for half in range(2):
            for p in range(INNER):
                @pl.when(valid[half])
                def _():
                    rws = pl.ds(p * blk, blk)
                    send(kv.at[slots[half], rws], kv.at[slots[half], rws], zs.at[half, step - 1, p],
                         zr.at[half, step - 1, p], (z * INNER + (h + 1) % INNER, f)).wait_recv()

                @pl.when(valid[half] & can[half])
                def _():
                    relay(half, slots[half], step + 1, p).start()

        @pl.loop(0, 2)
        def _(half):
            @pl.when(jnp.where(half == 0, z - step, depth - 1 - z - step) >= 0)
            def _():
                zz = jnp.where(half == 0, z - step, z + step)
                q_base = jnp.where(half == 0, base_of(0, z), base_of(1, z))
                k_base = jnp.where(half == 0, base_of(0, zz), base_of(1, zz))
                tile(half, jnp.where(half == 0, step - 1, z + step - 1), q_base, k_base, False)

    ob[:, :, 2 * HD:3 * HD] = jnp.zeros((2, rows, HD), BF)
    for half in range(2):
        lse_ref[half] = top[half] + jnp.log(tot[half])
        for head in range(3):
            feats = slice(head * HD, (head + 1) * HD)
            acc[half, feats, :] = acc[half, feats, :] / tot[half, head:head + 1, :]
        ob[half, :, :2 * HD] = acc[half, :2 * HD, :].T.astype(BF)
        ob[half, :, 3 * HD:] = acc[half, 2 * HD:, :].T.astype(BF)
    outs = [pltpu.make_async_copy(qb, qb_ref, osem.at[0]), pltpu.make_async_copy(kv, kv_ref, osem.at[1]),
            pltpu.make_async_copy(acc, ot_ref, osem.at[2])]
    for cp in outs:
        cp.start()

    def back(j, half):
        i = (h + j) % INNER
        return send(ob.at[half, piece(half, i)], land.at[half_rows[half], pl.ds(pl.multiple_of(h * QW, 128), QW)],
                    bs.at[half, j - 1], br.at[half, j - 1], (z * INNER + i, f))

    for half in range(2):
        for j in range(1, INNER):
            back(j, half).start()
        mine = pltpu.make_async_copy(ob.at[half, piece(half, h)],
                                     land.at[half_rows[half], pl.ds(pl.multiple_of(h * QW, 128), QW)], lsem.at[half, 0])
        mine.start()
        mine.wait()
    for half in range(2):
        for j in range(1, INNER):
            back(j, half).wait_recv()
    ungroup_rows(land, out_ref)
    for half in range(2):
        for j in range(1, INNER):
            a2a(j, half, 1).wait_send()
            a2a(j, half, 0).wait_send()
            back(j, half).wait_send()

        @pl.when(can[half])
        def _():
            for p in range(INNER):
                relay(half, own[half], 1, p).wait_send()

    @pl.loop(1, depth)
    def _(step):
        valid = (z - step >= 0, z + step <= depth - 1)
        for half in range(2):
            @pl.when(valid[half] & can[half])
            def _():
                for p in range(INNER):
                    relay(half, own[half], step + 1, p).wait_send()
    for cp in outs:
        cp.wait()


def attend(starts, x, length, cid):
    depth = lax.axis_size("ctx") // INNER
    blk = x.shape[0] // 2
    rows = INNER * blk
    dma = pltpu.SemaphoreType.DMA
    shapes = (
        jax.ShapeDtypeStruct((x.shape[0], H * HD), BF),
        jax.ShapeDtypeStruct((2, rows, QW), BF),
        jax.ShapeDtypeStruct((depth + 1, rows, KW), BF),
        jax.ShapeDtypeStruct((2, 3 * HD, rows), F32),
        jax.ShapeDtypeStruct((2, 8, rows), F32),
    )
    vm = pl.BlockSpec(memory_space=pltpu.VMEM)
    anyspec = pl.BlockSpec(memory_space=pl.ANY)
    return pl.pallas_call(
        functools.partial(attend_kernel, depth, length),
        out_shape=shapes,
        in_specs=[pl.BlockSpec(memory_space=pltpu.SMEM), vm],
        out_specs=(vm, anyspec, anyspec, anyspec, vm),
        scratch_shapes=[
            pltpu.VMEM((2 * blk, INNER * GW), BF),
            pltpu.VMEM((2, rows, QW), BF),
            pltpu.VMEM((depth + 1, rows, KW), BF),
            pltpu.VMEM((2, 3 * HD, rows), F32),
            pltpu.VMEM((2, 8, rows), F32),
            pltpu.VMEM((2, 8, rows), F32),
            pltpu.VMEM((2, rows, QW), BF),
            pltpu.VMEM((2 * blk, INNER * QW), BF),
            dma((2, 2)), dma((2, 3)), dma((2, 3)), dma((2, 3)), dma((2, 3)),
            dma((2, depth, INNER)), dma((2, depth, INNER)), dma((2, 3)), dma((2, 3)), dma((3,)),
        ],
        compiler_params=pltpu.CompilerParams(collective_id=cid, has_side_effects=True, vmem_limit_bytes=48 << 20),
        name="attend",
    )(starts, x)


def attend_back_kernel(depth, length, starts_ref, raw_ref, qb, kv, ot, lse, out_ref,
                       do_ref, dob, dots, dq, dkv, sbuf, rbuf, dqb, fin, land,
                       lsem, as_o, ar_o, zs, zr, bq, brq, bk, brk):
    z, h, f = places()
    blk = raw_ref.shape[0] // 2
    rows = INNER * blk
    half_rows = (pl.ds(0, blk), pl.ds(blk, blk))

    def piece(half, i):
        p = i if half == 0 else INNER - 1 - i
        return pl.ds(pl.multiple_of(p * blk, blk), blk)

    group_rows(raw_ref, do_ref)
    greet(z, h, f, depth)

    def a2a(j, half):
        i = (h + j) % INNER
        return send(do_ref.at[half_rows[half], pl.ds(pl.multiple_of(i * QW, 128), QW)], dob.at[half, piece(half, h)],
                    as_o.at[half, j - 1], ar_o.at[half, j - 1], (z * INNER + i, f))

    mine = []
    for half in range(2):
        for j in range(1, INNER):
            a2a(j, half).start()
        cp = pltpu.make_async_copy(do_ref.at[half_rows[half], pl.ds(pl.multiple_of(h * QW, 128), QW)],
                                   dob.at[half, piece(half, h)], lsem.at[half])
        cp.start()
        mine.append(cp)
    dq[...] = jnp.zeros_like(dq)
    for half in range(2):
        mine[half].wait()
        for j in range(1, INNER):
            a2a(j, half).wait_recv()
        for head in range(3):
            lanes = slice(0, 128) if head < 2 else slice(128, 256)
            g = dob[half, :, lanes].astype(F32).T[(0 if head == 0 else HD):(HD if head == 0 else 2 * HD)]
            dots[half, head:head + 1, :] = jnp.sum(g * ot[half, head * HD:(head + 1) * HD, :], axis=0, keepdims=True)

    def base_of(half, zz):
        return zz * rows if half == 0 else length - (zz + 1) * rows

    cols = rows // 2

    def tile(half, slot, q_base, k_base, diag):
        for head in range(3):
            k_all = kv[slot, :, K_LANES[head]:K_LANES[head] + 128]
            v_all = kv[slot, :, V_LANES[head]:V_LANES[head] + 128]
            k_t = k_all.T[(HD if head == 1 else 0):(2 * HD if head == 1 else HD)]
            for part in range(2):
                keys = (part + 1) * cols if diag else rows
                lanes = slice(part * cols, (part + 1) * cols)
                q = head_lanes(qb[half, lanes, Q_LANES[head]:Q_LANES[head] + 128], head)
                g = head_lanes(dob[half, lanes, Q_LANES[head]:Q_LANES[head] + 128], head)
                pos = q_base + part * cols + lax.broadcasted_iota(jnp.int32, (1, cols), 1)
                first = first_keys(starts_ref, pos) - k_base
                s = nt(k_all[:keys], q)
                row = lax.broadcasted_iota(jnp.int32, (keys, cols), 0)
                ok = row >= first
                if diag:
                    ok = ok & (row <= pos - k_base)
                line = slice(head, head + 1)
                w = jnp.where(ok, jnp.exp(s - lse[half, line, lanes]), 0.0)
                gp = nt(v_all[:keys], g)
                ds = (w * (gp - dots[half, line, lanes])).astype(BF)
                wb = w.astype(BF)
                dv = nn(wb, g)
                dk = nn(ds, q)
                kl = slice(K_LANES[head], K_LANES[head] + 128)
                vl = slice(V_LANES[head], V_LANES[head] + 128)
                if head == 2:
                    both = dk + dv
                    if part == 0:
                        dkv[:keys, kl] = both
                    elif keys == rows and diag:
                        dkv[:cols, kl] = dkv[:cols, kl] + both[:cols]
                        dkv[cols:, kl] = both[cols:]
                    else:
                        dkv[:, kl] = dkv[:, kl] + both
                else:
                    for sl, val in ((kl, dk), (vl, dv)):
                        if head == 0 and part == 0:
                            dkv[:keys, sl] = val
                        elif head == 0 and diag:
                            dkv[:cols, sl] = dkv[:cols, sl] + val[:cols]
                            dkv[cols:, sl] = val[cols:]
                        else:
                            dkv[:keys, sl] = dkv[:keys, sl] + val
                feats = slice(head * HD, (head + 1) * HD)
                dq[half, feats, lanes] = dq[half, feats, lanes] + nn(k_t[:, :keys], ds)

    has = (z < depth - 1, z > 0)

    def pass_on(half, step):
        peer = (z - 1) * INNER + h if half == 0 else (z + 1) * INNER + h
        return send(sbuf.at[half, step - 1], rbuf.at[half, step - 1], zs.at[half, step - 1], zr.at[half, step - 1], (peer, f))

    def take(half, step):
        return send(sbuf.at[half, 0], rbuf.at[half, step], zs.at[half, step], zr.at[half, step],
                    (z * INNER + (h + 1) % INNER, f))

    @pl.loop(1, depth)
    def _(turn):
        step = depth - turn

        @pl.loop(0, 2)
        def _(half):
            @pl.when(jnp.where(half == 0, z - step, depth - 1 - z - step) >= 0)
            def _():
                zz = jnp.where(half == 0, z - step, z + step)
                q_base = jnp.where(half == 0, base_of(0, z), base_of(1, z))
                k_base = jnp.where(half == 0, base_of(0, zz), base_of(1, zz))
                tile(half, jnp.where(half == 0, step - 1, z + step - 1), q_base, k_base, False)

                @pl.when(jnp.where(half == 0, depth - 1 - z, z) > 0)
                def _():
                    take(half, step).wait_recv()

                    @pl.loop(0, rows // 64)
                    def _(b):
                        rws = pl.ds(pl.multiple_of(b * 64, 64), 64)
                        sbuf[half, step - 1, rws, :] = (dkv[rws, :] + rbuf[half, step, rws, :].astype(F32)).astype(BF)

                @pl.when(jnp.where(half == 0, depth - 1 - z, z) == 0)
                def _():
                    sbuf[half, step - 1] = dkv[...].astype(BF)

                @pl.when(half == 0)
                def _():
                    pass_on(0, step).start()

                @pl.when(half == 1)
                def _():
                    pass_on(1, step).start()

    def back(j, half, kind):
        i = (h + j) % INNER
        lanes = pl.ds(pl.multiple_of(h * GW + (QW if kind else 0), 128), KW if kind else QW)
        src = fin if kind else dqb
        sems = (bk.at[half, j - 1], brk.at[half, j - 1]) if kind else (bq.at[half, j - 1], brq.at[half, j - 1])
        return send(src.at[half, piece(half, i)], land.at[half_rows[half], lanes], *sems, (z * INNER + i, f))

    def keep(half, kind):
        lanes = pl.ds(pl.multiple_of(h * GW + (QW if kind else 0), 128), KW if kind else QW)
        src = fin if kind else dqb
        return pltpu.make_async_copy(src.at[half, piece(half, h)], land.at[half_rows[half], lanes], lsem.at[2 + 2 * half + kind])

    dqb[:, :, 3 * HD:] = jnp.zeros((2, rows, HD), BF)
    for half in range(2):
        q_base = base_of(half, z)
        tile(half, depth - 1 + half, q_base, q_base, True)
        dqb[half, :, :2 * HD] = (dq[half, :2 * HD, :] * (HD ** -0.5)).T.astype(BF)
        dqb[half, :, 2 * HD:3 * HD] = (dq[half, 2 * HD:, :] * (HD ** -0.5)).T.astype(BF)
        for j in range(1, INNER):
            back(j, half, 0).start()
        keep(half, 0).start()

        @pl.when(has[half])
        def _():
            take(half, 0).wait_recv()

            @pl.loop(0, rows // 64)
            def _(b):
                rws = pl.ds(pl.multiple_of(b * 64, 64), 64)
                fin[half, rws, :] = (dkv[rws, :] + rbuf[half, 0, rws, :].astype(F32)).astype(BF)

        @pl.when(jnp.logical_not(has[half]))
        def _():
            fin[half] = dkv[...].astype(BF)
        for j in range(1, INNER):
            back(j, half, 1).start()
        keep(half, 1).start()
    for half in range(2):
        for kind in range(2):
            keep(half, kind).wait()
            for j in range(1, INNER):
                back(j, half, kind).wait_recv()
    ungroup_qkv(land, out_ref)
    for half in range(2):
        for j in range(1, INNER):
            a2a(j, half).wait_send()
            for kind in range(2):
                back(j, half, kind).wait_send()

    @pl.loop(1, depth)
    def _(step):
        valid = (z - step >= 0, z + step <= depth - 1)
        for half in range(2):
            @pl.when(valid[half])
            def _():
                pass_on(half, step).wait_send()


def attend_back(starts, g, qb, kv, ot, lse, length, cid):
    depth = lax.axis_size("ctx") // INNER
    blk = g.shape[0] // 2
    rows = INNER * blk
    dma = pltpu.SemaphoreType.DMA
    vm = pl.BlockSpec(memory_space=pltpu.VMEM)
    return pl.pallas_call(
        functools.partial(attend_back_kernel, depth, length),
        out_shape=jax.ShapeDtypeStruct((2 * blk, 3 * H * HD), BF),
        in_specs=[pl.BlockSpec(memory_space=pltpu.SMEM)] + [vm] * 5,
        out_specs=vm,
        scratch_shapes=[
            pltpu.VMEM((2 * blk, INNER * QW), BF),
            pltpu.VMEM((2, rows, QW), BF),
            pltpu.VMEM((2, 8, rows), F32),
            pltpu.VMEM((2, 3 * HD, rows), F32),
            pltpu.VMEM((rows, KW), F32),
            pltpu.VMEM((2, depth - 1, rows, KW), BF),
            pltpu.VMEM((2, depth, rows, KW), BF),
            pltpu.VMEM((2, rows, QW), BF),
            pltpu.VMEM((2, rows, KW), BF),
            pltpu.VMEM((2 * blk, INNER * GW), BF),
            dma((6,)), dma((2, 3)), dma((2, 3)), dma((2, depth)), dma((2, depth)),
            dma((2, 3)), dma((2, 3)), dma((2, 3)), dma((2, 3)),
        ],
        compiler_params=pltpu.CompilerParams(collective_id=cid, has_side_effects=True, vmem_limit_bytes=56 << 20),
        name="attend_back",
    )(starts, g, qb, kv, ot, lse)


EPS = 1e-05


def layer_norm(values, gain, shift):
    center = values - jnp.mean(values, axis=-1, keepdims=True)
    spread = jnp.mean(center * center, axis=-1, keepdims=True)
    return center * lax.rsqrt(spread + EPS) * gain + shift


def gelu_tanh(values):
    return jax.nn.gelu(values, approximate=True)


def per_device(
    stream,
    doc_starts,
    ln1_gain,
    ln1_bias,
    qkv_weight,
    q_bias,
    v_bias,
    out_weight,
    out_bias,
    ln2_gain,
    ln2_bias,
    fc1_weight,
    fc1_bias,
    fc2_weight,
    fc2_bias,
    cotangent,
):
    f32 = jnp.float32
    bf16 = jnp.bfloat16
    ctx_count = lax.axis_size("ctx")
    tok_rows = stream.shape[1]
    width = stream.shape[2]
    length = ctx_count * tok_rows
    params = (
        lax.all_gather(ln1_gain, "fsdp", axis=0, tiled=True),
        lax.all_gather(ln1_bias, "fsdp", axis=0, tiled=True),
        lax.all_gather(qkv_weight, "fsdp", axis=0, tiled=True),
        lax.all_gather(q_bias, "fsdp", axis=0, tiled=True),
        lax.all_gather(v_bias, "fsdp", axis=0, tiled=True),
        lax.all_gather(out_weight, "fsdp", axis=0, tiled=True),
        lax.all_gather(out_bias, "fsdp", axis=0, tiled=True),
        lax.all_gather(ln2_gain, "fsdp", axis=0, tiled=True),
        lax.all_gather(ln2_bias, "fsdp", axis=0, tiled=True),
        lax.all_gather(fc1_weight, "fsdp", axis=0, tiled=True),
        lax.all_gather(fc1_bias, "fsdp", axis=0, tiled=True),
        lax.all_gather(fc2_weight, "fsdp", axis=0, tiled=True),
        lax.all_gather(fc2_bias, "fsdp", axis=0, tiled=True),
    )
    (
        g_one,
        b_one,
        w_qkv,
        q_shift,
        v_shift,
        w_out,
        o_shift,
        g_two,
        b_two,
        w_fc1,
        c_fc1,
        w_fc2,
        c_fc2,
    ) = params
    inputs = stream[0].astype(f32)
    normed_f, ln1_pull = jax.vjp(layer_norm, inputs, g_one.astype(f32), b_one.astype(f32))
    normed_in = normed_f.astype(bf16)
    shift_qkv = jnp.concatenate([q_shift, jnp.zeros_like(q_shift), v_shift]).astype(f32)
    projected = (jnp.dot(normed_in, w_qkv, preferred_element_type=f32) + shift_qkv).astype(bf16)
    attn, q_kept, kv_kept, out_kept, lse = attend(doc_starts, projected, length, 1)
    hidden = inputs + jnp.dot(attn, w_out, preferred_element_type=f32) + o_shift.astype(f32)
    normed_mf, ln2_pull = jax.vjp(layer_norm, hidden, g_two.astype(f32), b_two.astype(f32))
    normed_mid = normed_mf.astype(bf16)
    pre_act = jnp.dot(normed_mid, w_fc1, preferred_element_type=f32) + c_fc1.astype(f32)
    activ_f, gelu_pull = jax.vjp(gelu_tanh, pre_act)
    activ = activ_f.astype(bf16)
    result = hidden + jnp.dot(activ, w_fc2, preferred_element_type=f32) + c_fc2.astype(f32)
    layer_out = result.astype(bf16)[None]
    params_back = (
        lax.all_gather(ln1_gain, "fsdp", axis=0, tiled=True),
        lax.all_gather(ln1_bias, "fsdp", axis=0, tiled=True),
        lax.all_gather(qkv_weight, "fsdp", axis=0, tiled=True),
        lax.all_gather(q_bias, "fsdp", axis=0, tiled=True),
        lax.all_gather(v_bias, "fsdp", axis=0, tiled=True),
        lax.all_gather(out_weight, "fsdp", axis=0, tiled=True),
        lax.all_gather(out_bias, "fsdp", axis=0, tiled=True),
        lax.all_gather(ln2_gain, "fsdp", axis=0, tiled=True),
        lax.all_gather(ln2_bias, "fsdp", axis=0, tiled=True),
        lax.all_gather(fc1_weight, "fsdp", axis=0, tiled=True),
        lax.all_gather(fc1_bias, "fsdp", axis=0, tiled=True),
        lax.all_gather(fc2_weight, "fsdp", axis=0, tiled=True),
        lax.all_gather(fc2_bias, "fsdp", axis=0, tiled=True),
    )
    wb_qkv = params_back[2]
    wb_out = params_back[5]
    wb_fc1 = params_back[9]
    wb_fc2 = params_back[11]
    grad_out = cotangent[0]
    grad_c_fc2 = jnp.sum(grad_out.astype(f32), axis=0)
    grad_activ = jnp.einsum("td,fd->tf", grad_out, wb_fc2, preferred_element_type=f32)
    grad_pre = gelu_pull(grad_activ)[0].astype(bf16)
    grad_c_fc1 = jnp.sum(grad_pre.astype(f32), axis=0)
    grad_norm_mid = jnp.einsum("tf,df->td", grad_pre, wb_fc1, preferred_element_type=f32)
    grad_hid_part, grad_g_two, grad_b_two = ln2_pull(grad_norm_mid)
    grad_hidden = grad_out.astype(f32) + grad_hid_part
    grad_branch = grad_hidden.astype(bf16)
    grad_o_shift = jnp.sum(grad_branch.astype(f32), axis=0)
    grad_attn = jnp.einsum("te,de->td", grad_branch, wb_out, preferred_element_type=f32).astype(
        bf16
    )
    grad_qkv = attend_back(doc_starts, grad_attn, q_kept, kv_kept, out_kept, lse, length, 2)
    grad_query = grad_qkv[:, :width]
    grad_values = grad_qkv[:, 2 * width :]
    grad_q_shift = jnp.sum(grad_query.astype(f32), axis=0)
    grad_v_shift = jnp.sum(grad_values.astype(f32), axis=0)
    grad_norm_in = jnp.einsum("te,de->td", grad_qkv, wb_qkv, preferred_element_type=f32)
    grad_in_part, grad_g_one, grad_b_one = ln1_pull(grad_norm_in)
    input_grad = (grad_hidden + grad_in_part)[None]
    shards = lax.axis_size("fsdp")
    part = width // shards
    vectors = [grad_g_one, grad_b_one, grad_q_shift, grad_v_shift, grad_o_shift, grad_g_two, grad_b_two, grad_c_fc2]
    lines = [one.reshape(shards, 1, part) for one in vectors]
    lines.append(grad_c_fc1.reshape(shards, -1, part))
    lines.append(jnp.zeros((shards, 4, part), f32))
    t_qkv, t_out, t_fc1, t_fc2, vec = reduce_grads(
        normed_in, grad_qkv, attn, grad_branch, normed_mid, grad_pre, activ, grad_out, jnp.concatenate(lines, axis=1), 0
    )
    return (
        layer_out, input_grad, vec[0], vec[1], t_qkv.astype(f32), vec[2], vec[3], t_out.astype(f32), vec[4], vec[5],
        vec[6], t_fc1.astype(f32), vec[8:12].reshape(-1), t_fc2.astype(f32), vec[7],
    )


def solution(mesh):
    in_specs = (
        P("fsdp", "ctx", None),
        P("fsdp", None),
        P("fsdp"),
        P("fsdp"),
        P("fsdp", None),
        P("fsdp"),
        P("fsdp"),
        P("fsdp", None),
        P("fsdp"),
        P("fsdp"),
        P("fsdp"),
        P("fsdp", None),
        P("fsdp"),
        P("fsdp", None),
        P("fsdp"),
        P("fsdp", "ctx", None),
    )
    out_specs = (
        P("fsdp", "ctx", None),
        P("fsdp", "ctx", None),
        P("fsdp"),
        P("fsdp"),
        P("fsdp", None),
        P("fsdp"),
        P("fsdp"),
        P("fsdp", None),
        P("fsdp"),
        P("fsdp"),
        P("fsdp"),
        P("fsdp", None),
        P("fsdp"),
        P("fsdp", None),
        P("fsdp"),
    )
    return jax.shard_map(
        per_device, mesh=mesh, in_specs=in_specs, out_specs=out_specs, check_vma=False
    )
```

```python
import functools

import jax
import jax.numpy as jnp
from jax import lax
from jax.experimental import pallas as pl
from jax.experimental.pallas import tpu as pltpu
from jax.sharding import PartitionSpec as P

H = 12
HD = 64
EPS = 1e-05
MESH = pl.DeviceIdType.MESH
BF = jnp.bfloat16
F32 = jnp.float32


def ring_of(ctx, n):
    g = ctx // 2
    return jnp.where(g % 2 == 0, g // 2, n - 1 - g // 2)

def ring_ctx(r, n, bit):
    r = lax.rem(r + n, n)
    g = jnp.where(r < n // 2, 2 * r, 2 * (n - 1 - r) + 1)
    return g * 2 + bit

def grads_kernel(n, fs, s_one, s_two, subs, x_one, g_qkv, x_out, g_out, x_mid, g_pre, x_act, g_top, v_ref,
                 w_one, tokens, g_hid, gain, o_qkv, o_out, o_fc1, o_fc2, vout_ref, o_in,
                 wbuf, wsem, xt, gbuf, acc, fbuf, xbuf1, rbuf1, xbuf2, rbuf2, outb,
                 vall, vacc, vf, vx, vr,
                 lsem, fsem, frec, xs, xr, rs, rr, vfs, vfr, vxs, vxr, vrs, vrr, osem, xgs, xgr):
    c = lax.axis_index("ctx")
    f = lax.axis_index("fsdp")
    bit = c % 2
    pos = ring_of(c, n)
    xpeer = (c + 1 - 2 * bit, f)
    right = (ring_ctx(pos + 1, n, bit), f)
    left = (ring_ctx(pos - 1, n, bit), f)
    rows = s_one + s_two
    width = acc.shape[1]
    half = width // 2
    part = width // fs
    used = 12 * part
    lanes = (pl.ds(0, half), pl.ds(half, half))
    fpeers = [(c, lax.rem(f + k, fs)) for k in range(1, fs)]
    barrier = pltpu.get_barrier_semaphore()
    for peer in [xpeer, right, left] + fpeers:
        pl.semaphore_signal(barrier, inc=1, device_id=peer, device_id_type=MESH)
    pl.semaphore_wait(barrier, 2 + fs)

    def remote(src, dst, ssem, rsem, peer):
        cp = pltpu.make_async_remote_copy(src_ref=src, dst_ref=dst, send_sem=ssem, recv_sem=rsem,
                                          device_id=peer, device_id_type=MESH)
        return cp

    pend = []

    def go(cp):
        cp.start()
        pend.append(cp)
        return cp
    wcopy = pltpu.make_async_copy(w_one, wbuf, wsem)
    wcopy.start()
    eye_n = 256
    rr_i = lax.broadcasted_iota(jnp.int32, (eye_n, eye_n), 0)
    eye = (rr_i == lax.broadcasted_iota(jnp.int32, (eye_n, eye_n), 1)).astype(BF)
    first_row = {}
    at = 0
    for name, ref in (("act", x_act), ("mid", x_mid), ("out", x_out), ("one", x_one)):
        first_row[name] = at

        @pl.loop(0, ref.shape[1] // eye_n)
        def _(b):
            o = pl.multiple_of(b * eye_n, eye_n)
            xt[pl.ds(pl.multiple_of(at + o, eye_n), eye_n), :] = nt(eye, ref[:, pl.ds(o, eye_n)]).astype(BF)
        at += ref.shape[1]

    def unit(name, start, g, dst, row):
        lhs = xt[pl.ds(pl.multiple_of(first_row[name] + start, 16), part), :]
        dst[pl.ds(pl.multiple_of(row, 16), part), :] = nn(lhs, g).astype(BF)

    cuts = ((max(8 * part, s_one), used), (s_one, max(8 * part, s_one)), (0, s_one))

    def grads_for(owner, dst, after):
        @pl.loop(0, 4)
        def _(j):
            unit("act", owner * 4 * part + j * part, g_top[...], dst, (8 + j) * part)
        after(0)

        @pl.loop(0, 4)
        def _(j):
            unit("mid", owner * part, g_pre[:, pl.ds(pl.multiple_of(j * width, 128), width)], dst, (4 + j) * part)
        after(1)
        unit("out", owner * part, g_out[...], dst, 3 * part)

        @pl.loop(0, 3)
        def _(j):
            unit("one", owner * part, g_qkv[:, pl.ds(pl.multiple_of(j * width, 128), width)], dst, j * part)
        after(2)

    for k in range(1, fs):
        def post(j):
            a, b = cuts[j]
            if b > a:
                go(remote(gbuf.at[k - 1, pl.ds(a, b - a)], fbuf.at[k - 1, pl.ds(a, b - a)],
                          fsem.at[k - 1, j], frec.at[k - 1, j], fpeers[k - 1]))
        grads_for(fpeers[k - 1][1], gbuf.at[k - 1], post)
    if used < rows:
        acc[used:, :] = jnp.zeros((rows - used, width), BF)

    def fadd(a, m):
        blk = 32

        @pl.loop(0, m // blk)
        def _(i):
            rws = pl.ds(pl.multiple_of(a + i * blk, blk), blk)
            tot = acc[rws, :].astype(F32)
            for k in range(fs - 1):
                tot = tot + fbuf[k, rws, :].astype(F32)
            acc[rws, :] = tot.astype(BF)

    def own_part(j):
        a, b = cuts[j]
        if b > a:
            for k in range(1, fs):
                remote(gbuf.at[k - 1, pl.ds(a, b - a)], fbuf.at[k - 1, pl.ds(a, b - a)],
                       fsem.at[k - 1, j], frec.at[k - 1, j], fpeers[k - 1]).wait_recv()
            fadd(a, b - a)

    grads_for(f, acc, lambda j: None)
    own_part(0)
    own_part(1)

    chunk2 = s_two // n
    sub2 = chunk2 // subs
    h1 = s_one // 2
    chunk1 = h1 // n
    sub1 = chunk1 // subs

    def rows_of(base, chunk, k, sub, j):
        k = lax.rem(k + 2 * n, n)
        return pl.ds(pl.multiple_of(base + k * chunk + j * sub, 16), sub)

    def rs_send(st, base, chunk, sub, rbuf, s, j):
        for d in range(2):
            k = pos - 1 - s if d == 0 else pos + 1 + s
            go(remote(acc.at[rows_of(base, chunk, k, sub, j), lanes[d]],
                      rbuf.at[s, pl.ds(j * sub, sub), lanes[d]],
                      rs.at[st, 0, d, s, j], rr.at[st, 0, d, s, j], right if d == 0 else left))

    def rs_recv(st, base, chunk, sub, rbuf, s, j):
        for d in range(2):
            k = pos - 2 - s if d == 0 else pos + 2 + s
            rws = rows_of(base, chunk, k, sub, j)
            cp = remote(acc.at[rws, lanes[d]], rbuf.at[s, pl.ds(j * sub, sub), lanes[d]],
                        rs.at[st, 0, d, s, j], rr.at[st, 0, d, s, j], right)
            cp.wait_recv()
            acc[rws, lanes[d]] = (acc[rws, lanes[d]].astype(F32)
                                  + rbuf[s, pl.ds(j * sub, sub), lanes[d]].astype(F32)).astype(BF)

    def ag_send(st, base, chunk, sub, s, j):
        for d in range(2):
            k = pos - s if d == 0 else pos + s
            rws = rows_of(base, chunk, k, sub, j)
            go(remote(outb.at[rws, lanes[d]], outb.at[rws, lanes[d]],
                      rs.at[st, 1, d, s, j], rr.at[st, 1, d, s, j], right if d == 0 else left))

    def ag_recv(st, base, chunk, sub, s, j):
        for d in range(2):
            k = pos - 1 - s if d == 0 else pos + 1 + s
            rws = rows_of(base, chunk, k, sub, j)
            remote(outb.at[rws, lanes[d]], outb.at[rws, lanes[d]],
                   rs.at[st, 1, d, s, j], rr.at[st, 1, d, s, j], right).wait_recv()

    two = (1, s_one, chunk2, sub2)
    base1 = pl.multiple_of(bit * h1, 16)
    other1 = pl.multiple_of((1 - bit) * h1, 16)
    one = (0, base1, chunk1, sub1)

    def vec_first():
        return [remote(vall.at[fpeers[k - 1][1]], vf.at[k - 1], vfs.at[k - 1], vfr.at[k - 1], fpeers[k - 1])
                for k in range(1, fs)]

    def norm_back():
        wcopy.wait()
        e = nt(g_qkv[...], wbuf[...])
        x = tokens[...].astype(F32)
        center = x - jnp.mean(x, axis=-1, keepdims=True)
        r = lax.rsqrt(jnp.mean(center * center, axis=-1, keepdims=True) + EPS)
        xh = center * r
        t = e * gain[...].astype(F32)
        o_in[...] = g_hid[...] + r * (t - jnp.mean(t, axis=-1, keepdims=True)
                                      - xh * jnp.mean(t * xh, axis=-1, keepdims=True))
        vall[...] = v_ref[...]
        gq = g_qkv[:, :width].astype(F32)
        gv = g_qkv[:, 2 * width:].astype(F32)
        for row, val in enumerate((e * xh, e, gq, gv)):
            line = jnp.sum(val, axis=0, keepdims=True)
            for i in range(fs):
                vall[i, row:row + 1, :] = line[:, i * part:(i + 1) * part]

    def vec_pair():
        for cp in vec_first():
            cp.wait_recv()
        vtot = vall[f]
        for k in range(fs - 1):
            vtot = vtot + vf[k]
        vacc[...] = vtot
        go(remote(vacc, vx, vxs, vxr, xpeer))

    def vec_send(s):
        w = lax.rem(pos - s + n, n)
        go(remote(vr.at[w], vr.at[w], vrs.at[s], vrr.at[s], right))

    def vec_ring(s):
        w = lax.rem(pos - 1 - s + n, n)
        remote(vr.at[w], vr.at[w], vrs.at[s], vrr.at[s], right).wait_recv()
        if s < n - 2:
            vec_send(s + 1)

    def vec_start():
        remote(vacc, vx, vxs, vxr, xpeer).wait_recv()
        vr[pos] = vacc[...] + vx[...]
        vec_send(0)

    for j in range(subs):
        rs_send(*two, rbuf2, 0, j)
    own_part(2)
    xc1 = go(remote(acc.at[pl.ds(other1, h1)], xbuf1, xs.at[0], xr.at[0], xpeer))
    norm_back()
    for cp in vec_first():
        go(cp)
    for s in range(n - 1):
        for j in range(subs):
            rs_recv(*two, rbuf2, s, j)
            if s < n - 2:
                rs_send(*two, rbuf2, s + 1, j)
        if s == min(2, n - 2):
            vec_pair()
        if s == min(4, n - 2):
            vec_start()
    mine2 = pl.ds(pl.multiple_of(s_one + pos * chunk2, 16), chunk2)
    xc2 = go(remote(acc.at[mine2], xbuf2, xs.at[1], xr.at[1], xpeer))
    xc1.wait_recv()
    blk = 16 * 4 if h1 % 64 == 0 else 16

    @pl.loop(0, h1 // blk)
    def _(i):
        rws = pl.ds(pl.multiple_of(base1 + i * blk, 16), blk)
        acc[rws, :] = (acc[rws, :].astype(F32)
                       + xbuf1[pl.ds(pl.multiple_of(i * blk, 16), blk), :].astype(F32)).astype(BF)
    for j in range(subs):
        rs_send(*one, rbuf1, 0, j)

    def cross(s, d):
        k = pos - s if d == 0 else pos + s
        rws = rows_of(base1, chunk1, k, chunk1, 0)
        return remote(outb.at[rws, lanes[d]], outb.at[rws, lanes[d]], xgs.at[d, s], xgr.at[d, s], xpeer)

    def one_scatter(s):
        for j in range(subs):
            rs_recv(*one, rbuf1, s, j)
            if s < n - 2:
                rs_send(*one, rbuf1, s + 1, j)
            else:
                rws = rows_of(base1, chunk1, pos, sub1, j)
                outb[rws, :] = acc[rws, :]
                ag_send(*one, 0, j)
        if s == n - 2:
            for d in range(2):
                go(cross(0, d))

    def one_gather(s):
        for j in range(subs):
            ag_recv(*one, s, j)
            if s < n - 2:
                ag_send(*one, s + 1, j)
        for d in range(2):
            go(cross(s + 1, d))

    def two_gather(s, j):
        ag_recv(*two, s, j)
        if s < n - 2:
            ag_send(*two, s + 1, j)

    def two_start():
        xc2.wait_recv()
        outb[mine2, :] = (acc[mine2, :].astype(F32) + xbuf2[...].astype(F32)).astype(BF)
        for j in range(subs):
            ag_send(*two, 0, j)

    first = [functools.partial(one_scatter, s) for s in range(n - 1)] + [functools.partial(one_gather, s) for s in range(n - 1)]
    second = [functools.partial(two_gather, s, j) for s in range(n - 1) for j in range(subs)]
    for s in range(4):
        first[s]()
        vec_ring(s)
    two_start()
    first = first[4:]
    for i in range(max(len(first), len(second))):
        if i < len(first):
            first[i]()
        if i < len(second):
            second[i]()
        if 4 + i < n - 1:
            vec_ring(4 + i)
    vsum = vr[0]
    for k in range(1, n):
        vsum = vsum + vr[k]
    vout_ref[...] = vsum
    for s in range(n):
        for d in range(2):
            k = pos - s if d == 0 else pos + s
            rws = rows_of(other1, chunk1, k, chunk1, 0)
            remote(outb.at[rws, lanes[d]], outb.at[rws, lanes[d]], xgs.at[d, s], xgr.at[d, s], xpeer).wait_recv()
    outs = []
    for u in range(12):
        src = outb.at[pl.ds(u * part, part)]
        if u < 3:
            dst = o_qkv.at[:, pl.ds(u * width, width)]
        elif u == 3:
            dst = o_out
        elif u < 8:
            dst = o_fc1.at[:, pl.ds((u - 4) * width, width)]
        else:
            dst = o_fc2.at[pl.ds((u - 8) * part, part)]
        cp = pltpu.make_async_copy(src, dst, osem.at[u])
        cp.start()
        outs.append(cp)
    for cp in pend:
        cp.wait_send()
    for cp in outs:
        cp.wait()


def split_rows(rows, n, subs):
    unit = 2 * n * subs * 16
    units = max(2, -(-rows // unit))
    one = max(1, (units * 4) // 9)
    return one * unit, (units - one) * unit


def reduce_grads(x_one, g_qkv, x_out, g_out, x_mid, g_pre, x_act, g_top, v, w_one, tokens, g_hid, gain, cid, subs=2):
    fs = lax.axis_size("fsdp")
    n = lax.axis_size("ctx") // 2
    toks, width = x_one.shape
    part = width // fs
    rows = 12 * part
    s_one, s_two = split_rows(rows, n, subs)
    tot = s_one + s_two
    vs = v.shape[1:]
    dma = pltpu.SemaphoreType.DMA
    chunk1, chunk2 = s_one // 2 // n, s_two // n
    feats = x_one.shape[1] + x_out.shape[1] + x_mid.shape[1] + x_act.shape[1]
    anyspec = pl.BlockSpec(memory_space=pl.ANY)
    vm = pl.BlockSpec(memory_space=pltpu.VMEM)
    return pl.pallas_call(
        functools.partial(grads_kernel, n, fs, s_one, s_two, subs),
        out_shape=(jax.ShapeDtypeStruct((part, 3 * width), BF), jax.ShapeDtypeStruct((part, width), BF),
                   jax.ShapeDtypeStruct((part, 4 * width), BF), jax.ShapeDtypeStruct((4 * part, width), BF),
                   jax.ShapeDtypeStruct(vs, F32),
                   jax.ShapeDtypeStruct((toks, width), F32)),
        in_specs=[vm] * 9 + [anyspec] + [vm] * 3,
        out_specs=(anyspec, anyspec, anyspec, anyspec, vm, vm),
        scratch_shapes=[
            pltpu.VMEM(w_one.shape, BF),
            dma(()),
            pltpu.VMEM((feats, toks), BF),
            pltpu.VMEM((fs - 1, rows, width), BF),
            pltpu.VMEM((tot, width), BF),
            pltpu.VMEM((fs - 1, rows, width), BF),
            pltpu.VMEM((s_one // 2, width), BF),
            pltpu.VMEM((n - 1, chunk1, width), BF),
            pltpu.VMEM((chunk2, width), BF),
            pltpu.VMEM((n - 1, chunk2, width), BF),
            pltpu.VMEM((tot, width), BF),
            pltpu.VMEM((fs,) + vs, F32),
            pltpu.VMEM(vs, F32),
            pltpu.VMEM((fs - 1,) + vs, F32),
            pltpu.VMEM(vs, F32),
            pltpu.VMEM((n,) + vs, F32),
            dma((2,)), dma((fs - 1, 3)), dma((fs - 1, 3)), dma((4,)), dma((4,)),
            dma((2, 2, 2, n - 1, subs)), dma((2, 2, 2, n - 1, subs)),
            dma((fs - 1,)), dma((fs - 1,)), dma(()), dma(()), dma((n - 1,)), dma((n - 1,)), dma((12,)),
            dma((2, n)), dma((2, n)),
        ],
        compiler_params=pltpu.CompilerParams(collective_id=cid, has_side_effects=True, vmem_limit_bytes=60 << 20),
        name="reduce_grads",
    )(x_one, g_qkv, x_out, g_out, x_mid, g_pre, x_act, g_top, v, w_one, tokens, g_hid, gain)


INNER = 4
QW, KW = 256, 384
GW = QW + KW
NEG = -1e30


def nt(a, b):
    return lax.dot_general(a, b, (((1,), (1,)), ((), ())), preferred_element_type=F32)


def nn(a, b):
    return lax.dot_general(a, b, (((1,), (0,)), ((), ())), preferred_element_type=F32)


def head_lanes(x, head):
    if head == 2:
        return x
    lane = lax.broadcasted_iota(jnp.int32, x.shape, 1)
    keep = lane < HD if head == 0 else lane >= HD
    return jnp.where(keep, x, jnp.zeros_like(x))


def first_keys(starts_ref, pos):
    first = jnp.zeros_like(pos)
    for d in range(starts_ref.shape[1]):
        one = starts_ref[0, d]
        first = jnp.maximum(first, jnp.where(one <= pos, one, 0))
    return first


def places():
    c = lax.axis_index("ctx")
    f = lax.axis_index("fsdp")
    return c // INNER, c % INNER, f


def greet(z, h, f, depth):
    barrier = pltpu.get_barrier_semaphore()
    for j in range(1, INNER):
        pl.semaphore_signal(barrier, inc=1, device_id=(z * INNER + (h + j) % INNER, f), device_id_type=MESH)

    @pl.when(z > 0)
    def _():
        pl.semaphore_signal(barrier, inc=1, device_id=((z - 1) * INNER + h, f), device_id_type=MESH)

    @pl.when(z < depth - 1)
    def _():
        pl.semaphore_signal(barrier, inc=1, device_id=((z + 1) * INNER + h, f), device_id_type=MESH)

    count = INNER - 1 + jnp.where(z > 0, 1, 0) + jnp.where(z < depth - 1, 1, 0)
    pl.semaphore_wait(barrier, count)


def send(src, dst, ssem, rsem, peer):
    return pltpu.make_async_remote_copy(
        src_ref=src, dst_ref=dst, send_sem=ssem, recv_sem=rsem, device_id=peer, device_id_type=MESH
    )


def group_qkv(src, dst):
    width = H * HD
    dst_zero = jnp.zeros((dst.shape[0], HD), dst.dtype)
    for i in range(INNER):
        a, o = 3 * i * HD, i * GW
        dst[:, o:o + 3 * HD] = (src[:, a:a + 3 * HD].astype(F32) * (HD ** -0.5)).astype(dst.dtype)
        dst[:, o + 3 * HD:o + QW] = dst_zero
        dst[:, o + QW:o + QW + 2 * HD] = src[:, width + a:width + a + 2 * HD]
        dst[:, o + QW + 2 * HD:o + QW + 4 * HD] = src[:, 2 * width + a:2 * width + a + 2 * HD]
        dst[:, o + QW + 4 * HD:o + QW + 5 * HD] = src[:, width + a + 2 * HD:width + a + 3 * HD]
        dst[:, o + QW + 5 * HD:o + QW + 6 * HD] = src[:, 2 * width + a + 2 * HD:2 * width + a + 3 * HD]


def ungroup_qkv(src, dst):
    width = H * HD
    for i in range(INNER):
        a, o = 3 * i * HD, i * GW
        dst[:, a:a + 3 * HD] = src[:, o:o + 3 * HD]
        dst[:, width + a:width + a + 2 * HD] = src[:, o + QW:o + QW + 2 * HD]
        dst[:, 2 * width + a:2 * width + a + 2 * HD] = src[:, o + QW + 2 * HD:o + QW + 4 * HD]
        dst[:, width + a + 2 * HD:width + a + 3 * HD] = src[:, o + QW + 4 * HD:o + QW + 5 * HD]
        dst[:, 2 * width + a + 2 * HD:2 * width + a + 3 * HD] = src[:, o + QW + 5 * HD:o + QW + 6 * HD]


def group_rows(src, dst):
    dst_zero = jnp.zeros((dst.shape[0], HD), dst.dtype)
    for i in range(INNER):
        a, o = 3 * i * HD, i * QW
        dst[:, o:o + 2 * HD] = src[:, a:a + 2 * HD]
        dst[:, o + 2 * HD:o + 3 * HD] = dst_zero
        dst[:, o + 3 * HD:o + 4 * HD] = src[:, a + 2 * HD:a + 3 * HD]


def ungroup_rows(src, dst):
    for i in range(INNER):
        a, o = 3 * i * HD, i * QW
        dst[:, a:a + 2 * HD] = src[:, o:o + 2 * HD]
        dst[:, a + 2 * HD:a + 3 * HD] = src[:, o + 3 * HD:o + 4 * HD]


K_LANES = (0, 0, 256)
V_LANES = (128, 128, 256)
Q_LANES = (0, 0, 128)


def attend_kernel(depth, length, starts_ref, raw_ref, out_ref, qb_ref, kv_ref, ot_ref, lse_ref,
                  x_ref, qb, kv, acc, top, tot, ob, land,
                  lsem, as_kv, ar_kv, as_q, ar_q, zs, zr, bs, br, osem):
    z, h, f = places()
    blk = raw_ref.shape[0] // 2
    rows = INNER * blk
    half_rows = (pl.ds(0, blk), pl.ds(blk, blk))
    my_piece = (h, INNER - 1 - h)

    def piece(half, i):
        p = i if half == 0 else INNER - 1 - i
        return pl.ds(pl.multiple_of(p * blk, blk), blk)

    own = (depth - 1, depth)
    group_qkv(raw_ref, x_ref)
    greet(z, h, f, depth)

    def a2a(j, half, kind):
        i = (h + j) % INNER
        lanes = pl.ds(pl.multiple_of(i * GW + (QW if kind else 0), 128), KW if kind else QW)
        dst = kv.at[own[half], piece(half, h)] if kind else qb.at[half, piece(half, h)]
        sems = (as_kv.at[half, j - 1], ar_kv.at[half, j - 1]) if kind else (as_q.at[half, j - 1], ar_q.at[half, j - 1])
        return send(x_ref.at[half_rows[half], lanes], dst, *sems, (z * INNER + i, f))

    def local(half, kind):
        lanes = pl.ds(pl.multiple_of(h * GW + (QW if kind else 0), 128), KW if kind else QW)
        dst = kv.at[own[half], piece(half, h)] if kind else qb.at[half, piece(half, h)]
        return pltpu.make_async_copy(x_ref.at[half_rows[half], lanes], dst, lsem.at[half, kind])

    for kind in (1, 0):
        for half in range(2):
            for j in range(1, INNER):
                a2a(j, half, kind).start()
            local(half, kind).start()

    def relay(half, src_slot, step, p):
        rws = pl.ds(pl.multiple_of(p * blk, blk), blk)
        if half == 0:
            peer, slot = (z + 1) * INNER + h, step - 1
        else:
            peer, slot = (z - 1) * INNER + h, z - 1 + step - 1
        return send(kv.at[src_slot, rws], kv.at[slot, rws], zs.at[half, step - 1, p], zr.at[half, step - 1, p], (peer, f))

    can = (z < depth - 1, z > 0)
    for j in range(INNER):
        i = (h + INNER - j) % INNER
        for half in range(2):
            if j == 0:
                local(half, 1).wait()
            else:
                a2a(j, half, 1).wait_recv()

            @pl.when(can[half])
            def _():
                relay(half, own[half], 1, i if half == 0 else INNER - 1 - i).start()

    for half in range(2):
        local(half, 0).wait()
        for j in range(1, INNER):
            a2a(j, half, 0).wait_recv()

    def base_of(half, zz):
        return zz * rows if half == 0 else length - (zz + 1) * rows

    cols = rows // 2

    def tile(half, slot, q_base, k_base, diag):
        for head in range(3):
            k_all = kv[slot, :, K_LANES[head]:K_LANES[head] + 128]
            v_all = kv[slot, :, V_LANES[head]:V_LANES[head] + 128]
            v_t = v_all.T[(0 if head == 0 else HD):(HD if head == 0 else 2 * HD)]
            for part in range(2):
                keys = (part + 1) * cols if diag else rows
                lanes = slice(part * cols, (part + 1) * cols)
                q = head_lanes(qb[half, lanes, Q_LANES[head]:Q_LANES[head] + 128], head)
                pos = q_base + part * cols + lax.broadcasted_iota(jnp.int32, (1, cols), 1)
                first = first_keys(starts_ref, pos) - k_base
                s = nt(k_all[:keys], q)
                row = lax.broadcasted_iota(jnp.int32, (keys, cols), 0)
                ok = row >= first
                if diag:
                    ok = ok & (row <= pos - k_base)
                s = jnp.where(ok, s, NEG)
                line = slice(head, head + 1)
                feats = slice(head * HD, (head + 1) * HD)
                high = jnp.max(s, axis=0, keepdims=True)
                if not diag:
                    before = top[half, line, lanes]
                    high = jnp.maximum(before, high)
                    fade = jnp.exp(before - high)
                w = jnp.exp(s - high)
                add = jnp.sum(w, axis=0, keepdims=True)
                o = nn(v_t[:, :keys], w.astype(BF))
                if diag:
                    tot[half, line, lanes] = add
                    acc[half, feats, lanes] = o
                else:
                    tot[half, line, lanes] = tot[half, line, lanes] * fade + add
                    acc[half, feats, lanes] = acc[half, feats, lanes] * fade + o
                top[half, line, lanes] = high

    @pl.loop(0, 2)
    def _(half):
        q_base = jnp.where(half == 0, base_of(0, z), base_of(1, z))
        tile(half, depth - 1 + half, q_base, q_base, True)

    @pl.loop(1, depth)
    def _(step):
        valid = (z - step >= 0, z + step <= depth - 1)
        slots = (step - 1, z + step - 1)
        for half in range(2):
            for p in range(INNER):
                @pl.when(valid[half])
                def _():
                    rws = pl.ds(p * blk, blk)
                    send(kv.at[slots[half], rws], kv.at[slots[half], rws], zs.at[half, step - 1, p],
                         zr.at[half, step - 1, p], (z * INNER + (h + 1) % INNER, f)).wait_recv()

                @pl.when(valid[half] & can[half])
                def _():
                    relay(half, slots[half], step + 1, p).start()

        @pl.loop(0, 2)
        def _(half):
            @pl.when(jnp.where(half == 0, z - step, depth - 1 - z - step) >= 0)
            def _():
                zz = jnp.where(half == 0, z - step, z + step)
                q_base = jnp.where(half == 0, base_of(0, z), base_of(1, z))
                k_base = jnp.where(half == 0, base_of(0, zz), base_of(1, zz))
                tile(half, jnp.where(half == 0, step - 1, z + step - 1), q_base, k_base, False)

    ob[:, :, 2 * HD:3 * HD] = jnp.zeros((2, rows, HD), BF)
    for half in range(2):
        lse_ref[half] = top[half] + jnp.log(tot[half])
        for head in range(3):
            feats = slice(head * HD, (head + 1) * HD)
            acc[half, feats, :] = acc[half, feats, :] / tot[half, head:head + 1, :]
        ob[half, :, :2 * HD] = acc[half, :2 * HD, :].T.astype(BF)
        ob[half, :, 3 * HD:] = acc[half, 2 * HD:, :].T.astype(BF)
    outs = [pltpu.make_async_copy(qb, qb_ref, osem.at[0]), pltpu.make_async_copy(kv, kv_ref, osem.at[1]),
            pltpu.make_async_copy(acc, ot_ref, osem.at[2])]
    for cp in outs:
        cp.start()

    def back(j, half):
        i = (h + j) % INNER
        return send(ob.at[half, piece(half, i)], land.at[half_rows[half], pl.ds(pl.multiple_of(h * QW, 128), QW)],
                    bs.at[half, j - 1], br.at[half, j - 1], (z * INNER + i, f))

    for half in range(2):
        for j in range(1, INNER):
            back(j, half).start()
        mine = pltpu.make_async_copy(ob.at[half, piece(half, h)],
                                     land.at[half_rows[half], pl.ds(pl.multiple_of(h * QW, 128), QW)], lsem.at[half, 0])
        mine.start()
        mine.wait()
    for half in range(2):
        for j in range(1, INNER):
            back(j, half).wait_recv()
    ungroup_rows(land, out_ref)
    for half in range(2):
        for j in range(1, INNER):
            a2a(j, half, 1).wait_send()
            a2a(j, half, 0).wait_send()
            back(j, half).wait_send()

        @pl.when(can[half])
        def _():
            for p in range(INNER):
                relay(half, own[half], 1, p).wait_send()

    @pl.loop(1, depth)
    def _(step):
        valid = (z - step >= 0, z + step <= depth - 1)
        for half in range(2):
            @pl.when(valid[half] & can[half])
            def _():
                for p in range(INNER):
                    relay(half, own[half], step + 1, p).wait_send()
    for cp in outs:
        cp.wait()


def attend(starts, x, length, cid):
    depth = lax.axis_size("ctx") // INNER
    blk = x.shape[0] // 2
    rows = INNER * blk
    dma = pltpu.SemaphoreType.DMA
    shapes = (
        jax.ShapeDtypeStruct((x.shape[0], H * HD), BF),
        jax.ShapeDtypeStruct((2, rows, QW), BF),
        jax.ShapeDtypeStruct((depth + 1, rows, KW), BF),
        jax.ShapeDtypeStruct((2, 3 * HD, rows), F32),
        jax.ShapeDtypeStruct((2, 8, rows), F32),
    )
    vm = pl.BlockSpec(memory_space=pltpu.VMEM)
    anyspec = pl.BlockSpec(memory_space=pl.ANY)
    return pl.pallas_call(
        functools.partial(attend_kernel, depth, length),
        out_shape=shapes,
        in_specs=[pl.BlockSpec(memory_space=pltpu.SMEM), vm],
        out_specs=(vm, anyspec, anyspec, anyspec, vm),
        scratch_shapes=[
            pltpu.VMEM((2 * blk, INNER * GW), BF),
            pltpu.VMEM((2, rows, QW), BF),
            pltpu.VMEM((depth + 1, rows, KW), BF),
            pltpu.VMEM((2, 3 * HD, rows), F32),
            pltpu.VMEM((2, 8, rows), F32),
            pltpu.VMEM((2, 8, rows), F32),
            pltpu.VMEM((2, rows, QW), BF),
            pltpu.VMEM((2 * blk, INNER * QW), BF),
            dma((2, 2)), dma((2, 3)), dma((2, 3)), dma((2, 3)), dma((2, 3)),
            dma((2, depth, INNER)), dma((2, depth, INNER)), dma((2, 3)), dma((2, 3)), dma((3,)),
        ],
        compiler_params=pltpu.CompilerParams(collective_id=cid, has_side_effects=True, vmem_limit_bytes=48 << 20),
        name="attend",
    )(starts, x)


def attend_back_kernel(depth, length, starts_ref, raw_ref, qb, kv, ot, lse, out_ref,
                       do_ref, dob, dots, dq, dkv, sbuf, rbuf, dqb, fin, land,
                       lsem, as_o, ar_o, zs, zr, bq, brq, bk, brk):
    z, h, f = places()
    blk = raw_ref.shape[0] // 2
    rows = INNER * blk
    half_rows = (pl.ds(0, blk), pl.ds(blk, blk))

    def piece(half, i):
        p = i if half == 0 else INNER - 1 - i
        return pl.ds(pl.multiple_of(p * blk, blk), blk)

    group_rows(raw_ref, do_ref)
    greet(z, h, f, depth)

    def a2a(j, half):
        i = (h + j) % INNER
        return send(do_ref.at[half_rows[half], pl.ds(pl.multiple_of(i * QW, 128), QW)], dob.at[half, piece(half, h)],
                    as_o.at[half, j - 1], ar_o.at[half, j - 1], (z * INNER + i, f))

    mine = []
    for half in range(2):
        for j in range(1, INNER):
            a2a(j, half).start()
        cp = pltpu.make_async_copy(do_ref.at[half_rows[half], pl.ds(pl.multiple_of(h * QW, 128), QW)],
                                   dob.at[half, piece(half, h)], lsem.at[half])
        cp.start()
        mine.append(cp)
    dq[...] = jnp.zeros_like(dq)
    for half in range(2):
        mine[half].wait()
        for j in range(1, INNER):
            a2a(j, half).wait_recv()
        for head in range(3):
            lanes = slice(0, 128) if head < 2 else slice(128, 256)
            g = dob[half, :, lanes].astype(F32).T[(0 if head == 0 else HD):(HD if head == 0 else 2 * HD)]
            dots[half, head:head + 1, :] = jnp.sum(g * ot[half, head * HD:(head + 1) * HD, :], axis=0, keepdims=True)

    def base_of(half, zz):
        return zz * rows if half == 0 else length - (zz + 1) * rows

    cols = rows // 2

    def tile(half, slot, q_base, k_base, diag):
        for head in range(3):
            k_all = kv[slot, :, K_LANES[head]:K_LANES[head] + 128]
            v_all = kv[slot, :, V_LANES[head]:V_LANES[head] + 128]
            k_t = k_all.T[(HD if head == 1 else 0):(2 * HD if head == 1 else HD)]
            for part in range(2):
                keys = (part + 1) * cols if diag else rows
                lanes = slice(part * cols, (part + 1) * cols)
                q = head_lanes(qb[half, lanes, Q_LANES[head]:Q_LANES[head] + 128], head)
                g = head_lanes(dob[half, lanes, Q_LANES[head]:Q_LANES[head] + 128], head)
                pos = q_base + part * cols + lax.broadcasted_iota(jnp.int32, (1, cols), 1)
                first = first_keys(starts_ref, pos) - k_base
                s = nt(k_all[:keys], q)
                row = lax.broadcasted_iota(jnp.int32, (keys, cols), 0)
                ok = row >= first
                if diag:
                    ok = ok & (row <= pos - k_base)
                line = slice(head, head + 1)
                w = jnp.where(ok, jnp.exp(s - lse[half, line, lanes]), 0.0)
                gp = nt(v_all[:keys], g)
                ds = (w * (gp - dots[half, line, lanes])).astype(BF)
                wb = w.astype(BF)
                dv = nn(wb, g)
                dk = nn(ds, q)
                kl = slice(K_LANES[head], K_LANES[head] + 128)
                vl = slice(V_LANES[head], V_LANES[head] + 128)
                if head == 2:
                    both = dk + dv
                    if part == 0:
                        dkv[:keys, kl] = both
                    elif keys == rows and diag:
                        dkv[:cols, kl] = dkv[:cols, kl] + both[:cols]
                        dkv[cols:, kl] = both[cols:]
                    else:
                        dkv[:, kl] = dkv[:, kl] + both
                else:
                    for sl, val in ((kl, dk), (vl, dv)):
                        if head == 0 and part == 0:
                            dkv[:keys, sl] = val
                        elif head == 0 and diag:
                            dkv[:cols, sl] = dkv[:cols, sl] + val[:cols]
                            dkv[cols:, sl] = val[cols:]
                        else:
                            dkv[:keys, sl] = dkv[:keys, sl] + val
                feats = slice(head * HD, (head + 1) * HD)
                dq[half, feats, lanes] = dq[half, feats, lanes] + nn(k_t[:, :keys], ds)

    has = (z < depth - 1, z > 0)

    def pass_on(half, step):
        peer = (z - 1) * INNER + h if half == 0 else (z + 1) * INNER + h
        return send(sbuf.at[half, step - 1], rbuf.at[half, step - 1], zs.at[half, step - 1], zr.at[half, step - 1], (peer, f))

    def take(half, step):
        return send(sbuf.at[half, 0], rbuf.at[half, step], zs.at[half, step], zr.at[half, step],
                    (z * INNER + (h + 1) % INNER, f))

    @pl.loop(1, depth)
    def _(turn):
        step = depth - turn

        @pl.loop(0, 2)
        def _(half):
            @pl.when(jnp.where(half == 0, z - step, depth - 1 - z - step) >= 0)
            def _():
                zz = jnp.where(half == 0, z - step, z + step)
                q_base = jnp.where(half == 0, base_of(0, z), base_of(1, z))
                k_base = jnp.where(half == 0, base_of(0, zz), base_of(1, zz))
                tile(half, jnp.where(half == 0, step - 1, z + step - 1), q_base, k_base, False)

                @pl.when(jnp.where(half == 0, depth - 1 - z, z) > 0)
                def _():
                    take(half, step).wait_recv()

                    @pl.loop(0, rows // 64)
                    def _(b):
                        rws = pl.ds(pl.multiple_of(b * 64, 64), 64)
                        sbuf[half, step - 1, rws, :] = (dkv[rws, :] + rbuf[half, step, rws, :].astype(F32)).astype(BF)

                @pl.when(jnp.where(half == 0, depth - 1 - z, z) == 0)
                def _():
                    sbuf[half, step - 1] = dkv[...].astype(BF)

                @pl.when(half == 0)
                def _():
                    pass_on(0, step).start()

                @pl.when(half == 1)
                def _():
                    pass_on(1, step).start()

    def back(j, half, kind):
        i = (h + j) % INNER
        lanes = pl.ds(pl.multiple_of(h * GW + (QW if kind else 0), 128), KW if kind else QW)
        src = fin if kind else dqb
        sems = (bk.at[half, j - 1], brk.at[half, j - 1]) if kind else (bq.at[half, j - 1], brq.at[half, j - 1])
        return send(src.at[half, piece(half, i)], land.at[half_rows[half], lanes], *sems, (z * INNER + i, f))

    def keep(half, kind):
        lanes = pl.ds(pl.multiple_of(h * GW + (QW if kind else 0), 128), KW if kind else QW)
        src = fin if kind else dqb
        return pltpu.make_async_copy(src.at[half, piece(half, h)], land.at[half_rows[half], lanes], lsem.at[2 + 2 * half + kind])

    dqb[:, :, 3 * HD:] = jnp.zeros((2, rows, HD), BF)
    for half in range(2):
        q_base = base_of(half, z)
        tile(half, depth - 1 + half, q_base, q_base, True)
        dqb[half, :, :2 * HD] = (dq[half, :2 * HD, :] * (HD ** -0.5)).T.astype(BF)
        dqb[half, :, 2 * HD:3 * HD] = (dq[half, 2 * HD:, :] * (HD ** -0.5)).T.astype(BF)
        for j in range(1, INNER):
            back(j, half, 0).start()
        keep(half, 0).start()

        @pl.when(has[half])
        def _():
            take(half, 0).wait_recv()

            @pl.loop(0, rows // 64)
            def _(b):
                rws = pl.ds(pl.multiple_of(b * 64, 64), 64)
                fin[half, rws, :] = (dkv[rws, :] + rbuf[half, 0, rws, :].astype(F32)).astype(BF)

        @pl.when(jnp.logical_not(has[half]))
        def _():
            fin[half] = dkv[...].astype(BF)
        for j in range(1, INNER):
            back(j, half, 1).start()
        keep(half, 1).start()
    for half in range(2):
        for kind in range(2):
            keep(half, kind).wait()
            for j in range(1, INNER):
                back(j, half, kind).wait_recv()
    ungroup_qkv(land, out_ref)
    for half in range(2):
        for j in range(1, INNER):
            a2a(j, half).wait_send()
            for kind in range(2):
                back(j, half, kind).wait_send()

    @pl.loop(1, depth)
    def _(step):
        valid = (z - step >= 0, z + step <= depth - 1)
        for half in range(2):
            @pl.when(valid[half])
            def _():
                pass_on(half, step).wait_send()


def attend_back(starts, g, qb, kv, ot, lse, length, cid):
    depth = lax.axis_size("ctx") // INNER
    blk = g.shape[0] // 2
    rows = INNER * blk
    dma = pltpu.SemaphoreType.DMA
    vm = pl.BlockSpec(memory_space=pltpu.VMEM)
    return pl.pallas_call(
        functools.partial(attend_back_kernel, depth, length),
        out_shape=jax.ShapeDtypeStruct((2 * blk, 3 * H * HD), BF),
        in_specs=[pl.BlockSpec(memory_space=pltpu.SMEM)] + [vm] * 5,
        out_specs=vm,
        scratch_shapes=[
            pltpu.VMEM((2 * blk, INNER * QW), BF),
            pltpu.VMEM((2, rows, QW), BF),
            pltpu.VMEM((2, 8, rows), F32),
            pltpu.VMEM((2, 3 * HD, rows), F32),
            pltpu.VMEM((rows, KW), F32),
            pltpu.VMEM((2, depth - 1, rows, KW), BF),
            pltpu.VMEM((2, depth, rows, KW), BF),
            pltpu.VMEM((2, rows, QW), BF),
            pltpu.VMEM((2, rows, KW), BF),
            pltpu.VMEM((2 * blk, INNER * GW), BF),
            dma((6,)), dma((2, 3)), dma((2, 3)), dma((2, depth)), dma((2, depth)),
            dma((2, 3)), dma((2, 3)), dma((2, 3)), dma((2, 3)),
        ],
        compiler_params=pltpu.CompilerParams(collective_id=cid, has_side_effects=True, vmem_limit_bytes=56 << 20),
        name="attend_back",
    )(starts, g, qb, kv, ot, lse)


def layer_norm(values, gain, shift):
    center = values - jnp.mean(values, axis=-1, keepdims=True)
    spread = jnp.mean(center * center, axis=-1, keepdims=True)
    return center * lax.rsqrt(spread + EPS) * gain + shift


def gelu_tanh(values):
    return jax.nn.gelu(values, approximate=True)


def per_device(
    stream,
    doc_starts,
    ln1_gain,
    ln1_bias,
    qkv_weight,
    q_bias,
    v_bias,
    out_weight,
    out_bias,
    ln2_gain,
    ln2_bias,
    fc1_weight,
    fc1_bias,
    fc2_weight,
    fc2_bias,
    cotangent,
):
    f32 = jnp.float32
    bf16 = jnp.bfloat16
    ctx_count = lax.axis_size("ctx")
    tok_rows = stream.shape[1]
    width = stream.shape[2]
    length = ctx_count * tok_rows
    params = (
        lax.all_gather(ln1_gain, "fsdp", axis=0, tiled=True),
        lax.all_gather(ln1_bias, "fsdp", axis=0, tiled=True),
        lax.all_gather(qkv_weight, "fsdp", axis=0, tiled=True),
        lax.all_gather(q_bias, "fsdp", axis=0, tiled=True),
        lax.all_gather(v_bias, "fsdp", axis=0, tiled=True),
        lax.all_gather(out_weight, "fsdp", axis=0, tiled=True),
        lax.all_gather(out_bias, "fsdp", axis=0, tiled=True),
        lax.all_gather(ln2_gain, "fsdp", axis=0, tiled=True),
        lax.all_gather(ln2_bias, "fsdp", axis=0, tiled=True),
        lax.all_gather(fc1_weight, "fsdp", axis=0, tiled=True),
        lax.all_gather(fc1_bias, "fsdp", axis=0, tiled=True),
        lax.all_gather(fc2_weight, "fsdp", axis=0, tiled=True),
        lax.all_gather(fc2_bias, "fsdp", axis=0, tiled=True),
    )
    (
        g_one,
        b_one,
        w_qkv,
        q_shift,
        v_shift,
        w_out,
        o_shift,
        g_two,
        b_two,
        w_fc1,
        c_fc1,
        w_fc2,
        c_fc2,
    ) = params
    inputs = stream[0].astype(f32)
    normed_f = layer_norm(inputs, g_one.astype(f32), b_one.astype(f32))
    normed_in = normed_f.astype(bf16)
    shift_qkv = jnp.concatenate([q_shift, jnp.zeros_like(q_shift), v_shift]).astype(f32)
    projected = (jnp.dot(normed_in, w_qkv, preferred_element_type=f32) + shift_qkv).astype(bf16)
    attn, q_kept, kv_kept, out_kept, lse = attend(doc_starts, projected, length, 1)
    hidden = inputs + jnp.dot(attn, w_out, preferred_element_type=f32) + o_shift.astype(f32)
    normed_mf, ln2_pull = jax.vjp(layer_norm, hidden, g_two.astype(f32), b_two.astype(f32))
    normed_mid = normed_mf.astype(bf16)
    pre_act = jnp.dot(normed_mid, w_fc1, preferred_element_type=f32) + c_fc1.astype(f32)
    activ_f, gelu_pull = jax.vjp(gelu_tanh, pre_act)
    activ = activ_f.astype(bf16)
    result = hidden + jnp.dot(activ, w_fc2, preferred_element_type=f32) + c_fc2.astype(f32)
    layer_out = result.astype(bf16)[None]
    params_back = (
        lax.all_gather(ln1_gain, "fsdp", axis=0, tiled=True),
        lax.all_gather(ln1_bias, "fsdp", axis=0, tiled=True),
        lax.all_gather(qkv_weight, "fsdp", axis=0, tiled=True),
        lax.all_gather(q_bias, "fsdp", axis=0, tiled=True),
        lax.all_gather(v_bias, "fsdp", axis=0, tiled=True),
        lax.all_gather(out_weight, "fsdp", axis=0, tiled=True),
        lax.all_gather(out_bias, "fsdp", axis=0, tiled=True),
        lax.all_gather(ln2_gain, "fsdp", axis=0, tiled=True),
        lax.all_gather(ln2_bias, "fsdp", axis=0, tiled=True),
        lax.all_gather(fc1_weight, "fsdp", axis=0, tiled=True),
        lax.all_gather(fc1_bias, "fsdp", axis=0, tiled=True),
        lax.all_gather(fc2_weight, "fsdp", axis=0, tiled=True),
        lax.all_gather(fc2_bias, "fsdp", axis=0, tiled=True),
    )
    wb_out = params_back[5]
    wb_fc1 = params_back[9]
    wb_fc2 = params_back[11]
    grad_out = cotangent[0]
    grad_c_fc2 = jnp.sum(grad_out.astype(f32), axis=0)
    grad_activ = jnp.einsum("td,fd->tf", grad_out, wb_fc2, preferred_element_type=f32)
    grad_pre = gelu_pull(grad_activ)[0].astype(bf16)
    grad_c_fc1 = jnp.sum(grad_pre.astype(f32), axis=0)
    grad_norm_mid = jnp.einsum("tf,df->td", grad_pre, wb_fc1, preferred_element_type=f32)
    grad_hid_part, grad_g_two, grad_b_two = ln2_pull(grad_norm_mid)
    grad_hidden = grad_out.astype(f32) + grad_hid_part
    grad_branch = grad_hidden.astype(bf16)
    grad_o_shift = jnp.sum(grad_branch.astype(f32), axis=0)
    grad_attn = jnp.einsum("te,de->td", grad_branch, wb_out, preferred_element_type=f32).astype(
        bf16
    )
    grad_qkv = attend_back(doc_starts, grad_attn, q_kept, kv_kept, out_kept, lse, length, 2)
    shards = lax.axis_size("fsdp")
    part = width // shards
    zeros = jnp.zeros((width,), f32)
    vectors = [zeros, zeros, zeros, zeros, grad_o_shift, grad_g_two, grad_b_two, grad_c_fc2]
    lines = [one.reshape(shards, 1, part) for one in vectors]
    lines.append(grad_c_fc1.reshape(shards, -1, part))
    lines.append(jnp.zeros((shards, 4, part), f32))
    t_qkv, t_out, t_fc1, t_fc2, vec, input_grad = reduce_grads(
        normed_in, grad_qkv, attn, grad_branch, normed_mid, grad_pre, activ, grad_out, jnp.concatenate(lines, axis=1),
        params_back[2], stream[0], grad_hidden, g_one[None], 0
    )
    return (
        layer_out, input_grad[None], vec[0], vec[1], t_qkv.astype(f32), vec[2], vec[3], t_out.astype(f32), vec[4], vec[5],
        vec[6], t_fc1.astype(f32), vec[8:12].reshape(-1), t_fc2.astype(f32), vec[7],
    )


def solution(mesh):
    in_specs = (
        P("fsdp", "ctx", None),
        P("fsdp", None),
        P("fsdp"),
        P("fsdp"),
        P("fsdp", None),
        P("fsdp"),
        P("fsdp"),
        P("fsdp", None),
        P("fsdp"),
        P("fsdp"),
        P("fsdp"),
        P("fsdp", None),
        P("fsdp"),
        P("fsdp", None),
        P("fsdp"),
        P("fsdp", "ctx", None),
    )
    out_specs = (
        P("fsdp", "ctx", None),
        P("fsdp", "ctx", None),
        P("fsdp"),
        P("fsdp"),
        P("fsdp", None),
        P("fsdp"),
        P("fsdp"),
        P("fsdp", None),
        P("fsdp"),
        P("fsdp"),
        P("fsdp"),
        P("fsdp", None),
        P("fsdp"),
        P("fsdp", None),
        P("fsdp"),
    )
    return jax.shard_map(
        per_device, mesh=mesh, in_specs=in_specs, out_specs=out_specs, check_vma=False
    )
```

```python
import functools

import jax
import jax.numpy as jnp
from jax import lax
from jax.experimental import pallas as pl
from jax.experimental.pallas import tpu as pltpu
from jax.sharding import PartitionSpec as P

H = 12
HD = 64
EPS = 1e-05
MESH = pl.DeviceIdType.MESH
BF = jnp.bfloat16
F32 = jnp.float32


INNER = 4
QW, KW = 256, 384
GW = QW + KW
NEG = -1e30


def nt(a, b):
    return lax.dot_general(a, b, (((1,), (1,)), ((), ())), preferred_element_type=F32)


def nn(a, b):
    return lax.dot_general(a, b, (((1,), (0,)), ((), ())), preferred_element_type=F32)


def head_lanes(x, head):
    if head == 2:
        return x
    lane = lax.broadcasted_iota(jnp.int32, x.shape, 1)
    keep = lane < HD if head == 0 else lane >= HD
    return jnp.where(keep, x, jnp.zeros_like(x))


def first_keys(starts_ref, pos):
    first = jnp.zeros_like(pos)
    for d in range(starts_ref.shape[1]):
        one = starts_ref[0, d]
        first = jnp.maximum(first, jnp.where(one <= pos, one, 0))
    return first


def places():
    c = lax.axis_index("ctx")
    f = lax.axis_index("fsdp")
    return c // INNER, c % INNER, f


def greet(z, h, f, depth):
    barrier = pltpu.get_barrier_semaphore()
    for j in range(1, INNER):
        pl.semaphore_signal(barrier, inc=1, device_id=(z * INNER + (h + j) % INNER, f), device_id_type=MESH)

    @pl.when(z > 0)
    def _():
        pl.semaphore_signal(barrier, inc=1, device_id=((z - 1) * INNER + h, f), device_id_type=MESH)

    @pl.when(z < depth - 1)
    def _():
        pl.semaphore_signal(barrier, inc=1, device_id=((z + 1) * INNER + h, f), device_id_type=MESH)

    count = INNER - 1 + jnp.where(z > 0, 1, 0) + jnp.where(z < depth - 1, 1, 0)
    pl.semaphore_wait(barrier, count)


def send(src, dst, ssem, rsem, peer):
    return pltpu.make_async_remote_copy(
        src_ref=src, dst_ref=dst, send_sem=ssem, recv_sem=rsem, device_id=peer, device_id_type=MESH
    )


def group_qkv(src, dst):
    width = H * HD
    dst_zero = jnp.zeros((dst.shape[0], HD), dst.dtype)
    for i in range(INNER):
        a, o = 3 * i * HD, i * GW
        dst[:, o:o + 3 * HD] = (src[:, a:a + 3 * HD].astype(F32) * (HD ** -0.5)).astype(dst.dtype)
        dst[:, o + 3 * HD:o + QW] = dst_zero
        dst[:, o + QW:o + QW + 2 * HD] = src[:, width + a:width + a + 2 * HD]
        dst[:, o + QW + 2 * HD:o + QW + 4 * HD] = src[:, 2 * width + a:2 * width + a + 2 * HD]
        dst[:, o + QW + 4 * HD:o + QW + 5 * HD] = src[:, width + a + 2 * HD:width + a + 3 * HD]
        dst[:, o + QW + 5 * HD:o + QW + 6 * HD] = src[:, 2 * width + a + 2 * HD:2 * width + a + 3 * HD]


def ungroup_qkv(src, dst):
    width = H * HD
    for i in range(INNER):
        a, o = 3 * i * HD, i * GW
        dst[:, a:a + 3 * HD] = src[:, o:o + 3 * HD]
        dst[:, width + a:width + a + 2 * HD] = src[:, o + QW:o + QW + 2 * HD]
        dst[:, 2 * width + a:2 * width + a + 2 * HD] = src[:, o + QW + 2 * HD:o + QW + 4 * HD]
        dst[:, width + a + 2 * HD:width + a + 3 * HD] = src[:, o + QW + 4 * HD:o + QW + 5 * HD]
        dst[:, 2 * width + a + 2 * HD:2 * width + a + 3 * HD] = src[:, o + QW + 5 * HD:o + QW + 6 * HD]


def group_rows(src, dst):
    dst_zero = jnp.zeros((dst.shape[0], HD), dst.dtype)
    for i in range(INNER):
        a, o = 3 * i * HD, i * QW
        dst[:, o:o + 2 * HD] = src[:, a:a + 2 * HD]
        dst[:, o + 2 * HD:o + 3 * HD] = dst_zero
        dst[:, o + 3 * HD:o + 4 * HD] = src[:, a + 2 * HD:a + 3 * HD]


def ungroup_rows(src, dst):
    for i in range(INNER):
        a, o = 3 * i * HD, i * QW
        dst[:, a:a + 2 * HD] = src[:, o:o + 2 * HD]
        dst[:, a + 2 * HD:a + 3 * HD] = src[:, o + 3 * HD:o + 4 * HD]


K_LANES = (0, 0, 256)
V_LANES = (128, 128, 256)
Q_LANES = (0, 0, 128)


def attend_kernel(depth, length, starts_ref, raw_ref, out_ref, qb_ref, kv_ref, ot_ref, lse_ref,
                  x_ref, qb, kv, acc, top, tot, ob, land,
                  lsem, as_kv, ar_kv, as_q, ar_q, zs, zr, bs, br, osem):
    z, h, f = places()
    blk = raw_ref.shape[0] // 2
    rows = INNER * blk
    half_rows = (pl.ds(0, blk), pl.ds(blk, blk))
    my_piece = (h, INNER - 1 - h)

    def piece(half, i):
        p = i if half == 0 else INNER - 1 - i
        return pl.ds(pl.multiple_of(p * blk, blk), blk)

    own = (depth - 1, depth)
    group_qkv(raw_ref, x_ref)
    greet(z, h, f, depth)

    def a2a(j, half, kind):
        i = (h + j) % INNER
        lanes = pl.ds(pl.multiple_of(i * GW + (QW if kind else 0), 128), KW if kind else QW)
        dst = kv.at[own[half], piece(half, h)] if kind else qb.at[half, piece(half, h)]
        sems = (as_kv.at[half, j - 1], ar_kv.at[half, j - 1]) if kind else (as_q.at[half, j - 1], ar_q.at[half, j - 1])
        return send(x_ref.at[half_rows[half], lanes], dst, *sems, (z * INNER + i, f))

    def local(half, kind):
        lanes = pl.ds(pl.multiple_of(h * GW + (QW if kind else 0), 128), KW if kind else QW)
        dst = kv.at[own[half], piece(half, h)] if kind else qb.at[half, piece(half, h)]
        return pltpu.make_async_copy(x_ref.at[half_rows[half], lanes], dst, lsem.at[half, kind])

    for kind in (1, 0):
        for half in range(2):
            for j in range(1, INNER):
                a2a(j, half, kind).start()
            local(half, kind).start()

    def relay(half, src_slot, step, p):
        rws = pl.ds(pl.multiple_of(p * blk, blk), blk)
        if half == 0:
            peer, slot = (z + 1) * INNER + h, step - 1
        else:
            peer, slot = (z - 1) * INNER + h, z - 1 + step - 1
        return send(kv.at[src_slot, rws], kv.at[slot, rws], zs.at[half, step - 1, p], zr.at[half, step - 1, p], (peer, f))

    can = (z < depth - 1, z > 0)
    for j in range(INNER):
        i = (h + INNER - j) % INNER
        for half in range(2):
            if j == 0:
                local(half, 1).wait()
            else:
                a2a(j, half, 1).wait_recv()

            @pl.when(can[half])
            def _():
                relay(half, own[half], 1, i if half == 0 else INNER - 1 - i).start()

    for half in range(2):
        local(half, 0).wait()
        for j in range(1, INNER):
            a2a(j, half, 0).wait_recv()

    def base_of(half, zz):
        return zz * rows if half == 0 else length - (zz + 1) * rows

    cols = rows // 2

    def tile(half, slot, q_base, k_base, diag):
        for head in range(3):
            k_all = kv[slot, :, K_LANES[head]:K_LANES[head] + 128]
            v_all = kv[slot, :, V_LANES[head]:V_LANES[head] + 128]
            v_t = v_all.T[(0 if head == 0 else HD):(HD if head == 0 else 2 * HD)]
            for part in range(2):
                keys = (part + 1) * cols if diag else rows
                lanes = slice(part * cols, (part + 1) * cols)
                q = head_lanes(qb[half, lanes, Q_LANES[head]:Q_LANES[head] + 128], head)
                pos = q_base + part * cols + lax.broadcasted_iota(jnp.int32, (1, cols), 1)
                first = first_keys(starts_ref, pos) - k_base
                s = nt(k_all[:keys], q)
                row = lax.broadcasted_iota(jnp.int32, (keys, cols), 0)
                ok = row >= first
                if diag:
                    ok = ok & (row <= pos - k_base)
                s = jnp.where(ok, s, NEG)
                line = slice(head, head + 1)
                feats = slice(head * HD, (head + 1) * HD)
                high = jnp.max(s, axis=0, keepdims=True)
                if not diag:
                    before = top[half, line, lanes]
                    high = jnp.maximum(before, high)
                    fade = jnp.exp(before - high)
                w = jnp.exp(s - high)
                add = jnp.sum(w, axis=0, keepdims=True)
                o = nn(v_t[:, :keys], w.astype(BF))
                if diag:
                    tot[half, line, lanes] = add
                    acc[half, feats, lanes] = o
                else:
                    tot[half, line, lanes] = tot[half, line, lanes] * fade + add
                    acc[half, feats, lanes] = acc[half, feats, lanes] * fade + o
                top[half, line, lanes] = high

    @pl.loop(0, 2)
    def _(half):
        q_base = jnp.where(half == 0, base_of(0, z), base_of(1, z))
        tile(half, depth - 1 + half, q_base, q_base, True)

    @pl.loop(1, depth)
    def _(step):
        valid = (z - step >= 0, z + step <= depth - 1)
        slots = (step - 1, z + step - 1)
        for half in range(2):
            for p in range(INNER):
                @pl.when(valid[half])
                def _():
                    rws = pl.ds(p * blk, blk)
                    send(kv.at[slots[half], rws], kv.at[slots[half], rws], zs.at[half, step - 1, p],
                         zr.at[half, step - 1, p], (z * INNER + (h + 1) % INNER, f)).wait_recv()

                @pl.when(valid[half] & can[half])
                def _():
                    relay(half, slots[half], step + 1, p).start()

        @pl.loop(0, 2)
        def _(half):
            @pl.when(jnp.where(half == 0, z - step, depth - 1 - z - step) >= 0)
            def _():
                zz = jnp.where(half == 0, z - step, z + step)
                q_base = jnp.where(half == 0, base_of(0, z), base_of(1, z))
                k_base = jnp.where(half == 0, base_of(0, zz), base_of(1, zz))
                tile(half, jnp.where(half == 0, step - 1, z + step - 1), q_base, k_base, False)

    ob[:, :, 2 * HD:3 * HD] = jnp.zeros((2, rows, HD), BF)
    for half in range(2):
        lse_ref[half] = top[half] + jnp.log(tot[half])
        for head in range(3):
            feats = slice(head * HD, (head + 1) * HD)
            acc[half, feats, :] = acc[half, feats, :] / tot[half, head:head + 1, :]
        ob[half, :, :2 * HD] = acc[half, :2 * HD, :].T.astype(BF)
        ob[half, :, 3 * HD:] = acc[half, 2 * HD:, :].T.astype(BF)
    outs = [pltpu.make_async_copy(qb, qb_ref, osem.at[0]), pltpu.make_async_copy(kv, kv_ref, osem.at[1]),
            pltpu.make_async_copy(acc, ot_ref, osem.at[2])]
    for cp in outs:
        cp.start()

    def back(j, half):
        i = (h + j) % INNER
        return send(ob.at[half, piece(half, i)], land.at[half_rows[half], pl.ds(pl.multiple_of(h * QW, 128), QW)],
                    bs.at[half, j - 1], br.at[half, j - 1], (z * INNER + i, f))

    for half in range(2):
        for j in range(1, INNER):
            back(j, half).start()
        mine = pltpu.make_async_copy(ob.at[half, piece(half, h)],
                                     land.at[half_rows[half], pl.ds(pl.multiple_of(h * QW, 128), QW)], lsem.at[half, 0])
        mine.start()
        mine.wait()
    for half in range(2):
        for j in range(1, INNER):
            back(j, half).wait_recv()
    ungroup_rows(land, out_ref)
    for half in range(2):
        for j in range(1, INNER):
            a2a(j, half, 1).wait_send()
            a2a(j, half, 0).wait_send()
            back(j, half).wait_send()

        @pl.when(can[half])
        def _():
            for p in range(INNER):
                relay(half, own[half], 1, p).wait_send()

    @pl.loop(1, depth)
    def _(step):
        valid = (z - step >= 0, z + step <= depth - 1)
        for half in range(2):
            @pl.when(valid[half] & can[half])
            def _():
                for p in range(INNER):
                    relay(half, own[half], step + 1, p).wait_send()
    for cp in outs:
        cp.wait()


def attend(starts, x, length, cid):
    depth = lax.axis_size("ctx") // INNER
    blk = x.shape[0] // 2
    rows = INNER * blk
    dma = pltpu.SemaphoreType.DMA
    shapes = (
        jax.ShapeDtypeStruct((x.shape[0], H * HD), BF),
        jax.ShapeDtypeStruct((2, rows, QW), BF),
        jax.ShapeDtypeStruct((depth + 1, rows, KW), BF),
        jax.ShapeDtypeStruct((2, 3 * HD, rows), F32),
        jax.ShapeDtypeStruct((2, 8, rows), F32),
    )
    vm = pl.BlockSpec(memory_space=pltpu.VMEM)
    anyspec = pl.BlockSpec(memory_space=pl.ANY)
    return pl.pallas_call(
        functools.partial(attend_kernel, depth, length),
        out_shape=shapes,
        in_specs=[pl.BlockSpec(memory_space=pltpu.SMEM), vm],
        out_specs=(vm, anyspec, anyspec, anyspec, vm),
        scratch_shapes=[
            pltpu.VMEM((2 * blk, INNER * GW), BF),
            pltpu.VMEM((2, rows, QW), BF),
            pltpu.VMEM((depth + 1, rows, KW), BF),
            pltpu.VMEM((2, 3 * HD, rows), F32),
            pltpu.VMEM((2, 8, rows), F32),
            pltpu.VMEM((2, 8, rows), F32),
            pltpu.VMEM((2, rows, QW), BF),
            pltpu.VMEM((2 * blk, INNER * QW), BF),
            dma((2, 2)), dma((2, 3)), dma((2, 3)), dma((2, 3)), dma((2, 3)),
            dma((2, depth, INNER)), dma((2, depth, INNER)), dma((2, 3)), dma((2, 3)), dma((3,)),
        ],
        compiler_params=pltpu.CompilerParams(collective_id=cid, has_side_effects=True, vmem_limit_bytes=48 << 20),
        name="attend",
    )(starts, x)


def ring_pos(z, bit, depth):
    return jnp.where(bit == 0, z, 2 * depth - 1 - z)


def ring_ctx(pos, depth, kind, fixed):
    pos = lax.rem(pos + 2 * depth, 2 * depth)
    z = jnp.where(pos < depth, pos, 2 * depth - 1 - pos)
    bit = jnp.where(pos < depth, 0, 1)
    return z * INNER + (bit * 2 + fixed if kind == 0 else fixed * 2 + bit)


def region_rows(used, n):
    return -(-used // (32 * n)) * 32 * n


def back_kernel(cfg, starts_ref, h_do, h_qb, h_kv, h_ot, h_lse, h_one, h_out, h_gout, h_mid, h_gpre, h_act, h_gtop,
                h_w, h_tok, h_hid, gain, v_ref,
                o_qkv, o_out, o_fc1, o_fc2, vout_ref, o_in,
                raw, qb, kv, ot, lse, x_one, x_out, g_out, x_mid, g_pre, x_act, g_top, wbuf, tokens, g_hid,
                do_ref, dob, dots, dq, dkvd, rbuf, dqb, fin, land, g_qkv,
                xt, gbuf, acc, fbuf, pa, pb, pa3, pb3, ra, rb, ra3, rb3,
                vall, vacc, vf, vx, vr,
                ldsem, lsem, as_o, ar_o, zs, zr, bq, brq, bk, brk,
                fsem, frec, ps, pr, rs, rr, xgs, xgr, vfs, vfr, vxs, vxr, vrs, vrr, osem):
    depth, length, n, fs, big, small_rows = cfg
    z, h, f = places()
    c = lax.axis_index("ctx")
    bits = (h % 2, h // 2)
    poss = (ring_pos(z, bits[1], depth), ring_pos(z, bits[0], depth))
    pairs_of = ((c + 1 - 2 * bits[0], f), (c + 2 - 4 * bits[1], f))
    rights = tuple((ring_ctx(poss[k] + 1, depth, k, bits[k]), f) for k in range(2))
    lefts = tuple((ring_ctx(poss[k] - 1, depth, k, bits[k]), f) for k in range(2))
    fpeers = [(c, lax.rem(f + k, fs)) for k in range(1, fs)]
    width = acc.shape[1]
    lanes = (pl.ds(0, width // 2), pl.ds(width // 2, width // 2))
    part = width // fs
    bases_of = (0, big, 2 * big, 2 * big + small_rows)
    outb = gbuf.at[0]
    slots = gbuf.shape[0]
    blk = raw.shape[0] // 2
    rows = INNER * blk
    cols = rows // 2
    half_rows = (pl.ds(0, blk), pl.ds(blk, blk))

    barrier = pltpu.get_barrier_semaphore()
    for j in range(1, INNER):
        pl.semaphore_signal(barrier, inc=1, device_id=(z * INNER + (h + j) % INNER, f), device_id_type=MESH)

    @pl.when(z > 0)
    def _():
        pl.semaphore_signal(barrier, inc=1, device_id=((z - 1) * INNER + h, f), device_id_type=MESH)

    @pl.when(z < depth - 1)
    def _():
        pl.semaphore_signal(barrier, inc=1, device_id=((z + 1) * INNER + h, f), device_id_type=MESH)

    for peer in list(rights) + list(lefts) + fpeers:
        pl.semaphore_signal(barrier, inc=1, device_id=peer, device_id_type=MESH)

    loads = {}
    pairs = (("do", h_do, raw), ("act", h_act, x_act), ("gtop", h_gtop, g_top), ("mid", h_mid, x_mid),
             ("gpre", h_gpre, g_pre), ("out", h_out, x_out), ("gout", h_gout, g_out), ("ot", h_ot, ot),
             ("kv", h_kv, kv), ("qb", h_qb, qb), ("lse", h_lse, lse), ("one", h_one, x_one), ("w", h_w, wbuf),
             ("tok", h_tok, tokens), ("hid", h_hid, g_hid))
    for i, (name, src, dst) in enumerate(pairs):
        loads[name] = pltpu.make_async_copy(src, dst, ldsem.at[i])
        loads[name].start()

    pend = []

    def go(cp):
        cp.start()
        pend.append(cp)
        return cp

    def piece(half, i):
        p = i if half == 0 else INNER - 1 - i
        return pl.ds(pl.multiple_of(p * blk, blk), blk)

    def spread(j, half):
        i = (h + j) % INNER
        return send(do_ref.at[half_rows[half], pl.ds(pl.multiple_of(i * QW, 128), QW)], dob.at[half, piece(half, h)],
                    as_o.at[half, j - 1], ar_o.at[half, j - 1], (z * INNER + i, f))

    loads["do"].wait()
    group_rows(raw, do_ref)
    pl.semaphore_wait(barrier, INNER - 1 + 4 + fs - 1 + jnp.where(z > 0, 1, 0) + jnp.where(z < depth - 1, 1, 0))
    mine = []
    for half in range(2):
        for j in range(1, INNER):
            go(spread(j, half))
        cp = pltpu.make_async_copy(do_ref.at[half_rows[half], pl.ds(pl.multiple_of(h * QW, 128), QW)],
                                   dob.at[half, piece(half, h)], lsem.at[half])
        cp.start()
        mine.append(cp)

    eye_n = 256
    eye = (lax.broadcasted_iota(jnp.int32, (eye_n, eye_n), 0)
           == lax.broadcasted_iota(jnp.int32, (eye_n, eye_n), 1)).astype(BF)
    offset = {"act": 0, "mid": 4 * width, "out": 5 * width, "one": 6 * width}

    def turn_over(name, ref):
        @pl.loop(0, ref.shape[1] // eye_n)
        def _(b):
            o = pl.multiple_of(b * eye_n, eye_n)
            xt[pl.ds(pl.multiple_of(offset[name] + o, eye_n), eye_n), :] = nt(eye, ref[:, pl.ds(o, eye_n)]).astype(BF)

    def unit(name, start, g, dst, row):
        lhs = xt[pl.ds(pl.multiple_of(offset[name] + start, 16), part), :]
        dst[pl.ds(pl.multiple_of(row, 16), part), :] = nn(lhs, g).astype(BF)

    def fc2_for(owner, dst):
        @pl.loop(0, 4)
        def _(j):
            unit("act", owner * 4 * part + j * part, g_top[...], dst, bases_of[1] + j * part)

    def fc1_for(owner, dst):
        @pl.loop(0, 4)
        def _(j):
            unit("mid", owner * part, g_pre[:, pl.ds(pl.multiple_of(j * width, 128), width)], dst, bases_of[0] + j * part)

    def out_q_for(owner, dst):
        unit("out", owner * part, g_out[...], dst, bases_of[2])
        unit("one", owner * part, g_qkv[:, :width], dst, bases_of[2] + part)

    def k_v_for(owner, dst):
        unit("one", owner * part, g_qkv[:, width:2 * width], dst, bases_of[3])
        unit("one", owner * part, g_qkv[:, 2 * width:], dst, bases_of[3] + part)

    cuts = ((bases_of[0], 4 * part, 0), (bases_of[1], 4 * part, 4 * part), (bases_of[2], 2 * part, 8 * part),
            (bases_of[3], 2 * part, 10 * part))

    def to_core(k, j):
        a, m, at = cuts[j]
        return remote(gbuf.at[(k - 1) % slots, pl.ds(a, m)], fbuf.at[k - 1, pl.ds(at, m)],
                      fsem.at[k - 1, j], frec.at[k - 1, j], fpeers[k - 1])

    def remote(src, dst, ssem, rsem, peer):
        return send(src, dst, ssem, rsem, peer)

    def share(j, make):
        for k in range(1, fs):
            if k - 1 >= slots:
                to_core(k - slots, j).wait_send()
            make(fpeers[k - 1][1], gbuf.at[(k - 1) % slots])
            to_core(k, j).start()

    def collect(j):
        for k in range(1, fs):
            if k > fs - 1 - slots:
                to_core(k, j).wait_send()
            to_core(k, j).wait_recv()
        a, m, at = cuts[j]
        step = 32

        @pl.loop(0, m // step)
        def _(i):
            rws = pl.ds(pl.multiple_of(a + i * step, step), step)
            tot = acc[rws, :].astype(F32)
            for k in range(fs - 1):
                tot = tot + fbuf[k, pl.ds(pl.multiple_of(at + i * step, step), step), :].astype(F32)
            acc[rws, :] = tot.astype(BF)

    for (a, m, _), size in zip(cuts, (big, big, small_rows, small_rows)):
        if size > m:
            acc[a + m:a + size, :] = jnp.zeros((size - m, width), BF)

    def stream(i, kind, pbuf, rbuf_):
        size = big if i < 2 else small_rows
        half = size // 2
        keep_at = pl.multiple_of(bases_of[i] + bits[kind] * half, 16)
        give_at = pl.multiple_of(bases_of[i] + (1 - bits[kind]) * half, 16)
        return (i, kind, keep_at, give_at, half, half // n, pbuf, rbuf_)

    sa, sb, sa3, sb3 = stream(0, 0, pa, ra), stream(1, 1, pb, rb), stream(2, 0, pa3, ra3), stream(3, 1, pb3, rb3)

    def rows_of(st, k, base=None):
        k = lax.rem(k + 2 * n, n)
        return pl.ds(pl.multiple_of((st[2] if base is None else base) + k * st[5], 16), st[5])

    def pair_copy(st):
        return remote(acc.at[pl.ds(st[3], st[4])], st[6], ps.at[st[0]], pr.at[st[0]], pairs_of[st[1]])

    def pair_add(st):
        pair_copy(st).wait_recv()
        step = 32 if st[4] % 32 == 0 else 16

        @pl.loop(0, st[4] // step)
        def _(i):
            rws = pl.ds(pl.multiple_of(st[2] + i * step, 16), step)
            acc[rws, :] = (acc[rws, :].astype(F32)
                           + st[6][pl.ds(pl.multiple_of(i * step, 16), step), :].astype(F32)).astype(BF)

    def rs_copy(st, s, d):
        p = poss[st[1]]
        k = p - 1 - s if d == 0 else p + 1 + s
        return remote(acc.at[rows_of(st, k), lanes[d]], st[7].at[s, :, lanes[d]],
                      rs.at[st[0], 0, d, s], rr.at[st[0], 0, d, s], (rights if d == 0 else lefts)[st[1]])

    def rs_start(st):
        for d in range(2):
            go(rs_copy(st, 0, d))

    def rs_step(st, s):
        p = poss[st[1]]
        for d in range(2):
            rws = rows_of(st, p - 2 - s if d == 0 else p + 2 + s)
            rs_copy(st, s, d).wait_recv()
            tot = (acc[rws, lanes[d]].astype(F32) + st[7][s, :, lanes[d]].astype(F32)).astype(BF)
            if s < n - 2:
                acc[rws, lanes[d]] = tot
                go(rs_copy(st, s + 1, d))
            elif d == 0:
                outb[rws, lanes[d]] = tot
            else:
                outb[rws, lanes[d]] = tot
                ag_start(st)

    def ag_copy(st, s, d):
        p = poss[st[1]]
        rws = rows_of(st, p - s if d == 0 else p + s)
        return remote(outb.at[rws, lanes[d]], outb.at[rws, lanes[d]],
                      rs.at[st[0], 1, d, s], rr.at[st[0], 1, d, s], (rights if d == 0 else lefts)[st[1]])

    def cross(st, s, d, base=None):
        p = poss[st[1]]
        rws = rows_of(st, p - s if d == 0 else p + s, base)
        return remote(outb.at[rws, lanes[d]], outb.at[rws, lanes[d]], xgs.at[st[0], d, s], xgr.at[st[0], d, s],
                      pairs_of[st[1]])

    def ag_start(st):
        for d in range(2):
            go(ag_copy(st, 0, d))
        for d in range(2):
            go(cross(st, 0, d))

    def ag_step(st, s):
        p = poss[st[1]]
        for d in range(2):
            rws = rows_of(st, p - 1 - s if d == 0 else p + 1 + s)
            remote(outb.at[rws, lanes[d]], outb.at[rws, lanes[d]],
                   rs.at[st[0], 1, d, s], rr.at[st[0], 1, d, s], pairs_of[0]).wait_recv()
            if s < n - 2:
                go(ag_copy(st, s + 1, d))
            go(cross(st, s + 1, d))

    def cross_wait(st):
        for s in range(n):
            for d in range(2):
                cross(st, s, d, st[3]).wait_recv()

    loads["act"].wait()
    turn_over("act", x_act)
    loads["gtop"].wait()
    share(1, fc2_for)
    loads["mid"].wait()
    turn_over("mid", x_mid)
    loads["gpre"].wait()
    share(0, fc1_for)
    fc2_for(f, acc)
    collect(1)
    go(pair_copy(sb))
    fc1_for(f, acc)
    collect(0)
    go(pair_copy(sa))

    dq[...] = jnp.zeros_like(dq)
    loads["ot"].wait()
    for half in range(2):
        mine[half].wait()
        for j in range(1, INNER):
            spread(j, half).wait_recv()
        for head in range(3):
            ln = slice(0, 128) if head < 2 else slice(128, 256)
            g = dob[half, :, ln].astype(F32).T[(0 if head == 0 else HD):(HD if head == 0 else 2 * HD)]
            dots[half, head:head + 1, :] = jnp.sum(g * ot[half, head * HD:(head + 1) * HD, :], axis=0, keepdims=True)
    for name in ("kv", "qb", "lse"):
        loads[name].wait()

    def base_of(half, zz):
        return zz * rows if half == 0 else length - (zz + 1) * rows

    def bases(half, zz):
        return jnp.where(half == 0, base_of(0, zz), base_of(1, zz))

    def tile(half, slot, q_base, k_base, diag, head):
        k_all = kv[slot, :, K_LANES[head]:K_LANES[head] + 128]
        v_all = kv[slot, :, V_LANES[head]:V_LANES[head] + 128]
        k_t = k_all.T[(HD if head == 1 else 0):(2 * HD if head == 1 else HD)]
        kl = slice(K_LANES[head], K_LANES[head] + 128)
        vl = slice(V_LANES[head], V_LANES[head] + 128)
        for half_cols in range(2):
            keys = (half_cols + 1) * cols if diag else rows
            ln = slice(half_cols * cols, (half_cols + 1) * cols)
            q = head_lanes(qb[half, ln, Q_LANES[head]:Q_LANES[head] + 128], head)
            g = head_lanes(dob[half, ln, Q_LANES[head]:Q_LANES[head] + 128], head)
            p = q_base + half_cols * cols + lax.broadcasted_iota(jnp.int32, (1, cols), 1)
            first = first_keys(starts_ref, p) - k_base
            s = nt(k_all[:keys], q)
            row = lax.broadcasted_iota(jnp.int32, (keys, cols), 0)
            ok = row >= first
            if diag:
                ok = ok & (row <= p - k_base)
            line = slice(head, head + 1)
            w = jnp.where(ok, jnp.exp(s - lse[half, line, ln]), 0.0)
            gp = nt(v_all[:keys], g)
            ds = (w * (gp - dots[half, line, ln])).astype(BF)
            dv = nn(w.astype(BF), g)
            dk = nn(ds, q)
            for sl, val in (((kl, dk + dv),) if head == 2 else ((kl, dk), (vl, dv))):
                if head != 1 and half_cols == 0:
                    dkvd[half, :keys, sl] = val
                elif head != 1 and diag:
                    dkvd[half, :cols, sl] = dkvd[half, :cols, sl] + val[:cols]
                    dkvd[half, cols:, sl] = val[cols:]
                else:
                    dkvd[half, :keys, sl] = dkvd[half, :keys, sl] + val
            feats = slice(head * HD, (head + 1) * HD)
            dq[half, feats, ln] = dq[half, feats, ln] + nn(k_t[:, :keys], ds)

    has = (z < depth - 1, z > 0)

    def pass_on(half, step):
        peer = (z - 1) * INNER + h if half == 0 else (z + 1) * INNER + h
        return send(rbuf.at[half, step], rbuf.at[half, step - 1], zs.at[half, step - 1], zr.at[half, step - 1], (peer, f))

    def take(half, step):
        return send(rbuf.at[half, step], rbuf.at[half, step], zs.at[half, step], zr.at[half, step],
                    (z * INNER + (h + 1) % INNER, f))

    @pl.loop(0, 2 * (depth - 1))
    def _(it):
        step = depth - 1 - it // 2
        half = it % 2
        valid = jnp.where(half == 0, z - step, depth - 1 - z - step) >= 0
        zz = jnp.where(half == 0, z - step, z + step)
        for head in range(3):
            @pl.when(valid)
            def _():
                tile(half, jnp.where(half == 0, step - 1, z + step - 1), bases(half, z), bases(half, zz), False, head)

        @pl.when(valid)
        def _():
            more = jnp.where(half == 0, depth - 1 - z, z) > 0

            @pl.when(more)
            def _():
                take(half, step).wait_recv()

                @pl.loop(0, rows // 64)
                def _(b):
                    rws = pl.ds(pl.multiple_of(b * 64, 64), 64)
                    rbuf[half, step, rws, :] = (dkvd[half, rws, :] + rbuf[half, step, rws, :].astype(F32)).astype(BF)

            @pl.when(jnp.logical_not(more))
            def _():
                rbuf[half, step] = dkvd[half].astype(BF)

            @pl.when(half == 0)
            def _():
                pass_on(0, step).start()

            @pl.when(half == 1)
            def _():
                pass_on(1, step).start()

    for st in (sb, sa):
        pair_add(st)
        rs_start(st)

    @pl.loop(0, 2)
    def _(half):
        for head in range(3):
            tile(half, depth - 1 + half, bases(half, z), bases(half, z), True, head)

    def back(j, half, kind):
        i = (h + j) % INNER
        ln = pl.ds(pl.multiple_of(h * GW + (QW if kind else 0), 128), KW if kind else QW)
        src = fin if kind else dqb
        sems = (bk.at[half, j - 1], brk.at[half, j - 1]) if kind else (bq.at[half, j - 1], brq.at[half, j - 1])
        return send(src.at[half, piece(half, i)], land.at[half_rows[half], ln], *sems, (z * INNER + i, f))

    def keep(half, kind):
        ln = pl.ds(pl.multiple_of(h * GW + (QW if kind else 0), 128), KW if kind else QW)
        src = fin if kind else dqb
        return pltpu.make_async_copy(src.at[half, piece(half, h)], land.at[half_rows[half], ln],
                                     lsem.at[2 + 2 * half + kind])

    dqb[:, :, 3 * HD:] = jnp.zeros((2, rows, HD), BF)
    for half in range(2):
        dqb[half, :, :2 * HD] = (dq[half, :2 * HD, :] * (HD ** -0.5)).T.astype(BF)
        dqb[half, :, 2 * HD:3 * HD] = (dq[half, 2 * HD:, :] * (HD ** -0.5)).T.astype(BF)
        for j in range(1, INNER):
            go(back(j, half, 0))
        keep(half, 0).start()
    rs_step(sb, 0)
    rs_step(sa, 0)
    for half in range(2):
        @pl.when(has[half])
        def _():
            take(half, 0).wait_recv()

            @pl.loop(0, rows // 64)
            def _(b):
                rws = pl.ds(pl.multiple_of(b * 64, 64), 64)
                fin[half, rws, :] = (dkvd[half, rws, :] + rbuf[half, 0, rws, :].astype(F32)).astype(BF)

        @pl.when(jnp.logical_not(has[half]))
        def _():
            fin[half] = dkvd[half].astype(BF)
        for j in range(1, INNER):
            go(back(j, half, 1))
        keep(half, 1).start()

    loads["out"].wait()
    turn_over("out", x_out)
    loads["gout"].wait()
    loads["one"].wait()
    turn_over("one", x_one)
    fc = []
    for s in range(1, n - 1):
        fc += [functools.partial(rs_step, sb, s), functools.partial(rs_step, sa, s)]
    for s in range(n - 1):
        fc += [functools.partial(ag_step, sb, s), functools.partial(ag_step, sa, s)]

    def some(count):
        for task in fc[:count]:
            task()
        del fc[:count]

    some(6)
    for half in range(2):
        for kind in range(2):
            keep(half, kind).wait()
            for j in range(1, INNER):
                back(j, half, kind).wait_recv()
    ungroup_qkv(land, g_qkv)
    share(2, out_q_for)
    share(3, k_v_for)
    out_q_for(f, acc)
    k_v_for(f, acc)

    def vec_copy(k):
        return remote(vall.at[fpeers[k - 1][1]], vf.at[k - 1], vfs.at[k - 1], vfr.at[k - 1], fpeers[k - 1])

    def norm_back():
        e = nt(g_qkv[...], wbuf[...])
        x = tokens[...].astype(F32)
        center = x - jnp.mean(x, axis=-1, keepdims=True)
        r = lax.rsqrt(jnp.mean(center * center, axis=-1, keepdims=True) + EPS)
        xh = center * r
        t = e * gain[...].astype(F32)
        o_in[...] = g_hid[...] + r * (t - jnp.mean(t, axis=-1, keepdims=True)
                                      - xh * jnp.mean(t * xh, axis=-1, keepdims=True))
        vall[...] = v_ref[...]
        gq = g_qkv[:, :width].astype(F32)
        gv = g_qkv[:, 2 * width:].astype(F32)
        for row, val in enumerate((e * xh, e, gq, gv)):
            line = jnp.sum(val, axis=0, keepdims=True)
            for i in range(fs):
                vall[i, row:row + 1, :] = line[:, i * part:(i + 1) * part]

    collect(2)
    go(pair_copy(sa3))
    collect(3)
    go(pair_copy(sb3))
    for name in ("w", "tok", "hid"):
        loads[name].wait()
    norm_back()
    for k in range(1, fs):
        go(vec_copy(k))

    def vec_pair():
        for k in range(1, fs):
            vec_copy(k).wait_recv()
        vtot = vall[f]
        for k in range(fs - 1):
            vtot = vtot + vf[k]
        vacc[...] = vtot
        go(remote(vacc, vx, vxs, vxr, pairs_of[0]))

    pos = poss[0]

    def vec_send(s):
        w = lax.rem(pos - s + n, n)
        go(remote(vr.at[w], vr.at[w], vrs.at[s], vrr.at[s], rights[0]))

    def vec_start():
        remote(vacc, vx, vxs, vxr, pairs_of[0]).wait_recv()
        vr[pos] = vacc[...] + vx[...]
        vec_send(0)

    def vec_ring(s):
        w = lax.rem(pos - 1 - s + n, n)
        remote(vr.at[w], vr.at[w], vrs.at[s], vrr.at[s], rights[0]).wait_recv()
        if s < n - 2:
            vec_send(s + 1)

    small = [vec_pair, vec_start] + [functools.partial(vec_ring, s) for s in range(n - 1)]
    some(4)

    def late_start():
        for st in (sa3, sb3):
            pair_add(st)
            rs_start(st)

    main = [late_start]
    for s in range(n - 1):
        main.append(lambda s=s: (rs_step(sa3, s), rs_step(sb3, s)))
    for s in range(n - 1):
        main.append(lambda s=s: (ag_step(sa3, s), ag_step(sb3, s)))
    outs = []

    def flush(u):
        if u < 4:
            src, dst = bases_of[0] + u * part, o_fc1.at[:, pl.ds(u * width, width)]
        elif u < 8:
            src, dst = bases_of[1] + (u - 4) * part, o_fc2.at[pl.ds((u - 4) * part, part)]
        elif u == 8:
            src, dst = bases_of[2], o_out
        else:
            src = bases_of[2] + part if u == 9 else bases_of[3] + (u - 10) * part
            dst = o_qkv.at[:, pl.ds((u - 9) * width, width)]
        cp = pltpu.make_async_copy(outb.at[pl.ds(src, part)], dst, osem.at[u])
        cp.start()
        outs.append(cp)

    def fc_done():
        for st in (sb, sa):
            cross_wait(st)
        for u in range(8):
            flush(u)

    fc.append(fc_done)
    for i in range(len(main)):
        main[i]()
        if i < len(small):
            small[i]()
        some(2)
    some(len(fc))
    for task in small[len(main):]:
        task()
    for st in (sa3, sb3):
        cross_wait(st)
    for u in range(8, 12):
        flush(u)
    vsum = vr[0]
    for k in range(1, n):
        vsum = vsum + vr[k]
    vout_ref[...] = vsum
    for cp in pend:
        cp.wait_send()

    @pl.loop(1, depth)
    def _(step):
        valid = (z - step >= 0, z + step <= depth - 1)
        for half in range(2):
            @pl.when(valid[half])
            def _():
                pass_on(half, step).wait_send()
    for cp in outs:
        cp.wait()


def block_back(starts, do, kept, lse, ops, w_one, tokens, g_hid, gain, v, length, cid):
    qb, kv, ot = kept
    fs = lax.axis_size("fsdp")
    depth = lax.axis_size("ctx") // INNER
    n = lax.axis_size("ctx") // 2
    toks, width = do.shape
    blk = toks // 2
    rows = INNER * blk
    part = width // fs
    big, few = region_rows(4 * part, n), region_rows(2 * part, n)
    tot = 2 * (big + few)
    slots = min(fs - 1, 2)
    vs = v.shape[1:]
    dma = pltpu.SemaphoreType.DMA
    vm = pl.BlockSpec(memory_space=pltpu.VMEM)
    anyspec = pl.BlockSpec(memory_space=pl.ANY)
    ins = (do, qb, kv, ot, lse) + tuple(ops) + (w_one, tokens, g_hid)
    order = [do, qb, kv, ot, lse] + list(ops) + [w_one, tokens, g_hid]
    cfg = (depth, length, n, fs, big, few)
    return pl.pallas_call(
        functools.partial(back_kernel, cfg),
        out_shape=(jax.ShapeDtypeStruct((part, 3 * width), BF), jax.ShapeDtypeStruct((part, width), BF),
                   jax.ShapeDtypeStruct((part, 4 * width), BF), jax.ShapeDtypeStruct((4 * part, width), BF),
                   jax.ShapeDtypeStruct(vs, F32), jax.ShapeDtypeStruct((toks, width), F32)),
        in_specs=[pl.BlockSpec(memory_space=pltpu.SMEM)] + [anyspec] * len(ins) + [vm, vm],
        out_specs=(anyspec, anyspec, anyspec, anyspec, vm, vm),
        scratch_shapes=[pltpu.VMEM(a.shape, a.dtype) for a in order] + [
            pltpu.VMEM((toks, INNER * QW), BF),
            pltpu.VMEM((2, rows, QW), BF),
            pltpu.VMEM((2, 8, rows), F32),
            pltpu.VMEM((2, 3 * HD, rows), F32),
            pltpu.VMEM((2, rows, KW), F32),
            pltpu.VMEM((2, depth, rows, KW), BF),
            pltpu.VMEM((2, rows, QW), BF),
            pltpu.VMEM((2, rows, KW), BF),
            pltpu.VMEM((toks, INNER * GW), BF),
            pltpu.VMEM((toks, 3 * width), BF),
            pltpu.VMEM((7 * width, toks), BF),
            pltpu.VMEM((slots, tot, width), BF),
            pltpu.VMEM((tot, width), BF),
            pltpu.VMEM((fs - 1, 12 * part, width), BF),
            pltpu.VMEM((big // 2, width), BF), pltpu.VMEM((big // 2, width), BF),
            pltpu.VMEM((few // 2, width), BF), pltpu.VMEM((few // 2, width), BF),
            pltpu.VMEM((n - 1, big // 2 // n, width), BF), pltpu.VMEM((n - 1, big // 2 // n, width), BF),
            pltpu.VMEM((n - 1, few // 2 // n, width), BF), pltpu.VMEM((n - 1, few // 2 // n, width), BF),
            pltpu.VMEM((fs,) + vs, F32),
            pltpu.VMEM(vs, F32),
            pltpu.VMEM((fs - 1,) + vs, F32),
            pltpu.VMEM(vs, F32),
            pltpu.VMEM((n,) + vs, F32),
            dma((15,)), dma((6,)), dma((2, 3)), dma((2, 3)), dma((2, depth)), dma((2, depth)),
            dma((2, 3)), dma((2, 3)), dma((2, 3)), dma((2, 3)),
            dma((fs - 1, 4)), dma((fs - 1, 4)), dma((4,)), dma((4,)),
            dma((4, 2, 2, n - 1)), dma((4, 2, 2, n - 1)), dma((4, 2, n)), dma((4, 2, n)),
            dma((fs - 1,)), dma((fs - 1,)), dma(()), dma(()), dma((n - 1,)), dma((n - 1,)), dma((12,)),
        ],
        compiler_params=pltpu.CompilerParams(collective_id=cid, has_side_effects=True, vmem_limit_bytes=62 << 20),
        name="block_back",
    )(starts, *ins, gain, v)


def layer_norm(values, gain, shift):
    center = values - jnp.mean(values, axis=-1, keepdims=True)
    spread = jnp.mean(center * center, axis=-1, keepdims=True)
    return center * lax.rsqrt(spread + EPS) * gain + shift


def gelu_tanh(values):
    return jax.nn.gelu(values, approximate=True)


def per_device(
    stream,
    doc_starts,
    ln1_gain,
    ln1_bias,
    qkv_weight,
    q_bias,
    v_bias,
    out_weight,
    out_bias,
    ln2_gain,
    ln2_bias,
    fc1_weight,
    fc1_bias,
    fc2_weight,
    fc2_bias,
    cotangent,
):
    f32 = jnp.float32
    bf16 = jnp.bfloat16
    ctx_count = lax.axis_size("ctx")
    tok_rows = stream.shape[1]
    width = stream.shape[2]
    length = ctx_count * tok_rows
    params = (
        lax.all_gather(ln1_gain, "fsdp", axis=0, tiled=True),
        lax.all_gather(ln1_bias, "fsdp", axis=0, tiled=True),
        lax.all_gather(qkv_weight, "fsdp", axis=0, tiled=True),
        lax.all_gather(q_bias, "fsdp", axis=0, tiled=True),
        lax.all_gather(v_bias, "fsdp", axis=0, tiled=True),
        lax.all_gather(out_weight, "fsdp", axis=0, tiled=True),
        lax.all_gather(out_bias, "fsdp", axis=0, tiled=True),
        lax.all_gather(ln2_gain, "fsdp", axis=0, tiled=True),
        lax.all_gather(ln2_bias, "fsdp", axis=0, tiled=True),
        lax.all_gather(fc1_weight, "fsdp", axis=0, tiled=True),
        lax.all_gather(fc1_bias, "fsdp", axis=0, tiled=True),
        lax.all_gather(fc2_weight, "fsdp", axis=0, tiled=True),
        lax.all_gather(fc2_bias, "fsdp", axis=0, tiled=True),
    )
    (
        g_one,
        b_one,
        w_qkv,
        q_shift,
        v_shift,
        w_out,
        o_shift,
        g_two,
        b_two,
        w_fc1,
        c_fc1,
        w_fc2,
        c_fc2,
    ) = params
    inputs = stream[0].astype(f32)
    normed_f = layer_norm(inputs, g_one.astype(f32), b_one.astype(f32))
    normed_in = normed_f.astype(bf16)
    shift_qkv = jnp.concatenate([q_shift, jnp.zeros_like(q_shift), v_shift]).astype(f32)
    projected = (jnp.dot(normed_in, w_qkv, preferred_element_type=f32) + shift_qkv).astype(bf16)
    attn, q_kept, kv_kept, out_kept, lse = attend(doc_starts, projected, length, 1)
    hidden = inputs + jnp.dot(attn, w_out, preferred_element_type=f32) + o_shift.astype(f32)
    normed_mf, ln2_pull = jax.vjp(layer_norm, hidden, g_two.astype(f32), b_two.astype(f32))
    normed_mid = normed_mf.astype(bf16)
    pre_act = jnp.dot(normed_mid, w_fc1, preferred_element_type=f32) + c_fc1.astype(f32)
    activ_f, gelu_pull = jax.vjp(gelu_tanh, pre_act)
    activ = activ_f.astype(bf16)
    result = hidden + jnp.dot(activ, w_fc2, preferred_element_type=f32) + c_fc2.astype(f32)
    layer_out = result.astype(bf16)[None]
    params_back = (
        lax.all_gather(ln1_gain, "fsdp", axis=0, tiled=True),
        lax.all_gather(ln1_bias, "fsdp", axis=0, tiled=True),
        lax.all_gather(qkv_weight, "fsdp", axis=0, tiled=True),
        lax.all_gather(q_bias, "fsdp", axis=0, tiled=True),
        lax.all_gather(v_bias, "fsdp", axis=0, tiled=True),
        lax.all_gather(out_weight, "fsdp", axis=0, tiled=True),
        lax.all_gather(out_bias, "fsdp", axis=0, tiled=True),
        lax.all_gather(ln2_gain, "fsdp", axis=0, tiled=True),
        lax.all_gather(ln2_bias, "fsdp", axis=0, tiled=True),
        lax.all_gather(fc1_weight, "fsdp", axis=0, tiled=True),
        lax.all_gather(fc1_bias, "fsdp", axis=0, tiled=True),
        lax.all_gather(fc2_weight, "fsdp", axis=0, tiled=True),
        lax.all_gather(fc2_bias, "fsdp", axis=0, tiled=True),
    )
    wb_out = params_back[5]
    wb_fc1 = params_back[9]
    wb_fc2 = params_back[11]
    grad_out = cotangent[0]
    grad_c_fc2 = jnp.sum(grad_out.astype(f32), axis=0)
    grad_activ = jnp.einsum("td,fd->tf", grad_out, wb_fc2, preferred_element_type=f32)
    grad_pre = gelu_pull(grad_activ)[0].astype(bf16)
    grad_c_fc1 = jnp.sum(grad_pre.astype(f32), axis=0)
    grad_norm_mid = jnp.einsum("tf,df->td", grad_pre, wb_fc1, preferred_element_type=f32)
    grad_hid_part, grad_g_two, grad_b_two = ln2_pull(grad_norm_mid)
    grad_hidden = grad_out.astype(f32) + grad_hid_part
    grad_branch = grad_hidden.astype(bf16)
    grad_o_shift = jnp.sum(grad_branch.astype(f32), axis=0)
    grad_attn = jnp.einsum("te,de->td", grad_branch, wb_out, preferred_element_type=f32).astype(
        bf16
    )
    shards = lax.axis_size("fsdp")
    part = width // shards
    zeros = jnp.zeros((width,), f32)
    vectors = [zeros, zeros, zeros, zeros, grad_o_shift, grad_g_two, grad_b_two, grad_c_fc2]
    lines = [one.reshape(shards, 1, part) for one in vectors]
    lines.append(grad_c_fc1.reshape(shards, -1, part))
    lines.append(jnp.zeros((shards, 4, part), f32))
    t_qkv, t_out, t_fc1, t_fc2, vec, input_grad = block_back(
        doc_starts, grad_attn, (q_kept, kv_kept, out_kept), lse,
        (normed_in, attn, grad_branch, normed_mid, grad_pre, activ, grad_out),
        params_back[2], stream[0], grad_hidden, g_one[None], jnp.concatenate(lines, axis=1), length, 0,
    )
    return (
        layer_out, input_grad[None], vec[0], vec[1], t_qkv.astype(f32), vec[2], vec[3], t_out.astype(f32), vec[4], vec[5],
        vec[6], t_fc1.astype(f32), vec[8:12].reshape(-1), t_fc2.astype(f32), vec[7],
    )


def solution(mesh):
    in_specs = (
        P("fsdp", "ctx", None),
        P("fsdp", None),
        P("fsdp"),
        P("fsdp"),
        P("fsdp", None),
        P("fsdp"),
        P("fsdp"),
        P("fsdp", None),
        P("fsdp"),
        P("fsdp"),
        P("fsdp"),
        P("fsdp", None),
        P("fsdp"),
        P("fsdp", None),
        P("fsdp"),
        P("fsdp", "ctx", None),
    )
    out_specs = (
        P("fsdp", "ctx", None),
        P("fsdp", "ctx", None),
        P("fsdp"),
        P("fsdp"),
        P("fsdp", None),
        P("fsdp"),
        P("fsdp"),
        P("fsdp", None),
        P("fsdp"),
        P("fsdp"),
        P("fsdp"),
        P("fsdp", None),
        P("fsdp"),
        P("fsdp", None),
        P("fsdp"),
    )
    return jax.shard_map(
        per_device, mesh=mesh, in_specs=in_specs, out_specs=out_specs, check_vma=False
    )
```

```python
import functools

import jax
import jax.numpy as jnp
from jax import lax
from jax.experimental import pallas as pl
from jax.experimental.pallas import tpu as pltpu
from jax.sharding import PartitionSpec as P

H = 12
HD = 64
EPS = 1e-05
MESH = pl.DeviceIdType.MESH
BF = jnp.bfloat16
F32 = jnp.float32


INNER = 4
QW, KW = 256, 384
GW = QW + KW
NEG = -1e30


def nt(a, b):
    return lax.dot_general(a, b, (((1,), (1,)), ((), ())), preferred_element_type=F32)


def nn(a, b):
    return lax.dot_general(a, b, (((1,), (0,)), ((), ())), preferred_element_type=F32)


def head_lanes(x, head):
    if head == 2:
        return x
    lane = lax.broadcasted_iota(jnp.int32, x.shape, 1)
    keep = lane < HD if head == 0 else lane >= HD
    return jnp.where(keep, x, jnp.zeros_like(x))


def first_keys(starts_ref, pos):
    first = jnp.zeros_like(pos)
    for d in range(starts_ref.shape[1]):
        one = starts_ref[0, d]
        first = jnp.maximum(first, jnp.where(one <= pos, one, 0))
    return first


def places():
    c = lax.axis_index("ctx")
    f = lax.axis_index("fsdp")
    return c // INNER, c % INNER, f


def send(src, dst, ssem, rsem, peer):
    return pltpu.make_async_remote_copy(
        src_ref=src, dst_ref=dst, send_sem=ssem, recv_sem=rsem, device_id=peer, device_id_type=MESH
    )


def group_q(src, dst):
    dst_zero = jnp.zeros((dst.shape[0], HD), dst.dtype)
    for i in range(INNER):
        a, o = 3 * i * HD, i * GW
        dst[:, o:o + 3 * HD] = (src[:, a:a + 3 * HD].astype(F32) * (HD ** -0.5)).astype(dst.dtype)
        dst[:, o + 3 * HD:o + QW] = dst_zero


def group_kv(src, dst):
    width = H * HD
    for i in range(INNER):
        a, o = 3 * i * HD, i * GW
        dst[:, o + QW:o + QW + 2 * HD] = src[:, width + a:width + a + 2 * HD]
        dst[:, o + QW + 2 * HD:o + QW + 4 * HD] = src[:, 2 * width + a:2 * width + a + 2 * HD]
        dst[:, o + QW + 4 * HD:o + QW + 5 * HD] = src[:, width + a + 2 * HD:width + a + 3 * HD]
        dst[:, o + QW + 5 * HD:o + QW + 6 * HD] = src[:, 2 * width + a + 2 * HD:2 * width + a + 3 * HD]


def ungroup_qkv(src, dst):
    width = H * HD
    for i in range(INNER):
        a, o = 3 * i * HD, i * GW
        dst[:, a:a + 3 * HD] = src[:, o:o + 3 * HD]
        dst[:, width + a:width + a + 2 * HD] = src[:, o + QW:o + QW + 2 * HD]
        dst[:, 2 * width + a:2 * width + a + 2 * HD] = src[:, o + QW + 2 * HD:o + QW + 4 * HD]
        dst[:, width + a + 2 * HD:width + a + 3 * HD] = src[:, o + QW + 4 * HD:o + QW + 5 * HD]
        dst[:, 2 * width + a + 2 * HD:2 * width + a + 3 * HD] = src[:, o + QW + 5 * HD:o + QW + 6 * HD]


def group_rows(src, dst):
    dst_zero = jnp.zeros((dst.shape[0], HD), dst.dtype)
    for i in range(INNER):
        a, o = 3 * i * HD, i * QW
        dst[:, o:o + 2 * HD] = src[:, a:a + 2 * HD]
        dst[:, o + 2 * HD:o + 3 * HD] = dst_zero
        dst[:, o + 3 * HD:o + 4 * HD] = src[:, a + 2 * HD:a + 3 * HD]


def ungroup_rows(src, dst):
    for i in range(INNER):
        a, o = 3 * i * HD, i * QW
        dst[:, a:a + 2 * HD] = src[:, o:o + 2 * HD]
        dst[:, a + 2 * HD:a + 3 * HD] = src[:, o + 3 * HD:o + 4 * HD]


K_LANES = (0, 0, 256)
V_LANES = (128, 128, 256)
Q_LANES = (0, 0, 128)


def attend_kernel(depth, length, fs, starts_ref, tok_ref, v_shard, w_shard,
                  out_ref, normed_ref, vec_ref, c_one_ref, w_ref, qb_ref, kv_ref, ot_ref, lse_ref,
                  w_all, vbuf, raw_ref, x_ref, qb, kv, acc, top, tot, ob, land,
                  wl, ws, wr, vs, vr, lsem, as_kv, ar_kv, as_q, ar_q, zs, zr, bs, br, osem):
    z, h, f = places()
    c = lax.axis_index("ctx")
    width = H * HD
    part = width // fs
    blk = raw_ref.shape[0] // 2
    rows = INNER * blk
    half_rows = (pl.ds(0, blk), pl.ds(blk, blk))
    fpeers = [(c, lax.rem(f + k, fs)) for k in range(1, fs)]

    barrier = pltpu.get_barrier_semaphore()
    for j in range(1, INNER):
        pl.semaphore_signal(barrier, inc=1, device_id=(z * INNER + (h + j) % INNER, f), device_id_type=MESH)

    @pl.when(z > 0)
    def _():
        pl.semaphore_signal(barrier, inc=1, device_id=((z - 1) * INNER + h, f), device_id_type=MESH)

    @pl.when(z < depth - 1)
    def _():
        pl.semaphore_signal(barrier, inc=1, device_id=((z + 1) * INNER + h, f), device_id_type=MESH)

    for peer in fpeers:
        pl.semaphore_signal(barrier, inc=1, device_id=peer, device_id_type=MESH)

    def piece(half, i):
        p = i if half == 0 else INNER - 1 - i
        return pl.ds(pl.multiple_of(p * blk, blk), blk)

    own = (depth - 1, depth)
    my_rows = pl.ds(pl.multiple_of(f * part, 16), part)

    def w_lanes(b):
        return pl.ds(b * width, width)

    w_own = [pltpu.make_async_copy(w_shard.at[:, w_lanes(b)], w_all.at[my_rows, w_lanes(b)], wl.at[b]) for b in range(3)]
    for b in (1, 2, 0):
        w_own[b].start()
    vbuf[f] = v_shard[...]

    def w_send(k, b):
        return send(w_shard.at[:, w_lanes(b)], w_all.at[my_rows, w_lanes(b)], ws.at[k - 1, b], wr.at[k - 1, b], fpeers[k - 1])

    def v_send(k):
        return send(v_shard, vbuf.at[f], vs.at[k - 1], vr.at[k - 1], fpeers[k - 1])

    pl.semaphore_wait(barrier, INNER - 1 + fs - 1 + jnp.where(z > 0, 1, 0) + jnp.where(z < depth - 1, 1, 0))
    for k in range(1, fs):
        v_send(k).start()
        for b in (1, 2, 0):
            w_send(k, b).start()
    x = tok_ref[...].astype(F32)
    center = x - jnp.mean(x, axis=-1, keepdims=True)
    unit = center * lax.rsqrt(jnp.mean(center * center, axis=-1, keepdims=True) + EPS)
    for k in range(1, fs):
        v_send(k).wait_recv()
    for i in range(fs):
        vec_ref[:, i * part:(i + 1) * part] = vbuf[i, :8, :]
        for j in range(4):
            c_one_ref[:, (4 * i + j) * part:(4 * i + j + 1) * part] = vbuf[i, 8 + j:9 + j, :]
    normed_ref[...] = (unit * vec_ref[0:1, :] + vec_ref[1:2, :]).astype(BF)

    def project(b):
        w_own[b].wait()
        for k in range(1, fs):
            w_send(k, b).wait_recv()
        y = nn(normed_ref[...], w_all[:, b * width:(b + 1) * width])
        if b != 1:
            y = y + vec_ref[(2 if b == 0 else 3):(3 if b == 0 else 4), :]
        raw_ref[:, b * width:(b + 1) * width] = y.astype(BF)

    def a2a(j, half, kind):
        i = (h + j) % INNER
        lanes = pl.ds(pl.multiple_of(i * GW + (QW if kind else 0), 128), KW if kind else QW)
        dst = kv.at[own[half], piece(half, h)] if kind else qb.at[half, piece(half, h)]
        sems = (as_kv.at[half, j - 1], ar_kv.at[half, j - 1]) if kind else (as_q.at[half, j - 1], ar_q.at[half, j - 1])
        return send(x_ref.at[half_rows[half], lanes], dst, *sems, (z * INNER + i, f))

    def local(half, kind):
        lanes = pl.ds(pl.multiple_of(h * GW + (QW if kind else 0), 128), KW if kind else QW)
        dst = kv.at[own[half], piece(half, h)] if kind else qb.at[half, piece(half, h)]
        return pltpu.make_async_copy(x_ref.at[half_rows[half], lanes], dst, lsem.at[half, kind])

    def spread(kind):
        for half in range(2):
            for j in range(1, INNER):
                a2a(j, half, kind).start()
            local(half, kind).start()

    project(1)
    project(2)
    group_kv(raw_ref, x_ref)
    spread(1)
    project(0)
    group_q(raw_ref, x_ref)
    spread(0)
    w_out_copy = pltpu.make_async_copy(w_all, w_ref, osem.at[3])
    w_out_copy.start()

    def relay(half, src_slot, step, p):
        rws = pl.ds(pl.multiple_of(p * blk, blk), blk)
        if half == 0:
            peer, slot = (z + 1) * INNER + h, step - 1
        else:
            peer, slot = (z - 1) * INNER + h, z - 1 + step - 1
        return send(kv.at[src_slot, rws], kv.at[slot, rws], zs.at[half, step - 1, p], zr.at[half, step - 1, p], (peer, f))

    can = (z < depth - 1, z > 0)
    for j in range(INNER):
        i = (h + INNER - j) % INNER
        for half in range(2):
            if j == 0:
                local(half, 1).wait()
            else:
                a2a(j, half, 1).wait_recv()

            @pl.when(can[half])
            def _():
                relay(half, own[half], 1, i if half == 0 else INNER - 1 - i).start()

    for half in range(2):
        local(half, 0).wait()
        for j in range(1, INNER):
            a2a(j, half, 0).wait_recv()

    def base_of(half, zz):
        return zz * rows if half == 0 else length - (zz + 1) * rows

    cols = rows // 2

    def tile(half, slot, q_base, k_base, diag):
        for head in range(3):
            k_all = kv[slot, :, K_LANES[head]:K_LANES[head] + 128]
            v_all = kv[slot, :, V_LANES[head]:V_LANES[head] + 128]
            v_t = v_all.T[(0 if head == 0 else HD):(HD if head == 0 else 2 * HD)]
            for part in range(2):
                keys = (part + 1) * cols if diag else rows
                lanes = slice(part * cols, (part + 1) * cols)
                q = head_lanes(qb[half, lanes, Q_LANES[head]:Q_LANES[head] + 128], head)
                pos = q_base + part * cols + lax.broadcasted_iota(jnp.int32, (1, cols), 1)
                first = first_keys(starts_ref, pos) - k_base
                s = nt(k_all[:keys], q)
                row = lax.broadcasted_iota(jnp.int32, (keys, cols), 0)
                ok = row >= first
                if diag:
                    ok = ok & (row <= pos - k_base)
                s = jnp.where(ok, s, NEG)
                line = slice(head, head + 1)
                feats = slice(head * HD, (head + 1) * HD)
                high = jnp.max(s, axis=0, keepdims=True)
                if not diag:
                    before = top[half, line, lanes]
                    high = jnp.maximum(before, high)
                    fade = jnp.exp(before - high)
                w = jnp.exp(s - high)
                add = jnp.sum(w, axis=0, keepdims=True)
                o = nn(v_t[:, :keys], w.astype(BF))
                if diag:
                    tot[half, line, lanes] = add
                    acc[half, feats, lanes] = o
                else:
                    tot[half, line, lanes] = tot[half, line, lanes] * fade + add
                    acc[half, feats, lanes] = acc[half, feats, lanes] * fade + o
                top[half, line, lanes] = high

    @pl.loop(0, 2)
    def _(half):
        q_base = jnp.where(half == 0, base_of(0, z), base_of(1, z))
        tile(half, depth - 1 + half, q_base, q_base, True)

    @pl.loop(1, depth)
    def _(step):
        valid = (z - step >= 0, z + step <= depth - 1)
        slots = (step - 1, z + step - 1)
        for half in range(2):
            for p in range(INNER):
                @pl.when(valid[half])
                def _():
                    rws = pl.ds(p * blk, blk)
                    send(kv.at[slots[half], rws], kv.at[slots[half], rws], zs.at[half, step - 1, p],
                         zr.at[half, step - 1, p], (z * INNER + (h + 1) % INNER, f)).wait_recv()

                @pl.when(valid[half] & can[half])
                def _():
                    relay(half, slots[half], step + 1, p).start()

        @pl.loop(0, 2)
        def _(half):
            @pl.when(jnp.where(half == 0, z - step, depth - 1 - z - step) >= 0)
            def _():
                zz = jnp.where(half == 0, z - step, z + step)
                q_base = jnp.where(half == 0, base_of(0, z), base_of(1, z))
                k_base = jnp.where(half == 0, base_of(0, zz), base_of(1, zz))
                tile(half, jnp.where(half == 0, step - 1, z + step - 1), q_base, k_base, False)

    ob[:, :, 2 * HD:3 * HD] = jnp.zeros((2, rows, HD), BF)
    for half in range(2):
        lse_ref[half] = top[half] + jnp.log(tot[half])
        for head in range(3):
            feats = slice(head * HD, (head + 1) * HD)
            acc[half, feats, :] = acc[half, feats, :] / tot[half, head:head + 1, :]
        ob[half, :, :2 * HD] = acc[half, :2 * HD, :].T.astype(BF)
        ob[half, :, 3 * HD:] = acc[half, 2 * HD:, :].T.astype(BF)
    outs = [pltpu.make_async_copy(qb, qb_ref, osem.at[0]), pltpu.make_async_copy(kv, kv_ref, osem.at[1]),
            pltpu.make_async_copy(acc, ot_ref, osem.at[2])]
    for cp in outs:
        cp.start()

    def back(j, half):
        i = (h + j) % INNER
        return send(ob.at[half, piece(half, i)], land.at[half_rows[half], pl.ds(pl.multiple_of(h * QW, 128), QW)],
                    bs.at[half, j - 1], br.at[half, j - 1], (z * INNER + i, f))

    for half in range(2):
        for j in range(1, INNER):
            back(j, half).start()
        mine = pltpu.make_async_copy(ob.at[half, piece(half, h)],
                                     land.at[half_rows[half], pl.ds(pl.multiple_of(h * QW, 128), QW)], lsem.at[half, 0])
        mine.start()
        mine.wait()
    for half in range(2):
        for j in range(1, INNER):
            back(j, half).wait_recv()
    ungroup_rows(land, out_ref)
    for half in range(2):
        for j in range(1, INNER):
            a2a(j, half, 1).wait_send()
            a2a(j, half, 0).wait_send()
            back(j, half).wait_send()

        @pl.when(can[half])
        def _():
            for p in range(INNER):
                relay(half, own[half], 1, p).wait_send()

    @pl.loop(1, depth)
    def _(step):
        valid = (z - step >= 0, z + step <= depth - 1)
        for half in range(2):
            @pl.when(valid[half] & can[half])
            def _():
                for p in range(INNER):
                    relay(half, own[half], step + 1, p).wait_send()
    for k in range(1, fs):
        v_send(k).wait_send()
        for b in range(3):
            w_send(k, b).wait_send()
    for cp in outs + [w_out_copy]:
        cp.wait()


def attend(starts, x, v_shard, w_shard, length, cid):
    depth = lax.axis_size("ctx") // INNER
    fs = lax.axis_size("fsdp")
    blk = x.shape[0] // 2
    width = x.shape[1]
    rows = INNER * blk
    dma = pltpu.SemaphoreType.DMA
    shapes = (
        jax.ShapeDtypeStruct((x.shape[0], width), BF),
        jax.ShapeDtypeStruct((x.shape[0], width), BF),
        jax.ShapeDtypeStruct((8, width), F32),
        jax.ShapeDtypeStruct((1, 4 * width), F32),
        jax.ShapeDtypeStruct((width, 3 * width), BF),
        jax.ShapeDtypeStruct((2, rows, QW), BF),
        jax.ShapeDtypeStruct((depth + 1, rows, KW), BF),
        jax.ShapeDtypeStruct((2, 3 * HD, rows), F32),
        jax.ShapeDtypeStruct((2, 8, rows), F32),
    )
    vm = pl.BlockSpec(memory_space=pltpu.VMEM)
    anyspec = pl.BlockSpec(memory_space=pl.ANY)
    return pl.pallas_call(
        functools.partial(attend_kernel, depth, length, fs),
        out_shape=shapes,
        in_specs=[pl.BlockSpec(memory_space=pltpu.SMEM), vm, vm, anyspec],
        out_specs=(vm, vm, vm, vm, anyspec, anyspec, anyspec, anyspec, vm),
        scratch_shapes=[
            pltpu.VMEM((width, 3 * width), BF),
            pltpu.VMEM((fs,) + v_shard.shape, F32),
            pltpu.VMEM((2 * blk, 3 * width), BF),
            pltpu.VMEM((2 * blk, INNER * GW), BF),
            pltpu.VMEM((2, rows, QW), BF),
            pltpu.VMEM((depth + 1, rows, KW), BF),
            pltpu.VMEM((2, 3 * HD, rows), F32),
            pltpu.VMEM((2, 8, rows), F32),
            pltpu.VMEM((2, 8, rows), F32),
            pltpu.VMEM((2, rows, QW), BF),
            pltpu.VMEM((2 * blk, INNER * QW), BF),
            dma((3,)), dma((fs - 1, 3)), dma((fs - 1, 3)), dma((fs - 1,)), dma((fs - 1,)),
            dma((2, 2)), dma((2, 3)), dma((2, 3)), dma((2, 3)), dma((2, 3)),
            dma((2, depth, INNER)), dma((2, depth, INNER)), dma((2, 3)), dma((2, 3)), dma((4,)),
        ],
        compiler_params=pltpu.CompilerParams(collective_id=cid, has_side_effects=True, vmem_limit_bytes=48 << 20),
        name="attend",
    )(starts, x, v_shard, w_shard)


def ring_pos(z, bit, depth):
    return jnp.where(bit == 0, z, 2 * depth - 1 - z)


def ring_ctx(pos, depth, kind, fixed):
    pos = lax.rem(pos + 2 * depth, 2 * depth)
    z = jnp.where(pos < depth, pos, 2 * depth - 1 - pos)
    bit = jnp.where(pos < depth, 0, 1)
    return z * INNER + (bit * 2 + fixed if kind == 0 else fixed * 2 + bit)


def region_rows(used, n):
    return -(-used // (32 * n)) * 32 * n


def back_kernel(cfg, starts_ref, h_do, h_qb, h_kv, h_ot, h_lse, h_one, h_out, h_gout, h_mid, h_gpre, h_act, h_gtop,
                h_w, h_tok, h_hid, gain, v_ref,
                o_qkv, o_out, o_fc1, o_fc2, vout_ref, o_in,
                raw, qb, kv, ot, lse, x_one, x_out, g_out, x_mid, g_pre, x_act, g_top, wbuf, tokens, g_hid,
                do_ref, dob, dots, dq, dkvd, rbuf, dqb, fin, land, g_qkv,
                xt, gbuf, acc, fbuf, pa, pb, pa3, pb3, ra, rb, ra3, rb3,
                vall, vacc, vf, vx, vr,
                ldsem, lsem, as_o, ar_o, zs, zr, bq, brq, bk, brk,
                fsem, frec, ps, pr, rs, rr, xgs, xgr, vfs, vfr, vxs, vxr, vrs, vrr, osem):
    depth, length, n, fs, big, small_rows = cfg
    z, h, f = places()
    c = lax.axis_index("ctx")
    bits = (h % 2, h // 2)
    poss = (ring_pos(z, bits[1], depth), ring_pos(z, bits[0], depth))
    pairs_of = ((c + 1 - 2 * bits[0], f), (c + 2 - 4 * bits[1], f))
    rights = tuple((ring_ctx(poss[k] + 1, depth, k, bits[k]), f) for k in range(2))
    lefts = tuple((ring_ctx(poss[k] - 1, depth, k, bits[k]), f) for k in range(2))
    fpeers = [(c, lax.rem(f + k, fs)) for k in range(1, fs)]
    width = acc.shape[1]
    lanes = (pl.ds(0, width // 2), pl.ds(width // 2, width // 2))
    part = width // fs
    bases_of = (0, big, 2 * big, 2 * big + small_rows)
    outb = gbuf.at[0]
    slots = gbuf.shape[0]
    blk = raw.shape[0] // 2
    rows = INNER * blk
    cols = rows // 2
    half_rows = (pl.ds(0, blk), pl.ds(blk, blk))

    barrier = pltpu.get_barrier_semaphore()
    for j in range(1, INNER):
        pl.semaphore_signal(barrier, inc=1, device_id=(z * INNER + (h + j) % INNER, f), device_id_type=MESH)

    @pl.when(z > 0)
    def _():
        pl.semaphore_signal(barrier, inc=1, device_id=((z - 1) * INNER + h, f), device_id_type=MESH)

    @pl.when(z < depth - 1)
    def _():
        pl.semaphore_signal(barrier, inc=1, device_id=((z + 1) * INNER + h, f), device_id_type=MESH)

    for peer in list(rights) + list(lefts) + fpeers:
        pl.semaphore_signal(barrier, inc=1, device_id=peer, device_id_type=MESH)

    loads = {}
    pairs = (("do", h_do, raw), ("act", h_act, x_act), ("gtop", h_gtop, g_top), ("mid", h_mid, x_mid),
             ("gpre", h_gpre, g_pre), ("out", h_out, x_out), ("gout", h_gout, g_out), ("ot", h_ot, ot),
             ("kv", h_kv, kv), ("qb", h_qb, qb), ("lse", h_lse, lse), ("one", h_one, x_one), ("w", h_w, wbuf),
             ("tok", h_tok, tokens), ("hid", h_hid, g_hid))
    for i, (name, src, dst) in enumerate(pairs):
        loads[name] = pltpu.make_async_copy(src, dst, ldsem.at[i])
        loads[name].start()

    pend = []

    def go(cp):
        cp.start()
        pend.append(cp)
        return cp

    def piece(half, i):
        p = i if half == 0 else INNER - 1 - i
        return pl.ds(pl.multiple_of(p * blk, blk), blk)

    def spread(j, half):
        i = (h + j) % INNER
        return send(do_ref.at[half_rows[half], pl.ds(pl.multiple_of(i * QW, 128), QW)], dob.at[half, piece(half, h)],
                    as_o.at[half, j - 1], ar_o.at[half, j - 1], (z * INNER + i, f))

    loads["do"].wait()
    group_rows(raw, do_ref)
    pl.semaphore_wait(barrier, INNER - 1 + 4 + fs - 1 + jnp.where(z > 0, 1, 0) + jnp.where(z < depth - 1, 1, 0))
    mine = []
    for half in range(2):
        for j in range(1, INNER):
            go(spread(j, half))
        cp = pltpu.make_async_copy(do_ref.at[half_rows[half], pl.ds(pl.multiple_of(h * QW, 128), QW)],
                                   dob.at[half, piece(half, h)], lsem.at[half])
        cp.start()
        mine.append(cp)

    eye_n = 256
    eye = (lax.broadcasted_iota(jnp.int32, (eye_n, eye_n), 0)
           == lax.broadcasted_iota(jnp.int32, (eye_n, eye_n), 1)).astype(BF)
    offset = {"act": 0, "mid": 4 * width, "out": 5 * width, "one": 6 * width}

    def turn_over(name, ref):
        @pl.loop(0, ref.shape[1] // eye_n)
        def _(b):
            o = pl.multiple_of(b * eye_n, eye_n)
            xt[pl.ds(pl.multiple_of(offset[name] + o, eye_n), eye_n), :] = nt(eye, ref[:, pl.ds(o, eye_n)]).astype(BF)

    def unit(name, start, g, dst, row):
        lhs = xt[pl.ds(pl.multiple_of(offset[name] + start, 16), part), :]
        dst[pl.ds(pl.multiple_of(row, 16), part), :] = nn(lhs, g).astype(BF)

    def fc2_for(owner, dst):
        @pl.loop(0, 4)
        def _(j):
            unit("act", owner * 4 * part + j * part, g_top[...], dst, bases_of[1] + j * part)

    def fc1_for(owner, dst):
        @pl.loop(0, 4)
        def _(j):
            unit("mid", owner * part, g_pre[:, pl.ds(pl.multiple_of(j * width, 128), width)], dst, bases_of[0] + j * part)

    def out_q_for(owner, dst):
        unit("out", owner * part, g_out[...], dst, bases_of[2])
        unit("one", owner * part, g_qkv[:, :width], dst, bases_of[2] + part)

    def k_v_for(owner, dst):
        unit("one", owner * part, g_qkv[:, width:2 * width], dst, bases_of[3])
        unit("one", owner * part, g_qkv[:, 2 * width:], dst, bases_of[3] + part)

    cuts = ((bases_of[0], 4 * part, 0), (bases_of[1], 4 * part, 4 * part), (bases_of[2], 2 * part, 8 * part),
            (bases_of[3], 2 * part, 10 * part))

    def to_core(k, j):
        a, m, at = cuts[j]
        return remote(gbuf.at[(k - 1) % slots, pl.ds(a, m)], fbuf.at[k - 1, pl.ds(at, m)],
                      fsem.at[k - 1, j], frec.at[k - 1, j], fpeers[k - 1])

    def remote(src, dst, ssem, rsem, peer):
        return send(src, dst, ssem, rsem, peer)

    def share(j, make):
        for k in range(1, fs):
            if k - 1 >= slots:
                to_core(k - slots, j).wait_send()
            make(fpeers[k - 1][1], gbuf.at[(k - 1) % slots])
            to_core(k, j).start()

    def collect(j):
        for k in range(1, fs):
            if k > fs - 1 - slots:
                to_core(k, j).wait_send()
            to_core(k, j).wait_recv()
        a, m, at = cuts[j]
        step = 32

        @pl.loop(0, m // step)
        def _(i):
            rws = pl.ds(pl.multiple_of(a + i * step, step), step)
            tot = acc[rws, :].astype(F32)
            for k in range(fs - 1):
                tot = tot + fbuf[k, pl.ds(pl.multiple_of(at + i * step, step), step), :].astype(F32)
            acc[rws, :] = tot.astype(BF)

    for (a, m, _), size in zip(cuts, (big, big, small_rows, small_rows)):
        if size > m:
            acc[a + m:a + size, :] = jnp.zeros((size - m, width), BF)

    def stream(i, kind, pbuf, rbuf_):
        size = big if i < 2 else small_rows
        half = size // 2
        keep_at = pl.multiple_of(bases_of[i] + bits[kind] * half, 16)
        give_at = pl.multiple_of(bases_of[i] + (1 - bits[kind]) * half, 16)
        return (i, kind, keep_at, give_at, half, half // n, pbuf, rbuf_)

    sa, sb, sa3, sb3 = stream(0, 0, pa, ra), stream(1, 1, pb, rb), stream(2, 0, pa3, ra3), stream(3, 1, pb3, rb3)

    def rows_of(st, k, base=None):
        k = lax.rem(k + 2 * n, n)
        return pl.ds(pl.multiple_of((st[2] if base is None else base) + k * st[5], 16), st[5])

    def pair_copy(st):
        return remote(acc.at[pl.ds(st[3], st[4])], st[6], ps.at[st[0]], pr.at[st[0]], pairs_of[st[1]])

    def pair_add(st):
        pair_copy(st).wait_recv()
        step = 32 if st[4] % 32 == 0 else 16

        @pl.loop(0, st[4] // step)
        def _(i):
            rws = pl.ds(pl.multiple_of(st[2] + i * step, 16), step)
            acc[rws, :] = (acc[rws, :].astype(F32)
                           + st[6][pl.ds(pl.multiple_of(i * step, 16), step), :].astype(F32)).astype(BF)

    def rs_copy(st, s, d):
        p = poss[st[1]]
        k = p - 1 - s if d == 0 else p + 1 + s
        return remote(acc.at[rows_of(st, k), lanes[d]], st[7].at[s, :, lanes[d]],
                      rs.at[st[0], 0, d, s], rr.at[st[0], 0, d, s], (rights if d == 0 else lefts)[st[1]])

    def rs_start(st):
        for d in range(2):
            go(rs_copy(st, 0, d))

    def rs_step(st, s):
        p = poss[st[1]]
        for d in range(2):
            rws = rows_of(st, p - 2 - s if d == 0 else p + 2 + s)
            rs_copy(st, s, d).wait_recv()
            tot = (acc[rws, lanes[d]].astype(F32) + st[7][s, :, lanes[d]].astype(F32)).astype(BF)
            if s < n - 2:
                acc[rws, lanes[d]] = tot
                go(rs_copy(st, s + 1, d))
            elif d == 0:
                outb[rws, lanes[d]] = tot
            else:
                outb[rws, lanes[d]] = tot
                ag_start(st)

    def ag_copy(st, s, d):
        p = poss[st[1]]
        rws = rows_of(st, p - s if d == 0 else p + s)
        return remote(outb.at[rws, lanes[d]], outb.at[rws, lanes[d]],
                      rs.at[st[0], 1, d, s], rr.at[st[0], 1, d, s], (rights if d == 0 else lefts)[st[1]])

    def cross(st, s, d, base=None):
        p = poss[st[1]]
        rws = rows_of(st, p - s if d == 0 else p + s, base)
        return remote(outb.at[rws, lanes[d]], outb.at[rws, lanes[d]], xgs.at[st[0], d, s], xgr.at[st[0], d, s],
                      pairs_of[st[1]])

    def ag_start(st):
        for d in range(2):
            go(ag_copy(st, 0, d))
        for d in range(2):
            go(cross(st, 0, d))

    def ag_step(st, s):
        p = poss[st[1]]
        for d in range(2):
            rws = rows_of(st, p - 1 - s if d == 0 else p + 1 + s)
            remote(outb.at[rws, lanes[d]], outb.at[rws, lanes[d]],
                   rs.at[st[0], 1, d, s], rr.at[st[0], 1, d, s], pairs_of[0]).wait_recv()
            if s < n - 2:
                go(ag_copy(st, s + 1, d))
            go(cross(st, s + 1, d))

    def cross_wait(st):
        for s in range(n):
            for d in range(2):
                cross(st, s, d, st[3]).wait_recv()

    loads["act"].wait()
    turn_over("act", x_act)
    loads["gtop"].wait()
    share(1, fc2_for)
    loads["mid"].wait()
    turn_over("mid", x_mid)
    loads["gpre"].wait()
    share(0, fc1_for)
    fc2_for(f, acc)
    collect(1)
    go(pair_copy(sb))
    fc1_for(f, acc)
    collect(0)
    go(pair_copy(sa))

    dq[...] = jnp.zeros_like(dq)
    loads["ot"].wait()
    for half in range(2):
        mine[half].wait()
        for j in range(1, INNER):
            spread(j, half).wait_recv()
        for head in range(3):
            ln = slice(0, 128) if head < 2 else slice(128, 256)
            g = dob[half, :, ln].astype(F32).T[(0 if head == 0 else HD):(HD if head == 0 else 2 * HD)]
            dots[half, head:head + 1, :] = jnp.sum(g * ot[half, head * HD:(head + 1) * HD, :], axis=0, keepdims=True)
    for name in ("kv", "qb", "lse"):
        loads[name].wait()

    def base_of(half, zz):
        return zz * rows if half == 0 else length - (zz + 1) * rows

    def bases(half, zz):
        return jnp.where(half == 0, base_of(0, zz), base_of(1, zz))

    def tile(half, slot, q_base, k_base, diag, head):
        k_all = kv[slot, :, K_LANES[head]:K_LANES[head] + 128]
        v_all = kv[slot, :, V_LANES[head]:V_LANES[head] + 128]
        k_t = k_all.T[(HD if head == 1 else 0):(2 * HD if head == 1 else HD)]
        kl = slice(K_LANES[head], K_LANES[head] + 128)
        vl = slice(V_LANES[head], V_LANES[head] + 128)
        for half_cols in range(2):
            keys = (half_cols + 1) * cols if diag else rows
            ln = slice(half_cols * cols, (half_cols + 1) * cols)
            q = head_lanes(qb[half, ln, Q_LANES[head]:Q_LANES[head] + 128], head)
            g = head_lanes(dob[half, ln, Q_LANES[head]:Q_LANES[head] + 128], head)
            p = q_base + half_cols * cols + lax.broadcasted_iota(jnp.int32, (1, cols), 1)
            first = first_keys(starts_ref, p) - k_base
            s = nt(k_all[:keys], q)
            row = lax.broadcasted_iota(jnp.int32, (keys, cols), 0)
            ok = row >= first
            if diag:
                ok = ok & (row <= p - k_base)
            line = slice(head, head + 1)
            w = jnp.where(ok, jnp.exp(s - lse[half, line, ln]), 0.0)
            gp = nt(v_all[:keys], g)
            ds = (w * (gp - dots[half, line, ln])).astype(BF)
            dv = nn(w.astype(BF), g)
            dk = nn(ds, q)
            for sl, val in (((kl, dk + dv),) if head == 2 else ((kl, dk), (vl, dv))):
                if head != 1 and half_cols == 0:
                    dkvd[half, :keys, sl] = val
                elif head != 1 and diag:
                    dkvd[half, :cols, sl] = dkvd[half, :cols, sl] + val[:cols]
                    dkvd[half, cols:, sl] = val[cols:]
                else:
                    dkvd[half, :keys, sl] = dkvd[half, :keys, sl] + val
            feats = slice(head * HD, (head + 1) * HD)
            dq[half, feats, ln] = dq[half, feats, ln] + nn(k_t[:, :keys], ds)

    has = (z < depth - 1, z > 0)

    def pass_on(half, step):
        peer = (z - 1) * INNER + h if half == 0 else (z + 1) * INNER + h
        return send(rbuf.at[half, step], rbuf.at[half, step - 1], zs.at[half, step - 1], zr.at[half, step - 1], (peer, f))

    def take(half, step):
        return send(rbuf.at[half, step], rbuf.at[half, step], zs.at[half, step], zr.at[half, step],
                    (z * INNER + (h + 1) % INNER, f))

    @pl.loop(0, 2 * (depth - 1))
    def _(it):
        step = depth - 1 - it // 2
        half = it % 2
        valid = jnp.where(half == 0, z - step, depth - 1 - z - step) >= 0
        zz = jnp.where(half == 0, z - step, z + step)
        for head in range(3):
            @pl.when(valid)
            def _():
                tile(half, jnp.where(half == 0, step - 1, z + step - 1), bases(half, z), bases(half, zz), False, head)

        @pl.when(valid)
        def _():
            more = jnp.where(half == 0, depth - 1 - z, z) > 0

            @pl.when(more)
            def _():
                take(half, step).wait_recv()

                @pl.loop(0, rows // 64)
                def _(b):
                    rws = pl.ds(pl.multiple_of(b * 64, 64), 64)
                    rbuf[half, step, rws, :] = (dkvd[half, rws, :] + rbuf[half, step, rws, :].astype(F32)).astype(BF)

            @pl.when(jnp.logical_not(more))
            def _():
                rbuf[half, step] = dkvd[half].astype(BF)

            @pl.when(half == 0)
            def _():
                pass_on(0, step).start()

            @pl.when(half == 1)
            def _():
                pass_on(1, step).start()

    for st in (sb, sa):
        pair_add(st)
        rs_start(st)

    @pl.loop(0, 2)
    def _(half):
        for head in range(3):
            tile(half, depth - 1 + half, bases(half, z), bases(half, z), True, head)

    def back(j, half, kind):
        i = (h + j) % INNER
        ln = pl.ds(pl.multiple_of(h * GW + (QW if kind else 0), 128), KW if kind else QW)
        src = fin if kind else dqb
        sems = (bk.at[half, j - 1], brk.at[half, j - 1]) if kind else (bq.at[half, j - 1], brq.at[half, j - 1])
        return send(src.at[half, piece(half, i)], land.at[half_rows[half], ln], *sems, (z * INNER + i, f))

    def keep(half, kind):
        ln = pl.ds(pl.multiple_of(h * GW + (QW if kind else 0), 128), KW if kind else QW)
        src = fin if kind else dqb
        return pltpu.make_async_copy(src.at[half, piece(half, h)], land.at[half_rows[half], ln],
                                     lsem.at[2 + 2 * half + kind])

    dqb[:, :, 3 * HD:] = jnp.zeros((2, rows, HD), BF)
    for half in range(2):
        dqb[half, :, :2 * HD] = (dq[half, :2 * HD, :] * (HD ** -0.5)).T.astype(BF)
        dqb[half, :, 2 * HD:3 * HD] = (dq[half, 2 * HD:, :] * (HD ** -0.5)).T.astype(BF)
        for j in range(1, INNER):
            go(back(j, half, 0))
        keep(half, 0).start()
    rs_step(sb, 0)
    rs_step(sa, 0)
    for half in range(2):
        @pl.when(has[half])
        def _():
            take(half, 0).wait_recv()

            @pl.loop(0, rows // 64)
            def _(b):
                rws = pl.ds(pl.multiple_of(b * 64, 64), 64)
                fin[half, rws, :] = (dkvd[half, rws, :] + rbuf[half, 0, rws, :].astype(F32)).astype(BF)

        @pl.when(jnp.logical_not(has[half]))
        def _():
            fin[half] = dkvd[half].astype(BF)
        for j in range(1, INNER):
            go(back(j, half, 1))
        keep(half, 1).start()

    loads["out"].wait()
    turn_over("out", x_out)
    loads["gout"].wait()
    loads["one"].wait()
    turn_over("one", x_one)
    fc = []
    for s in range(1, n - 1):
        fc += [functools.partial(rs_step, sb, s), functools.partial(rs_step, sa, s)]
    for s in range(n - 1):
        fc += [functools.partial(ag_step, sb, s), functools.partial(ag_step, sa, s)]

    def some(count):
        for task in fc[:count]:
            task()
        del fc[:count]

    some(6)
    for half in range(2):
        for kind in range(2):
            keep(half, kind).wait()
            for j in range(1, INNER):
                back(j, half, kind).wait_recv()
    ungroup_qkv(land, g_qkv)
    share(2, out_q_for)
    share(3, k_v_for)
    out_q_for(f, acc)
    k_v_for(f, acc)

    def vec_copy(k):
        return remote(vall.at[fpeers[k - 1][1]], vf.at[k - 1], vfs.at[k - 1], vfr.at[k - 1], fpeers[k - 1])

    def norm_back():
        e = nt(g_qkv[...], wbuf[...])
        x = tokens[...].astype(F32)
        center = x - jnp.mean(x, axis=-1, keepdims=True)
        r = lax.rsqrt(jnp.mean(center * center, axis=-1, keepdims=True) + EPS)
        xh = center * r
        t = e * gain[0:1, :]
        o_in[...] = g_hid[...] + r * (t - jnp.mean(t, axis=-1, keepdims=True)
                                      - xh * jnp.mean(t * xh, axis=-1, keepdims=True))
        vall[...] = v_ref[...]
        gq = g_qkv[:, :width].astype(F32)
        gv = g_qkv[:, 2 * width:].astype(F32)
        for row, val in enumerate((e * xh, e, gq, gv)):
            line = jnp.sum(val, axis=0, keepdims=True)
            for i in range(fs):
                vall[i, row:row + 1, :] = line[:, i * part:(i + 1) * part]

    collect(2)
    go(pair_copy(sa3))
    collect(3)
    go(pair_copy(sb3))
    for name in ("w", "tok", "hid"):
        loads[name].wait()
    norm_back()
    for k in range(1, fs):
        go(vec_copy(k))

    def vec_pair():
        for k in range(1, fs):
            vec_copy(k).wait_recv()
        vtot = vall[f]
        for k in range(fs - 1):
            vtot = vtot + vf[k]
        vacc[...] = vtot
        go(remote(vacc, vx, vxs, vxr, pairs_of[0]))

    pos = poss[0]

    def vec_send(s):
        w = lax.rem(pos - s + n, n)
        go(remote(vr.at[w], vr.at[w], vrs.at[s], vrr.at[s], rights[0]))

    def vec_start():
        remote(vacc, vx, vxs, vxr, pairs_of[0]).wait_recv()
        vr[pos] = vacc[...] + vx[...]
        vec_send(0)

    def vec_ring(s):
        w = lax.rem(pos - 1 - s + n, n)
        remote(vr.at[w], vr.at[w], vrs.at[s], vrr.at[s], rights[0]).wait_recv()
        if s < n - 2:
            vec_send(s + 1)

    small = [vec_pair, vec_start] + [functools.partial(vec_ring, s) for s in range(n - 1)]
    some(4)

    def late_start():
        for st in (sa3, sb3):
            pair_add(st)
            rs_start(st)

    main = [late_start]
    for s in range(n - 1):
        main.append(lambda s=s: (rs_step(sa3, s), rs_step(sb3, s)))
    for s in range(n - 1):
        main.append(lambda s=s: (ag_step(sa3, s), ag_step(sb3, s)))
    outs = []

    def flush(u):
        if u < 4:
            src, dst = bases_of[0] + u * part, o_fc1.at[:, pl.ds(u * width, width)]
        elif u < 8:
            src, dst = bases_of[1] + (u - 4) * part, o_fc2.at[pl.ds((u - 4) * part, part)]
        elif u == 8:
            src, dst = bases_of[2], o_out
        else:
            src = bases_of[2] + part if u == 9 else bases_of[3] + (u - 10) * part
            dst = o_qkv.at[:, pl.ds((u - 9) * width, width)]
        cp = pltpu.make_async_copy(outb.at[pl.ds(src, part)], dst, osem.at[u])
        cp.start()
        outs.append(cp)

    def fc_done():
        for st in (sb, sa):
            cross_wait(st)
        for u in range(8):
            flush(u)

    fc.append(fc_done)
    for i in range(len(main)):
        main[i]()
        if i < len(small):
            small[i]()
        some(2)
    some(len(fc))
    for task in small[len(main):]:
        task()
    for st in (sa3, sb3):
        cross_wait(st)
    for u in range(8, 12):
        flush(u)
    vsum = vr[0]
    for k in range(1, n):
        vsum = vsum + vr[k]
    vout_ref[...] = vsum
    for cp in pend:
        cp.wait_send()

    @pl.loop(1, depth)
    def _(step):
        valid = (z - step >= 0, z + step <= depth - 1)
        for half in range(2):
            @pl.when(valid[half])
            def _():
                pass_on(half, step).wait_send()
    for cp in outs:
        cp.wait()


def block_back(starts, do, kept, lse, ops, w_one, tokens, g_hid, gain, v, length, cid):
    qb, kv, ot = kept
    fs = lax.axis_size("fsdp")
    depth = lax.axis_size("ctx") // INNER
    n = lax.axis_size("ctx") // 2
    toks, width = do.shape
    blk = toks // 2
    rows = INNER * blk
    part = width // fs
    big, few = region_rows(4 * part, n), region_rows(2 * part, n)
    tot = 2 * (big + few)
    slots = min(fs - 1, 2)
    vs = v.shape[1:]
    dma = pltpu.SemaphoreType.DMA
    vm = pl.BlockSpec(memory_space=pltpu.VMEM)
    anyspec = pl.BlockSpec(memory_space=pl.ANY)
    ins = (do, qb, kv, ot, lse) + tuple(ops) + (w_one, tokens, g_hid)
    order = [do, qb, kv, ot, lse] + list(ops) + [w_one, tokens, g_hid]
    cfg = (depth, length, n, fs, big, few)
    return pl.pallas_call(
        functools.partial(back_kernel, cfg),
        out_shape=(jax.ShapeDtypeStruct((part, 3 * width), BF), jax.ShapeDtypeStruct((part, width), BF),
                   jax.ShapeDtypeStruct((part, 4 * width), BF), jax.ShapeDtypeStruct((4 * part, width), BF),
                   jax.ShapeDtypeStruct(vs, F32), jax.ShapeDtypeStruct((toks, width), F32)),
        in_specs=[pl.BlockSpec(memory_space=pltpu.SMEM)] + [anyspec] * len(ins) + [vm, vm],
        out_specs=(anyspec, anyspec, anyspec, anyspec, vm, vm),
        scratch_shapes=[pltpu.VMEM(a.shape, a.dtype) for a in order] + [
            pltpu.VMEM((toks, INNER * QW), BF),
            pltpu.VMEM((2, rows, QW), BF),
            pltpu.VMEM((2, 8, rows), F32),
            pltpu.VMEM((2, 3 * HD, rows), F32),
            pltpu.VMEM((2, rows, KW), F32),
            pltpu.VMEM((2, depth, rows, KW), BF),
            pltpu.VMEM((2, rows, QW), BF),
            pltpu.VMEM((2, rows, KW), BF),
            pltpu.VMEM((toks, INNER * GW), BF),
            pltpu.VMEM((toks, 3 * width), BF),
            pltpu.VMEM((7 * width, toks), BF),
            pltpu.VMEM((slots, tot, width), BF),
            pltpu.VMEM((tot, width), BF),
            pltpu.VMEM((fs - 1, 12 * part, width), BF),
            pltpu.VMEM((big // 2, width), BF), pltpu.VMEM((big // 2, width), BF),
            pltpu.VMEM((few // 2, width), BF), pltpu.VMEM((few // 2, width), BF),
            pltpu.VMEM((n - 1, big // 2 // n, width), BF), pltpu.VMEM((n - 1, big // 2 // n, width), BF),
            pltpu.VMEM((n - 1, few // 2 // n, width), BF), pltpu.VMEM((n - 1, few // 2 // n, width), BF),
            pltpu.VMEM((fs,) + vs, F32),
            pltpu.VMEM(vs, F32),
            pltpu.VMEM((fs - 1,) + vs, F32),
            pltpu.VMEM(vs, F32),
            pltpu.VMEM((n,) + vs, F32),
            dma((15,)), dma((6,)), dma((2, 3)), dma((2, 3)), dma((2, depth)), dma((2, depth)),
            dma((2, 3)), dma((2, 3)), dma((2, 3)), dma((2, 3)),
            dma((fs - 1, 4)), dma((fs - 1, 4)), dma((4,)), dma((4,)),
            dma((4, 2, 2, n - 1)), dma((4, 2, 2, n - 1)), dma((4, 2, n)), dma((4, 2, n)),
            dma((fs - 1,)), dma((fs - 1,)), dma(()), dma(()), dma((n - 1,)), dma((n - 1,)), dma((12,)),
        ],
        compiler_params=pltpu.CompilerParams(collective_id=cid, has_side_effects=True, vmem_limit_bytes=62 << 20),
        name="block_back",
    )(starts, *ins, gain, v)


def middle_kernel(fs, attn, tok, cot, vec, c_one, w_out_h, w_one_h, w_two_h,
                  o_layer, o_mid, o_pre, o_act, o_hid, o_branch, o_attn, o_vec,
                  w_out, w_one, w_two, hidden, acc, e_acc, line, sem):
    width = attn.shape[1]
    part = width // fs
    first = pltpu.make_async_copy(w_out_h, w_out, sem.at[0])
    first.start()
    ones, twos = [], []
    for j in range(4):
        ones.append(pltpu.make_async_copy(w_one_h.at[:, pl.ds(j * width, width)], w_one.at[j], sem.at[1 + j]))
        twos.append(pltpu.make_async_copy(w_two_h.at[pl.ds(j * width, width)], w_two.at[j], sem.at[5 + j]))
        ones[j].start()
        twos[j].start()
    g = cot[...]
    first.wait()
    hid = tok[...].astype(F32) + nn(attn[...], w_out[...]) + vec[4:5, :]
    hidden[...] = hid
    center = hid - jnp.mean(hid, axis=-1, keepdims=True)
    r = lax.rsqrt(jnp.mean(center * center, axis=-1, keepdims=True) + EPS)
    o_mid[...] = (center * r * vec[5:6, :] + vec[6:7, :]).astype(BF)
    root = (2.0 / jnp.pi) ** 0.5
    for j in range(4):
        lanes = slice(j * width, (j + 1) * width)
        ones[j].wait()
        twos[j].wait()
        p = nn(o_mid[...], w_one[j]) + c_one[:, lanes]
        t = jnp.tanh(root * (p + 0.044715 * (p * p * p)))
        act = (0.5 * p * (1.0 + t)).astype(BF)
        slope = 0.5 * (1.0 + t) + 0.5 * p * (1.0 - t * t) * (root * (1.0 + 3 * 0.044715 * (p * p)))
        o_act[:, lanes] = act
        gp = (nt(g, w_two[j]) * slope).astype(BF)
        o_pre[:, lanes] = gp
        line[:, lanes] = jnp.sum(gp.astype(F32), axis=0, keepdims=True)
        add = nn(act, w_two[j])
        back = nt(gp, w_one[j])
        if j == 0:
            acc[...] = add
            e_acc[...] = back
        else:
            acc[...] = acc[...] + add
            e_acc[...] = e_acc[...] + back
    o_layer[...] = (hidden[...] + acc[...] + vec[7:8, :]).astype(BF)
    hid = hidden[...]
    center = hid - jnp.mean(hid, axis=-1, keepdims=True)
    r = lax.rsqrt(jnp.mean(center * center, axis=-1, keepdims=True) + EPS)
    xh = center * r
    e = e_acc[...]
    t = e * vec[5:6, :]
    gf = g.astype(F32)
    grad = gf + r * (t - jnp.mean(t, axis=-1, keepdims=True) - xh * jnp.mean(t * xh, axis=-1, keepdims=True))
    o_hid[...] = grad
    branch = grad.astype(BF)
    o_branch[...] = branch
    o_attn[...] = nt(branch, w_out[...]).astype(BF)
    o_vec[...] = jnp.zeros_like(o_vec)
    for row, val in ((4, branch.astype(F32)), (5, e * xh), (6, e), (7, gf)):
        total = jnp.sum(val, axis=0, keepdims=True)
        for i in range(fs):
            o_vec[i, row:row + 1, :] = total[:, i * part:(i + 1) * part]
    for i in range(fs):
        for j in range(4):
            o_vec[i, 8 + j:9 + j, :] = line[:, (4 * i + j) * part:(4 * i + j + 1) * part]


def middle(attn, tok, cot, vec, c_one, w_out, w_one, w_two):
    fs = lax.axis_size("fsdp")
    toks, width = tok.shape
    full = jax.ShapeDtypeStruct((toks, width), BF)
    wide = jax.ShapeDtypeStruct((toks, 4 * width), BF)
    vm = pl.BlockSpec(memory_space=pltpu.VMEM)
    anyspec = pl.BlockSpec(memory_space=pl.ANY)
    return pl.pallas_call(
        functools.partial(middle_kernel, fs),
        out_shape=(full, full, wide, wide, jax.ShapeDtypeStruct((toks, width), F32), full, full,
                   jax.ShapeDtypeStruct((fs, 16, width // fs), F32)),
        in_specs=[vm] * 5 + [anyspec] * 3,
        out_specs=(vm,) * 8,
        scratch_shapes=[
            pltpu.VMEM((width, width), BF),
            pltpu.VMEM((4, width, width), BF),
            pltpu.VMEM((4, width, width), BF),
            pltpu.VMEM((toks, width), F32),
            pltpu.VMEM((toks, width), F32),
            pltpu.VMEM((toks, width), F32),
            pltpu.VMEM((1, 4 * width), F32),
            pltpu.SemaphoreType.DMA((9,)),
        ],
        compiler_params=pltpu.CompilerParams(vmem_limit_bytes=48 << 20),
        name="middle",
    )(attn, tok, cot, vec, c_one, w_out, w_one, w_two)


def per_device(
    stream,
    doc_starts,
    ln1_gain,
    ln1_bias,
    qkv_weight,
    q_bias,
    v_bias,
    out_weight,
    out_bias,
    ln2_gain,
    ln2_bias,
    fc1_weight,
    fc1_bias,
    fc2_weight,
    fc2_bias,
    cotangent,
):
    length = lax.axis_size("ctx") * stream.shape[1]
    part = ln1_gain.shape[0]
    lines = [one.reshape(-1, part) for one in (ln1_gain, ln1_bias, q_bias, v_bias, out_bias, ln2_gain, ln2_bias, fc2_bias,
                                               fc1_bias)]
    v_shard = jnp.concatenate(lines + [jnp.zeros((4, part), BF)], axis=0).astype(F32)
    w_out = lax.all_gather(out_weight, "fsdp", axis=0, tiled=True)
    w_one = lax.all_gather(fc1_weight, "fsdp", axis=0, tiled=True)
    w_two = lax.all_gather(fc2_weight, "fsdp", axis=0, tiled=True)
    tokens, cot = stream[0], cotangent[0]
    attn, normed_in, vec, c_one, w_qkv, q_kept, kv_kept, out_kept, lse = attend(
        doc_starts, tokens, v_shard, qkv_weight, length, 1
    )
    layer_out, normed_mid, grad_pre, activ, grad_hidden, grad_branch, grad_attn, v_part = middle(
        attn, tokens, cot, vec, c_one, w_out, w_one, w_two
    )
    t_qkv, t_out, t_fc1, t_fc2, total, input_grad = block_back(
        doc_starts, grad_attn, (q_kept, kv_kept, out_kept), lse,
        (normed_in, attn, grad_branch, normed_mid, grad_pre, activ, cot),
        w_qkv, tokens, grad_hidden, vec, v_part, length, 0,
    )
    return (
        layer_out[None], input_grad[None], total[0], total[1], t_qkv.astype(F32), total[2], total[3], t_out.astype(F32),
        total[4], total[5], total[6], t_fc1.astype(F32), total[8:12].reshape(-1), t_fc2.astype(F32), total[7],
    )


def solution(mesh):
    in_specs = (
        P("fsdp", "ctx", None),
        P("fsdp", None),
        P("fsdp"),
        P("fsdp"),
        P("fsdp", None),
        P("fsdp"),
        P("fsdp"),
        P("fsdp", None),
        P("fsdp"),
        P("fsdp"),
        P("fsdp"),
        P("fsdp", None),
        P("fsdp"),
        P("fsdp", None),
        P("fsdp"),
        P("fsdp", "ctx", None),
    )
    out_specs = (
        P("fsdp", "ctx", None),
        P("fsdp", "ctx", None),
        P("fsdp"),
        P("fsdp"),
        P("fsdp", None),
        P("fsdp"),
        P("fsdp"),
        P("fsdp", None),
        P("fsdp"),
        P("fsdp"),
        P("fsdp"),
        P("fsdp", None),
        P("fsdp"),
        P("fsdp", None),
        P("fsdp"),
    )
    return jax.shard_map(
        per_device, mesh=mesh, in_specs=in_specs, out_specs=out_specs, check_vma=False
    )
```

```python
import functools

import jax
import jax.numpy as jnp
from jax import lax
from jax.experimental import pallas as pl
from jax.experimental.pallas import tpu as pltpu
from jax.sharding import PartitionSpec as P

H = 12
HD = 64
EPS = 1e-05
MESH = pl.DeviceIdType.MESH
BF = jnp.bfloat16
F32 = jnp.float32


INNER = 4
QW, KW = 256, 384
GW = QW + KW
NEG = -1e30


def nt(a, b):
    return lax.dot_general(a, b, (((1,), (1,)), ((), ())), preferred_element_type=F32)


def nn(a, b):
    return lax.dot_general(a, b, (((1,), (0,)), ((), ())), preferred_element_type=F32)


def head_lanes(x, head):
    if head == 2:
        return x
    lane = lax.broadcasted_iota(jnp.int32, x.shape, 1)
    keep = lane < HD if head == 0 else lane >= HD
    return jnp.where(keep, x, jnp.zeros_like(x))


def first_keys(starts_ref, pos):
    first = jnp.zeros_like(pos)
    for d in range(starts_ref.shape[1]):
        one = starts_ref[0, d]
        first = jnp.maximum(first, jnp.where(one <= pos, one, 0))
    return first


def places():
    c = lax.axis_index("ctx")
    f = lax.axis_index("fsdp")
    return c // INNER, c % INNER, f


def send(src, dst, ssem, rsem, peer):
    return pltpu.make_async_remote_copy(
        src_ref=src, dst_ref=dst, send_sem=ssem, recv_sem=rsem, device_id=peer, device_id_type=MESH
    )


def group_q(src, dst):
    dst_zero = jnp.zeros((dst.shape[0], HD), dst.dtype)
    for i in range(INNER):
        a, o = 3 * i * HD, i * GW
        dst[:, o:o + 3 * HD] = (src[:, a:a + 3 * HD].astype(F32) * (HD ** -0.5)).astype(dst.dtype)
        dst[:, o + 3 * HD:o + QW] = dst_zero


def group_kv(src, dst):
    width = H * HD
    for i in range(INNER):
        a, o = 3 * i * HD, i * GW
        dst[:, o + QW:o + QW + 2 * HD] = src[:, width + a:width + a + 2 * HD]
        dst[:, o + QW + 2 * HD:o + QW + 4 * HD] = src[:, 2 * width + a:2 * width + a + 2 * HD]
        dst[:, o + QW + 4 * HD:o + QW + 5 * HD] = src[:, width + a + 2 * HD:width + a + 3 * HD]
        dst[:, o + QW + 5 * HD:o + QW + 6 * HD] = src[:, 2 * width + a + 2 * HD:2 * width + a + 3 * HD]


def ungroup_qkv(src, dst):
    width = H * HD
    for i in range(INNER):
        a, o = 3 * i * HD, i * GW
        dst[:, a:a + 3 * HD] = src[:, o:o + 3 * HD]
        dst[:, width + a:width + a + 2 * HD] = src[:, o + QW:o + QW + 2 * HD]
        dst[:, 2 * width + a:2 * width + a + 2 * HD] = src[:, o + QW + 2 * HD:o + QW + 4 * HD]
        dst[:, width + a + 2 * HD:width + a + 3 * HD] = src[:, o + QW + 4 * HD:o + QW + 5 * HD]
        dst[:, 2 * width + a + 2 * HD:2 * width + a + 3 * HD] = src[:, o + QW + 5 * HD:o + QW + 6 * HD]


def ungroup_one(i, src, dst):
    width = H * HD
    a = 3 * i * HD
    dst[:, a:a + 3 * HD] = src[:, :3 * HD]
    dst[:, width + a:width + a + 2 * HD] = src[:, QW:QW + 2 * HD]
    dst[:, 2 * width + a:2 * width + a + 2 * HD] = src[:, QW + 2 * HD:QW + 4 * HD]
    dst[:, width + a + 2 * HD:width + a + 3 * HD] = src[:, QW + 4 * HD:QW + 5 * HD]
    dst[:, 2 * width + a + 2 * HD:2 * width + a + 3 * HD] = src[:, QW + 5 * HD:QW + 6 * HD]


def group_rows(src, dst):
    dst_zero = jnp.zeros((dst.shape[0], HD), dst.dtype)
    for i in range(INNER):
        a, o = 3 * i * HD, i * QW
        dst[:, o:o + 2 * HD] = src[:, a:a + 2 * HD]
        dst[:, o + 2 * HD:o + 3 * HD] = dst_zero
        dst[:, o + 3 * HD:o + 4 * HD] = src[:, a + 2 * HD:a + 3 * HD]


def ungroup_rows(src, dst):
    for i in range(INNER):
        a, o = 3 * i * HD, i * QW
        dst[:, a:a + 2 * HD] = src[:, o:o + 2 * HD]
        dst[:, a + 2 * HD:a + 3 * HD] = src[:, o + 3 * HD:o + 4 * HD]


K_LANES = (0, 0, 256)
V_LANES = (128, 128, 256)
Q_LANES = (0, 0, 128)


def attend_kernel(depth, length, fs, starts_ref, tok_ref, v_shard, w_shard,
                  out_ref, xg_ref, vec_ref, c_one_ref, w_ref, qb_ref, kv_ref, ot_ref, lse_ref,
                  normed_ref, xg, xgs, xgr, xgl, w_all, vbuf, raw_ref, x_ref, qb, kv, acc, top, tot, ob, land,
                  wl, ws, wr, vs, vr, lsem, as_kv, ar_kv, as_q, ar_q, zs, zr, bs, br, osem):
    z, h, f = places()
    c = lax.axis_index("ctx")
    width = H * HD
    part = width // fs
    blk = raw_ref.shape[0] // 2
    rows = INNER * blk
    half_rows = (pl.ds(0, blk), pl.ds(blk, blk))
    fpeers = [(c, lax.rem(f + k, fs)) for k in range(1, fs)]

    barrier = pltpu.get_barrier_semaphore()
    for j in range(1, INNER):
        pl.semaphore_signal(barrier, inc=1, device_id=(z * INNER + (h + j) % INNER, f), device_id_type=MESH)

    @pl.when(z > 0)
    def _():
        pl.semaphore_signal(barrier, inc=1, device_id=((z - 1) * INNER + h, f), device_id_type=MESH)

    @pl.when(z < depth - 1)
    def _():
        pl.semaphore_signal(barrier, inc=1, device_id=((z + 1) * INNER + h, f), device_id_type=MESH)

    for peer in fpeers:
        pl.semaphore_signal(barrier, inc=1, device_id=peer, device_id_type=MESH)

    def piece(half, i):
        p = i if half == 0 else INNER - 1 - i
        return pl.ds(pl.multiple_of(p * blk, blk), blk)

    own = (depth - 1, depth)
    my_rows = pl.ds(pl.multiple_of(f * part, 16), part)

    def w_lanes(b):
        return pl.ds(b * width, width)

    w_own = [pltpu.make_async_copy(w_shard.at[:, w_lanes(b)], w_all.at[my_rows, w_lanes(b)], wl.at[b]) for b in range(3)]
    for b in (1, 2, 0):
        w_own[b].start()
    vbuf[f] = v_shard[...]

    def w_send(k, b):
        return send(w_shard.at[:, w_lanes(b)], w_all.at[my_rows, w_lanes(b)], ws.at[k - 1, b], wr.at[k - 1, b], fpeers[k - 1])

    def v_send(k):
        return send(v_shard, vbuf.at[f], vs.at[k - 1], vr.at[k - 1], fpeers[k - 1])

    pl.semaphore_wait(barrier, INNER - 1 + fs - 1 + jnp.where(z > 0, 1, 0) + jnp.where(z < depth - 1, 1, 0))
    for k in range(1, fs):
        v_send(k).start()
        for b in (1, 2, 0):
            w_send(k, b).start()
    x = tok_ref[...].astype(F32)
    center = x - jnp.mean(x, axis=-1, keepdims=True)
    unit = center * lax.rsqrt(jnp.mean(center * center, axis=-1, keepdims=True) + EPS)
    for k in range(1, fs):
        v_send(k).wait_recv()
    for i in range(fs):
        vec_ref[:, i * part:(i + 1) * part] = vbuf[i, :8, :]
        for j in range(4):
            c_one_ref[:, (4 * i + j) * part:(4 * i + j + 1) * part] = vbuf[i, 8 + j:9 + j, :]
    normed_ref[...] = (unit * vec_ref[0:1, :] + vec_ref[1:2, :]).astype(BF)

    def project(b):
        w_own[b].wait()
        for k in range(1, fs):
            w_send(k, b).wait_recv()
        y = nn(normed_ref[...], w_all[:, b * width:(b + 1) * width])
        if b != 1:
            y = y + vec_ref[(2 if b == 0 else 3):(3 if b == 0 else 4), :]
        raw_ref[:, b * width:(b + 1) * width] = y.astype(BF)

    def a2a(j, half, kind):
        i = (h + j) % INNER
        lanes = pl.ds(pl.multiple_of(i * GW + (QW if kind else 0), 128), KW if kind else QW)
        dst = kv.at[own[half], piece(half, h)] if kind else qb.at[half, piece(half, h)]
        sems = (as_kv.at[half, j - 1], ar_kv.at[half, j - 1]) if kind else (as_q.at[half, j - 1], ar_q.at[half, j - 1])
        return send(x_ref.at[half_rows[half], lanes], dst, *sems, (z * INNER + i, f))

    def local(half, kind):
        lanes = pl.ds(pl.multiple_of(h * GW + (QW if kind else 0), 128), KW if kind else QW)
        dst = kv.at[own[half], piece(half, h)] if kind else qb.at[half, piece(half, h)]
        return pltpu.make_async_copy(x_ref.at[half_rows[half], lanes], dst, lsem.at[half, kind])

    def spread(kind):
        for half in range(2):
            for j in range(1, INNER):
                a2a(j, half, kind).start()
            local(half, kind).start()

    project(1)
    project(2)
    group_kv(raw_ref, x_ref)
    spread(1)
    project(0)
    group_q(raw_ref, x_ref)
    spread(0)
    w_out_copy = pltpu.make_async_copy(w_all, w_ref, osem.at[3])
    w_out_copy.start()

    def plane(j, half):
        return send(normed_ref.at[half_rows[half]], xg.at[half, piece(half, h)], xgs.at[half, j - 1], xgr.at[half, j - 1],
                    (z * INNER + (h + j) % INNER, f))

    def plane_own(half):
        return pltpu.make_async_copy(normed_ref.at[half_rows[half]], xg.at[half, piece(half, h)], xgl.at[half])

    for half in range(2):
        plane_own(half).start()

    def relay(half, src_slot, step, p):
        rws = pl.ds(pl.multiple_of(p * blk, blk), blk)
        if half == 0:
            peer, slot = (z + 1) * INNER + h, step - 1
        else:
            peer, slot = (z - 1) * INNER + h, z - 1 + step - 1
        return send(kv.at[src_slot, rws], kv.at[slot, rws], zs.at[half, step - 1, p], zr.at[half, step - 1, p], (peer, f))

    can = (z < depth - 1, z > 0)
    for j in range(INNER):
        i = (h + INNER - j) % INNER
        for half in range(2):
            if j == 0:
                local(half, 1).wait()
            else:
                a2a(j, half, 1).wait_recv()

            @pl.when(can[half])
            def _():
                relay(half, own[half], 1, i if half == 0 else INNER - 1 - i).start()

    for half in range(2):
        local(half, 0).wait()
        for j in range(1, INNER):
            a2a(j, half, 0).wait_recv()
    for half in range(2):
        for j in range(1, INNER):
            plane(j, half).start()

    def base_of(half, zz):
        return zz * rows if half == 0 else length - (zz + 1) * rows

    cols = rows // 2

    def tile(half, slot, q_base, k_base, diag):
        for head in range(3):
            k_all = kv[slot, :, K_LANES[head]:K_LANES[head] + 128]
            v_all = kv[slot, :, V_LANES[head]:V_LANES[head] + 128]
            v_t = v_all.T[(0 if head == 0 else HD):(HD if head == 0 else 2 * HD)]
            for part in range(2):
                keys = (part + 1) * cols if diag else rows
                lanes = slice(part * cols, (part + 1) * cols)
                q = head_lanes(qb[half, lanes, Q_LANES[head]:Q_LANES[head] + 128], head)
                pos = q_base + part * cols + lax.broadcasted_iota(jnp.int32, (1, cols), 1)
                first = first_keys(starts_ref, pos) - k_base
                s = nt(k_all[:keys], q)
                row = lax.broadcasted_iota(jnp.int32, (keys, cols), 0)
                ok = row >= first
                if diag:
                    ok = ok & (row <= pos - k_base)
                s = jnp.where(ok, s, NEG)
                line = slice(head, head + 1)
                feats = slice(head * HD, (head + 1) * HD)
                high = jnp.max(s, axis=0, keepdims=True)
                if not diag:
                    before = top[half, line, lanes]
                    high = jnp.maximum(before, high)
                    fade = jnp.exp(before - high)
                w = jnp.exp(s - high)
                add = jnp.sum(w, axis=0, keepdims=True)
                o = nn(v_t[:, :keys], w.astype(BF))
                if diag:
                    tot[half, line, lanes] = add
                    acc[half, feats, lanes] = o
                else:
                    tot[half, line, lanes] = tot[half, line, lanes] * fade + add
                    acc[half, feats, lanes] = acc[half, feats, lanes] * fade + o
                top[half, line, lanes] = high

    @pl.loop(0, 2)
    def _(half):
        q_base = jnp.where(half == 0, base_of(0, z), base_of(1, z))
        tile(half, depth - 1 + half, q_base, q_base, True)

    @pl.loop(1, depth)
    def _(step):
        valid = (z - step >= 0, z + step <= depth - 1)
        slots = (step - 1, z + step - 1)
        for half in range(2):
            for p in range(INNER):
                @pl.when(valid[half])
                def _():
                    rws = pl.ds(p * blk, blk)
                    send(kv.at[slots[half], rws], kv.at[slots[half], rws], zs.at[half, step - 1, p],
                         zr.at[half, step - 1, p], (z * INNER + (h + 1) % INNER, f)).wait_recv()

                @pl.when(valid[half] & can[half])
                def _():
                    relay(half, slots[half], step + 1, p).start()

        @pl.loop(0, 2)
        def _(half):
            @pl.when(jnp.where(half == 0, z - step, depth - 1 - z - step) >= 0)
            def _():
                zz = jnp.where(half == 0, z - step, z + step)
                q_base = jnp.where(half == 0, base_of(0, z), base_of(1, z))
                k_base = jnp.where(half == 0, base_of(0, zz), base_of(1, zz))
                tile(half, jnp.where(half == 0, step - 1, z + step - 1), q_base, k_base, False)

    for half in range(2):
        plane_own(half).wait()
        for j in range(1, INNER):
            plane(j, half).wait_recv()
    ob[:, :, 2 * HD:3 * HD] = jnp.zeros((2, rows, HD), BF)
    for half in range(2):
        lse_ref[half] = top[half] + jnp.log(tot[half])
        for head in range(3):
            feats = slice(head * HD, (head + 1) * HD)
            acc[half, feats, :] = acc[half, feats, :] / tot[half, head:head + 1, :]
        ob[half, :, :2 * HD] = acc[half, :2 * HD, :].T.astype(BF)
        ob[half, :, 3 * HD:] = acc[half, 2 * HD:, :].T.astype(BF)
    outs = [pltpu.make_async_copy(qb, qb_ref, osem.at[0]), pltpu.make_async_copy(kv, kv_ref, osem.at[1]),
            pltpu.make_async_copy(acc, ot_ref, osem.at[2]), pltpu.make_async_copy(xg, xg_ref, osem.at[4])]
    for cp in outs:
        cp.start()

    def back(j, half):
        i = (h + j) % INNER
        return send(ob.at[half, piece(half, i)], land.at[half_rows[half], pl.ds(pl.multiple_of(h * QW, 128), QW)],
                    bs.at[half, j - 1], br.at[half, j - 1], (z * INNER + i, f))

    for half in range(2):
        for j in range(1, INNER):
            back(j, half).start()
        mine = pltpu.make_async_copy(ob.at[half, piece(half, h)],
                                     land.at[half_rows[half], pl.ds(pl.multiple_of(h * QW, 128), QW)], lsem.at[half, 0])
        mine.start()
        mine.wait()
    for half in range(2):
        for j in range(1, INNER):
            back(j, half).wait_recv()
    ungroup_rows(land, out_ref)
    for half in range(2):
        for j in range(1, INNER):
            a2a(j, half, 1).wait_send()
            a2a(j, half, 0).wait_send()
            back(j, half).wait_send()
            plane(j, half).wait_send()

        @pl.when(can[half])
        def _():
            for p in range(INNER):
                relay(half, own[half], 1, p).wait_send()

    @pl.loop(1, depth)
    def _(step):
        valid = (z - step >= 0, z + step <= depth - 1)
        for half in range(2):
            @pl.when(valid[half] & can[half])
            def _():
                for p in range(INNER):
                    relay(half, own[half], step + 1, p).wait_send()
    for k in range(1, fs):
        v_send(k).wait_send()
        for b in range(3):
            w_send(k, b).wait_send()
    for cp in outs + [w_out_copy]:
        cp.wait()


def attend(starts, x, v_shard, w_shard, length, cid):
    depth = lax.axis_size("ctx") // INNER
    fs = lax.axis_size("fsdp")
    blk = x.shape[0] // 2
    width = x.shape[1]
    rows = INNER * blk
    dma = pltpu.SemaphoreType.DMA
    shapes = (
        jax.ShapeDtypeStruct((x.shape[0], width), BF),
        jax.ShapeDtypeStruct((2, rows, width), BF),
        jax.ShapeDtypeStruct((8, width), F32),
        jax.ShapeDtypeStruct((1, 4 * width), F32),
        jax.ShapeDtypeStruct((width, 3 * width), BF),
        jax.ShapeDtypeStruct((2, rows, QW), BF),
        jax.ShapeDtypeStruct((depth + 1, rows, KW), BF),
        jax.ShapeDtypeStruct((2, 3 * HD, rows), F32),
        jax.ShapeDtypeStruct((2, 8, rows), F32),
    )
    vm = pl.BlockSpec(memory_space=pltpu.VMEM)
    anyspec = pl.BlockSpec(memory_space=pl.ANY)
    return pl.pallas_call(
        functools.partial(attend_kernel, depth, length, fs),
        out_shape=shapes,
        in_specs=[pl.BlockSpec(memory_space=pltpu.SMEM), vm, vm, anyspec],
        out_specs=(vm, anyspec, vm, vm, anyspec, anyspec, anyspec, anyspec, vm),
        scratch_shapes=[
            pltpu.VMEM((x.shape[0], width), BF),
            pltpu.VMEM((2, rows, width), BF),
            dma((2, 3)), dma((2, 3)), dma((2,)),
            pltpu.VMEM((width, 3 * width), BF),
            pltpu.VMEM((fs,) + v_shard.shape, F32),
            pltpu.VMEM((2 * blk, 3 * width), BF),
            pltpu.VMEM((2 * blk, INNER * GW), BF),
            pltpu.VMEM((2, rows, QW), BF),
            pltpu.VMEM((depth + 1, rows, KW), BF),
            pltpu.VMEM((2, 3 * HD, rows), F32),
            pltpu.VMEM((2, 8, rows), F32),
            pltpu.VMEM((2, 8, rows), F32),
            pltpu.VMEM((2, rows, QW), BF),
            pltpu.VMEM((2 * blk, INNER * QW), BF),
            dma((3,)), dma((fs - 1, 3)), dma((fs - 1, 3)), dma((fs - 1,)), dma((fs - 1,)),
            dma((2, 2)), dma((2, 3)), dma((2, 3)), dma((2, 3)), dma((2, 3)),
            dma((2, depth, INNER)), dma((2, depth, INNER)), dma((2, 3)), dma((2, 3)), dma((5,)),
        ],
        compiler_params=pltpu.CompilerParams(collective_id=cid, has_side_effects=True, vmem_limit_bytes=62 << 20),
        name="attend",
    )(starts, x, v_shard, w_shard)


def ring_pos(z, bit, depth):
    return jnp.where(bit == 0, z, 2 * depth - 1 - z)


def ring_ctx(pos, depth, kind, fixed):
    pos = lax.rem(pos + 2 * depth, 2 * depth)
    z = jnp.where(pos < depth, pos, 2 * depth - 1 - pos)
    bit = jnp.where(pos < depth, 0, 1)
    return z * INNER + (bit * 2 + fixed if kind == 0 else fixed * 2 + bit)


def region_rows(used, n):
    return -(-used // (32 * n)) * 32 * n


def back_kernel(cfg, starts_ref, h_do, h_qb, h_kv, h_ot, h_lse, h_xg, h_out, h_gout, h_mid, h_gpre, h_act, h_gtop,
                h_w, h_tok, h_hid, gain, v_ref,
                o_qkv, o_out, o_fc1, o_fc2, vout_ref, o_in,
                raw, qb, kv, ot, lse, xg, x_out, g_out, x_mid, g_pre, x_act, g_top, wbuf, tokens, g_hid,
                do_ref, dob, dots, dq, dkvd, rbuf, dqb, fin, land, g_qkv,
                xt, xtg, gbuf, acc, fbuf, pa, pb, ra, rb, gl, accl, fl, zb, outl, stage,
                vall, vacc, vf, vx, vr,
                ldsem, lsem, as_o, ar_o, zs, zr, bq, brq, bk, brk,
                fsem, frec, ps, pr, rs, rr, xgs, xgr, lfs, lfr, lzs, lzr, las, lar, lps, lpr, vfs, vfr, vxs, vxr, vrs, vrr, osem):
    depth, length, n, fs, big, zrows = cfg
    z, h, f = places()
    c = lax.axis_index("ctx")
    bits = (h % 2, h // 2)
    poss = (ring_pos(z, bits[1], depth), ring_pos(z, bits[0], depth))
    pairs_of = ((c + 1 - 2 * bits[0], f), (c + 2 - 4 * bits[1], f))
    rights = tuple((ring_ctx(poss[k] + 1, depth, k, bits[k]), f) for k in range(2))
    lefts = tuple((ring_ctx(poss[k] - 1, depth, k, bits[k]), f) for k in range(2))
    fpeers = [(c, lax.rem(f + k, fs)) for k in range(1, fs)]
    width = acc.shape[1]
    lanes = (pl.ds(0, width // 2), pl.ds(width // 2, width // 2))
    part = width // fs
    bases_of = (0, big)
    outb = gbuf.at[0]
    slots = gbuf.shape[0]
    blk = raw.shape[0] // 2
    rows = INNER * blk
    cols = rows // 2
    half_rows = (pl.ds(0, blk), pl.ds(blk, blk))

    zpeers = [(lax.rem(z + k, depth) * INNER + h, f) for k in range(1, depth)]
    hpeers = [(z * INNER + (h + j) % INNER, f) for j in range(1, INNER)]
    barrier = pltpu.get_barrier_semaphore()
    for peer in hpeers + zpeers + list(rights) + list(lefts) + fpeers:
        pl.semaphore_signal(barrier, inc=1, device_id=peer, device_id_type=MESH)

    loads = {}
    pairs = (("do", h_do, raw), ("act", h_act, x_act), ("gtop", h_gtop, g_top), ("out", h_out, x_out),
             ("gout", h_gout, g_out), ("mid", h_mid, x_mid), ("gpre", h_gpre, g_pre), ("ot", h_ot, ot),
             ("kv", h_kv, kv), ("qb", h_qb, qb), ("lse", h_lse, lse), ("xg", h_xg, xg), ("w", h_w, wbuf),
             ("tok", h_tok, tokens), ("hid", h_hid, g_hid))
    for i, (name, src, dst) in enumerate(pairs):
        loads[name] = pltpu.make_async_copy(src, dst, ldsem.at[i])
        loads[name].start()

    pend = []

    def go(cp):
        cp.start()
        pend.append(cp)
        return cp

    def piece(half, i):
        p = i if half == 0 else INNER - 1 - i
        return pl.ds(pl.multiple_of(p * blk, blk), blk)

    def spread(j, half):
        i = (h + j) % INNER
        return send(do_ref.at[half_rows[half], pl.ds(pl.multiple_of(i * QW, 128), QW)], dob.at[half, piece(half, h)],
                    as_o.at[half, j - 1], ar_o.at[half, j - 1], (z * INNER + i, f))

    loads["do"].wait()
    group_rows(raw, do_ref)
    pl.semaphore_wait(barrier, INNER - 1 + depth - 1 + 4 + fs - 1)
    mine = []
    for half in range(2):
        for j in range(1, INNER):
            go(spread(j, half))
        cp = pltpu.make_async_copy(do_ref.at[half_rows[half], pl.ds(pl.multiple_of(h * QW, 128), QW)],
                                   dob.at[half, piece(half, h)], lsem.at[half])
        cp.start()
        mine.append(cp)

    eye_n = 256
    eye = (lax.broadcasted_iota(jnp.int32, (eye_n, eye_n), 0)
           == lax.broadcasted_iota(jnp.int32, (eye_n, eye_n), 1)).astype(BF)
    offset = {"act": 0, "mid": 4 * width, "out": 5 * width}

    def turn_over(name, ref):
        @pl.loop(0, ref.shape[1] // eye_n)
        def _(b):
            o = pl.multiple_of(b * eye_n, eye_n)
            xt[pl.ds(pl.multiple_of(offset[name] + o, eye_n), eye_n), :] = nt(eye, ref[:, pl.ds(o, eye_n)]).astype(BF)

    def unit(name, start, g, dst, row, size):
        lhs = xt[pl.ds(pl.multiple_of(offset[name] + start, 16), size), :]
        dst[pl.ds(pl.multiple_of(row, 16), size), :] = nn(lhs, g).astype(BF)

    half_part = part // 2

    def fc2_for(owner, dst):
        @pl.loop(0, 4)
        def _(j):
            unit("act", owner * 4 * part + j * part, g_top[...], dst, bases_of[1] + j * part, part)
        unit("out", owner * part + half_part, g_out[...], dst, bases_of[1] + 4 * part, half_part)

    def fc1_for(owner, dst):
        @pl.loop(0, 4)
        def _(j):
            unit("mid", owner * part, g_pre[:, pl.ds(pl.multiple_of(j * width, 128), width)], dst,
                 bases_of[0] + j * part, part)
        unit("out", owner * part, g_out[...], dst, bases_of[0] + 4 * part, half_part)

    used = 4 * part + half_part
    cuts = ((bases_of[0], used, 0), (bases_of[1], used, used))

    def to_core(k, j):
        a, m, at = cuts[j]
        return remote(gbuf.at[(k - 1) % slots, pl.ds(a, m)], fbuf.at[k - 1, pl.ds(at, m)],
                      fsem.at[k - 1, j], frec.at[k - 1, j], fpeers[k - 1])

    def remote(src, dst, ssem, rsem, peer):
        return send(src, dst, ssem, rsem, peer)

    def share(j, make):
        for k in range(1, fs):
            if k - 1 >= slots:
                to_core(k - slots, j).wait_send()
            make(fpeers[k - 1][1], gbuf.at[(k - 1) % slots])
            to_core(k, j).start()

    def collect(j):
        for k in range(1, fs):
            if k > fs - 1 - slots:
                to_core(k, j).wait_send()
            to_core(k, j).wait_recv()
        a, m, at = cuts[j]
        step = 32 if m % 32 == 0 else 16

        @pl.loop(0, m // step)
        def _(i):
            rws = pl.ds(pl.multiple_of(a + i * step, step), step)
            tot = acc[rws, :].astype(F32)
            for k in range(fs - 1):
                tot = tot + fbuf[k, pl.ds(pl.multiple_of(at + i * step, step), step), :].astype(F32)
            acc[rws, :] = tot.astype(BF)

    for (a, m, _), size in zip(cuts, (big, big)):
        if size > m:
            acc[a + m:a + size, :] = jnp.zeros((size - m, width), BF)

    def stream(i, kind, pbuf, rbuf_):
        half = big // 2
        keep_at = pl.multiple_of(bases_of[i] + bits[kind] * half, 16)
        give_at = pl.multiple_of(bases_of[i] + (1 - bits[kind]) * half, 16)
        return (i, kind, keep_at, give_at, half, half // n, pbuf, rbuf_)

    sa, sb = stream(0, 0, pa, ra), stream(1, 1, pb, rb)

    def rows_of(st, k, base=None):
        k = lax.rem(k + 2 * n, n)
        return pl.ds(pl.multiple_of((st[2] if base is None else base) + k * st[5], 16), st[5])

    def pair_copy(st):
        return remote(acc.at[pl.ds(st[3], st[4])], st[6], ps.at[st[0]], pr.at[st[0]], pairs_of[st[1]])

    def pair_add(st):
        pair_copy(st).wait_recv()
        step = 32 if st[4] % 32 == 0 else 16

        @pl.loop(0, st[4] // step)
        def _(i):
            rws = pl.ds(pl.multiple_of(st[2] + i * step, 16), step)
            acc[rws, :] = (acc[rws, :].astype(F32)
                           + st[6][pl.ds(pl.multiple_of(i * step, 16), step), :].astype(F32)).astype(BF)

    def rs_copy(st, s, d):
        p = poss[st[1]]
        k = p - 1 - s if d == 0 else p + 1 + s
        return remote(acc.at[rows_of(st, k), lanes[d]], st[7].at[s, :, lanes[d]],
                      rs.at[st[0], 0, d, s], rr.at[st[0], 0, d, s], (rights if d == 0 else lefts)[st[1]])

    def rs_start(st):
        for d in range(2):
            go(rs_copy(st, 0, d))

    def rs_step(st, s):
        p = poss[st[1]]
        for d in range(2):
            rws = rows_of(st, p - 2 - s if d == 0 else p + 2 + s)
            rs_copy(st, s, d).wait_recv()
            tot = (acc[rws, lanes[d]].astype(F32) + st[7][s, :, lanes[d]].astype(F32)).astype(BF)
            if s < n - 2:
                acc[rws, lanes[d]] = tot
                go(rs_copy(st, s + 1, d))
            elif d == 0:
                outb[rws, lanes[d]] = tot
            else:
                outb[rws, lanes[d]] = tot
                ag_start(st)

    def ag_copy(st, s, d):
        p = poss[st[1]]
        rws = rows_of(st, p - s if d == 0 else p + s)
        return remote(outb.at[rws, lanes[d]], outb.at[rws, lanes[d]],
                      rs.at[st[0], 1, d, s], rr.at[st[0], 1, d, s], (rights if d == 0 else lefts)[st[1]])

    def cross(st, s, d, base=None):
        p = poss[st[1]]
        rws = rows_of(st, p - s if d == 0 else p + s, base)
        return remote(outb.at[rws, lanes[d]], outb.at[rws, lanes[d]], xgs.at[st[0], d, s], xgr.at[st[0], d, s],
                      pairs_of[st[1]])

    def ag_start(st):
        for d in range(2):
            go(ag_copy(st, 0, d))
        for d in range(2):
            go(cross(st, 0, d))

    def ag_step(st, s):
        p = poss[st[1]]
        for d in range(2):
            rws = rows_of(st, p - 1 - s if d == 0 else p + 1 + s)
            remote(outb.at[rws, lanes[d]], outb.at[rws, lanes[d]],
                   rs.at[st[0], 1, d, s], rr.at[st[0], 1, d, s], pairs_of[0]).wait_recv()
            if s < n - 2:
                go(ag_copy(st, s + 1, d))
            go(cross(st, s + 1, d))

    def cross_wait(st):
        for s in range(n):
            for d in range(2):
                cross(st, s, d, st[3]).wait_recv()

    loads["act"].wait()
    turn_over("act", x_act)
    loads["gtop"].wait()
    loads["out"].wait()
    turn_over("out", x_out)
    loads["gout"].wait()
    share(1, fc2_for)
    loads["mid"].wait()
    turn_over("mid", x_mid)
    loads["gpre"].wait()
    share(0, fc1_for)
    fc2_for(f, acc)
    collect(1)
    go(pair_copy(sb))
    fc1_for(f, acc)
    collect(0)
    go(pair_copy(sa))

    dq[...] = jnp.zeros_like(dq)
    loads["ot"].wait()
    for half in range(2):
        mine[half].wait()
        for j in range(1, INNER):
            spread(j, half).wait_recv()
        for head in range(3):
            ln = slice(0, 128) if head < 2 else slice(128, 256)
            g = dob[half, :, ln].astype(F32).T[(0 if head == 0 else HD):(HD if head == 0 else 2 * HD)]
            dots[half, head:head + 1, :] = jnp.sum(g * ot[half, head * HD:(head + 1) * HD, :], axis=0, keepdims=True)
    for name in ("kv", "qb", "lse"):
        loads[name].wait()

    def base_of(half, zz):
        return zz * rows if half == 0 else length - (zz + 1) * rows

    def bases(half, zz):
        return jnp.where(half == 0, base_of(0, zz), base_of(1, zz))

    def tile(half, slot, q_base, k_base, diag, head):
        k_all = kv[slot, :, K_LANES[head]:K_LANES[head] + 128]
        v_all = kv[slot, :, V_LANES[head]:V_LANES[head] + 128]
        k_t = k_all.T[(HD if head == 1 else 0):(2 * HD if head == 1 else HD)]
        kl = slice(K_LANES[head], K_LANES[head] + 128)
        vl = slice(V_LANES[head], V_LANES[head] + 128)
        for half_cols in range(2):
            keys = (half_cols + 1) * cols if diag else rows
            ln = slice(half_cols * cols, (half_cols + 1) * cols)
            q = head_lanes(qb[half, ln, Q_LANES[head]:Q_LANES[head] + 128], head)
            g = head_lanes(dob[half, ln, Q_LANES[head]:Q_LANES[head] + 128], head)
            p = q_base + half_cols * cols + lax.broadcasted_iota(jnp.int32, (1, cols), 1)
            first = first_keys(starts_ref, p) - k_base
            s = nt(k_all[:keys], q)
            row = lax.broadcasted_iota(jnp.int32, (keys, cols), 0)
            ok = row >= first
            if diag:
                ok = ok & (row <= p - k_base)
            line = slice(head, head + 1)
            w = jnp.where(ok, jnp.exp(s - lse[half, line, ln]), 0.0)
            gp = nt(v_all[:keys], g)
            ds = (w * (gp - dots[half, line, ln])).astype(BF)
            dv = nn(w.astype(BF), g)
            dk = nn(ds, q)
            for sl, val in (((kl, dk + dv),) if head == 2 else ((kl, dk), (vl, dv))):
                if head != 1 and half_cols == 0:
                    dkvd[half, :keys, sl] = val
                elif head != 1 and diag:
                    dkvd[half, :cols, sl] = dkvd[half, :cols, sl] + val[:cols]
                    dkvd[half, cols:, sl] = val[cols:]
                else:
                    dkvd[half, :keys, sl] = dkvd[half, :keys, sl] + val
            feats = slice(head * HD, (head + 1) * HD)
            dq[half, feats, ln] = dq[half, feats, ln] + nn(k_t[:, :keys], ds)

    has = (z < depth - 1, z > 0)

    def pass_on(half, step):
        peer = (z - 1) * INNER + h if half == 0 else (z + 1) * INNER + h
        return send(rbuf.at[half, step], rbuf.at[half, step - 1], zs.at[half, step - 1], zr.at[half, step - 1], (peer, f))

    def take(half, step):
        return send(rbuf.at[half, step], rbuf.at[half, step], zs.at[half, step], zr.at[half, step],
                    (z * INNER + (h + 1) % INNER, f))

    @pl.loop(0, 2 * (depth - 1))
    def _(it):
        step = depth - 1 - it // 2
        half = it % 2
        valid = jnp.where(half == 0, z - step, depth - 1 - z - step) >= 0
        zz = jnp.where(half == 0, z - step, z + step)
        for head in range(3):
            @pl.when(valid)
            def _():
                tile(half, jnp.where(half == 0, step - 1, z + step - 1), bases(half, z), bases(half, zz), False, head)

        @pl.when(valid)
        def _():
            more = jnp.where(half == 0, depth - 1 - z, z) > 0

            @pl.when(more)
            def _():
                take(half, step).wait_recv()

                @pl.loop(0, rows // 64)
                def _(b):
                    rws = pl.ds(pl.multiple_of(b * 64, 64), 64)
                    rbuf[half, step, rws, :] = (dkvd[half, rws, :] + rbuf[half, step, rws, :].astype(F32)).astype(BF)

            @pl.when(jnp.logical_not(more))
            def _():
                rbuf[half, step] = dkvd[half].astype(BF)

            @pl.when(half == 0)
            def _():
                pass_on(0, step).start()

            @pl.when(half == 1)
            def _():
                pass_on(1, step).start()

    for st in (sb, sa):
        pair_add(st)
        rs_start(st)

    @pl.loop(0, 2)
    def _(half):
        for head in range(3):
            tile(half, depth - 1 + half, bases(half, z), bases(half, z), True, head)

    def back(j, half, kind):
        i = (h + j) % INNER
        ln = pl.ds(pl.multiple_of(h * GW + (QW if kind else 0), 128), KW if kind else QW)
        src = fin if kind else dqb
        sems = (bk.at[half, j - 1], brk.at[half, j - 1]) if kind else (bq.at[half, j - 1], brq.at[half, j - 1])
        return send(src.at[half, piece(half, i)], land.at[half_rows[half], ln], *sems, (z * INNER + i, f))

    def keep(half, kind):
        ln = pl.ds(pl.multiple_of(h * GW + (QW if kind else 0), 128), KW if kind else QW)
        src = fin if kind else dqb
        return pltpu.make_async_copy(src.at[half, piece(half, h)], land.at[half_rows[half], ln],
                                     lsem.at[2 + 2 * half + kind])

    dqb[:, :, 3 * HD:] = jnp.zeros((2, rows, HD), BF)
    for half in range(2):
        dqb[half, :, :2 * HD] = (dq[half, :2 * HD, :] * (HD ** -0.5)).T.astype(BF)
        dqb[half, :, 2 * HD:3 * HD] = (dq[half, 2 * HD:, :] * (HD ** -0.5)).T.astype(BF)
        for j in range(1, INNER):
            go(back(j, half, 0))
        keep(half, 0).start()
    rs_step(sb, 0)
    rs_step(sa, 0)
    def late_core(k):
        return remote(gl.at[(k - 1) % slots], fl.at[k - 1], lfs.at[k - 1], lfr.at[k - 1], fpeers[k - 1])

    def late_grad(owner, dst):
        for lo, hi, src in ((0, QW, dqb), (QW, GW, fin)):
            tot = None
            for half in range(2):
                one = nn(xtg[pl.ds(pl.multiple_of(owner * part, 16), part), half * rows:(half + 1) * rows], src[half])
                tot = one if tot is None else tot + one
            dst[:part, lo:hi] = tot.astype(BF)

    loads["xg"].wait()
    for half in range(2):
        for r in range(rows // eye_n):
            @pl.loop(0, width // eye_n)
            def _(b):
                o = pl.multiple_of(b * eye_n, eye_n)
                xtg[pl.ds(o, eye_n), half * rows + r * eye_n:half * rows + (r + 1) * eye_n] = nt(
                    eye, xg[half, r * eye_n:(r + 1) * eye_n, pl.ds(o, eye_n)]).astype(BF)
    for half in range(2):
        @pl.when(has[half])
        def _():
            take(half, 0).wait_recv()

            @pl.loop(0, rows // 64)
            def _(b):
                rws = pl.ds(pl.multiple_of(b * 64, 64), 64)
                fin[half, rws, :] = (dkvd[half, rws, :] + rbuf[half, 0, rws, :].astype(F32)).astype(BF)

        @pl.when(jnp.logical_not(has[half]))
        def _():
            fin[half] = dkvd[half].astype(BF)
    for k in range(1, fs):
        if k - 1 >= slots:
            late_core(k - slots).wait_send()
        late_grad(fpeers[k - 1][1], gl.at[(k - 1) % slots])
        late_core(k).start()
    for half in range(2):
        for j in range(1, INNER):
            go(back(j, half, 1))
        keep(half, 1).start()
    late_grad(f, accl)
    zchunk = zrows // depth
    if zrows > part:
        accl[part:, :] = jnp.zeros((zrows - part, GW), BF)

    def chunk_of(k):
        return pl.ds(pl.multiple_of(k * zchunk, 16), zchunk)

    def late_scatter(k):
        to = lax.rem(z + k, depth)
        return remote(accl.at[chunk_of(to)], zb.at[z], lzs.at[k - 1], lzr.at[k - 1], zpeers[k - 1])

    def late_reduce():
        for k in range(1, fs):
            if k > fs - 1 - slots:
                late_core(k).wait_send()
            late_core(k).wait_recv()
        tot = accl[:part, :].astype(F32)
        for k in range(fs - 1):
            tot = tot + fl[k, :part, :].astype(F32)
        accl[:part, :] = tot.astype(BF)
        for k in range(1, depth):
            late_scatter(k).start()

    def late_gather(k):
        return remote(outl.at[h, chunk_of(z)], outl.at[h, chunk_of(z)], las.at[k - 1], lar.at[k - 1], zpeers[k - 1])

    def late_plane(j, k):
        rws = chunk_of(lax.rem(z - k + depth, depth))
        return remote(outl.at[h, rws], outl.at[h, rws], lps.at[j - 1, k], lpr.at[j - 1, k], hpeers[j - 1])

    def late_sum():
        tot = accl[chunk_of(z), :].astype(F32)
        for k in range(1, depth):
            late_scatter(k).wait_recv()
            tot = tot + zb[lax.rem(z - k + depth, depth)].astype(F32)
        outl[h, chunk_of(z), :] = tot.astype(BF)
        for k in range(1, depth):
            go(late_gather(k))
        for j in range(1, INNER):
            go(late_plane(j, 0))

    def late_forward(k):
        rws = chunk_of(lax.rem(z - k + depth, depth))
        remote(outl.at[h, rws], outl.at[h, rws], las.at[k - 1], lar.at[k - 1], zpeers[k - 1]).wait_recv()
        for j in range(1, INNER):
            go(late_plane(j, k))

    def late_end():
        for j in range(1, INNER):
            i = (h + INNER - j) % INNER
            for k in range(depth):
                rws = chunk_of(lax.rem(z - k + depth, depth))
                remote(outl.at[i, rws], outl.at[i, rws], lps.at[j - 1, k], lpr.at[j - 1, k], hpeers[0]).wait_recv()
        for k in range(1, depth):
            late_scatter(k).wait_send()
        for i in range(INNER):
            ungroup_one(i, outl.at[i, pl.ds(0, part)], stage)
        cp = pltpu.make_async_copy(stage, o_qkv, osem.at[10])
        cp.start()
        outs.append(cp)

    fc = []
    for s in range(1, n - 1):
        fc += [functools.partial(rs_step, sb, s), functools.partial(rs_step, sa, s)]
    for s in range(n - 1):
        fc += [functools.partial(ag_step, sb, s), functools.partial(ag_step, sa, s)]

    def some(count):
        for task in fc[:count]:
            task()
        del fc[:count]

    some(2)
    late_reduce()
    some(4)
    late_sum()
    for half in range(2):
        for kind in range(2):
            keep(half, kind).wait()
            for j in range(1, INNER):
                back(j, half, kind).wait_recv()
    ungroup_qkv(land, g_qkv)

    def vec_copy(k):
        return remote(vall.at[fpeers[k - 1][1]], vf.at[k - 1], vfs.at[k - 1], vfr.at[k - 1], fpeers[k - 1])

    def norm_back():
        e = nt(g_qkv[...], wbuf[...])
        x = tokens[...].astype(F32)
        center = x - jnp.mean(x, axis=-1, keepdims=True)
        r = lax.rsqrt(jnp.mean(center * center, axis=-1, keepdims=True) + EPS)
        xh = center * r
        t = e * gain[0:1, :]
        o_in[...] = g_hid[...] + r * (t - jnp.mean(t, axis=-1, keepdims=True)
                                      - xh * jnp.mean(t * xh, axis=-1, keepdims=True))
        vall[...] = v_ref[...]
        gq = g_qkv[:, :width].astype(F32)
        gv = g_qkv[:, 2 * width:].astype(F32)
        for row, val in enumerate((e * xh, e, gq, gv)):
            line = jnp.sum(val, axis=0, keepdims=True)
            for i in range(fs):
                vall[i, row:row + 1, :] = line[:, i * part:(i + 1) * part]

    for name in ("w", "tok", "hid"):
        loads[name].wait()
    norm_back()
    for k in range(1, fs):
        go(vec_copy(k))

    def vec_pair():
        for k in range(1, fs):
            vec_copy(k).wait_recv()
        vtot = vall[f]
        for k in range(fs - 1):
            vtot = vtot + vf[k]
        vacc[...] = vtot
        go(remote(vacc, vx, vxs, vxr, pairs_of[0]))

    pos = poss[0]

    def vec_send(s):
        w = lax.rem(pos - s + n, n)
        go(remote(vr.at[w], vr.at[w], vrs.at[s], vrr.at[s], rights[0]))

    def vec_start():
        remote(vacc, vx, vxs, vxr, pairs_of[0]).wait_recv()
        vr[pos] = vacc[...] + vx[...]
        vec_send(0)

    def vec_ring(s):
        w = lax.rem(pos - 1 - s + n, n)
        remote(vr.at[w], vr.at[w], vrs.at[s], vrr.at[s], rights[0]).wait_recv()
        if s < n - 2:
            vec_send(s + 1)

    small = [vec_pair, vec_start] + [functools.partial(vec_ring, s) for s in range(n - 1)]
    outs = []

    def flush(src, size, dst, u):
        cp = pltpu.make_async_copy(outb.at[pl.ds(src, size)], dst, osem.at[u])
        cp.start()
        outs.append(cp)

    late = [functools.partial(late_forward, k) for k in range(1, depth)]
    i = 0
    while fc or late or small:
        some(2)
        if late:
            late.pop(0)()
        if small:
            small.pop(0)()
    late_end()
    for st in (sb, sa):
        cross_wait(st)
    for u in range(4):
        flush(bases_of[0] + u * part, part, o_fc1.at[:, pl.ds(u * width, width)], u)
        flush(bases_of[1] + u * part, part, o_fc2.at[pl.ds(u * part, part)], 4 + u)
    for i in range(2):
        flush(bases_of[i] + 4 * part, half_part, o_out.at[pl.ds(i * half_part, half_part)], 8 + i)
    vsum = vr[0]
    for k in range(1, n):
        vsum = vsum + vr[k]
    vout_ref[...] = vsum
    for cp in pend:
        cp.wait_send()

    @pl.loop(1, depth)
    def _(step):
        valid = (z - step >= 0, z + step <= depth - 1)
        for half in range(2):
            @pl.when(valid[half])
            def _():
                pass_on(half, step).wait_send()
    for cp in outs:
        cp.wait()


def block_back(starts, do, kept, lse, ops, w_one, tokens, g_hid, gain, v, length, cid):
    qb, kv, ot = kept
    fs = lax.axis_size("fsdp")
    depth = lax.axis_size("ctx") // INNER
    n = lax.axis_size("ctx") // 2
    toks, width = do.shape
    blk = toks // 2
    rows = INNER * blk
    part = width // fs
    big = region_rows(4 * part + part // 2, n)
    tot = 2 * big
    zchunk = -(-part // (16 * depth)) * 16
    zrows = zchunk * depth
    slots = min(fs - 1, 2)
    vs = v.shape[1:]
    dma = pltpu.SemaphoreType.DMA
    vm = pl.BlockSpec(memory_space=pltpu.VMEM)
    anyspec = pl.BlockSpec(memory_space=pl.ANY)
    ins = (do, qb, kv, ot, lse) + tuple(ops) + (w_one, tokens, g_hid)
    order = [do, qb, kv, ot, lse] + list(ops) + [w_one, tokens, g_hid]
    cfg = (depth, length, n, fs, big, zrows)
    return pl.pallas_call(
        functools.partial(back_kernel, cfg),
        out_shape=(jax.ShapeDtypeStruct((part, 3 * width), BF), jax.ShapeDtypeStruct((part, width), BF),
                   jax.ShapeDtypeStruct((part, 4 * width), BF), jax.ShapeDtypeStruct((4 * part, width), BF),
                   jax.ShapeDtypeStruct(vs, F32), jax.ShapeDtypeStruct((toks, width), F32)),
        in_specs=[pl.BlockSpec(memory_space=pltpu.SMEM)] + [anyspec] * len(ins) + [vm, vm],
        out_specs=(anyspec, anyspec, anyspec, anyspec, vm, vm),
        scratch_shapes=[pltpu.VMEM(a.shape, a.dtype) for a in order] + [
            pltpu.VMEM((toks, INNER * QW), BF),
            pltpu.VMEM((2, rows, QW), BF),
            pltpu.VMEM((2, 8, rows), F32),
            pltpu.VMEM((2, 3 * HD, rows), F32),
            pltpu.VMEM((2, rows, KW), F32),
            pltpu.VMEM((2, depth, rows, KW), BF),
            pltpu.VMEM((2, rows, QW), BF),
            pltpu.VMEM((2, rows, KW), BF),
            pltpu.VMEM((toks, INNER * GW), BF),
            pltpu.VMEM((toks, 3 * width), BF),
            pltpu.VMEM((6 * width, toks), BF),
            pltpu.VMEM((width, 2 * rows), BF),
            pltpu.VMEM((slots, tot, width), BF),
            pltpu.VMEM((tot, width), BF),
            pltpu.VMEM((fs - 1, 9 * part, width), BF),
            pltpu.VMEM((big // 2, width), BF), pltpu.VMEM((big // 2, width), BF),
            pltpu.VMEM((n - 1, big // 2 // n, width), BF), pltpu.VMEM((n - 1, big // 2 // n, width), BF),
            pltpu.VMEM((slots, part, GW), BF),
            pltpu.VMEM((zrows, GW), BF),
            pltpu.VMEM((fs - 1, part, GW), BF),
            pltpu.VMEM((depth, zchunk, GW), BF),
            pltpu.VMEM((INNER, zrows, GW), BF),
            pltpu.VMEM((part, 3 * width), BF),
            pltpu.VMEM((fs,) + vs, F32),
            pltpu.VMEM(vs, F32),
            pltpu.VMEM((fs - 1,) + vs, F32),
            pltpu.VMEM(vs, F32),
            pltpu.VMEM((n,) + vs, F32),
            dma((15,)), dma((6,)), dma((2, 3)), dma((2, 3)), dma((2, depth)), dma((2, depth)),
            dma((2, 3)), dma((2, 3)), dma((2, 3)), dma((2, 3)),
            dma((fs - 1, 2)), dma((fs - 1, 2)), dma((2,)), dma((2,)),
            dma((2, 2, 2, n - 1)), dma((2, 2, 2, n - 1)), dma((2, 2, n)), dma((2, 2, n)),
            dma((fs - 1,)), dma((fs - 1,)), dma((depth - 1,)), dma((depth - 1,)), dma((depth - 1,)), dma((depth - 1,)),
            dma((INNER - 1, depth)), dma((INNER - 1, depth)),
            dma((fs - 1,)), dma((fs - 1,)), dma(()), dma(()), dma((n - 1,)), dma((n - 1,)), dma((12,)),
        ],
        compiler_params=pltpu.CompilerParams(collective_id=cid, has_side_effects=True, vmem_limit_bytes=62 << 20),
        name="block_back",
    )(starts, *ins, gain, v)


def middle_kernel(fs, attn, tok, cot, vec, c_one, w_out_h, w_one_h, w_two_h,
                  o_layer, o_mid, o_pre, o_act, o_hid, o_branch, o_attn, o_vec,
                  w_out, w_one, w_two, hidden, acc, e_acc, line, b_pre, b_act, b_mid, osem, sem):
    width = attn.shape[1]
    part = width // fs
    first = pltpu.make_async_copy(w_out_h, w_out, sem.at[0])
    first.start()
    ones, twos = [], []
    for j in range(4):
        ones.append(pltpu.make_async_copy(w_one_h.at[:, pl.ds(j * width, width)], w_one.at[j], sem.at[1 + j]))
        twos.append(pltpu.make_async_copy(w_two_h.at[pl.ds(j * width, width)], w_two.at[j], sem.at[5 + j]))
        ones[j].start()
        twos[j].start()
    g = cot[...]
    first.wait()
    hid = tok[...].astype(F32) + nn(attn[...], w_out[...]) + vec[4:5, :]
    hidden[...] = hid
    center = hid - jnp.mean(hid, axis=-1, keepdims=True)
    r = lax.rsqrt(jnp.mean(center * center, axis=-1, keepdims=True) + EPS)
    b_mid[...] = (center * r * vec[5:6, :] + vec[6:7, :]).astype(BF)
    outs = [pltpu.make_async_copy(b_mid, o_mid, osem.at[0])]
    outs[0].start()
    root = (2.0 / jnp.pi) ** 0.5
    for j in range(4):
        lanes = slice(j * width, (j + 1) * width)
        ones[j].wait()
        twos[j].wait()
        p = nn(b_mid[...], w_one[j]) + c_one[:, lanes]
        t = jnp.tanh(root * (p + 0.044715 * (p * p * p)))
        act = (0.5 * p * (1.0 + t)).astype(BF)
        slope = 0.5 * (1.0 + t) + 0.5 * p * (1.0 - t * t) * (root * (1.0 + 3 * 0.044715 * (p * p)))
        b_act[:, lanes] = act
        gp = (nt(g, w_two[j]) * slope).astype(BF)
        b_pre[:, lanes] = gp
        for i, (src, dst) in enumerate(((b_act, o_act), (b_pre, o_pre))):
            outs.append(pltpu.make_async_copy(src.at[:, lanes], dst.at[:, lanes], osem.at[1 + 2 * j + i]))
            outs[-1].start()
        line[:, lanes] = jnp.sum(gp.astype(F32), axis=0, keepdims=True)
        add = nn(act, w_two[j])
        back = nt(gp, w_one[j])
        if j == 0:
            acc[...] = add
            e_acc[...] = back
        else:
            acc[...] = acc[...] + add
            e_acc[...] = e_acc[...] + back
    o_layer[...] = (hidden[...] + acc[...] + vec[7:8, :]).astype(BF)
    hid = hidden[...]
    center = hid - jnp.mean(hid, axis=-1, keepdims=True)
    r = lax.rsqrt(jnp.mean(center * center, axis=-1, keepdims=True) + EPS)
    xh = center * r
    e = e_acc[...]
    t = e * vec[5:6, :]
    gf = g.astype(F32)
    grad = gf + r * (t - jnp.mean(t, axis=-1, keepdims=True) - xh * jnp.mean(t * xh, axis=-1, keepdims=True))
    o_hid[...] = grad
    branch = grad.astype(BF)
    o_branch[...] = branch
    o_attn[...] = nt(branch, w_out[...]).astype(BF)
    o_vec[...] = jnp.zeros_like(o_vec)
    for row, val in ((4, branch.astype(F32)), (5, e * xh), (6, e), (7, gf)):
        total = jnp.sum(val, axis=0, keepdims=True)
        for i in range(fs):
            o_vec[i, row:row + 1, :] = total[:, i * part:(i + 1) * part]
    for i in range(fs):
        for j in range(4):
            o_vec[i, 8 + j:9 + j, :] = line[:, (4 * i + j) * part:(4 * i + j + 1) * part]
    for cp in outs:
        cp.wait()


def middle(attn, tok, cot, vec, c_one, w_out, w_one, w_two):
    fs = lax.axis_size("fsdp")
    toks, width = tok.shape
    full = jax.ShapeDtypeStruct((toks, width), BF)
    wide = jax.ShapeDtypeStruct((toks, 4 * width), BF)
    vm = pl.BlockSpec(memory_space=pltpu.VMEM)
    anyspec = pl.BlockSpec(memory_space=pl.ANY)
    return pl.pallas_call(
        functools.partial(middle_kernel, fs),
        out_shape=(full, full, wide, wide, jax.ShapeDtypeStruct((toks, width), F32), full, full,
                   jax.ShapeDtypeStruct((fs, 16, width // fs), F32)),
        in_specs=[vm] * 5 + [anyspec] * 3,
        out_specs=(vm, anyspec, anyspec, anyspec, vm, vm, vm, vm),
        scratch_shapes=[
            pltpu.VMEM((width, width), BF),
            pltpu.VMEM((4, width, width), BF),
            pltpu.VMEM((4, width, width), BF),
            pltpu.VMEM((toks, width), F32),
            pltpu.VMEM((toks, width), F32),
            pltpu.VMEM((toks, width), F32),
            pltpu.VMEM((1, 4 * width), F32),
            pltpu.VMEM((toks, 4 * width), BF),
            pltpu.VMEM((toks, 4 * width), BF),
            pltpu.VMEM((toks, width), BF),
            pltpu.SemaphoreType.DMA((9,)),
            pltpu.SemaphoreType.DMA((9,)),
        ],
        compiler_params=pltpu.CompilerParams(vmem_limit_bytes=62 << 20),
        name="middle",
    )(attn, tok, cot, vec, c_one, w_out, w_one, w_two)


def per_device(
    stream,
    doc_starts,
    ln1_gain,
    ln1_bias,
    qkv_weight,
    q_bias,
    v_bias,
    out_weight,
    out_bias,
    ln2_gain,
    ln2_bias,
    fc1_weight,
    fc1_bias,
    fc2_weight,
    fc2_bias,
    cotangent,
):
    length = lax.axis_size("ctx") * stream.shape[1]
    part = ln1_gain.shape[0]
    lines = [one.reshape(-1, part) for one in (ln1_gain, ln1_bias, q_bias, v_bias, out_bias, ln2_gain, ln2_bias, fc2_bias,
                                               fc1_bias)]
    v_shard = jnp.concatenate(lines + [jnp.zeros((4, part), BF)], axis=0).astype(F32)
    w_out = lax.all_gather(out_weight, "fsdp", axis=0, tiled=True)
    w_one = lax.all_gather(fc1_weight, "fsdp", axis=0, tiled=True)
    w_two = lax.all_gather(fc2_weight, "fsdp", axis=0, tiled=True)
    tokens, cot = stream[0], cotangent[0]
    attn, normed_group, vec, c_one, w_qkv, q_kept, kv_kept, out_kept, lse = attend(
        doc_starts, tokens, v_shard, qkv_weight, length, 1
    )
    layer_out, normed_mid, grad_pre, activ, grad_hidden, grad_branch, grad_attn, v_part = middle(
        attn, tokens, cot, vec, c_one, w_out, w_one, w_two
    )
    t_qkv, t_out, t_fc1, t_fc2, total, input_grad = block_back(
        doc_starts, grad_attn, (q_kept, kv_kept, out_kept), lse,
        (normed_group, attn, grad_branch, normed_mid, grad_pre, activ, cot),
        w_qkv, tokens, grad_hidden, vec, v_part, length, 0,
    )
    return (
        layer_out[None], input_grad[None], total[0], total[1], t_qkv.astype(F32), total[2], total[3], t_out.astype(F32),
        total[4], total[5], total[6], t_fc1.astype(F32), total[8:12].reshape(-1), t_fc2.astype(F32), total[7],
    )


def solution(mesh):
    in_specs = (
        P("fsdp", "ctx", None),
        P("fsdp", None),
        P("fsdp"),
        P("fsdp"),
        P("fsdp", None),
        P("fsdp"),
        P("fsdp"),
        P("fsdp", None),
        P("fsdp"),
        P("fsdp"),
        P("fsdp"),
        P("fsdp", None),
        P("fsdp"),
        P("fsdp", None),
        P("fsdp"),
        P("fsdp", "ctx", None),
    )
    out_specs = (
        P("fsdp", "ctx", None),
        P("fsdp", "ctx", None),
        P("fsdp"),
        P("fsdp"),
        P("fsdp", None),
        P("fsdp"),
        P("fsdp"),
        P("fsdp", None),
        P("fsdp"),
        P("fsdp"),
        P("fsdp"),
        P("fsdp", None),
        P("fsdp"),
        P("fsdp", None),
        P("fsdp"),
    )
    return jax.shard_map(
        per_device, mesh=mesh, in_specs=in_specs, out_specs=out_specs, check_vma=False
    )
```

```python
import functools

import jax
import jax.numpy as jnp
from jax import lax
from jax.experimental import pallas as pl
from jax.experimental.pallas import tpu as pltpu
from jax.sharding import PartitionSpec as P

H = 12
HD = 64
EPS = 1e-05
MESH = pl.DeviceIdType.MESH
BF = jnp.bfloat16
F32 = jnp.float32


INNER = 4
QW, KW = 256, 384
GW = QW + KW
NEG = -1e30


def nt(a, b):
    return lax.dot_general(a, b, (((1,), (1,)), ((), ())), preferred_element_type=F32)


def nn(a, b):
    return lax.dot_general(a, b, (((1,), (0,)), ((), ())), preferred_element_type=F32)


def head_lanes(x, head):
    if head == 2:
        return x
    lane = lax.broadcasted_iota(jnp.int32, x.shape, 1)
    keep = lane < HD if head == 0 else lane >= HD
    return jnp.where(keep, x, jnp.zeros_like(x))


def first_keys(starts_ref, pos):
    first = jnp.zeros_like(pos)
    for d in range(starts_ref.shape[1]):
        one = starts_ref[0, d]
        first = jnp.maximum(first, jnp.where(one <= pos, one, 0))
    return first


def places():
    c = lax.axis_index("ctx")
    f = lax.axis_index("fsdp")
    return c // INNER, c % INNER, f


def send(src, dst, ssem, rsem, peer):
    return pltpu.make_async_remote_copy(
        src_ref=src, dst_ref=dst, send_sem=ssem, recv_sem=rsem, device_id=peer, device_id_type=MESH
    )


def group_q(src, dst):
    dst_zero = jnp.zeros((dst.shape[0], HD), dst.dtype)
    for i in range(INNER):
        a, o = 3 * i * HD, i * GW
        dst[:, o:o + 3 * HD] = (src[:, a:a + 3 * HD].astype(F32) * (HD ** -0.5)).astype(dst.dtype)
        dst[:, o + 3 * HD:o + QW] = dst_zero


def group_kv(src, dst):
    width = H * HD
    for i in range(INNER):
        a, o = 3 * i * HD, i * GW
        dst[:, o + QW:o + QW + 2 * HD] = src[:, width + a:width + a + 2 * HD]
        dst[:, o + QW + 2 * HD:o + QW + 4 * HD] = src[:, 2 * width + a:2 * width + a + 2 * HD]
        dst[:, o + QW + 4 * HD:o + QW + 5 * HD] = src[:, width + a + 2 * HD:width + a + 3 * HD]
        dst[:, o + QW + 5 * HD:o + QW + 6 * HD] = src[:, 2 * width + a + 2 * HD:2 * width + a + 3 * HD]


def ungroup_qkv(src, dst):
    width = H * HD
    for i in range(INNER):
        a, o = 3 * i * HD, i * GW
        dst[:, a:a + 3 * HD] = src[:, o:o + 3 * HD]
        dst[:, width + a:width + a + 2 * HD] = src[:, o + QW:o + QW + 2 * HD]
        dst[:, 2 * width + a:2 * width + a + 2 * HD] = src[:, o + QW + 2 * HD:o + QW + 4 * HD]
        dst[:, width + a + 2 * HD:width + a + 3 * HD] = src[:, o + QW + 4 * HD:o + QW + 5 * HD]
        dst[:, 2 * width + a + 2 * HD:2 * width + a + 3 * HD] = src[:, o + QW + 5 * HD:o + QW + 6 * HD]


def ungroup_one(i, src, dst):
    width = H * HD
    a = 3 * i * HD
    dst[:, a:a + 3 * HD] = src[:, :3 * HD]
    dst[:, width + a:width + a + 2 * HD] = src[:, QW:QW + 2 * HD]
    dst[:, 2 * width + a:2 * width + a + 2 * HD] = src[:, QW + 2 * HD:QW + 4 * HD]
    dst[:, width + a + 2 * HD:width + a + 3 * HD] = src[:, QW + 4 * HD:QW + 5 * HD]
    dst[:, 2 * width + a + 2 * HD:2 * width + a + 3 * HD] = src[:, QW + 5 * HD:QW + 6 * HD]


def group_rows(src, dst):
    dst_zero = jnp.zeros((dst.shape[0], HD), dst.dtype)
    for i in range(INNER):
        a, o = 3 * i * HD, i * QW
        dst[:, o:o + 2 * HD] = src[:, a:a + 2 * HD]
        dst[:, o + 2 * HD:o + 3 * HD] = dst_zero
        dst[:, o + 3 * HD:o + 4 * HD] = src[:, a + 2 * HD:a + 3 * HD]


def ungroup_rows(src, dst):
    for i in range(INNER):
        a, o = 3 * i * HD, i * QW
        dst[:, a:a + 2 * HD] = src[:, o:o + 2 * HD]
        dst[:, a + 2 * HD:a + 3 * HD] = src[:, o + 3 * HD:o + 4 * HD]


K_LANES = (0, 0, 256)
V_LANES = (128, 128, 256)
Q_LANES = (0, 0, 128)


def attend_kernel(depth, length, fs, starts_ref, tok_ref, v_shard, w_shard,
                  out_ref, xg_ref, vec_ref, c_one_ref, w_ref, qb_ref, kv_ref, ot_ref, lse_ref,
                  normed_ref, xg, xgs, xgr, xgl, w_all, vbuf, raw_ref, x_ref, qb, kv, acc, top, tot, ob, land,
                  wl, ws, wr, vs, vr, lsem, as_kv, ar_kv, as_q, ar_q, zs, zr, bs, br, osem):
    z, h, f = places()
    c = lax.axis_index("ctx")
    width = H * HD
    part = width // fs
    blk = raw_ref.shape[0] // 2
    rows = INNER * blk
    half_rows = (pl.ds(0, blk), pl.ds(blk, blk))
    fpeers = [(c, lax.rem(f + k, fs)) for k in range(1, fs)]

    barrier = pltpu.get_barrier_semaphore()
    for j in range(1, INNER):
        pl.semaphore_signal(barrier, inc=1, device_id=(z * INNER + (h + j) % INNER, f), device_id_type=MESH)

    @pl.when(z > 0)
    def _():
        pl.semaphore_signal(barrier, inc=1, device_id=((z - 1) * INNER + h, f), device_id_type=MESH)

    @pl.when(z < depth - 1)
    def _():
        pl.semaphore_signal(barrier, inc=1, device_id=((z + 1) * INNER + h, f), device_id_type=MESH)

    for peer in fpeers:
        pl.semaphore_signal(barrier, inc=1, device_id=peer, device_id_type=MESH)

    def piece(half, i):
        p = i if half == 0 else INNER - 1 - i
        return pl.ds(pl.multiple_of(p * blk, blk), blk)

    own = (depth - 1, depth)
    my_rows = pl.ds(pl.multiple_of(f * part, 16), part)

    def w_lanes(b):
        return pl.ds(b * width, width)

    w_own = [pltpu.make_async_copy(w_shard.at[:, w_lanes(b)], w_all.at[my_rows, w_lanes(b)], wl.at[b]) for b in range(3)]
    for b in (1, 2, 0):
        w_own[b].start()
    vbuf[f] = v_shard[...]

    def w_send(k, b):
        return send(w_shard.at[:, w_lanes(b)], w_all.at[my_rows, w_lanes(b)], ws.at[k - 1, b], wr.at[k - 1, b], fpeers[k - 1])

    def v_send(k):
        return send(v_shard, vbuf.at[f], vs.at[k - 1], vr.at[k - 1], fpeers[k - 1])

    pl.semaphore_wait(barrier, INNER - 1 + fs - 1 + jnp.where(z > 0, 1, 0) + jnp.where(z < depth - 1, 1, 0))
    for k in range(1, fs):
        v_send(k).start()
        for b in (1, 2, 0):
            w_send(k, b).start()
    x = tok_ref[...].astype(F32)
    center = x - jnp.mean(x, axis=-1, keepdims=True)
    unit = center * lax.rsqrt(jnp.mean(center * center, axis=-1, keepdims=True) + EPS)
    for k in range(1, fs):
        v_send(k).wait_recv()
    for i in range(fs):
        vec_ref[:, i * part:(i + 1) * part] = vbuf[i, :8, :]
        for j in range(4):
            c_one_ref[:, (4 * i + j) * part:(4 * i + j + 1) * part] = vbuf[i, 8 + j:9 + j, :]
    normed_ref[...] = (unit * vec_ref[0:1, :] + vec_ref[1:2, :]).astype(BF)

    def project(b):
        w_own[b].wait()
        for k in range(1, fs):
            w_send(k, b).wait_recv()
        y = nn(normed_ref[...], w_all[:, b * width:(b + 1) * width])
        if b != 1:
            y = y + vec_ref[(2 if b == 0 else 3):(3 if b == 0 else 4), :]
        raw_ref[:, b * width:(b + 1) * width] = y.astype(BF)

    def a2a(j, half, kind):
        i = (h + j) % INNER
        lanes = pl.ds(pl.multiple_of(i * GW + (QW if kind else 0), 128), KW if kind else QW)
        dst = kv.at[own[half], piece(half, h)] if kind else qb.at[half, piece(half, h)]
        sems = (as_kv.at[half, j - 1], ar_kv.at[half, j - 1]) if kind else (as_q.at[half, j - 1], ar_q.at[half, j - 1])
        return send(x_ref.at[half_rows[half], lanes], dst, *sems, (z * INNER + i, f))

    def local(half, kind):
        lanes = pl.ds(pl.multiple_of(h * GW + (QW if kind else 0), 128), KW if kind else QW)
        dst = kv.at[own[half], piece(half, h)] if kind else qb.at[half, piece(half, h)]
        return pltpu.make_async_copy(x_ref.at[half_rows[half], lanes], dst, lsem.at[half, kind])

    def spread(kind):
        for half in range(2):
            for j in range(1, INNER):
                a2a(j, half, kind).start()
            local(half, kind).start()

    project(1)
    project(2)
    group_kv(raw_ref, x_ref)
    spread(1)
    project(0)
    group_q(raw_ref, x_ref)
    spread(0)
    w_out_copy = pltpu.make_async_copy(w_all, w_ref, osem.at[3])
    w_out_copy.start()

    def plane(j, half):
        return send(normed_ref.at[half_rows[half]], xg.at[half, piece(half, h)], xgs.at[half, j - 1], xgr.at[half, j - 1],
                    (z * INNER + (h + j) % INNER, f))

    def plane_own(half):
        return pltpu.make_async_copy(normed_ref.at[half_rows[half]], xg.at[half, piece(half, h)], xgl.at[half])

    for half in range(2):
        plane_own(half).start()

    def relay(half, src_slot, step, p):
        rws = pl.ds(pl.multiple_of(p * blk, blk), blk)
        if half == 0:
            peer, slot = (z + 1) * INNER + h, step - 1
        else:
            peer, slot = (z - 1) * INNER + h, z - 1 + step - 1
        return send(kv.at[src_slot, rws], kv.at[slot, rws], zs.at[half, step - 1, p], zr.at[half, step - 1, p], (peer, f))

    can = (z < depth - 1, z > 0)
    for j in range(INNER):
        i = (h + INNER - j) % INNER
        for half in range(2):
            if j == 0:
                local(half, 1).wait()
            else:
                a2a(j, half, 1).wait_recv()

            @pl.when(can[half])
            def _():
                relay(half, own[half], 1, i if half == 0 else INNER - 1 - i).start()

    for half in range(2):
        local(half, 0).wait()
        for j in range(1, INNER):
            a2a(j, half, 0).wait_recv()
    for half in range(2):
        for j in range(1, INNER):
            plane(j, half).start()

    def base_of(half, zz):
        return zz * rows if half == 0 else length - (zz + 1) * rows

    cols = rows // 2

    def tile(half, slot, q_base, k_base, diag):
        for head in range(3):
            k_all = kv[slot, :, K_LANES[head]:K_LANES[head] + 128]
            v_all = kv[slot, :, V_LANES[head]:V_LANES[head] + 128]
            v_t = v_all.T[(0 if head == 0 else HD):(HD if head == 0 else 2 * HD)]
            for part in range(2):
                keys = (part + 1) * cols if diag else rows
                lanes = slice(part * cols, (part + 1) * cols)
                q = head_lanes(qb[half, lanes, Q_LANES[head]:Q_LANES[head] + 128], head)
                pos = q_base + part * cols + lax.broadcasted_iota(jnp.int32, (1, cols), 1)
                first = first_keys(starts_ref, pos) - k_base
                s = nt(k_all[:keys], q)
                row = lax.broadcasted_iota(jnp.int32, (keys, cols), 0)
                ok = row >= first
                if diag:
                    ok = ok & (row <= pos - k_base)
                s = jnp.where(ok, s, NEG)
                line = slice(head, head + 1)
                feats = slice(head * HD, (head + 1) * HD)
                high = jnp.max(s, axis=0, keepdims=True)
                if not diag:
                    before = top[half, line, lanes]
                    high = jnp.maximum(before, high)
                    fade = jnp.exp(before - high)
                w = jnp.exp(s - high)
                add = jnp.sum(w, axis=0, keepdims=True)
                o = nn(v_t[:, :keys], w.astype(BF))
                if diag:
                    tot[half, line, lanes] = add
                    acc[half, feats, lanes] = o
                else:
                    tot[half, line, lanes] = tot[half, line, lanes] * fade + add
                    acc[half, feats, lanes] = acc[half, feats, lanes] * fade + o
                top[half, line, lanes] = high

    @pl.loop(0, 2)
    def _(half):
        q_base = jnp.where(half == 0, base_of(0, z), base_of(1, z))
        tile(half, depth - 1 + half, q_base, q_base, True)

    @pl.loop(1, depth)
    def _(step):
        valid = (z - step >= 0, z + step <= depth - 1)
        slots = (step - 1, z + step - 1)
        for half in range(2):
            for p in range(INNER):
                @pl.when(valid[half])
                def _():
                    rws = pl.ds(p * blk, blk)
                    send(kv.at[slots[half], rws], kv.at[slots[half], rws], zs.at[half, step - 1, p],
                         zr.at[half, step - 1, p], (z * INNER + (h + 1) % INNER, f)).wait_recv()

                @pl.when(valid[half] & can[half])
                def _():
                    relay(half, slots[half], step + 1, p).start()

        @pl.loop(0, 2)
        def _(half):
            @pl.when(jnp.where(half == 0, z - step, depth - 1 - z - step) >= 0)
            def _():
                zz = jnp.where(half == 0, z - step, z + step)
                q_base = jnp.where(half == 0, base_of(0, z), base_of(1, z))
                k_base = jnp.where(half == 0, base_of(0, zz), base_of(1, zz))
                tile(half, jnp.where(half == 0, step - 1, z + step - 1), q_base, k_base, False)

    for half in range(2):
        plane_own(half).wait()
        for j in range(1, INNER):
            plane(j, half).wait_recv()
    ob[:, :, 2 * HD:3 * HD] = jnp.zeros((2, rows, HD), BF)
    for half in range(2):
        lse_ref[half] = top[half] + jnp.log(tot[half])
        for head in range(3):
            feats = slice(head * HD, (head + 1) * HD)
            acc[half, feats, :] = acc[half, feats, :] / tot[half, head:head + 1, :]
        ob[half, :, :2 * HD] = acc[half, :2 * HD, :].T.astype(BF)
        ob[half, :, 3 * HD:] = acc[half, 2 * HD:, :].T.astype(BF)
    outs = [pltpu.make_async_copy(qb, qb_ref, osem.at[0]), pltpu.make_async_copy(kv, kv_ref, osem.at[1]),
            pltpu.make_async_copy(acc, ot_ref, osem.at[2]), pltpu.make_async_copy(xg, xg_ref, osem.at[4])]
    for cp in outs:
        cp.start()

    def back(j, half):
        i = (h + j) % INNER
        return send(ob.at[half, piece(half, i)], land.at[half_rows[half], pl.ds(pl.multiple_of(h * QW, 128), QW)],
                    bs.at[half, j - 1], br.at[half, j - 1], (z * INNER + i, f))

    for half in range(2):
        for j in range(1, INNER):
            back(j, half).start()
        mine = pltpu.make_async_copy(ob.at[half, piece(half, h)],
                                     land.at[half_rows[half], pl.ds(pl.multiple_of(h * QW, 128), QW)], lsem.at[half, 0])
        mine.start()
        mine.wait()
    for half in range(2):
        for j in range(1, INNER):
            back(j, half).wait_recv()
    ungroup_rows(land, out_ref)
    for half in range(2):
        for j in range(1, INNER):
            a2a(j, half, 1).wait_send()
            a2a(j, half, 0).wait_send()
            back(j, half).wait_send()
            plane(j, half).wait_send()

        @pl.when(can[half])
        def _():
            for p in range(INNER):
                relay(half, own[half], 1, p).wait_send()

    @pl.loop(1, depth)
    def _(step):
        valid = (z - step >= 0, z + step <= depth - 1)
        for half in range(2):
            @pl.when(valid[half] & can[half])
            def _():
                for p in range(INNER):
                    relay(half, own[half], step + 1, p).wait_send()
    for k in range(1, fs):
        v_send(k).wait_send()
        for b in range(3):
            w_send(k, b).wait_send()
    for cp in outs + [w_out_copy]:
        cp.wait()


def attend(starts, x, v_shard, w_shard, length, cid):
    depth = lax.axis_size("ctx") // INNER
    fs = lax.axis_size("fsdp")
    blk = x.shape[0] // 2
    width = x.shape[1]
    rows = INNER * blk
    dma = pltpu.SemaphoreType.DMA
    shapes = (
        jax.ShapeDtypeStruct((x.shape[0], width), BF),
        jax.ShapeDtypeStruct((2, rows, width), BF),
        jax.ShapeDtypeStruct((8, width), F32),
        jax.ShapeDtypeStruct((1, 4 * width), F32),
        jax.ShapeDtypeStruct((width, 3 * width), BF),
        jax.ShapeDtypeStruct((2, rows, QW), BF),
        jax.ShapeDtypeStruct((depth + 1, rows, KW), BF),
        jax.ShapeDtypeStruct((2, 3 * HD, rows), F32),
        jax.ShapeDtypeStruct((2, 8, rows), F32),
    )
    vm = pl.BlockSpec(memory_space=pltpu.VMEM)
    anyspec = pl.BlockSpec(memory_space=pl.ANY)
    return pl.pallas_call(
        functools.partial(attend_kernel, depth, length, fs),
        out_shape=shapes,
        in_specs=[pl.BlockSpec(memory_space=pltpu.SMEM), vm, vm, anyspec],
        out_specs=(vm, anyspec, vm, vm, anyspec, anyspec, anyspec, anyspec, vm),
        scratch_shapes=[
            pltpu.VMEM((x.shape[0], width), BF),
            pltpu.VMEM((2, rows, width), BF),
            dma((2, 3)), dma((2, 3)), dma((2,)),
            pltpu.VMEM((width, 3 * width), BF),
            pltpu.VMEM((fs,) + v_shard.shape, F32),
            pltpu.VMEM((2 * blk, 3 * width), BF),
            pltpu.VMEM((2 * blk, INNER * GW), BF),
            pltpu.VMEM((2, rows, QW), BF),
            pltpu.VMEM((depth + 1, rows, KW), BF),
            pltpu.VMEM((2, 3 * HD, rows), F32),
            pltpu.VMEM((2, 8, rows), F32),
            pltpu.VMEM((2, 8, rows), F32),
            pltpu.VMEM((2, rows, QW), BF),
            pltpu.VMEM((2 * blk, INNER * QW), BF),
            dma((3,)), dma((fs - 1, 3)), dma((fs - 1, 3)), dma((fs - 1,)), dma((fs - 1,)),
            dma((2, 2)), dma((2, 3)), dma((2, 3)), dma((2, 3)), dma((2, 3)),
            dma((2, depth, INNER)), dma((2, depth, INNER)), dma((2, 3)), dma((2, 3)), dma((5,)),
        ],
        compiler_params=pltpu.CompilerParams(collective_id=cid, has_side_effects=True, vmem_limit_bytes=62 << 20),
        name="attend",
    )(starts, x, v_shard, w_shard)


def ring_pos(z, bit, depth):
    return jnp.where(bit == 0, z, 2 * depth - 1 - z)


def ring_ctx(pos, depth, kind, fixed):
    pos = lax.rem(pos + 2 * depth, 2 * depth)
    z = jnp.where(pos < depth, pos, 2 * depth - 1 - pos)
    bit = jnp.where(pos < depth, 0, 1)
    return z * INNER + (bit * 2 + fixed if kind == 0 else fixed * 2 + bit)


def region_rows(used, n):
    return -(-used // (32 * n)) * 32 * n


def back_kernel(cfg, starts_ref, h_do, h_qb, h_kv, h_ot, h_lse, h_xg, h_out, h_gout, h_mid, h_gpre, h_act, h_gtop,
                h_w, h_tok, h_hid, gain, v_ref,
                o_qkv, o_out, o_fc1, o_fc2, vout_ref, o_in,
                raw, qb, kv, ot, lse, xg, x_out, g_out, x_mid, g_pre, x_act, g_top, wbuf, tokens, g_hid,
                do_ref, dob, dots, dq, dkvd, rbuf, dqb, fin, land, g_qkv,
                xt, xtg, gbuf, acc, fbuf, pa, pb, ra, rb, gl, accl, fl, zb, outl, stage,
                vall, vf, vx, vr,
                ldsem, lsem, as_o, ar_o, zs, zr, bq, brq, bk, brk,
                fsem, frec, ps, pr, rs, rr, xgs, xgr, lfs, lfr, lzs, lzr, las, lar, lps, lpr, vfs, vfr, vxs, vxr, vrs, vrr, osem):
    depth, length, n, fs, big, zrows = cfg
    z, h, f = places()
    c = lax.axis_index("ctx")
    bits = (h % 2, h // 2)
    poss = (ring_pos(z, bits[1], depth), ring_pos(z, bits[0], depth))
    pairs_of = ((c + 1 - 2 * bits[0], f), (c + 2 - 4 * bits[1], f))
    rights = tuple((ring_ctx(poss[k] + 1, depth, k, bits[k]), f) for k in range(2))
    lefts = tuple((ring_ctx(poss[k] - 1, depth, k, bits[k]), f) for k in range(2))
    fpeers = [(c, lax.rem(f + k, fs)) for k in range(1, fs)]
    width = acc.shape[1]
    lanes = (pl.ds(0, width // 2), pl.ds(width // 2, width // 2))
    part = width // fs
    bases_of = (0, big)
    outb = gbuf.at[0]
    slots = gbuf.shape[0]
    blk = raw.shape[0] // 2
    rows = INNER * blk
    cols = rows // 2
    half_rows = (pl.ds(0, blk), pl.ds(blk, blk))

    zpeers = [(lax.rem(z + k, depth) * INNER + h, f) for k in range(1, depth)]
    hpeers = [(z * INNER + (h + j) % INNER, f) for j in range(1, INNER)]
    barrier = pltpu.get_barrier_semaphore()
    for peer in hpeers + zpeers + list(rights) + list(lefts) + fpeers:
        pl.semaphore_signal(barrier, inc=1, device_id=peer, device_id_type=MESH)

    loads = {}
    pairs = (("do", h_do, raw), ("act", h_act, x_act), ("gtop", h_gtop, g_top), ("out", h_out, x_out),
             ("gout", h_gout, g_out), ("mid", h_mid, x_mid), ("gpre", h_gpre, g_pre), ("ot", h_ot, ot),
             ("kv", h_kv, kv), ("qb", h_qb, qb), ("lse", h_lse, lse), ("xg", h_xg, xg), ("w", h_w, wbuf),
             ("tok", h_tok, tokens), ("hid", h_hid, g_hid))
    for i, (name, src, dst) in enumerate(pairs):
        loads[name] = pltpu.make_async_copy(src, dst, ldsem.at[i])
        loads[name].start()

    pend = []

    def go(cp):
        cp.start()
        pend.append(cp)
        return cp

    def piece(half, i):
        p = i if half == 0 else INNER - 1 - i
        return pl.ds(pl.multiple_of(p * blk, blk), blk)

    def spread(j, half):
        i = (h + j) % INNER
        return send(do_ref.at[half_rows[half], pl.ds(pl.multiple_of(i * QW, 128), QW)], dob.at[half, piece(half, h)],
                    as_o.at[half, j - 1], ar_o.at[half, j - 1], (z * INNER + i, f))

    loads["do"].wait()
    group_rows(raw, do_ref)
    pl.semaphore_wait(barrier, INNER - 1 + depth - 1 + 4 + fs - 1)
    mine = []
    for half in range(2):
        for j in range(1, INNER):
            go(spread(j, half))
        cp = pltpu.make_async_copy(do_ref.at[half_rows[half], pl.ds(pl.multiple_of(h * QW, 128), QW)],
                                   dob.at[half, piece(half, h)], lsem.at[half])
        cp.start()
        mine.append(cp)

    eye_n = 256
    eye = (lax.broadcasted_iota(jnp.int32, (eye_n, eye_n), 0)
           == lax.broadcasted_iota(jnp.int32, (eye_n, eye_n), 1)).astype(BF)
    offset = {"act": 0, "mid": 4 * width, "out": 5 * width}

    def turn_over(name, ref):
        @pl.loop(0, ref.shape[1] // eye_n)
        def _(b):
            o = pl.multiple_of(b * eye_n, eye_n)
            xt[pl.ds(pl.multiple_of(offset[name] + o, eye_n), eye_n), :] = nt(eye, ref[:, pl.ds(o, eye_n)]).astype(BF)

    def unit(name, start, g, dst, row, size):
        lhs = xt[pl.ds(pl.multiple_of(offset[name] + start, 16), size), :]
        dst[pl.ds(pl.multiple_of(row, 16), size), :] = nn(lhs, g).astype(BF)

    half_part = part // 2

    def fc2_for(owner, dst):
        @pl.loop(0, 4)
        def _(j):
            unit("act", owner * 4 * part + j * part, g_top[...], dst, bases_of[1] + j * part, part)
        unit("out", owner * part + half_part, g_out[...], dst, bases_of[1] + 4 * part, half_part)

    def fc1_for(owner, dst):
        @pl.loop(0, 4)
        def _(j):
            unit("mid", owner * part, g_pre[:, pl.ds(pl.multiple_of(j * width, 128), width)], dst,
                 bases_of[0] + j * part, part)
        unit("out", owner * part, g_out[...], dst, bases_of[0] + 4 * part, half_part)

    used = 4 * part + half_part
    cuts = ((bases_of[0], used, 0), (bases_of[1], used, used))

    def to_core(k, j):
        a, m, at = cuts[j]
        return remote(gbuf.at[(k - 1) % slots, pl.ds(a, m)], fbuf.at[k - 1, pl.ds(at, m)],
                      fsem.at[k - 1, j], frec.at[k - 1, j], fpeers[k - 1])

    def remote(src, dst, ssem, rsem, peer):
        return send(src, dst, ssem, rsem, peer)

    def share(j, make):
        for k in range(1, fs):
            if k - 1 >= slots:
                to_core(k - slots, j).wait_send()
            make(fpeers[k - 1][1], gbuf.at[(k - 1) % slots])
            to_core(k, j).start()

    def collect(j):
        for k in range(1, fs):
            if k > fs - 1 - slots:
                to_core(k, j).wait_send()
            to_core(k, j).wait_recv()
        a, m, at = cuts[j]
        step = 32 if m % 32 == 0 else 16

        @pl.loop(0, m // step)
        def _(i):
            rws = pl.ds(pl.multiple_of(a + i * step, step), step)
            tot = acc[rws, :].astype(F32)
            for k in range(fs - 1):
                tot = tot + fbuf[k, pl.ds(pl.multiple_of(at + i * step, step), step), :].astype(F32)
            acc[rws, :] = tot.astype(BF)

    for (a, m, _), size in zip(cuts, (big, big)):
        if size > m:
            acc[a + m:a + size, :] = jnp.zeros((size - m, width), BF)

    def stream(i, kind, pbuf, rbuf_):
        half = big // 2
        keep_at = pl.multiple_of(bases_of[i] + bits[kind] * half, 16)
        give_at = pl.multiple_of(bases_of[i] + (1 - bits[kind]) * half, 16)
        return (i, kind, keep_at, give_at, half, half // n, pbuf, rbuf_)

    sa, sb = stream(0, 0, pa, ra), stream(1, 1, pb, rb)

    def rows_of(st, k, base=None):
        k = lax.rem(k + 2 * n, n)
        return pl.ds(pl.multiple_of((st[2] if base is None else base) + k * st[5], 16), st[5])

    def pair_copy(st):
        return remote(acc.at[pl.ds(st[3], st[4])], st[6], ps.at[st[0]], pr.at[st[0]], pairs_of[st[1]])

    def pair_add(st):
        pair_copy(st).wait_recv()
        step = 32 if st[4] % 32 == 0 else 16

        @pl.loop(0, st[4] // step)
        def _(i):
            rws = pl.ds(pl.multiple_of(st[2] + i * step, 16), step)
            acc[rws, :] = (acc[rws, :].astype(F32)
                           + st[6][pl.ds(pl.multiple_of(i * step, 16), step), :].astype(F32)).astype(BF)

    def rs_copy(st, s, d):
        p = poss[st[1]]
        k = p - 1 - s if d == 0 else p + 1 + s
        return remote(acc.at[rows_of(st, k), lanes[d]], st[7].at[s, :, lanes[d]],
                      rs.at[st[0], 0, d, s], rr.at[st[0], 0, d, s], (rights if d == 0 else lefts)[st[1]])

    def rs_start(st):
        for d in range(2):
            go(rs_copy(st, 0, d))

    def rs_step(st, s):
        p = poss[st[1]]
        for d in range(2):
            rws = rows_of(st, p - 2 - s if d == 0 else p + 2 + s)
            rs_copy(st, s, d).wait_recv()
            tot = (acc[rws, lanes[d]].astype(F32) + st[7][s, :, lanes[d]].astype(F32)).astype(BF)
            if s < n - 2:
                acc[rws, lanes[d]] = tot
                go(rs_copy(st, s + 1, d))
            elif d == 0:
                outb[rws, lanes[d]] = tot
            else:
                outb[rws, lanes[d]] = tot
                ag_start(st)

    def ag_copy(st, s, d):
        p = poss[st[1]]
        rws = rows_of(st, p - s if d == 0 else p + s)
        return remote(outb.at[rws, lanes[d]], outb.at[rws, lanes[d]],
                      rs.at[st[0], 1, d, s], rr.at[st[0], 1, d, s], (rights if d == 0 else lefts)[st[1]])

    def cross(st, s, d, base=None):
        p = poss[st[1]]
        rws = rows_of(st, p - s if d == 0 else p + s, base)
        return remote(outb.at[rws, lanes[d]], outb.at[rws, lanes[d]], xgs.at[st[0], d, s], xgr.at[st[0], d, s],
                      pairs_of[st[1]])

    def ag_start(st):
        for d in range(2):
            go(ag_copy(st, 0, d))
        for d in range(2):
            go(cross(st, 0, d))

    def ag_step(st, s):
        p = poss[st[1]]
        for d in range(2):
            rws = rows_of(st, p - 1 - s if d == 0 else p + 1 + s)
            remote(outb.at[rws, lanes[d]], outb.at[rws, lanes[d]],
                   rs.at[st[0], 1, d, s], rr.at[st[0], 1, d, s], pairs_of[0]).wait_recv()
            if s < n - 2:
                go(ag_copy(st, s + 1, d))
            go(cross(st, s + 1, d))

    def cross_wait(st):
        for s in range(n):
            for d in range(2):
                cross(st, s, d, st[3]).wait_recv()

    loads["act"].wait()
    turn_over("act", x_act)
    loads["gtop"].wait()
    loads["out"].wait()
    turn_over("out", x_out)
    loads["gout"].wait()
    share(1, fc2_for)
    loads["mid"].wait()
    turn_over("mid", x_mid)
    loads["gpre"].wait()
    share(0, fc1_for)
    dq[...] = jnp.zeros_like(dq)
    loads["ot"].wait()
    for half in range(2):
        mine[half].wait()
        for j in range(1, INNER):
            spread(j, half).wait_recv()
        for head in range(3):
            ln = slice(0, 128) if head < 2 else slice(128, 256)
            g = dob[half, :, ln].astype(F32).T[(0 if head == 0 else HD):(HD if head == 0 else 2 * HD)]
            dots[half, head:head + 1, :] = jnp.sum(g * ot[half, head * HD:(head + 1) * HD, :], axis=0, keepdims=True)
    for name in ("kv", "qb", "lse"):
        loads[name].wait()

    def base_of(half, zz):
        return zz * rows if half == 0 else length - (zz + 1) * rows

    def bases(half, zz):
        return jnp.where(half == 0, base_of(0, zz), base_of(1, zz))

    def tile(half, slot, q_base, k_base, diag, head):
        k_all = kv[slot, :, K_LANES[head]:K_LANES[head] + 128]
        v_all = kv[slot, :, V_LANES[head]:V_LANES[head] + 128]
        k_t = k_all.T[(HD if head == 1 else 0):(2 * HD if head == 1 else HD)]
        kl = slice(K_LANES[head], K_LANES[head] + 128)
        vl = slice(V_LANES[head], V_LANES[head] + 128)
        for half_cols in range(2):
            keys = (half_cols + 1) * cols if diag else rows
            ln = slice(half_cols * cols, (half_cols + 1) * cols)
            q = head_lanes(qb[half, ln, Q_LANES[head]:Q_LANES[head] + 128], head)
            g = head_lanes(dob[half, ln, Q_LANES[head]:Q_LANES[head] + 128], head)
            p = q_base + half_cols * cols + lax.broadcasted_iota(jnp.int32, (1, cols), 1)
            first = first_keys(starts_ref, p) - k_base
            s = nt(k_all[:keys], q)
            row = lax.broadcasted_iota(jnp.int32, (keys, cols), 0)
            ok = row >= first
            if diag:
                ok = ok & (row <= p - k_base)
            line = slice(head, head + 1)
            w = jnp.where(ok, jnp.exp(s - lse[half, line, ln]), 0.0)
            gp = nt(v_all[:keys], g)
            ds = (w * (gp - dots[half, line, ln])).astype(BF)
            dv = nn(w.astype(BF), g)
            dk = nn(ds, q)
            for sl, val in (((kl, dk + dv),) if head == 2 else ((kl, dk), (vl, dv))):
                if head != 1 and half_cols == 0:
                    dkvd[half, :keys, sl] = val
                elif head != 1 and diag:
                    dkvd[half, :cols, sl] = dkvd[half, :cols, sl] + val[:cols]
                    dkvd[half, cols:, sl] = val[cols:]
                else:
                    dkvd[half, :keys, sl] = dkvd[half, :keys, sl] + val
            feats = slice(head * HD, (head + 1) * HD)
            dq[half, feats, ln] = dq[half, feats, ln] + nn(k_t[:, :keys], ds)

    has = (z < depth - 1, z > 0)

    def pass_on(half, step):
        peer = (z - 1) * INNER + h if half == 0 else (z + 1) * INNER + h
        return send(rbuf.at[half, step], rbuf.at[half, step - 1], zs.at[half, step - 1], zr.at[half, step - 1], (peer, f))

    def take(half, step):
        return send(rbuf.at[half, step], rbuf.at[half, step], zs.at[half, step], zr.at[half, step],
                    (z * INNER + (h + 1) % INNER, f))

    @pl.loop(0, 2 * (depth - 1))
    def _(it):
        step = depth - 1 - it // 2
        half = it % 2
        valid = jnp.where(half == 0, z - step, depth - 1 - z - step) >= 0
        zz = jnp.where(half == 0, z - step, z + step)

        @pl.when(it == 2)
        def _():
            fc2_for(f, acc)
            collect(1)
            pair_copy(sb).start()
            fc1_for(f, acc)
            collect(0)
            pair_copy(sa).start()

        for head in range(3):
            @pl.when(valid)
            def _():
                tile(half, jnp.where(half == 0, step - 1, z + step - 1), bases(half, z), bases(half, zz), False, head)

        @pl.when(valid)
        def _():
            more = jnp.where(half == 0, depth - 1 - z, z) > 0

            @pl.when(more)
            def _():
                take(half, step).wait_recv()

                @pl.loop(0, rows // 64)
                def _(b):
                    rws = pl.ds(pl.multiple_of(b * 64, 64), 64)
                    rbuf[half, step, rws, :] = (dkvd[half, rws, :] + rbuf[half, step, rws, :].astype(F32)).astype(BF)

            @pl.when(jnp.logical_not(more))
            def _():
                rbuf[half, step] = dkvd[half].astype(BF)

            @pl.when(half == 0)
            def _():
                pass_on(0, step).start()

            @pl.when(half == 1)
            def _():
                pass_on(1, step).start()

    pend.extend((pair_copy(sb), pair_copy(sa)))

    @pl.loop(0, 2)
    def _(half):
        for head in range(3):
            tile(half, depth - 1 + half, bases(half, z), bases(half, z), True, head)

    def back(j, half, kind):
        i = (h + j) % INNER
        ln = pl.ds(pl.multiple_of(h * GW + (QW if kind else 0), 128), KW if kind else QW)
        src = fin if kind else dqb
        sems = (bk.at[half, j - 1], brk.at[half, j - 1]) if kind else (bq.at[half, j - 1], brq.at[half, j - 1])
        return send(src.at[half, piece(half, i)], land.at[half_rows[half], ln], *sems, (z * INNER + i, f))

    def keep(half, kind):
        ln = pl.ds(pl.multiple_of(h * GW + (QW if kind else 0), 128), KW if kind else QW)
        src = fin if kind else dqb
        return pltpu.make_async_copy(src.at[half, piece(half, h)], land.at[half_rows[half], ln],
                                     lsem.at[2 + 2 * half + kind])

    dqb[:, :, 3 * HD:] = jnp.zeros((2, rows, HD), BF)
    for half in range(2):
        dqb[half, :, :2 * HD] = (dq[half, :2 * HD, :] * (HD ** -0.5)).T.astype(BF)
        dqb[half, :, 2 * HD:3 * HD] = (dq[half, 2 * HD:, :] * (HD ** -0.5)).T.astype(BF)
        for j in range(1, INNER):
            go(back(j, half, 0))
        keep(half, 0).start()
    for st in (sb, sa):
        pair_add(st)
        rs_start(st)
    def late_core(k):
        return remote(gl.at[(k - 1) % slots], fl.at[k - 1], lfs.at[k - 1], lfr.at[k - 1], fpeers[k - 1])

    def late_grad(owner, dst):
        for lo, hi, src in ((0, QW, dqb), (QW, GW, fin)):
            tot = None
            for half in range(2):
                one = nn(xtg[pl.ds(pl.multiple_of(owner * part, 16), part), half * rows:(half + 1) * rows], src[half])
                tot = one if tot is None else tot + one
            dst[:part, lo:hi] = tot.astype(BF)

    loads["xg"].wait()
    for half in range(2):
        for r in range(rows // eye_n):
            @pl.loop(0, width // eye_n)
            def _(b):
                o = pl.multiple_of(b * eye_n, eye_n)
                xtg[pl.ds(o, eye_n), half * rows + r * eye_n:half * rows + (r + 1) * eye_n] = nt(
                    eye, xg[half, r * eye_n:(r + 1) * eye_n, pl.ds(o, eye_n)]).astype(BF)
    for half in range(2):
        @pl.when(has[half])
        def _():
            take(half, 0).wait_recv()

            @pl.loop(0, rows // 64)
            def _(b):
                rws = pl.ds(pl.multiple_of(b * 64, 64), 64)
                fin[half, rws, :] = (dkvd[half, rws, :] + rbuf[half, 0, rws, :].astype(F32)).astype(BF)

        @pl.when(jnp.logical_not(has[half]))
        def _():
            fin[half] = dkvd[half].astype(BF)
    for k in range(1, fs):
        if k - 1 >= slots:
            late_core(k - slots).wait_send()
        late_grad(fpeers[k - 1][1], gl.at[(k - 1) % slots])
        late_core(k).start()
    for half in range(2):
        for j in range(1, INNER):
            go(back(j, half, 1))
        keep(half, 1).start()
    late_grad(f, accl)
    zchunk = zrows // depth
    if zrows > part:
        accl[part:, :] = jnp.zeros((zrows - part, GW), BF)

    def chunk_of(k):
        return pl.ds(pl.multiple_of(k * zchunk, 16), zchunk)

    def late_scatter(k):
        to = lax.rem(z + k, depth)
        return remote(accl.at[chunk_of(to)], zb.at[z], lzs.at[k - 1], lzr.at[k - 1], zpeers[k - 1])

    def late_reduce():
        for k in range(1, fs):
            if k > fs - 1 - slots:
                late_core(k).wait_send()
            late_core(k).wait_recv()
        tot = accl[:part, :].astype(F32)
        for k in range(fs - 1):
            tot = tot + fl[k, :part, :].astype(F32)
        accl[:part, :] = tot.astype(BF)
        for k in range(1, depth):
            late_scatter(k).start()

    def late_gather(k):
        return remote(outl.at[h, chunk_of(z)], outl.at[h, chunk_of(z)], las.at[k - 1], lar.at[k - 1], zpeers[k - 1])

    def late_plane(j, k):
        rws = chunk_of(lax.rem(z - k + depth, depth))
        return remote(outl.at[h, rws], outl.at[h, rws], lps.at[j - 1, k], lpr.at[j - 1, k], hpeers[j - 1])

    def late_sum():
        tot = accl[chunk_of(z), :].astype(F32)
        for k in range(1, depth):
            late_scatter(k).wait_recv()
            tot = tot + zb[lax.rem(z - k + depth, depth)].astype(F32)
        outl[h, chunk_of(z), :] = tot.astype(BF)
        for k in range(1, depth):
            go(late_gather(k))
        for j in range(1, INNER):
            go(late_plane(j, 0))

    def late_forward(k):
        rws = chunk_of(lax.rem(z - k + depth, depth))
        remote(outl.at[h, rws], outl.at[h, rws], las.at[k - 1], lar.at[k - 1], zpeers[k - 1]).wait_recv()
        for j in range(1, INNER):
            go(late_plane(j, k))

    def late_end():
        for j in range(1, INNER):
            i = (h + INNER - j) % INNER
            for k in range(depth):
                rws = chunk_of(lax.rem(z - k + depth, depth))
                remote(outl.at[i, rws], outl.at[i, rws], lps.at[j - 1, k], lpr.at[j - 1, k], hpeers[0]).wait_recv()
        for k in range(1, depth):
            late_scatter(k).wait_send()
        for i in range(INNER):
            ungroup_one(i, outl.at[i, pl.ds(0, part)], stage)
        cp = pltpu.make_async_copy(stage, o_qkv, osem.at[10])
        cp.start()
        outs.append(cp)

    fc = []
    for s in range(n - 1):
        fc += [functools.partial(rs_step, sb, s), functools.partial(rs_step, sa, s)]
    for s in range(n - 1):
        fc += [functools.partial(ag_step, sb, s), functools.partial(ag_step, sa, s)]

    def some(count):
        for task in fc[:count]:
            task()
        del fc[:count]

    some(2)
    late_reduce()
    some(4)
    late_sum()
    for half in range(2):
        for kind in range(2):
            keep(half, kind).wait()
            for j in range(1, INNER):
                back(j, half, kind).wait_recv()
    ungroup_qkv(land, g_qkv)

    def vec_copy(k):
        return remote(vall.at[fpeers[k - 1][1]], vf.at[k - 1], vfs.at[k - 1], vfr.at[k - 1], fpeers[k - 1])

    def norm_back():
        e = nt(g_qkv[...], wbuf[...])
        x = tokens[...].astype(F32)
        center = x - jnp.mean(x, axis=-1, keepdims=True)
        r = lax.rsqrt(jnp.mean(center * center, axis=-1, keepdims=True) + EPS)
        xh = center * r
        t = e * gain[0:1, :]
        o_in[...] = g_hid[...] + r * (t - jnp.mean(t, axis=-1, keepdims=True)
                                      - xh * jnp.mean(t * xh, axis=-1, keepdims=True))
        vall[...] = v_ref[...]
        gq = g_qkv[:, :width].astype(F32)
        gv = g_qkv[:, 2 * width:].astype(F32)
        for row, val in enumerate((e * xh, e, gq, gv)):
            line = jnp.sum(val, axis=0, keepdims=True)
            for i in range(fs):
                vall[i, row:row + 1, :] = line[:, i * part:(i + 1) * part]

    for name in ("w", "tok", "hid"):
        loads[name].wait()
    norm_back()
    for k in range(1, fs):
        go(vec_copy(k))

    def vec_to(peers, buf, at, ssem, rsem):
        return [remote(buf.at[at], buf.at[at], ssem.at[k], rsem.at[k], peer) for k, peer in enumerate(peers)]

    def vec_total(buf, count):
        tot = buf[0]
        for k in range(1, count):
            tot = tot + buf[k]
        return tot

    def vec_plane():
        for k in range(1, fs):
            vec_copy(k).wait_recv()
        tot = vall[f]
        for k in range(fs - 1):
            tot = tot + vf[k]
        vx[h] = tot
        for cp in vec_to(hpeers, vx, h, vxs, vxr):
            go(cp)

    def vec_line():
        for cp in vec_to(hpeers, vx, h, vxs, vxr):
            cp.wait_recv()
        vr[z] = vec_total(vx, INNER)
        for cp in vec_to(zpeers, vr, z, vrs, vrr):
            go(cp)

    def vec_end():
        for cp in vec_to(zpeers, vr, z, vrs, vrr):
            cp.wait_recv()
        vout_ref[...] = vec_total(vr, depth)

    small = [vec_plane, vec_line, vec_end]
    outs = []

    def flush(src, size, dst, u):
        cp = pltpu.make_async_copy(outb.at[pl.ds(src, size)], dst, osem.at[u])
        cp.start()
        outs.append(cp)

    late = [functools.partial(late_forward, k) for k in range(1, depth)]
    i = 0
    while fc or late or small:
        some(2)
        if late:
            late.pop(0)()
        if small:
            small.pop(0)()
    late_end()
    for st in (sb, sa):
        cross_wait(st)
    for u in range(4):
        flush(bases_of[0] + u * part, part, o_fc1.at[:, pl.ds(u * width, width)], u)
        flush(bases_of[1] + u * part, part, o_fc2.at[pl.ds(u * part, part)], 4 + u)
    for i in range(2):
        flush(bases_of[i] + 4 * part, half_part, o_out.at[pl.ds(i * half_part, half_part)], 8 + i)
    for cp in pend:
        cp.wait_send()

    @pl.loop(1, depth)
    def _(step):
        valid = (z - step >= 0, z + step <= depth - 1)
        for half in range(2):
            @pl.when(valid[half])
            def _():
                pass_on(half, step).wait_send()
    for cp in outs:
        cp.wait()


def block_back(starts, do, kept, lse, ops, w_one, tokens, g_hid, gain, v, length, cid):
    qb, kv, ot = kept
    fs = lax.axis_size("fsdp")
    depth = lax.axis_size("ctx") // INNER
    n = lax.axis_size("ctx") // 2
    toks, width = do.shape
    blk = toks // 2
    rows = INNER * blk
    part = width // fs
    big = region_rows(4 * part + part // 2, n)
    tot = 2 * big
    zchunk = -(-part // (16 * depth)) * 16
    zrows = zchunk * depth
    slots = min(fs - 1, 2)
    vs = v.shape[1:]
    dma = pltpu.SemaphoreType.DMA
    vm = pl.BlockSpec(memory_space=pltpu.VMEM)
    anyspec = pl.BlockSpec(memory_space=pl.ANY)
    ins = (do, qb, kv, ot, lse) + tuple(ops) + (w_one, tokens, g_hid)
    order = [do, qb, kv, ot, lse] + list(ops) + [w_one, tokens, g_hid]
    cfg = (depth, length, n, fs, big, zrows)
    return pl.pallas_call(
        functools.partial(back_kernel, cfg),
        out_shape=(jax.ShapeDtypeStruct((part, 3 * width), BF), jax.ShapeDtypeStruct((part, width), BF),
                   jax.ShapeDtypeStruct((part, 4 * width), BF), jax.ShapeDtypeStruct((4 * part, width), BF),
                   jax.ShapeDtypeStruct(vs, F32), jax.ShapeDtypeStruct((toks, width), F32)),
        in_specs=[pl.BlockSpec(memory_space=pltpu.SMEM)] + [anyspec] * len(ins) + [vm, vm],
        out_specs=(anyspec, anyspec, anyspec, anyspec, vm, vm),
        scratch_shapes=[pltpu.VMEM(a.shape, a.dtype) for a in order] + [
            pltpu.VMEM((toks, INNER * QW), BF),
            pltpu.VMEM((2, rows, QW), BF),
            pltpu.VMEM((2, 8, rows), F32),
            pltpu.VMEM((2, 3 * HD, rows), F32),
            pltpu.VMEM((2, rows, KW), F32),
            pltpu.VMEM((2, depth, rows, KW), BF),
            pltpu.VMEM((2, rows, QW), BF),
            pltpu.VMEM((2, rows, KW), BF),
            pltpu.VMEM((toks, INNER * GW), BF),
            pltpu.VMEM((toks, 3 * width), BF),
            pltpu.VMEM((6 * width, toks), BF),
            pltpu.VMEM((width, 2 * rows), BF),
            pltpu.VMEM((slots, tot, width), BF),
            pltpu.VMEM((tot, width), BF),
            pltpu.VMEM((fs - 1, 9 * part, width), BF),
            pltpu.VMEM((big // 2, width), BF), pltpu.VMEM((big // 2, width), BF),
            pltpu.VMEM((n - 1, big // 2 // n, width), BF), pltpu.VMEM((n - 1, big // 2 // n, width), BF),
            pltpu.VMEM((slots, part, GW), BF),
            pltpu.VMEM((zrows, GW), BF),
            pltpu.VMEM((fs - 1, part, GW), BF),
            pltpu.VMEM((depth, zchunk, GW), BF),
            pltpu.VMEM((INNER, zrows, GW), BF),
            pltpu.VMEM((part, 3 * width), BF),
            pltpu.VMEM((fs,) + vs, F32),
            pltpu.VMEM((fs - 1,) + vs, F32),
            pltpu.VMEM((INNER,) + vs, F32),
            pltpu.VMEM((depth,) + vs, F32),
            dma((15,)), dma((6,)), dma((2, 3)), dma((2, 3)), dma((2, depth)), dma((2, depth)),
            dma((2, 3)), dma((2, 3)), dma((2, 3)), dma((2, 3)),
            dma((fs - 1, 2)), dma((fs - 1, 2)), dma((2,)), dma((2,)),
            dma((2, 2, 2, n - 1)), dma((2, 2, 2, n - 1)), dma((2, 2, n)), dma((2, 2, n)),
            dma((fs - 1,)), dma((fs - 1,)), dma((depth - 1,)), dma((depth - 1,)), dma((depth - 1,)), dma((depth - 1,)),
            dma((INNER - 1, depth)), dma((INNER - 1, depth)),
            dma((fs - 1,)), dma((fs - 1,)), dma((INNER - 1,)), dma((INNER - 1,)), dma((depth - 1,)), dma((depth - 1,)), dma((12,)),
        ],
        compiler_params=pltpu.CompilerParams(collective_id=cid, has_side_effects=True, vmem_limit_bytes=62 << 20),
        name="block_back",
    )(starts, *ins, gain, v)


def middle_kernel(fs, attn, tok, cot, vec, c_one, w_out_h, w_one_h, w_two_h,
                  o_layer, o_mid, o_pre, o_act, o_hid, o_branch, o_attn, o_vec,
                  w_out, w_one, w_two, hidden, acc, e_acc, line, b_pre, b_act, b_mid, osem, sem):
    width = attn.shape[1]
    part = width // fs
    first = pltpu.make_async_copy(w_out_h, w_out, sem.at[0])
    first.start()
    ones, twos = [], []
    for j in range(4):
        ones.append(pltpu.make_async_copy(w_one_h.at[:, pl.ds(j * width, width)], w_one.at[j], sem.at[1 + j]))
        twos.append(pltpu.make_async_copy(w_two_h.at[pl.ds(j * width, width)], w_two.at[j], sem.at[5 + j]))
        ones[j].start()
        twos[j].start()
    g = cot[...]
    first.wait()
    hid = tok[...].astype(F32) + nn(attn[...], w_out[...]) + vec[4:5, :]
    hidden[...] = hid
    center = hid - jnp.mean(hid, axis=-1, keepdims=True)
    r = lax.rsqrt(jnp.mean(center * center, axis=-1, keepdims=True) + EPS)
    b_mid[...] = (center * r * vec[5:6, :] + vec[6:7, :]).astype(BF)
    outs = [pltpu.make_async_copy(b_mid, o_mid, osem.at[0])]
    outs[0].start()
    root = (2.0 / jnp.pi) ** 0.5
    for j in range(4):
        lanes = slice(j * width, (j + 1) * width)
        ones[j].wait()
        twos[j].wait()
        p = nn(b_mid[...], w_one[j]) + c_one[:, lanes]
        t = jnp.tanh(root * (p + 0.044715 * (p * p * p)))
        act = (0.5 * p * (1.0 + t)).astype(BF)
        slope = 0.5 * (1.0 + t) + 0.5 * p * (1.0 - t * t) * (root * (1.0 + 3 * 0.044715 * (p * p)))
        b_act[:, lanes] = act
        gp = (nt(g, w_two[j]) * slope).astype(BF)
        b_pre[:, lanes] = gp
        for i, (src, dst) in enumerate(((b_act, o_act), (b_pre, o_pre))):
            outs.append(pltpu.make_async_copy(src.at[:, lanes], dst.at[:, lanes], osem.at[1 + 2 * j + i]))
            outs[-1].start()
        line[:, lanes] = jnp.sum(gp.astype(F32), axis=0, keepdims=True)
        add = nn(act, w_two[j])
        back = nt(gp, w_one[j])
        if j == 0:
            acc[...] = add
            e_acc[...] = back
        else:
            acc[...] = acc[...] + add
            e_acc[...] = e_acc[...] + back
    o_layer[...] = (hidden[...] + acc[...] + vec[7:8, :]).astype(BF)
    hid = hidden[...]
    center = hid - jnp.mean(hid, axis=-1, keepdims=True)
    r = lax.rsqrt(jnp.mean(center * center, axis=-1, keepdims=True) + EPS)
    xh = center * r
    e = e_acc[...]
    t = e * vec[5:6, :]
    gf = g.astype(F32)
    grad = gf + r * (t - jnp.mean(t, axis=-1, keepdims=True) - xh * jnp.mean(t * xh, axis=-1, keepdims=True))
    o_hid[...] = grad
    branch = grad.astype(BF)
    o_branch[...] = branch
    o_attn[...] = nt(branch, w_out[...]).astype(BF)
    o_vec[...] = jnp.zeros_like(o_vec)
    for row, val in ((4, branch.astype(F32)), (5, e * xh), (6, e), (7, gf)):
        total = jnp.sum(val, axis=0, keepdims=True)
        for i in range(fs):
            o_vec[i, row:row + 1, :] = total[:, i * part:(i + 1) * part]
    for i in range(fs):
        for j in range(4):
            o_vec[i, 8 + j:9 + j, :] = line[:, (4 * i + j) * part:(4 * i + j + 1) * part]
    for cp in outs:
        cp.wait()


def middle(attn, tok, cot, vec, c_one, w_out, w_one, w_two):
    fs = lax.axis_size("fsdp")
    toks, width = tok.shape
    full = jax.ShapeDtypeStruct((toks, width), BF)
    wide = jax.ShapeDtypeStruct((toks, 4 * width), BF)
    vm = pl.BlockSpec(memory_space=pltpu.VMEM)
    anyspec = pl.BlockSpec(memory_space=pl.ANY)
    return pl.pallas_call(
        functools.partial(middle_kernel, fs),
        out_shape=(full, full, wide, wide, jax.ShapeDtypeStruct((toks, width), F32), full, full,
                   jax.ShapeDtypeStruct((fs, 16, width // fs), F32)),
        in_specs=[vm] * 5 + [anyspec] * 3,
        out_specs=(vm, anyspec, anyspec, anyspec, vm, vm, vm, vm),
        scratch_shapes=[
            pltpu.VMEM((width, width), BF),
            pltpu.VMEM((4, width, width), BF),
            pltpu.VMEM((4, width, width), BF),
            pltpu.VMEM((toks, width), F32),
            pltpu.VMEM((toks, width), F32),
            pltpu.VMEM((toks, width), F32),
            pltpu.VMEM((1, 4 * width), F32),
            pltpu.VMEM((toks, 4 * width), BF),
            pltpu.VMEM((toks, 4 * width), BF),
            pltpu.VMEM((toks, width), BF),
            pltpu.SemaphoreType.DMA((9,)),
            pltpu.SemaphoreType.DMA((9,)),
        ],
        compiler_params=pltpu.CompilerParams(vmem_limit_bytes=62 << 20),
        name="middle",
    )(attn, tok, cot, vec, c_one, w_out, w_one, w_two)


def per_device(
    stream,
    doc_starts,
    ln1_gain,
    ln1_bias,
    qkv_weight,
    q_bias,
    v_bias,
    out_weight,
    out_bias,
    ln2_gain,
    ln2_bias,
    fc1_weight,
    fc1_bias,
    fc2_weight,
    fc2_bias,
    cotangent,
):
    length = lax.axis_size("ctx") * stream.shape[1]
    part = ln1_gain.shape[0]
    lines = [one.reshape(-1, part) for one in (ln1_gain, ln1_bias, q_bias, v_bias, out_bias, ln2_gain, ln2_bias, fc2_bias,
                                               fc1_bias)]
    v_shard = jnp.concatenate(lines + [jnp.zeros((4, part), BF)], axis=0).astype(F32)
    w_out = lax.all_gather(out_weight, "fsdp", axis=0, tiled=True)
    w_one = lax.all_gather(fc1_weight, "fsdp", axis=0, tiled=True)
    w_two = lax.all_gather(fc2_weight, "fsdp", axis=0, tiled=True)
    tokens, cot = stream[0], cotangent[0]
    attn, normed_group, vec, c_one, w_qkv, q_kept, kv_kept, out_kept, lse = attend(
        doc_starts, tokens, v_shard, qkv_weight, length, 1
    )
    layer_out, normed_mid, grad_pre, activ, grad_hidden, grad_branch, grad_attn, v_part = middle(
        attn, tokens, cot, vec, c_one, w_out, w_one, w_two
    )
    t_qkv, t_out, t_fc1, t_fc2, total, input_grad = block_back(
        doc_starts, grad_attn, (q_kept, kv_kept, out_kept), lse,
        (normed_group, attn, grad_branch, normed_mid, grad_pre, activ, cot),
        w_qkv, tokens, grad_hidden, vec, v_part, length, 0,
    )
    return (
        layer_out[None], input_grad[None], total[0], total[1], t_qkv.astype(F32), total[2], total[3], t_out.astype(F32),
        total[4], total[5], total[6], t_fc1.astype(F32), total[8:12].reshape(-1), t_fc2.astype(F32), total[7],
    )


def solution(mesh):
    in_specs = (
        P("fsdp", "ctx", None),
        P("fsdp", None),
        P("fsdp"),
        P("fsdp"),
        P("fsdp", None),
        P("fsdp"),
        P("fsdp"),
        P("fsdp", None),
        P("fsdp"),
        P("fsdp"),
        P("fsdp"),
        P("fsdp", None),
        P("fsdp"),
        P("fsdp", None),
        P("fsdp"),
        P("fsdp", "ctx", None),
    )
    out_specs = (
        P("fsdp", "ctx", None),
        P("fsdp", "ctx", None),
        P("fsdp"),
        P("fsdp"),
        P("fsdp", None),
        P("fsdp"),
        P("fsdp"),
        P("fsdp", None),
        P("fsdp"),
        P("fsdp"),
        P("fsdp"),
        P("fsdp", None),
        P("fsdp"),
        P("fsdp", None),
        P("fsdp"),
    )
    return jax.shard_map(
        per_device, mesh=mesh, in_specs=in_specs, out_specs=out_specs, check_vma=False
    )
```

```python
import functools

import jax
import jax.numpy as jnp
from jax import lax
from jax.experimental import pallas as pl
from jax.experimental.pallas import tpu as pltpu
from jax.sharding import PartitionSpec as P

H = 12
HD = 64
EPS = 1e-05
MESH = pl.DeviceIdType.MESH
BF = jnp.bfloat16
F32 = jnp.float32


INNER = 4
QW, KW = 256, 384
GW = QW + KW
NEG = -1e30


def nt(a, b):
    return lax.dot_general(a, b, (((1,), (1,)), ((), ())), preferred_element_type=F32)


def nn(a, b):
    return lax.dot_general(a, b, (((1,), (0,)), ((), ())), preferred_element_type=F32)


def head_lanes(x, head):
    if head == 2:
        return x
    lane = lax.broadcasted_iota(jnp.int32, x.shape, 1)
    keep = lane < HD if head == 0 else lane >= HD
    return jnp.where(keep, x, jnp.zeros_like(x))


def first_keys(starts_ref, pos):
    first = jnp.zeros_like(pos)
    for d in range(starts_ref.shape[1]):
        one = starts_ref[0, d]
        first = jnp.maximum(first, jnp.where(one <= pos, one, 0))
    return first


def places():
    c = lax.axis_index("ctx")
    f = lax.axis_index("fsdp")
    return c // INNER, c % INNER, f


def send(src, dst, ssem, rsem, peer):
    return pltpu.make_async_remote_copy(
        src_ref=src, dst_ref=dst, send_sem=ssem, recv_sem=rsem, device_id=peer, device_id_type=MESH
    )


def group_q(src, dst):
    dst_zero = jnp.zeros((dst.shape[0], HD), dst.dtype)
    for i in range(INNER):
        a, o = 3 * i * HD, i * GW
        dst[:, o:o + 3 * HD] = (src[:, a:a + 3 * HD].astype(F32) * (HD ** -0.5)).astype(dst.dtype)
        dst[:, o + 3 * HD:o + QW] = dst_zero


def group_kv(src, dst):
    width = H * HD
    for i in range(INNER):
        a, o = 3 * i * HD, i * GW
        dst[:, o + QW:o + QW + 2 * HD] = src[:, width + a:width + a + 2 * HD]
        dst[:, o + QW + 2 * HD:o + QW + 4 * HD] = src[:, 2 * width + a:2 * width + a + 2 * HD]
        dst[:, o + QW + 4 * HD:o + QW + 5 * HD] = src[:, width + a + 2 * HD:width + a + 3 * HD]
        dst[:, o + QW + 5 * HD:o + QW + 6 * HD] = src[:, 2 * width + a + 2 * HD:2 * width + a + 3 * HD]


def ungroup_qkv(src, dst):
    width = H * HD
    for i in range(INNER):
        a, o = 3 * i * HD, i * GW
        dst[:, a:a + 3 * HD] = src[:, o:o + 3 * HD]
        dst[:, width + a:width + a + 2 * HD] = src[:, o + QW:o + QW + 2 * HD]
        dst[:, 2 * width + a:2 * width + a + 2 * HD] = src[:, o + QW + 2 * HD:o + QW + 4 * HD]
        dst[:, width + a + 2 * HD:width + a + 3 * HD] = src[:, o + QW + 4 * HD:o + QW + 5 * HD]
        dst[:, 2 * width + a + 2 * HD:2 * width + a + 3 * HD] = src[:, o + QW + 5 * HD:o + QW + 6 * HD]


def ungroup_one(i, src, dst):
    width = H * HD
    a = 3 * i * HD
    dst[:, a:a + 3 * HD] = src[:, :3 * HD]
    dst[:, width + a:width + a + 2 * HD] = src[:, QW:QW + 2 * HD]
    dst[:, 2 * width + a:2 * width + a + 2 * HD] = src[:, QW + 2 * HD:QW + 4 * HD]
    dst[:, width + a + 2 * HD:width + a + 3 * HD] = src[:, QW + 4 * HD:QW + 5 * HD]
    dst[:, 2 * width + a + 2 * HD:2 * width + a + 3 * HD] = src[:, QW + 5 * HD:QW + 6 * HD]


def group_rows(src, dst):
    dst_zero = jnp.zeros((dst.shape[0], HD), dst.dtype)
    for i in range(INNER):
        a, o = 3 * i * HD, i * QW
        dst[:, o:o + 2 * HD] = src[:, a:a + 2 * HD]
        dst[:, o + 2 * HD:o + 3 * HD] = dst_zero
        dst[:, o + 3 * HD:o + 4 * HD] = src[:, a + 2 * HD:a + 3 * HD]


def ungroup_rows(src, dst):
    for i in range(INNER):
        a, o = 3 * i * HD, i * QW
        dst[:, a:a + 2 * HD] = src[:, o:o + 2 * HD]
        dst[:, a + 2 * HD:a + 3 * HD] = src[:, o + 3 * HD:o + 4 * HD]


K_LANES = (0, 0, 256)
V_LANES = (128, 128, 256)
Q_LANES = (0, 0, 128)


def mate(h, j):
    return (h + 1 - 2 * (h % 2), h + 2 - 4 * (h // 2), INNER - 1 - h)[j - 1]


def attend_kernel(depth, length, fs, starts_ref, tok_ref, v_shard, w_shard,
                  out_ref, xg_ref, vec_ref, c_one_ref, w_ref, qb_ref, kv_ref, ot_ref, lse_ref,
                  normed_ref, xg, xgs, xgr, xgl, w_all, vbuf, raw_ref, x_ref, qb, kv, acc, top, tot, ob, land,
                  wl, ws, wr, vs, vr, lsem, as_kv, ar_kv, as_q, ar_q, zs, zr, bs, br, osem):
    z, h, f = places()
    c = lax.axis_index("ctx")
    width = H * HD
    part = width // fs
    blk = raw_ref.shape[0] // 2
    rows = INNER * blk
    half_rows = (pl.ds(0, blk), pl.ds(blk, blk))
    fpeers = [(c, lax.rem(f + k, fs)) for k in range(1, fs)]

    barrier = pltpu.get_barrier_semaphore()
    for j in range(1, INNER):
        pl.semaphore_signal(barrier, inc=1, device_id=(z * INNER + (h + j) % INNER, f), device_id_type=MESH)

    @pl.when(z > 0)
    def _():
        pl.semaphore_signal(barrier, inc=1, device_id=((z - 1) * INNER + h, f), device_id_type=MESH)

    @pl.when(z < depth - 1)
    def _():
        pl.semaphore_signal(barrier, inc=1, device_id=((z + 1) * INNER + h, f), device_id_type=MESH)

    for peer in fpeers:
        pl.semaphore_signal(barrier, inc=1, device_id=peer, device_id_type=MESH)

    def piece(half, i):
        p = i if half == 0 else INNER - 1 - i
        return pl.ds(pl.multiple_of(p * blk, blk), blk)

    own = (depth - 1, depth)
    my_rows = pl.ds(pl.multiple_of(f * part, 16), part)

    def w_lanes(b):
        return pl.ds(b * width, width)

    w_own = [pltpu.make_async_copy(w_shard.at[:, w_lanes(b)], w_all.at[my_rows, w_lanes(b)], wl.at[b]) for b in range(3)]
    for b in (1, 2, 0):
        w_own[b].start()
    vbuf[f] = v_shard[...]

    def w_send(k, b):
        return send(w_shard.at[:, w_lanes(b)], w_all.at[my_rows, w_lanes(b)], ws.at[k - 1, b], wr.at[k - 1, b], fpeers[k - 1])

    def v_send(k):
        return send(v_shard, vbuf.at[f], vs.at[k - 1], vr.at[k - 1], fpeers[k - 1])

    pl.semaphore_wait(barrier, INNER - 1 + fs - 1 + jnp.where(z > 0, 1, 0) + jnp.where(z < depth - 1, 1, 0))
    for k in range(1, fs):
        v_send(k).start()
        for b in (1, 2, 0):
            w_send(k, b).start()
    x = tok_ref[...].astype(F32)
    center = x - jnp.mean(x, axis=-1, keepdims=True)
    unit = center * lax.rsqrt(jnp.mean(center * center, axis=-1, keepdims=True) + EPS)
    for k in range(1, fs):
        v_send(k).wait_recv()
    for i in range(fs):
        vec_ref[:, i * part:(i + 1) * part] = vbuf[i, :8, :]
        for j in range(4):
            c_one_ref[:, (4 * i + j) * part:(4 * i + j + 1) * part] = vbuf[i, 8 + j:9 + j, :]
    normed_ref[...] = (unit * vec_ref[0:1, :] + vec_ref[1:2, :]).astype(BF)

    def project(b):
        w_own[b].wait()
        for k in range(1, fs):
            w_send(k, b).wait_recv()
        y = nn(normed_ref[...], w_all[:, b * width:(b + 1) * width])
        if b != 1:
            y = y + vec_ref[(2 if b == 0 else 3):(3 if b == 0 else 4), :]
        raw_ref[:, b * width:(b + 1) * width] = y.astype(BF)

    def a2a(j, half, kind):
        i = mate(h, j)
        lanes = pl.ds(pl.multiple_of(i * GW + (QW if kind else 0), 128), KW if kind else QW)
        dst = kv.at[own[half], piece(half, h)] if kind else qb.at[half, piece(half, h)]
        sems = (as_kv.at[half, j - 1], ar_kv.at[half, j - 1]) if kind else (as_q.at[half, j - 1], ar_q.at[half, j - 1])
        return send(x_ref.at[half_rows[half], lanes], dst, *sems, (z * INNER + i, f))

    def local(half, kind):
        lanes = pl.ds(pl.multiple_of(h * GW + (QW if kind else 0), 128), KW if kind else QW)
        dst = kv.at[own[half], piece(half, h)] if kind else qb.at[half, piece(half, h)]
        return pltpu.make_async_copy(x_ref.at[half_rows[half], lanes], dst, lsem.at[half, kind])

    def spread(kind):
        for j in range(1, INNER):
            for half in range(2):
                a2a(j, half, kind).start()
                if j == 1:
                    local(half, kind).start()

    project(1)
    project(2)
    group_kv(raw_ref, x_ref)
    spread(1)
    project(0)
    group_q(raw_ref, x_ref)
    spread(0)
    w_out_copy = pltpu.make_async_copy(w_all, w_ref, osem.at[3])
    w_out_copy.start()

    def plane(j, half):
        return send(normed_ref.at[half_rows[half]], xg.at[half, piece(half, h)], xgs.at[half, j - 1], xgr.at[half, j - 1],
                    (z * INNER + mate(h, j), f))

    def plane_own(half):
        return pltpu.make_async_copy(normed_ref.at[half_rows[half]], xg.at[half, piece(half, h)], xgl.at[half])

    for half in range(2):
        plane_own(half).start()

    def relay(half, src_slot, step, p):
        rws = pl.ds(pl.multiple_of(p * blk, blk), blk)
        if half == 0:
            peer, slot = (z + 1) * INNER + h, step - 1
        else:
            peer, slot = (z - 1) * INNER + h, z - 1 + step - 1
        return send(kv.at[src_slot, rws], kv.at[slot, rws], zs.at[half, step - 1, p], zr.at[half, step - 1, p], (peer, f))

    can = (z < depth - 1, z > 0)
    for j in range(INNER):
        i = h if j == 0 else mate(h, j)
        for half in range(2):
            if j == 0:
                local(half, 1).wait()
            else:
                a2a(j, half, 1).wait_recv()

            @pl.when(can[half])
            def _():
                relay(half, own[half], 1, i if half == 0 else INNER - 1 - i).start()

    for half in range(2):
        local(half, 0).wait()
        for j in range(1, INNER):
            a2a(j, half, 0).wait_recv()
    for half in range(2):
        for j in range(1, INNER):
            plane(j, half).start()

    def base_of(half, zz):
        return zz * rows if half == 0 else length - (zz + 1) * rows

    cols = rows // 2

    def tile(half, slot, q_base, k_base, diag):
        for head in range(3):
            k_all = kv[slot, :, K_LANES[head]:K_LANES[head] + 128]
            v_all = kv[slot, :, V_LANES[head]:V_LANES[head] + 128]
            v_t = v_all.T[(0 if head == 0 else HD):(HD if head == 0 else 2 * HD)]
            for part in range(2):
                keys = (part + 1) * cols if diag else rows
                lanes = slice(part * cols, (part + 1) * cols)
                q = head_lanes(qb[half, lanes, Q_LANES[head]:Q_LANES[head] + 128], head)
                pos = q_base + part * cols + lax.broadcasted_iota(jnp.int32, (1, cols), 1)
                first = first_keys(starts_ref, pos) - k_base
                s = nt(k_all[:keys], q)
                row = lax.broadcasted_iota(jnp.int32, (keys, cols), 0)
                ok = row >= first
                if diag:
                    ok = ok & (row <= pos - k_base)
                s = jnp.where(ok, s, NEG)
                line = slice(head, head + 1)
                feats = slice(head * HD, (head + 1) * HD)
                high = jnp.max(s, axis=0, keepdims=True)
                if not diag:
                    before = top[half, line, lanes]
                    high = jnp.maximum(before, high)
                    fade = jnp.exp(before - high)
                w = jnp.exp(s - high)
                add = jnp.sum(w, axis=0, keepdims=True)
                o = nn(v_t[:, :keys], w.astype(BF))
                if diag:
                    tot[half, line, lanes] = add
                    acc[half, feats, lanes] = o
                else:
                    tot[half, line, lanes] = tot[half, line, lanes] * fade + add
                    acc[half, feats, lanes] = acc[half, feats, lanes] * fade + o
                top[half, line, lanes] = high

    @pl.loop(0, 2)
    def _(half):
        q_base = jnp.where(half == 0, base_of(0, z), base_of(1, z))
        tile(half, depth - 1 + half, q_base, q_base, True)

    @pl.loop(1, depth)
    def _(step):
        valid = (z - step >= 0, z + step <= depth - 1)
        slots = (step - 1, z + step - 1)
        for half in range(2):
            for p in range(INNER):
                @pl.when(valid[half])
                def _():
                    rws = pl.ds(p * blk, blk)
                    send(kv.at[slots[half], rws], kv.at[slots[half], rws], zs.at[half, step - 1, p],
                         zr.at[half, step - 1, p], (z * INNER + (h + 1) % INNER, f)).wait_recv()

                @pl.when(valid[half] & can[half])
                def _():
                    relay(half, slots[half], step + 1, p).start()

        @pl.loop(0, 2)
        def _(half):
            @pl.when(jnp.where(half == 0, z - step, depth - 1 - z - step) >= 0)
            def _():
                zz = jnp.where(half == 0, z - step, z + step)
                q_base = jnp.where(half == 0, base_of(0, z), base_of(1, z))
                k_base = jnp.where(half == 0, base_of(0, zz), base_of(1, zz))
                tile(half, jnp.where(half == 0, step - 1, z + step - 1), q_base, k_base, False)

    for half in range(2):
        plane_own(half).wait()
        for j in range(1, INNER):
            plane(j, half).wait_recv()
    ob[:, :, 2 * HD:3 * HD] = jnp.zeros((2, rows, HD), BF)
    for half in range(2):
        lse_ref[half] = top[half] + jnp.log(tot[half])
        for head in range(3):
            feats = slice(head * HD, (head + 1) * HD)
            acc[half, feats, :] = acc[half, feats, :] / tot[half, head:head + 1, :]
        ob[half, :, :2 * HD] = acc[half, :2 * HD, :].T.astype(BF)
        ob[half, :, 3 * HD:] = acc[half, 2 * HD:, :].T.astype(BF)
    outs = [pltpu.make_async_copy(qb, qb_ref, osem.at[0]), pltpu.make_async_copy(kv, kv_ref, osem.at[1]),
            pltpu.make_async_copy(acc, ot_ref, osem.at[2]), pltpu.make_async_copy(xg, xg_ref, osem.at[4])]
    for cp in outs:
        cp.start()

    def back(j, half):
        i = mate(h, j)
        return send(ob.at[half, piece(half, i)], land.at[half_rows[half], pl.ds(pl.multiple_of(h * QW, 128), QW)],
                    bs.at[half, j - 1], br.at[half, j - 1], (z * INNER + i, f))

    for half in range(2):
        for j in range(1, INNER):
            back(j, half).start()
        mine = pltpu.make_async_copy(ob.at[half, piece(half, h)],
                                     land.at[half_rows[half], pl.ds(pl.multiple_of(h * QW, 128), QW)], lsem.at[half, 0])
        mine.start()
        mine.wait()
    for half in range(2):
        for j in range(1, INNER):
            back(j, half).wait_recv()
    ungroup_rows(land, out_ref)
    for half in range(2):
        for j in range(1, INNER):
            a2a(j, half, 1).wait_send()
            a2a(j, half, 0).wait_send()
            back(j, half).wait_send()
            plane(j, half).wait_send()

        @pl.when(can[half])
        def _():
            for p in range(INNER):
                relay(half, own[half], 1, p).wait_send()

    @pl.loop(1, depth)
    def _(step):
        valid = (z - step >= 0, z + step <= depth - 1)
        for half in range(2):
            @pl.when(valid[half] & can[half])
            def _():
                for p in range(INNER):
                    relay(half, own[half], step + 1, p).wait_send()
    for k in range(1, fs):
        v_send(k).wait_send()
        for b in range(3):
            w_send(k, b).wait_send()
    for cp in outs + [w_out_copy]:
        cp.wait()


def attend(starts, x, v_shard, w_shard, length, cid):
    depth = lax.axis_size("ctx") // INNER
    fs = lax.axis_size("fsdp")
    blk = x.shape[0] // 2
    width = x.shape[1]
    rows = INNER * blk
    dma = pltpu.SemaphoreType.DMA
    shapes = (
        jax.ShapeDtypeStruct((x.shape[0], width), BF),
        jax.ShapeDtypeStruct((2, rows, width), BF),
        jax.ShapeDtypeStruct((8, width), F32),
        jax.ShapeDtypeStruct((1, 4 * width), F32),
        jax.ShapeDtypeStruct((width, 3 * width), BF),
        jax.ShapeDtypeStruct((2, rows, QW), BF),
        jax.ShapeDtypeStruct((depth + 1, rows, KW), BF),
        jax.ShapeDtypeStruct((2, 3 * HD, rows), F32),
        jax.ShapeDtypeStruct((2, 8, rows), F32),
    )
    vm = pl.BlockSpec(memory_space=pltpu.VMEM)
    anyspec = pl.BlockSpec(memory_space=pl.ANY)
    return pl.pallas_call(
        functools.partial(attend_kernel, depth, length, fs),
        out_shape=shapes,
        in_specs=[pl.BlockSpec(memory_space=pltpu.SMEM), vm, vm, anyspec],
        out_specs=(vm, anyspec, vm, vm, anyspec, anyspec, anyspec, anyspec, vm),
        scratch_shapes=[
            pltpu.VMEM((x.shape[0], width), BF),
            pltpu.VMEM((2, rows, width), BF),
            dma((2, 3)), dma((2, 3)), dma((2,)),
            pltpu.VMEM((width, 3 * width), BF),
            pltpu.VMEM((fs,) + v_shard.shape, F32),
            pltpu.VMEM((2 * blk, 3 * width), BF),
            pltpu.VMEM((2 * blk, INNER * GW), BF),
            pltpu.VMEM((2, rows, QW), BF),
            pltpu.VMEM((depth + 1, rows, KW), BF),
            pltpu.VMEM((2, 3 * HD, rows), F32),
            pltpu.VMEM((2, 8, rows), F32),
            pltpu.VMEM((2, 8, rows), F32),
            pltpu.VMEM((2, rows, QW), BF),
            pltpu.VMEM((2 * blk, INNER * QW), BF),
            dma((3,)), dma((fs - 1, 3)), dma((fs - 1, 3)), dma((fs - 1,)), dma((fs - 1,)),
            dma((2, 2)), dma((2, 3)), dma((2, 3)), dma((2, 3)), dma((2, 3)),
            dma((2, depth, INNER)), dma((2, depth, INNER)), dma((2, 3)), dma((2, 3)), dma((5,)),
        ],
        compiler_params=pltpu.CompilerParams(collective_id=cid, has_side_effects=True, vmem_limit_bytes=62 << 20),
        name="attend",
    )(starts, x, v_shard, w_shard)


def ring_pos(z, bit, depth):
    return jnp.where(bit == 0, z, 2 * depth - 1 - z)


def ring_ctx(pos, depth, kind, fixed):
    pos = lax.rem(pos + 2 * depth, 2 * depth)
    z = jnp.where(pos < depth, pos, 2 * depth - 1 - pos)
    bit = jnp.where(pos < depth, 0, 1)
    return z * INNER + (bit * 2 + fixed if kind == 0 else fixed * 2 + bit)


def halves_of(chunk):
    first = -(-(chunk // 16) // 2) * 16
    return ((0, first), (first, chunk - first)) if chunk > first else ((0, chunk),)


def region_rows(used, n):
    return -(-used // (32 * n)) * 32 * n


def back_kernel(cfg, starts_ref, h_do, h_qb, h_kv, h_ot, h_lse, h_xg, h_out, h_gout, h_mid, h_gpre, h_act, h_gtop,
                h_w, h_tok, h_hid, gain, v_ref,
                o_qkv, o_out, o_fc1, o_fc2, vout_ref, o_in,
                raw, qb, kv, ot, lse, xg, x_out, g_out, x_mid, g_pre, x_act, g_top, wbuf, tokens, g_hid,
                do_ref, dob, dots, dq, dkvd, rbuf, dqb, fin, land, g_qkv,
                xt, xtg, gbuf, acc, fbuf, pa, pb, ra, rb, gl, accl, fl, zb, outl, stage,
                vall, vf, vx, vr,
                ldsem, lsem, as_o, ar_o, zs, zr, bq, brq, bk, brk,
                fsem, frec, ps, pr, rs, rr, xgs, xgr, lfs, lfr, lzs, lzr, las, lar, lps, lpr, vfs, vfr, vxs, vxr, vrs, vrr, osem):
    depth, length, n, fs, big, zrows = cfg
    z, h, f = places()
    c = lax.axis_index("ctx")
    bits = (h % 2, h // 2)
    poss = (ring_pos(z, bits[1], depth), ring_pos(z, bits[0], depth))
    pairs_of = ((c + 1 - 2 * bits[0], f), (c + 2 - 4 * bits[1], f))
    rights = tuple((ring_ctx(poss[k] + 1, depth, k, bits[k]), f) for k in range(2))
    lefts = tuple((ring_ctx(poss[k] - 1, depth, k, bits[k]), f) for k in range(2))
    fpeers = [(c, lax.rem(f + k, fs)) for k in range(1, fs)]
    width = acc.shape[1]
    lanes = (pl.ds(0, width // 2), pl.ds(width // 2, width // 2))
    part = width // fs
    bases_of = (0, big)
    outb = gbuf.at[0]
    slots = gbuf.shape[0]
    blk = raw.shape[0] // 2
    rows = INNER * blk
    cols = rows // 2
    half_rows = (pl.ds(0, blk), pl.ds(blk, blk))

    zpeers = [(lax.rem(z + k, depth) * INNER + h, f) for k in range(1, depth)]
    hpeers = [(z * INNER + (h + j) % INNER, f) for j in range(1, INNER)]
    barrier = pltpu.get_barrier_semaphore()
    for peer in hpeers + zpeers + list(rights) + list(lefts) + fpeers:
        pl.semaphore_signal(barrier, inc=1, device_id=peer, device_id_type=MESH)

    loads = {}
    pairs = (("do", h_do, raw), ("act", h_act, x_act), ("gtop", h_gtop, g_top), ("out", h_out, x_out),
             ("gout", h_gout, g_out), ("mid", h_mid, x_mid), ("gpre", h_gpre, g_pre), ("ot", h_ot, ot),
             ("kv", h_kv, kv), ("qb", h_qb, qb), ("lse", h_lse, lse), ("xg", h_xg, xg), ("w", h_w, wbuf),
             ("tok", h_tok, tokens), ("hid", h_hid, g_hid))
    for i, (name, src, dst) in enumerate(pairs):
        loads[name] = pltpu.make_async_copy(src, dst, ldsem.at[i])
        loads[name].start()

    pend = []

    def go(cp):
        cp.start()
        pend.append(cp)
        return cp

    def piece(half, i):
        p = i if half == 0 else INNER - 1 - i
        return pl.ds(pl.multiple_of(p * blk, blk), blk)

    def spread(j, half):
        i = (h + j) % INNER
        return send(do_ref.at[half_rows[half], pl.ds(pl.multiple_of(i * QW, 128), QW)], dob.at[half, piece(half, h)],
                    as_o.at[half, j - 1], ar_o.at[half, j - 1], (z * INNER + i, f))

    loads["do"].wait()
    group_rows(raw, do_ref)
    pl.semaphore_wait(barrier, INNER - 1 + depth - 1 + 4 + fs - 1)
    mine = []
    for half in range(2):
        for j in range(1, INNER):
            go(spread(j, half))
        cp = pltpu.make_async_copy(do_ref.at[half_rows[half], pl.ds(pl.multiple_of(h * QW, 128), QW)],
                                   dob.at[half, piece(half, h)], lsem.at[half])
        cp.start()
        mine.append(cp)

    eye_n = 256
    eye = (lax.broadcasted_iota(jnp.int32, (eye_n, eye_n), 0)
           == lax.broadcasted_iota(jnp.int32, (eye_n, eye_n), 1)).astype(BF)
    offset = {"act": 0, "mid": 4 * width, "out": 5 * width}

    def turn_over(name, ref):
        @pl.loop(0, ref.shape[1] // eye_n)
        def _(b):
            o = pl.multiple_of(b * eye_n, eye_n)
            xt[pl.ds(pl.multiple_of(offset[name] + o, eye_n), eye_n), :] = nt(eye, ref[:, pl.ds(o, eye_n)]).astype(BF)

    def unit(name, start, g, dst, row, size):
        lhs = xt[pl.ds(pl.multiple_of(offset[name] + start, 16), size), :]
        dst[pl.ds(pl.multiple_of(row, 16), size), :] = nn(lhs, g).astype(BF)

    half_part = part // 2

    def fc2_for(owner, dst):
        @pl.loop(0, 4)
        def _(j):
            unit("act", owner * 4 * part + j * part, g_top[...], dst, bases_of[1] + j * part, part)
        unit("out", owner * part + half_part, g_out[...], dst, bases_of[1] + 4 * part, half_part)

    def fc1_for(owner, dst):
        @pl.loop(0, 4)
        def _(j):
            unit("mid", owner * part, g_pre[:, pl.ds(pl.multiple_of(j * width, 128), width)], dst,
                 bases_of[0] + j * part, part)
        unit("out", owner * part, g_out[...], dst, bases_of[0] + 4 * part, half_part)

    used = 4 * part + half_part
    cuts = ((bases_of[0], used, 0), (bases_of[1], used, used))

    def to_core(k, j):
        a, m, at = cuts[j]
        return remote(gbuf.at[(k - 1) % slots, pl.ds(a, m)], fbuf.at[k - 1, pl.ds(at, m)],
                      fsem.at[k - 1, j], frec.at[k - 1, j], fpeers[k - 1])

    def remote(src, dst, ssem, rsem, peer):
        return send(src, dst, ssem, rsem, peer)

    def share(j, make):
        for k in range(1, fs):
            if k - 1 >= slots:
                to_core(k - slots, j).wait_send()
            make(fpeers[k - 1][1], gbuf.at[(k - 1) % slots])
            to_core(k, j).start()

    def collect(j):
        for k in range(1, fs):
            if k > fs - 1 - slots:
                to_core(k, j).wait_send()
            to_core(k, j).wait_recv()
        a, m, at = cuts[j]
        step = 32 if m % 32 == 0 else 16

        @pl.loop(0, m // step)
        def _(i):
            rws = pl.ds(pl.multiple_of(a + i * step, step), step)
            tot = acc[rws, :].astype(F32)
            for k in range(fs - 1):
                tot = tot + fbuf[k, pl.ds(pl.multiple_of(at + i * step, step), step), :].astype(F32)
            acc[rws, :] = tot.astype(BF)

    for (a, m, _), size in zip(cuts, (big, big)):
        if size > m:
            acc[a + m:a + size, :] = jnp.zeros((size - m, width), BF)

    def stream(i, kind, pbuf, rbuf_):
        half = big // 2
        keep_at = pl.multiple_of(bases_of[i] + bits[kind] * half, 16)
        give_at = pl.multiple_of(bases_of[i] + (1 - bits[kind]) * half, 16)
        return (i, kind, keep_at, give_at, half, half // n, pbuf, rbuf_)

    sa, sb = stream(0, 0, pa, ra), stream(1, 1, pb, rb)

    def rows_of(st, k, base=None):
        k = lax.rem(k + 2 * n, n)
        return pl.ds(pl.multiple_of((st[2] if base is None else base) + k * st[5], 16), st[5])

    def pair_copy(st):
        return remote(acc.at[pl.ds(st[3], st[4])], st[6], ps.at[st[0]], pr.at[st[0]], pairs_of[st[1]])

    def pair_add(st):
        pair_copy(st).wait_recv()
        step = 32 if st[4] % 32 == 0 else 16

        @pl.loop(0, st[4] // step)
        def _(i):
            rws = pl.ds(pl.multiple_of(st[2] + i * step, 16), step)
            acc[rws, :] = (acc[rws, :].astype(F32)
                           + st[6][pl.ds(pl.multiple_of(i * step, 16), step), :].astype(F32)).astype(BF)

    def sub_rows(st, k, j):
        off, size = halves_of(st[5])[j]
        k = lax.rem(k + 2 * n, n)
        return pl.ds(pl.multiple_of(st[2] + k * st[5] + off, 16), size)

    subs = range(len(halves_of(big // 2 // n)))

    def rs_copy(st, s, d, j):
        p = poss[st[1]]
        off, size = halves_of(st[5])[j]
        return remote(acc.at[sub_rows(st, p - 1 - s if d == 0 else p + 1 + s, j), lanes[d]],
                      st[7].at[s, pl.ds(off, size), lanes[d]],
                      rs.at[st[0], 0, d, s, j], rr.at[st[0], 0, d, s, j], (rights if d == 0 else lefts)[st[1]])

    def rs_start(st):
        for j in subs:
            for d in range(2):
                go(rs_copy(st, 0, d, j))

    def rs_step(st, s):
        p = poss[st[1]]
        for j in subs:
            off, size = halves_of(st[5])[j]
            for d in range(2):
                rws = sub_rows(st, p - 2 - s if d == 0 else p + 2 + s, j)
                rs_copy(st, s, d, j).wait_recv()
                tot = (acc[rws, lanes[d]].astype(F32) + st[7][s, off:off + size, lanes[d]].astype(F32)).astype(BF)
                if s < n - 2:
                    acc[rws, lanes[d]] = tot
                    go(rs_copy(st, s + 1, d, j))
                else:
                    outb[rws, lanes[d]] = tot
                    go(ag_copy(st, 0, d, j))
        if s == n - 2:
            for d in range(2):
                go(cross(st, 0, d))

    def ag_copy(st, s, d, j):
        p = poss[st[1]]
        rws = sub_rows(st, p - s if d == 0 else p + s, j)
        return remote(outb.at[rws, lanes[d]], outb.at[rws, lanes[d]],
                      rs.at[st[0], 1, d, s, j], rr.at[st[0], 1, d, s, j], (rights if d == 0 else lefts)[st[1]])

    def cross(st, s, d, base=None):
        p = poss[st[1]]
        rws = rows_of(st, p - s if d == 0 else p + s, base)
        return remote(outb.at[rws, lanes[d]], outb.at[rws, lanes[d]], xgs.at[st[0], d, s], xgr.at[st[0], d, s],
                      pairs_of[st[1]])

    def ag_step(st, s):
        p = poss[st[1]]
        for j in subs:
            for d in range(2):
                rws = sub_rows(st, p - 1 - s if d == 0 else p + 1 + s, j)
                remote(outb.at[rws, lanes[d]], outb.at[rws, lanes[d]],
                       rs.at[st[0], 1, d, s, j], rr.at[st[0], 1, d, s, j], pairs_of[0]).wait_recv()
                if s < n - 2:
                    go(ag_copy(st, s + 1, d, j))
        for d in range(2):
            go(cross(st, s + 1, d))

    def cross_wait(st):
        for s in range(n):
            for d in range(2):
                cross(st, s, d, st[3]).wait_recv()

    loads["act"].wait()
    turn_over("act", x_act)
    loads["gtop"].wait()
    loads["out"].wait()
    turn_over("out", x_out)
    loads["gout"].wait()
    share(1, fc2_for)
    loads["mid"].wait()
    turn_over("mid", x_mid)
    loads["gpre"].wait()
    share(0, fc1_for)
    dq[...] = jnp.zeros_like(dq)
    loads["ot"].wait()
    for half in range(2):
        mine[half].wait()
        for j in range(1, INNER):
            spread(j, half).wait_recv()
        for head in range(3):
            ln = slice(0, 128) if head < 2 else slice(128, 256)
            g = dob[half, :, ln].astype(F32).T[(0 if head == 0 else HD):(HD if head == 0 else 2 * HD)]
            dots[half, head:head + 1, :] = jnp.sum(g * ot[half, head * HD:(head + 1) * HD, :], axis=0, keepdims=True)
    for name in ("kv", "qb", "lse"):
        loads[name].wait()

    def base_of(half, zz):
        return zz * rows if half == 0 else length - (zz + 1) * rows

    def bases(half, zz):
        return jnp.where(half == 0, base_of(0, zz), base_of(1, zz))

    def tile(half, slot, q_base, k_base, diag, head):
        k_all = kv[slot, :, K_LANES[head]:K_LANES[head] + 128]
        v_all = kv[slot, :, V_LANES[head]:V_LANES[head] + 128]
        k_t = k_all.T[(HD if head == 1 else 0):(2 * HD if head == 1 else HD)]
        kl = slice(K_LANES[head], K_LANES[head] + 128)
        vl = slice(V_LANES[head], V_LANES[head] + 128)
        for half_cols in range(2):
            keys = (half_cols + 1) * cols if diag else rows
            ln = slice(half_cols * cols, (half_cols + 1) * cols)
            q = head_lanes(qb[half, ln, Q_LANES[head]:Q_LANES[head] + 128], head)
            g = head_lanes(dob[half, ln, Q_LANES[head]:Q_LANES[head] + 128], head)
            p = q_base + half_cols * cols + lax.broadcasted_iota(jnp.int32, (1, cols), 1)
            first = first_keys(starts_ref, p) - k_base
            s = nt(k_all[:keys], q)
            row = lax.broadcasted_iota(jnp.int32, (keys, cols), 0)
            ok = row >= first
            if diag:
                ok = ok & (row <= p - k_base)
            line = slice(head, head + 1)
            w = jnp.where(ok, jnp.exp(s - lse[half, line, ln]), 0.0)
            gp = nt(v_all[:keys], g)
            ds = (w * (gp - dots[half, line, ln])).astype(BF)
            dv = nn(w.astype(BF), g)
            dk = nn(ds, q)
            for sl, val in (((kl, dk + dv),) if head == 2 else ((kl, dk), (vl, dv))):
                if head != 1 and half_cols == 0:
                    dkvd[half, :keys, sl] = val
                elif head != 1 and diag:
                    dkvd[half, :cols, sl] = dkvd[half, :cols, sl] + val[:cols]
                    dkvd[half, cols:, sl] = val[cols:]
                else:
                    dkvd[half, :keys, sl] = dkvd[half, :keys, sl] + val
            feats = slice(head * HD, (head + 1) * HD)
            dq[half, feats, ln] = dq[half, feats, ln] + nn(k_t[:, :keys], ds)

    has = (z < depth - 1, z > 0)

    def pass_on(half, step):
        peer = (z - 1) * INNER + h if half == 0 else (z + 1) * INNER + h
        return send(rbuf.at[half, step], rbuf.at[half, step - 1], zs.at[half, step - 1], zr.at[half, step - 1], (peer, f))

    def take(half, step):
        return send(rbuf.at[half, step], rbuf.at[half, step], zs.at[half, step], zr.at[half, step],
                    (z * INNER + (h + 1) % INNER, f))

    @pl.loop(0, 2 * (depth - 1))
    def _(it):
        step = depth - 1 - it // 2
        half = it % 2
        valid = jnp.where(half == 0, z - step, depth - 1 - z - step) >= 0
        zz = jnp.where(half == 0, z - step, z + step)

        @pl.when(it == 2)
        def _():
            fc2_for(f, acc)
            collect(1)
            pair_copy(sb).start()
            fc1_for(f, acc)
            collect(0)
            pair_copy(sa).start()

        for head in range(3):
            @pl.when(valid)
            def _():
                tile(half, jnp.where(half == 0, step - 1, z + step - 1), bases(half, z), bases(half, zz), False, head)

        @pl.when(valid)
        def _():
            more = jnp.where(half == 0, depth - 1 - z, z) > 0

            @pl.when(more)
            def _():
                take(half, step).wait_recv()

                @pl.loop(0, rows // 64)
                def _(b):
                    rws = pl.ds(pl.multiple_of(b * 64, 64), 64)
                    rbuf[half, step, rws, :] = (dkvd[half, rws, :] + rbuf[half, step, rws, :].astype(F32)).astype(BF)

            @pl.when(jnp.logical_not(more))
            def _():
                rbuf[half, step] = dkvd[half].astype(BF)

            @pl.when(half == 0)
            def _():
                pass_on(0, step).start()

            @pl.when(half == 1)
            def _():
                pass_on(1, step).start()

    pend.extend((pair_copy(sb), pair_copy(sa)))

    @pl.loop(0, 2)
    def _(half):
        for head in range(3):
            tile(half, depth - 1 + half, bases(half, z), bases(half, z), True, head)

    def back(j, half, kind):
        i = (h + j) % INNER
        ln = pl.ds(pl.multiple_of(h * GW + (QW if kind else 0), 128), KW if kind else QW)
        src = fin if kind else dqb
        sems = (bk.at[half, j - 1], brk.at[half, j - 1]) if kind else (bq.at[half, j - 1], brq.at[half, j - 1])
        return send(src.at[half, piece(half, i)], land.at[half_rows[half], ln], *sems, (z * INNER + i, f))

    def keep(half, kind):
        ln = pl.ds(pl.multiple_of(h * GW + (QW if kind else 0), 128), KW if kind else QW)
        src = fin if kind else dqb
        return pltpu.make_async_copy(src.at[half, piece(half, h)], land.at[half_rows[half], ln],
                                     lsem.at[2 + 2 * half + kind])

    dqb[:, :, 3 * HD:] = jnp.zeros((2, rows, HD), BF)
    for half in range(2):
        dqb[half, :, :2 * HD] = (dq[half, :2 * HD, :] * (HD ** -0.5)).T.astype(BF)
        dqb[half, :, 2 * HD:3 * HD] = (dq[half, 2 * HD:, :] * (HD ** -0.5)).T.astype(BF)
        for j in range(1, INNER):
            go(back(j, half, 0))
        keep(half, 0).start()
    for st in (sb, sa):
        pair_add(st)
        rs_start(st)
    def late_core(k):
        return remote(gl.at[(k - 1) % slots], fl.at[k - 1], lfs.at[k - 1], lfr.at[k - 1], fpeers[k - 1])

    def late_grad(owner, dst):
        for lo, hi, src in ((0, QW, dqb), (QW, GW, fin)):
            tot = None
            for half in range(2):
                one = nn(xtg[pl.ds(pl.multiple_of(owner * part, 16), part), half * rows:(half + 1) * rows], src[half])
                tot = one if tot is None else tot + one
            dst[:part, lo:hi] = tot.astype(BF)

    loads["xg"].wait()
    for half in range(2):
        for r in range(rows // eye_n):
            @pl.loop(0, width // eye_n)
            def _(b):
                o = pl.multiple_of(b * eye_n, eye_n)
                xtg[pl.ds(o, eye_n), half * rows + r * eye_n:half * rows + (r + 1) * eye_n] = nt(
                    eye, xg[half, r * eye_n:(r + 1) * eye_n, pl.ds(o, eye_n)]).astype(BF)
    for half in range(2):
        @pl.when(has[half])
        def _():
            take(half, 0).wait_recv()

            @pl.loop(0, rows // 64)
            def _(b):
                rws = pl.ds(pl.multiple_of(b * 64, 64), 64)
                fin[half, rws, :] = (dkvd[half, rws, :] + rbuf[half, 0, rws, :].astype(F32)).astype(BF)

        @pl.when(jnp.logical_not(has[half]))
        def _():
            fin[half] = dkvd[half].astype(BF)
    for k in range(1, fs):
        if k - 1 >= slots:
            late_core(k - slots).wait_send()
        late_grad(fpeers[k - 1][1], gl.at[(k - 1) % slots])
        late_core(k).start()
    for half in range(2):
        for j in range(1, INNER):
            go(back(j, half, 1))
        keep(half, 1).start()
    late_grad(f, accl)
    zchunk = zrows // depth
    if zrows > part:
        accl[part:, :] = jnp.zeros((zrows - part, GW), BF)

    def chunk_of(k):
        return pl.ds(pl.multiple_of(k * zchunk, 16), zchunk)

    def late_scatter(k):
        to = lax.rem(z + k, depth)
        return remote(accl.at[chunk_of(to)], zb.at[z], lzs.at[k - 1], lzr.at[k - 1], zpeers[k - 1])

    def late_reduce():
        for k in range(1, fs):
            if k > fs - 1 - slots:
                late_core(k).wait_send()
            late_core(k).wait_recv()
        tot = accl[:part, :].astype(F32)
        for k in range(fs - 1):
            tot = tot + fl[k, :part, :].astype(F32)
        accl[:part, :] = tot.astype(BF)
        for k in range(1, depth):
            late_scatter(k).start()

    def late_gather(k):
        return remote(outl.at[h, chunk_of(z)], outl.at[h, chunk_of(z)], las.at[k - 1], lar.at[k - 1], zpeers[k - 1])

    def late_plane(j, k):
        rws = chunk_of(lax.rem(z - k + depth, depth))
        return remote(outl.at[h, rws], outl.at[h, rws], lps.at[j - 1, k], lpr.at[j - 1, k], hpeers[j - 1])

    def late_sum():
        tot = accl[chunk_of(z), :].astype(F32)
        for k in range(1, depth):
            late_scatter(k).wait_recv()
            tot = tot + zb[lax.rem(z - k + depth, depth)].astype(F32)
        outl[h, chunk_of(z), :] = tot.astype(BF)
        for k in range(1, depth):
            go(late_gather(k))
        for j in range(1, INNER):
            go(late_plane(j, 0))

    def late_forward(k):
        rws = chunk_of(lax.rem(z - k + depth, depth))
        remote(outl.at[h, rws], outl.at[h, rws], las.at[k - 1], lar.at[k - 1], zpeers[k - 1]).wait_recv()
        for j in range(1, INNER):
            go(late_plane(j, k))

    def late_end():
        for j in range(1, INNER):
            i = (h + INNER - j) % INNER
            for k in range(depth):
                rws = chunk_of(lax.rem(z - k + depth, depth))
                remote(outl.at[i, rws], outl.at[i, rws], lps.at[j - 1, k], lpr.at[j - 1, k], hpeers[0]).wait_recv()
        for k in range(1, depth):
            late_scatter(k).wait_send()
        for i in range(INNER):
            ungroup_one(i, outl.at[i, pl.ds(0, part)], stage)
        cp = pltpu.make_async_copy(stage, o_qkv, osem.at[10])
        cp.start()
        outs.append(cp)

    fc = []
    for s in range(n - 1):
        fc += [functools.partial(rs_step, sb, s), functools.partial(rs_step, sa, s)]
    for s in range(n - 1):
        fc += [functools.partial(ag_step, sb, s), functools.partial(ag_step, sa, s)]

    def some(count):
        for task in fc[:count]:
            task()
        del fc[:count]

    some(2)
    late_reduce()
    some(4)
    late_sum()
    for half in range(2):
        for kind in range(2):
            keep(half, kind).wait()
            for j in range(1, INNER):
                back(j, half, kind).wait_recv()
    ungroup_qkv(land, g_qkv)

    def vec_copy(k):
        return remote(vall.at[fpeers[k - 1][1]], vf.at[k - 1], vfs.at[k - 1], vfr.at[k - 1], fpeers[k - 1])

    def norm_back():
        e = nt(g_qkv[...], wbuf[...])
        x = tokens[...].astype(F32)
        center = x - jnp.mean(x, axis=-1, keepdims=True)
        r = lax.rsqrt(jnp.mean(center * center, axis=-1, keepdims=True) + EPS)
        xh = center * r
        t = e * gain[0:1, :]
        o_in[...] = g_hid[...] + r * (t - jnp.mean(t, axis=-1, keepdims=True)
                                      - xh * jnp.mean(t * xh, axis=-1, keepdims=True))
        vall[...] = v_ref[...]
        gq = g_qkv[:, :width].astype(F32)
        gv = g_qkv[:, 2 * width:].astype(F32)
        for row, val in enumerate((e * xh, e, gq, gv)):
            line = jnp.sum(val, axis=0, keepdims=True)
            for i in range(fs):
                vall[i, row:row + 1, :] = line[:, i * part:(i + 1) * part]

    for name in ("w", "tok", "hid"):
        loads[name].wait()
    norm_back()
    for k in range(1, fs):
        go(vec_copy(k))

    def vec_to(peers, buf, at, ssem, rsem):
        return [remote(buf.at[at], buf.at[at], ssem.at[k], rsem.at[k], peer) for k, peer in enumerate(peers)]

    def vec_total(buf, count):
        tot = buf[0]
        for k in range(1, count):
            tot = tot + buf[k]
        return tot

    def vec_plane():
        for k in range(1, fs):
            vec_copy(k).wait_recv()
        tot = vall[f]
        for k in range(fs - 1):
            tot = tot + vf[k]
        vx[h] = tot
        for cp in vec_to(hpeers, vx, h, vxs, vxr):
            go(cp)

    def vec_line():
        for cp in vec_to(hpeers, vx, h, vxs, vxr):
            cp.wait_recv()
        vr[z] = vec_total(vx, INNER)
        for cp in vec_to(zpeers, vr, z, vrs, vrr):
            go(cp)

    def vec_end():
        for cp in vec_to(zpeers, vr, z, vrs, vrr):
            cp.wait_recv()
        vout_ref[...] = vec_total(vr, depth)

    small = [vec_plane, vec_line, vec_end]
    outs = []

    def flush(src, size, dst, u):
        cp = pltpu.make_async_copy(outb.at[pl.ds(src, size)], dst, osem.at[u])
        cp.start()
        outs.append(cp)

    late = [functools.partial(late_forward, k) for k in range(1, depth)]
    i = 0
    while fc or late or small:
        some(2)
        if late:
            late.pop(0)()
        if small:
            small.pop(0)()
    late_end()
    for st in (sb, sa):
        cross_wait(st)
    for u in range(4):
        flush(bases_of[0] + u * part, part, o_fc1.at[:, pl.ds(u * width, width)], u)
        flush(bases_of[1] + u * part, part, o_fc2.at[pl.ds(u * part, part)], 4 + u)
    for i in range(2):
        flush(bases_of[i] + 4 * part, half_part, o_out.at[pl.ds(i * half_part, half_part)], 8 + i)
    for cp in pend:
        cp.wait_send()

    @pl.loop(1, depth)
    def _(step):
        valid = (z - step >= 0, z + step <= depth - 1)
        for half in range(2):
            @pl.when(valid[half])
            def _():
                pass_on(half, step).wait_send()
    for cp in outs:
        cp.wait()


def block_back(starts, do, kept, lse, ops, w_one, tokens, g_hid, gain, v, length, cid):
    qb, kv, ot = kept
    fs = lax.axis_size("fsdp")
    depth = lax.axis_size("ctx") // INNER
    n = lax.axis_size("ctx") // 2
    toks, width = do.shape
    blk = toks // 2
    rows = INNER * blk
    part = width // fs
    big = region_rows(4 * part + part // 2, n)
    tot = 2 * big
    zchunk = -(-part // (16 * depth)) * 16
    zrows = zchunk * depth
    slots = min(fs - 1, 2)
    vs = v.shape[1:]
    dma = pltpu.SemaphoreType.DMA
    vm = pl.BlockSpec(memory_space=pltpu.VMEM)
    anyspec = pl.BlockSpec(memory_space=pl.ANY)
    ins = (do, qb, kv, ot, lse) + tuple(ops) + (w_one, tokens, g_hid)
    order = [do, qb, kv, ot, lse] + list(ops) + [w_one, tokens, g_hid]
    cfg = (depth, length, n, fs, big, zrows)
    return pl.pallas_call(
        functools.partial(back_kernel, cfg),
        out_shape=(jax.ShapeDtypeStruct((part, 3 * width), BF), jax.ShapeDtypeStruct((part, width), BF),
                   jax.ShapeDtypeStruct((part, 4 * width), BF), jax.ShapeDtypeStruct((4 * part, width), BF),
                   jax.ShapeDtypeStruct(vs, F32), jax.ShapeDtypeStruct((toks, width), F32)),
        in_specs=[pl.BlockSpec(memory_space=pltpu.SMEM)] + [anyspec] * len(ins) + [vm, vm],
        out_specs=(anyspec, anyspec, anyspec, anyspec, vm, vm),
        scratch_shapes=[pltpu.VMEM(a.shape, a.dtype) for a in order] + [
            pltpu.VMEM((toks, INNER * QW), BF),
            pltpu.VMEM((2, rows, QW), BF),
            pltpu.VMEM((2, 8, rows), F32),
            pltpu.VMEM((2, 3 * HD, rows), F32),
            pltpu.VMEM((2, rows, KW), F32),
            pltpu.VMEM((2, depth, rows, KW), BF),
            pltpu.VMEM((2, rows, QW), BF),
            pltpu.VMEM((2, rows, KW), BF),
            pltpu.VMEM((toks, INNER * GW), BF),
            pltpu.VMEM((toks, 3 * width), BF),
            pltpu.VMEM((6 * width, toks), BF),
            pltpu.VMEM((width, 2 * rows), BF),
            pltpu.VMEM((slots, tot, width), BF),
            pltpu.VMEM((tot, width), BF),
            pltpu.VMEM((fs - 1, 9 * part, width), BF),
            pltpu.VMEM((big // 2, width), BF), pltpu.VMEM((big // 2, width), BF),
            pltpu.VMEM((n - 1, big // 2 // n, width), BF), pltpu.VMEM((n - 1, big // 2 // n, width), BF),
            pltpu.VMEM((slots, part, GW), BF),
            pltpu.VMEM((zrows, GW), BF),
            pltpu.VMEM((fs - 1, part, GW), BF),
            pltpu.VMEM((depth, zchunk, GW), BF),
            pltpu.VMEM((INNER, zrows, GW), BF),
            pltpu.VMEM((part, 3 * width), BF),
            pltpu.VMEM((fs,) + vs, F32),
            pltpu.VMEM((fs - 1,) + vs, F32),
            pltpu.VMEM((INNER,) + vs, F32),
            pltpu.VMEM((depth,) + vs, F32),
            dma((15,)), dma((6,)), dma((2, 3)), dma((2, 3)), dma((2, depth)), dma((2, depth)),
            dma((2, 3)), dma((2, 3)), dma((2, 3)), dma((2, 3)),
            dma((fs - 1, 2)), dma((fs - 1, 2)), dma((2,)), dma((2,)),
            dma((2, 2, 2, n - 1, 2)), dma((2, 2, 2, n - 1, 2)), dma((2, 2, n)), dma((2, 2, n)),
            dma((fs - 1,)), dma((fs - 1,)), dma((depth - 1,)), dma((depth - 1,)), dma((depth - 1,)), dma((depth - 1,)),
            dma((INNER - 1, depth)), dma((INNER - 1, depth)),
            dma((fs - 1,)), dma((fs - 1,)), dma((INNER - 1,)), dma((INNER - 1,)), dma((depth - 1,)), dma((depth - 1,)), dma((12,)),
        ],
        compiler_params=pltpu.CompilerParams(collective_id=cid, has_side_effects=True, vmem_limit_bytes=62 << 20),
        name="block_back",
    )(starts, *ins, gain, v)


def middle_kernel(fs, attn, tok, cot, vec, c_one, w_out_h, w_one_h, w_two_h,
                  o_layer, o_mid, o_pre, o_act, o_hid, o_branch, o_attn, o_vec,
                  w_out, w_one, w_two, hidden, acc, e_acc, line, b_pre, b_act, b_mid, osem, sem):
    width = attn.shape[1]
    part = width // fs
    first = pltpu.make_async_copy(w_out_h, w_out, sem.at[0])
    first.start()
    ones, twos = [], []
    for j in range(4):
        ones.append(pltpu.make_async_copy(w_one_h.at[:, pl.ds(j * width, width)], w_one.at[j], sem.at[1 + j]))
        twos.append(pltpu.make_async_copy(w_two_h.at[pl.ds(j * width, width)], w_two.at[j], sem.at[5 + j]))
        ones[j].start()
        twos[j].start()
    g = cot[...]
    first.wait()
    hid = tok[...].astype(F32) + nn(attn[...], w_out[...]) + vec[4:5, :]
    hidden[...] = hid
    center = hid - jnp.mean(hid, axis=-1, keepdims=True)
    r = lax.rsqrt(jnp.mean(center * center, axis=-1, keepdims=True) + EPS)
    b_mid[...] = (center * r * vec[5:6, :] + vec[6:7, :]).astype(BF)
    outs = [pltpu.make_async_copy(b_mid, o_mid, osem.at[0])]
    outs[0].start()
    root = (2.0 / jnp.pi) ** 0.5
    for j in range(4):
        lanes = slice(j * width, (j + 1) * width)
        ones[j].wait()
        twos[j].wait()
        p = nn(b_mid[...], w_one[j]) + c_one[:, lanes]
        t = jnp.tanh(root * (p + 0.044715 * (p * p * p)))
        act = (0.5 * p * (1.0 + t)).astype(BF)
        slope = 0.5 * (1.0 + t) + 0.5 * p * (1.0 - t * t) * (root * (1.0 + 3 * 0.044715 * (p * p)))
        b_act[:, lanes] = act
        gp = (nt(g, w_two[j]) * slope).astype(BF)
        b_pre[:, lanes] = gp
        for i, (src, dst) in enumerate(((b_act, o_act), (b_pre, o_pre))):
            outs.append(pltpu.make_async_copy(src.at[:, lanes], dst.at[:, lanes], osem.at[1 + 2 * j + i]))
            outs[-1].start()
        line[:, lanes] = jnp.sum(gp.astype(F32), axis=0, keepdims=True)
        add = nn(act, w_two[j])
        back = nt(gp, w_one[j])
        if j == 0:
            acc[...] = add
            e_acc[...] = back
        else:
            acc[...] = acc[...] + add
            e_acc[...] = e_acc[...] + back
    o_layer[...] = (hidden[...] + acc[...] + vec[7:8, :]).astype(BF)
    hid = hidden[...]
    center = hid - jnp.mean(hid, axis=-1, keepdims=True)
    r = lax.rsqrt(jnp.mean(center * center, axis=-1, keepdims=True) + EPS)
    xh = center * r
    e = e_acc[...]
    t = e * vec[5:6, :]
    gf = g.astype(F32)
    grad = gf + r * (t - jnp.mean(t, axis=-1, keepdims=True) - xh * jnp.mean(t * xh, axis=-1, keepdims=True))
    o_hid[...] = grad
    branch = grad.astype(BF)
    o_branch[...] = branch
    o_attn[...] = nt(branch, w_out[...]).astype(BF)
    o_vec[...] = jnp.zeros_like(o_vec)
    for row, val in ((4, branch.astype(F32)), (5, e * xh), (6, e), (7, gf)):
        total = jnp.sum(val, axis=0, keepdims=True)
        for i in range(fs):
            o_vec[i, row:row + 1, :] = total[:, i * part:(i + 1) * part]
    for i in range(fs):
        for j in range(4):
            o_vec[i, 8 + j:9 + j, :] = line[:, (4 * i + j) * part:(4 * i + j + 1) * part]
    for cp in outs:
        cp.wait()


def middle(attn, tok, cot, vec, c_one, w_out, w_one, w_two):
    fs = lax.axis_size("fsdp")
    toks, width = tok.shape
    full = jax.ShapeDtypeStruct((toks, width), BF)
    wide = jax.ShapeDtypeStruct((toks, 4 * width), BF)
    vm = pl.BlockSpec(memory_space=pltpu.VMEM)
    anyspec = pl.BlockSpec(memory_space=pl.ANY)
    return pl.pallas_call(
        functools.partial(middle_kernel, fs),
        out_shape=(full, full, wide, wide, jax.ShapeDtypeStruct((toks, width), F32), full, full,
                   jax.ShapeDtypeStruct((fs, 16, width // fs), F32)),
        in_specs=[vm] * 5 + [anyspec] * 3,
        out_specs=(vm, anyspec, anyspec, anyspec, vm, vm, vm, vm),
        scratch_shapes=[
            pltpu.VMEM((width, width), BF),
            pltpu.VMEM((4, width, width), BF),
            pltpu.VMEM((4, width, width), BF),
            pltpu.VMEM((toks, width), F32),
            pltpu.VMEM((toks, width), F32),
            pltpu.VMEM((toks, width), F32),
            pltpu.VMEM((1, 4 * width), F32),
            pltpu.VMEM((toks, 4 * width), BF),
            pltpu.VMEM((toks, 4 * width), BF),
            pltpu.VMEM((toks, width), BF),
            pltpu.SemaphoreType.DMA((9,)),
            pltpu.SemaphoreType.DMA((9,)),
        ],
        compiler_params=pltpu.CompilerParams(vmem_limit_bytes=62 << 20),
        name="middle",
    )(attn, tok, cot, vec, c_one, w_out, w_one, w_two)


def per_device(
    stream,
    doc_starts,
    ln1_gain,
    ln1_bias,
    qkv_weight,
    q_bias,
    v_bias,
    out_weight,
    out_bias,
    ln2_gain,
    ln2_bias,
    fc1_weight,
    fc1_bias,
    fc2_weight,
    fc2_bias,
    cotangent,
):
    length = lax.axis_size("ctx") * stream.shape[1]
    part = ln1_gain.shape[0]
    lines = [one.reshape(-1, part) for one in (ln1_gain, ln1_bias, q_bias, v_bias, out_bias, ln2_gain, ln2_bias, fc2_bias,
                                               fc1_bias)]
    v_shard = jnp.concatenate(lines + [jnp.zeros((4, part), BF)], axis=0).astype(F32)
    w_out = lax.all_gather(out_weight, "fsdp", axis=0, tiled=True)
    w_one = lax.all_gather(fc1_weight, "fsdp", axis=0, tiled=True)
    w_two = lax.all_gather(fc2_weight, "fsdp", axis=0, tiled=True)
    tokens, cot = stream[0], cotangent[0]
    attn, normed_group, vec, c_one, w_qkv, q_kept, kv_kept, out_kept, lse = attend(
        doc_starts, tokens, v_shard, qkv_weight, length, 1
    )
    layer_out, normed_mid, grad_pre, activ, grad_hidden, grad_branch, grad_attn, v_part = middle(
        attn, tokens, cot, vec, c_one, w_out, w_one, w_two
    )
    t_qkv, t_out, t_fc1, t_fc2, total, input_grad = block_back(
        doc_starts, grad_attn, (q_kept, kv_kept, out_kept), lse,
        (normed_group, attn, grad_branch, normed_mid, grad_pre, activ, cot),
        w_qkv, tokens, grad_hidden, vec, v_part, length, 0,
    )
    return (
        layer_out[None], input_grad[None], total[0], total[1], t_qkv.astype(F32), total[2], total[3], t_out.astype(F32),
        total[4], total[5], total[6], t_fc1.astype(F32), total[8:12].reshape(-1), t_fc2.astype(F32), total[7],
    )


def solution(mesh):
    in_specs = (
        P("fsdp", "ctx", None),
        P("fsdp", None),
        P("fsdp"),
        P("fsdp"),
        P("fsdp", None),
        P("fsdp"),
        P("fsdp"),
        P("fsdp", None),
        P("fsdp"),
        P("fsdp"),
        P("fsdp"),
        P("fsdp", None),
        P("fsdp"),
        P("fsdp", None),
        P("fsdp"),
        P("fsdp", "ctx", None),
    )
    out_specs = (
        P("fsdp", "ctx", None),
        P("fsdp", "ctx", None),
        P("fsdp"),
        P("fsdp"),
        P("fsdp", None),
        P("fsdp"),
        P("fsdp"),
        P("fsdp", None),
        P("fsdp"),
        P("fsdp"),
        P("fsdp"),
        P("fsdp", None),
        P("fsdp"),
        P("fsdp", None),
        P("fsdp"),
    )
    return jax.shard_map(
        per_device, mesh=mesh, in_specs=in_specs, out_specs=out_specs, check_vma=False
    )
```
